32 devices in a mesh: stream: 4 (over y, x), ctx: 4 (over z), head: 2 (over core).
Axes of the slice: x: 2, y: 2, z: 4, core: 2. Of those that a mesh axis runs over, the one named last changes fastest.
Arguments:
- tokens: bfloat16 [4, 1024, 2048], P('stream', 'ctx'), may hold values from -6 to 6
- doc_lengths: int32 [4, 6], P('stream'), may hold values from 1 to 512, 1024 in all within a row
- ln1_gain: bfloat16 [2048], replicated, may hold values from 0.25 to 1.75
- ln1_bias: bfloat16 [2048], replicated, may hold values from -1.5 to 1.5
- qkv_weight: bfloat16 [3, 2048, 2048], P(None, 'ctx', 'head'), may hold values from -0.125 to 0.125
- qkv_bias: bfloat16 [3, 2048], P(None, 'head'), may hold values from -0.5 to 0.5
- out_weight: bfloat16 [2048, 2048], P('head', 'ctx'), may hold values from -1 to 1
- out_bias: bfloat16 [2048], replicated, may hold values from -3 to 3
- ln2_gain: bfloat16 [2048], replicated, may hold values from 0.25 to 1.75
- ln2_bias: bfloat16 [2048], replicated, may hold values from -1.5 to 1.5
- up_weight: bfloat16 [2048, 8192], P('ctx', 'head'), may hold values from -0.125 to 0.125
- up_bias: bfloat16 [8192], P('head'), may hold values from -1.5 to 1.5
- down_weight: bfloat16 [8192, 2048], P('head', 'ctx'), may hold values from -0.0625 to 0.0625
- down_bias: bfloat16 [2048], replicated, may hold values from -3 to 3
- cotangent: bfloat16 [4, 1024, 2048], P('stream', 'ctx'), may hold values from -6 to 6
Outputs:
- output: bfloat16 [4, 1024, 2048], P('stream', 'ctx')
- input_grad: float32 [4, 1024, 2048], P('stream', 'ctx')
- ln1_gain_grad: float32 [2048], replicated
- ln1_bias_grad: float32 [2048], replicated
- qkv_weight_grad: float32 [3, 2048, 2048], P(None, 'ctx', 'head')
- qkv_bias_grad: float32 [3, 2048], P(None, 'head')
- out_weight_grad: float32 [2048, 2048], P('head', 'ctx')
- out_bias_grad: float32 [2048], replicated
- ln2_gain_grad: float32 [2048], replicated
- ln2_bias_grad: float32 [2048], replicated
- up_weight_grad: float32 [2048, 8192], P('ctx', 'head')
- up_bias_grad: float32 [8192], P('head')
- down_weight_grad: float32 [8192, 2048], P('head', 'ctx')
- down_bias_grad: float32 [2048], replicated
The draws below stay inside these ranges and needn't reach their ends.
Inputs may be any that keep to these rules, and one draw needn't show every extreme that they name: `doc_lengths`: each sequence's 6 document lengths sum to 1024, the documents lie end to end in the given order, and the longest has exactly 512 tokens.
All inputs are finite; a program needn't handle non-finite values.
Results may differ from the reference program's by a relative error of at most 0.025.
Values may be sent and summed in bfloat16 or wider, within the bound.
A program may use at most 256 MiB of HBM per device.

```python
import math
import jax
import jax.numpy as jnp
import numpy as np
from jax import lax

D = 2048
HEADS = 8
HEAD = 256
ROT = 64
FF = 8192
NDOCS = 6
SEQS = 4
SEQ = 1024
DOC_MAX = 512


def strengthened(values, own_key, source, target, shards_of, factor):
    def block_of(dim):
        return (jnp.arange(values.shape[dim]) // (values.shape[dim] // shards_of)).reshape((-1,) + (1,) * (values.ndim - 1 - dim))

    first = jax.random.permutation(own_key, shards_of)[block_of(target)]
    second = (block_of(target) + shards_of // 2) % shards_of
    return jnp.where((block_of(source) == first) | (block_of(source) == second), factor * values, values)


def block_levels(rng, extent, split, smallest, high):
    def one(axis_at, shards_of):
        heights = jax.random.uniform(jax.random.fold_in(jax.random.fold_in(rng, 6), axis_at), (shards_of,), jnp.float32, smallest / len(split), high / len(split))
        return jnp.repeat(jnp.exp(heights), extent[axis_at] // shards_of).reshape((-1,) + (1,) * (len(extent) - axis_at - 1))

    factor_of = one(*split[0])
    for cut in split[1:]:
        factor_of = factor_of * one(*cut)
    return factor_of


def profile(amount, total, bound, lean):
    portions = [(1 << 20) // math.isqrt(rank ** lean) + 1 for rank in range(2, amount + 1)]
    surplus, holding = total - bound - (amount - 1), [1] * (amount - 1)
    while surplus > 0:
        movable = [i for i in range(amount - 1) if holding[i] < bound]
        mass, left = sum([portions[i] for i in movable]), surplus
        for i in movable:
            extra = min(bound - holding[i], max(1, left * portions[i] // mass), surplus)
            holding[i] = holding[i] + extra
            surplus = surplus - extra
    return np.array([bound] + holding)


def ragged(own_key, number_of, total, reach, lean):
    if number_of == 2:
        one = jax.random.randint(own_key, (), max(1, total - reach), min(reach, total - 1) + 1)
        return jnp.stack([one, total - one])
    tallies = jnp.asarray(profile(number_of, total, reach, lean), jnp.int32)
    couples = (number_of - 1) // 2
    source_of, sink = tallies[1:1 + 2 * couples:2], tallies[2:2 + 2 * couples:2]
    room = jnp.minimum(source_of - 1, reach - sink)
    moved = jax.random.randint(jax.random.fold_in(own_key, 1), (couples,), 0, 1 << 20) % (room + 1)
    tallies = tallies.at[1:1 + 2 * couples:2].set(source_of - moved).at[2:2 + 2 * couples:2].set(sink + moved)
    return tallies[jax.random.permutation(jax.random.fold_in(own_key, 2), number_of)]


def noise(own_key, dims, width, most, shards=(), held_as=jnp.bfloat16):
    values = width * jax.random.normal(own_key, dims, jnp.float32)
    if shards:
        values = values * block_levels(own_key, dims, shards, -0.22, 0.18)
    return jnp.clip(values, -most, most).astype(held_as)


def bell_draw_with(own_key, dims, deviation, limit, shards, heavy, kind=jnp.bfloat16):
    entries = deviation * jax.random.normal(own_key, dims, jnp.float32)
    if shards:
        entries = entries * block_levels(own_key, dims, shards, -0.22, 0.18)
    return jnp.clip(strengthened(entries, jax.random.fold_in(own_key, 3), *heavy), -limit, limit).astype(kind)


def setup_inputs(seed: int = 0) -> dict:
    key_list = jax.random.split(jax.random.key(seed), 16)
    tokens = noise(key_list[0], (SEQS, SEQ, D), 1.0, 6.0, ((0, 4), (1, 4)))
    doc_lengths = jax.vmap(lambda own: ragged(own, NDOCS, SEQ, DOC_MAX, 1))(jax.random.split(key_list[1], SEQS)).reshape((SEQS, NDOCS)).astype(jnp.int32)
    ln1_gain = jnp.clip(1.0 + 0.15 * jax.random.normal(key_list[2], (D,), jnp.float32), 0.25, 1.75).astype(jnp.bfloat16)
    ln1_bias = noise(key_list[3], (D,), 0.3, 1.5)
    qkv_weight = noise(key_list[4], (3, D, D), D ** -0.5, 0.125, ((1, 4), (2, 2)))
    qkv_bias = noise(key_list[5], (3, D), 0.1, 0.5, ((1, 2),))
    out_weight = noise(key_list[6], (D, D), (D // 64) ** -0.5, 1.0, ((0, 2), (1, 4)))
    out_bias = noise(key_list[7], (D,), 0.6, 3.0)
    ln2_gain = jnp.clip(1.0 + 0.15 * jax.random.normal(key_list[8], (D,), jnp.float32), 0.25, 1.75).astype(jnp.bfloat16)
    ln2_bias = noise(key_list[9], (D,), 0.3, 1.5)
    up_weight = noise(key_list[10], (D, FF), D ** -0.5, 0.125, ((0, 4), (1, 2)))
    up_bias = noise(key_list[11], (FF,), 0.3, 1.5, ((0, 2),))
    down_weight = noise(key_list[12], (FF, D), FF ** -0.5, 0.0625, ((0, 2), (1, 4)))
    down_bias = noise(key_list[13], (D,), 0.6, 3.0)
    cotangent = bell_draw_with(key_list[14], (SEQS, SEQ, D), 1.0, 6.0, ((0, 4), (1, 4)), (1, 2, 4, 2.0))
    return {"tokens": tokens, "doc_lengths": doc_lengths, "ln1_gain": ln1_gain, "ln1_bias": ln1_bias, "qkv_weight": qkv_weight, "qkv_bias": qkv_bias, "out_weight": out_weight, "out_bias": out_bias, "ln2_gain": ln2_gain, "ln2_bias": ln2_bias, "up_weight": up_weight, "up_bias": up_bias, "down_weight": down_weight, "down_bias": down_bias, "cotangent": cotangent}


@jax.custom_vjp
def low(v):
    return lax.optimization_barrier(v.astype(jnp.bfloat16)).astype(jnp.float32)

@jax.custom_vjp
def low_back(v):
    return v

def low_keep(v):
    return (low(v), None)

def low_pass(kept, grad):
    return (grad,)

def back_keep(v):
    return (v, None)

def back_low(kept, grad):
    return (low(grad),)
low.defvjp(low_keep, low_pass)
low_back.defvjp(back_keep, back_low)

def layer_norm(values, gain, offset):
    centre = lax.optimization_barrier(jnp.mean(values, axis=-1, keepdims=True))
    centred = values - centre
    spread = lax.optimization_barrier(jnp.mean(centred * centred, axis=-1, keepdims=True))
    return centred * lax.rsqrt(spread + 1e-05) * gain + offset

def rotary(values, angles):
    half = angles.shape[-1]
    cosine = jnp.cos(angles)[:, None, :]
    sine = jnp.sin(angles)[:, None, :]
    first = values[..., :half]
    second = values[..., half:2 * half]
    return jnp.concatenate([first * cosine - second * sine, second * cosine + first * sine, values[..., 2 * half:]], axis=-1)

def doc_starts(doc_sizes, positions):
    ends = jnp.cumsum(doc_sizes)
    starts = ends - doc_sizes
    return lax.optimization_barrier(jnp.max(jnp.where(starts[None, :] <= positions[:, None], starts[None, :], 0), axis=1))

def stream_forward(inputs, doc_sizes, weights):
    ln1_gain, ln1_bias, qkv_weight, qkv_bias, out_weight, out_bias, ln2_gain, ln2_bias, up_weight, up_bias, down_weight, down_bias = weights
    highest = lax.Precision.HIGHEST
    count = inputs.shape[0]
    positions = jnp.arange(count, dtype=jnp.int32)
    starts = doc_starts(doc_sizes, positions)
    frequency = 10000.0 ** (-jnp.arange(0, ROT, 2, dtype=jnp.float32) / ROT)
    angles = (positions - starts).astype(jnp.float32)[:, None] * frequency[None, :]
    normed_one = low(layer_norm(inputs, ln1_gain, ln1_bias))
    normed_two = low(layer_norm(inputs, ln2_gain, ln2_bias))
    projected = low_back(jnp.einsum('nd,cde->cne', normed_one, qkv_weight, precision=highest) + qkv_bias[:, None, :])
    query = low(rotary(projected[0].reshape(count, HEADS, HEAD), angles))
    keys = low(rotary(projected[1].reshape(count, HEADS, HEAD), angles))
    values = low(projected[2].reshape(count, HEADS, HEAD))
    scale = HEAD ** (-0.5)
    block = math.gcd(count, 512)
    block_count = count // block

    def attend(item):
        query_block, index_block, start_block = item
        scores = low_back(jnp.einsum('qhe,khe->hqk', query_block, keys, precision=highest) * scale)
        allowed = (positions[None, :] <= index_block[:, None]) & (positions[None, :] >= start_block[:, None])
        masked = jnp.where(allowed[None], scores, -1e+30)
        peak = lax.optimization_barrier(jnp.max(masked, axis=-1, keepdims=True))
        raised = jnp.where(allowed[None], jnp.exp(masked - peak), 0.0)
        shares = low(raised / lax.optimization_barrier(jnp.sum(raised, axis=-1, keepdims=True)))
        return jnp.einsum('hqk,khe->qhe', shares, values, precision=highest)
    mixed = lax.map(jax.checkpoint(attend), (query.reshape(block_count, block, HEADS, HEAD), positions.reshape(block_count, block), starts.reshape(block_count, block)))
    mixed = low(low_back(mixed.reshape(count, D)))
    attention = jnp.dot(mixed, out_weight, precision=highest)
    hidden = low_back(jnp.dot(normed_two, up_weight, precision=highest) + up_bias)
    activated = low(jax.nn.gelu(hidden, approximate=False))
    feed = jnp.dot(activated, down_weight, precision=highest)
    return inputs + attention + out_bias + feed + down_bias

def reference(tokens, doc_lengths, ln1_gain, ln1_bias, qkv_weight, qkv_bias, out_weight, out_bias, ln2_gain, ln2_bias, up_weight, up_bias, down_weight, down_bias, cotangent):
    params = tuple((param.astype(jnp.float32) for param in (ln1_gain, ln1_bias, qkv_weight, qkv_bias, out_weight, out_bias, ln2_gain, ln2_bias, up_weight, up_bias, down_weight, down_bias)))

    def forward_all(inputs, *weights):

        def one_sequence(pair):
            return stream_forward(pair[0], pair[1], weights)
        return lax.map(one_sequence, (inputs, doc_lengths))
    outputs, pull_back = jax.vjp(forward_all, tokens.astype(jnp.float32), *params)
    grads = pull_back(cotangent.astype(jnp.float32))
    return (outputs.astype(jnp.bfloat16), grads[0], grads[1], grads[2], grads[3], grads[4], grads[5], grads[6], grads[7], grads[8], grads[9], grads[10], grads[11], grads[12])
```

```python
from functools import partial
import math

import jax
import jax.numpy as jnp
from jax import lax
from jax.sharding import PartitionSpec as P

HEAD = 256
ROT = 64


def layer_norm(values, gain, offset):
    centre = jnp.mean(values, axis=-1, keepdims=True)
    centred = values - centre
    spread = jnp.mean(centred * centred, axis=-1, keepdims=True)
    return centred * lax.rsqrt(spread + 1e-05) * gain + offset


def rotary(values, angles):
    half = angles.shape[-1]
    cosine = jnp.cos(angles)[:, None, :]
    sine = jnp.sin(angles)[:, None, :]
    first = values[..., :half]
    second = values[..., half : 2 * half]
    return jnp.concatenate(
        [first * cosine - second * sine, second * cosine + first * sine, values[..., 2 * half :]],
        axis=-1,
    )


def doc_starts(doc_sizes, positions):
    place = jnp.arange(doc_sizes.shape[0])
    before = place[None, :] < place[:, None]
    starts = jnp.sum(jnp.where(before, doc_sizes[None, :], 0), axis=1)
    return jnp.max(jnp.where(starts[None, :] <= positions[:, None], starts[None, :], 0), axis=1)


def general_device(
    tokens,
    doc_lengths,
    ln1_gain,
    ln1_bias,
    qkv_weight,
    qkv_bias,
    out_weight,
    out_bias,
    ln2_gain,
    ln2_bias,
    up_weight,
    up_bias,
    down_weight,
    down_bias,
    cotangent,
):
    inputs = tokens[0].astype(jnp.float32)
    count = inputs.shape[0]
    ctx_count = lax.axis_size("ctx")
    length = count * ctx_count
    positions = lax.axis_index("ctx") * count + jnp.arange(count, dtype=jnp.int32)
    starts = doc_starts(doc_lengths[0], positions)
    frequency = 10000.0 ** (-jnp.arange(0, ROT, 2, dtype=jnp.float32) / ROT)
    angles = (positions - starts).astype(jnp.float32)[:, None] * frequency[None, :]
    scale = HEAD ** (-0.5)
    full_qkv, full_out, full_up, full_down = (
        lax.all_gather(qkv_weight, "ctx", axis=1, tiled=True),
        lax.all_gather(out_weight, "ctx", axis=1, tiled=True),
        lax.all_gather(up_weight, "ctx", axis=0, tiled=True),
        lax.all_gather(down_weight, "ctx", axis=1, tiled=True),
    )
    gain_one = ln1_gain.astype(jnp.float32)
    offset_one = ln1_bias.astype(jnp.float32)
    gain_two = ln2_gain.astype(jnp.float32)
    offset_two = ln2_bias.astype(jnp.float32)
    low_one = layer_norm(inputs, gain_one, offset_one).astype(jnp.bfloat16)
    low_two = layer_norm(inputs, gain_two, offset_two).astype(jnp.bfloat16)
    projected = (
        jnp.einsum("nd,cde->cne", low_one, full_qkv, preferred_element_type=jnp.float32)
        + qkv_bias.astype(jnp.float32)[:, None, :]
    )
    width = projected.shape[2]
    local_heads = width // HEAD
    query = rotary(projected[0].reshape(count, local_heads, HEAD), angles).astype(jnp.bfloat16)
    keys_flat = (
        rotary(projected[1].reshape(count, local_heads, HEAD), angles)
        .reshape(count, width)
        .astype(jnp.bfloat16)
    )
    values_flat = projected[2].astype(jnp.bfloat16)
    all_keys, all_values = (
        lax.all_gather(keys_flat, "ctx", axis=0, tiled=True),
        lax.all_gather(values_flat, "ctx", axis=0, tiled=True),
    )
    block = math.gcd(length, 512)
    block_count = length // block
    key_blocks = all_keys.reshape(block_count, block, local_heads, HEAD)
    value_blocks = all_values.reshape(block_count, block, local_heads, HEAD)
    firsts = jnp.arange(block_count, dtype=jnp.int32) * block

    def block_scores(key_block, first):
        key_index = first + jnp.arange(block, dtype=jnp.int32)
        allowed = (key_index[None, :] <= positions[:, None]) & (
            key_index[None, :] >= starts[:, None]
        )
        scores = (
            jnp.einsum("qhe,khe->hqk", query, key_block, preferred_element_type=jnp.float32) * scale
        )
        return (jnp.where(allowed[None], scores, -1e30), allowed[None])

    def statistics(carry, item):
        running, norm_sum = carry
        key_block, first = item
        masked, allowed = block_scores(key_block, first)
        newest = jnp.maximum(running, jnp.max(masked, axis=-1))
        raised = jnp.where(allowed, jnp.exp(masked - newest[..., None]), 0.0)
        norm_sum = norm_sum * jnp.exp(running - newest) + jnp.sum(raised, axis=-1)
        return ((newest, norm_sum), None)

    initial = (
        jnp.full((local_heads, count), -1e30, jnp.float32),
        jnp.zeros((local_heads, count), jnp.float32),
    )
    (running, norm_sum), _ = lax.scan(statistics, initial, (key_blocks, firsts))
    log_norm = running + jnp.log(norm_sum)

    def share_block(key_block, first):
        masked, allowed = block_scores(key_block, first)
        return jnp.where(allowed, jnp.exp(masked - log_norm[..., None]), 0.0)

    def accumulate(mixed, item):
        key_block, value_block, first = item
        shares_low = share_block(key_block, first).astype(jnp.bfloat16)
        return (
            mixed
            + jnp.einsum(
                "hqk,khe->qhe", shares_low, value_block, preferred_element_type=jnp.float32
            ),
            None,
        )

    mixed, _ = lax.scan(
        accumulate,
        jnp.zeros((count, local_heads, HEAD), jnp.float32),
        (key_blocks, value_blocks, firsts),
    )
    mixed_low = mixed.reshape(count, width).astype(jnp.bfloat16)
    attention = jnp.dot(mixed_low, full_out, preferred_element_type=jnp.float32)
    hidden = jnp.dot(low_two, full_up, preferred_element_type=jnp.float32) + up_bias.astype(
        jnp.float32
    )
    activated = jax.nn.gelu(hidden, approximate=False).astype(jnp.bfloat16)
    branches = attention + jnp.dot(activated, full_down, preferred_element_type=jnp.float32)
    joint = lax.psum(branches.astype(jnp.bfloat16), "head").astype(jnp.float32)
    output = inputs + joint + out_bias.astype(jnp.float32) + down_bias.astype(jnp.float32)
    upstream = cotangent[0]
    down_grad = jnp.dot(activated.T, upstream, preferred_element_type=jnp.float32)
    activated_grad = jnp.dot(upstream, full_down.T, preferred_element_type=jnp.float32)
    _, gelu_back = jax.vjp(partial(jax.nn.gelu, approximate=False), hidden)
    hidden_grad = gelu_back(activated_grad)[0].astype(jnp.bfloat16)
    up_grad = jnp.dot(low_two.T, hidden_grad, preferred_element_type=jnp.float32)
    up_bias_grad = jnp.sum(hidden_grad.astype(jnp.float32), axis=0)
    normed_two_grad = jnp.dot(hidden_grad, full_up.T, preferred_element_type=jnp.float32)
    out_grad = jnp.dot(mixed_low.T, upstream, preferred_element_type=jnp.float32)
    mixed_grad = jnp.dot(upstream, full_out.T, preferred_element_type=jnp.float32).astype(
        jnp.bfloat16
    )
    mixed_grad_heads = mixed_grad.reshape(count, local_heads, HEAD)
    delta = jnp.sum(mixed_grad_heads.astype(jnp.float32) * mixed, axis=-1).T

    def backward_block(query_grad, item):
        key_block, value_block, first = item
        shares = share_block(key_block, first)
        share_grad = jnp.einsum(
            "qhe,khe->hqk", mixed_grad_heads, value_block, preferred_element_type=jnp.float32
        )
        score_grad = (shares * (share_grad - delta[..., None])).astype(jnp.bfloat16)
        query_grad = (
            query_grad
            + jnp.einsum("hqk,khe->qhe", score_grad, key_block, preferred_element_type=jnp.float32)
            * scale
        )
        key_grad = (
            jnp.einsum("hqk,qhe->khe", score_grad, query, preferred_element_type=jnp.float32)
            * scale
        )
        value_grad = jnp.einsum(
            "hqk,qhe->khe",
            shares.astype(jnp.bfloat16),
            mixed_grad_heads,
            preferred_element_type=jnp.float32,
        )
        return (
            query_grad,
            jnp.concatenate(
                [key_grad.reshape(block, width), value_grad.reshape(block, width)], axis=1
            ),
        )

    query_grad, key_terms = lax.scan(
        backward_block,
        jnp.zeros((count, local_heads, HEAD), jnp.float32),
        (key_blocks, value_blocks, firsts),
    )
    own_grads = lax.psum_scatter(
        key_terms.reshape(length, 2 * width).astype(jnp.bfloat16),
        "ctx",
        scatter_dimension=0,
        tiled=True,
    ).astype(jnp.float32)
    query_pre = rotary(query_grad, -angles).reshape(count, width)
    key_pre = rotary(own_grads[:, :width].reshape(count, local_heads, HEAD), -angles).reshape(
        count, width
    )
    projected_grad = jnp.stack([query_pre, key_pre, own_grads[:, width:]]).astype(jnp.bfloat16)
    qkv_grad = jnp.einsum(
        "nd,cne->cde", low_one, projected_grad, preferred_element_type=jnp.float32
    )
    qkv_bias_grad = jnp.sum(projected_grad.astype(jnp.float32), axis=1)
    normed_one_grad = jnp.einsum(
        "cne,cde->nd", projected_grad, full_qkv, preferred_element_type=jnp.float32
    )
    normed_one_grad, normed_two_grad = (
        lax.psum(normed_one_grad.astype(jnp.bfloat16), "head").astype(jnp.float32),
        lax.psum(normed_two_grad.astype(jnp.bfloat16), "head").astype(jnp.float32),
    )
    _, norm_back_one = jax.vjp(layer_norm, inputs, gain_one, offset_one)
    input_one, gain_grad_one, offset_grad_one = norm_back_one(normed_one_grad)
    _, norm_back_two = jax.vjp(layer_norm, inputs, gain_two, offset_two)
    input_two, gain_grad_two, offset_grad_two = norm_back_two(normed_two_grad)
    upstream_wide = upstream.astype(jnp.float32)
    input_grad = upstream_wide + input_one + input_two
    bias_grad = jnp.sum(upstream_wide, axis=0)
    small = lax.psum(
        (
            gain_grad_one,
            offset_grad_one,
            qkv_bias_grad,
            bias_grad,
            gain_grad_two,
            offset_grad_two,
            up_bias_grad,
        ),
        ("stream", "ctx"),
    )
    slices = (
        lax.psum_scatter(
            qkv_grad.astype(jnp.bfloat16), "ctx", scatter_dimension=1, tiled=True
        ).astype(jnp.float32),
        lax.psum_scatter(
            out_grad.astype(jnp.bfloat16), "ctx", scatter_dimension=1, tiled=True
        ).astype(jnp.float32),
        lax.psum_scatter(
            up_grad.astype(jnp.bfloat16), "ctx", scatter_dimension=0, tiled=True
        ).astype(jnp.float32),
        lax.psum_scatter(
            down_grad.astype(jnp.bfloat16), "ctx", scatter_dimension=1, tiled=True
        ).astype(jnp.float32),
    )
    shards = (
        lax.psum(slices[0].astype(jnp.bfloat16), "stream").astype(jnp.float32),
        lax.psum(slices[1].astype(jnp.bfloat16), "stream").astype(jnp.float32),
        lax.psum(slices[2].astype(jnp.bfloat16), "stream").astype(jnp.float32),
        lax.psum(slices[3].astype(jnp.bfloat16), "stream").astype(jnp.float32),
    )
    return (
        output.astype(jnp.bfloat16)[None],
        input_grad[None],
        small[0],
        small[1],
        shards[0],
        small[2],
        shards[1],
        small[3],
        small[4],
        small[5],
        shards[2],
        small[6],
        shards[3],
        small[3],
    )


def token_places(doc_sizes, length):
    positions = jnp.arange(length, dtype=jnp.int32)
    return positions, doc_starts(doc_sizes, positions)


def regroup(piece, axis):
    return lax.all_to_all(piece, "ctx", split_axis=0, concat_axis=axis, tiled=False)


def per_device(
    tokens,
    doc_lengths,
    ln1_gain,
    ln1_bias,
    qkv_weight,
    qkv_bias,
    out_weight,
    out_bias,
    ln2_gain,
    ln2_bias,
    up_weight,
    up_bias,
    down_weight,
    down_bias,
    cotangent,
):
    f32, bf16 = jnp.float32, jnp.bfloat16
    ctx_count, stream_count = lax.axis_size("ctx"), lax.axis_size("stream")
    head_count = lax.axis_size("head")
    c = lax.axis_index("ctx")
    h = lax.axis_index("head")
    count, model = tokens.shape[1], tokens.shape[2]
    length = count * ctx_count
    slab = model // ctx_count
    width = qkv_weight.shape[2] // ctx_count
    units = up_weight.shape[1] // ctx_count

    all_tokens = lax.all_gather(tokens[0], "ctx", axis=0, tiled=True)
    upstream = lax.all_gather(cotangent[0], "ctx", axis=0, tiled=True)
    w_qkv = regroup(
        qkv_weight.reshape(3, slab, ctx_count, width).transpose(2, 0, 1, 3), 1
    ).reshape(3, model, width)
    w_up = regroup(up_weight.reshape(slab, ctx_count, units).transpose(1, 0, 2), 0).reshape(
        model, units
    )
    w_out = regroup(out_weight.reshape(ctx_count, width, slab), 1).reshape(width, model)
    w_down = regroup(down_weight.reshape(ctx_count, units, slab), 1).reshape(units, model)

    gain_one, offset_one = ln1_gain.astype(f32), ln1_bias.astype(f32)
    gain_two, offset_two = ln2_gain.astype(f32), ln2_bias.astype(f32)
    wide = all_tokens.astype(f32)
    centred = wide - jnp.mean(wide, axis=-1, keepdims=True)
    scale_of = lax.rsqrt(jnp.mean(centred * centred, axis=-1, keepdims=True) + 1e-05)
    unit = centred * scale_of
    low_one = (unit * gain_one + offset_one).astype(bf16)
    low_two = (unit * gain_two + offset_two).astype(bf16)

    positions, starts = token_places(doc_lengths[0], length)
    frequency = 10000.0 ** (-jnp.arange(0, ROT, 2, dtype=f32) / ROT)
    angles = (positions - starts).astype(f32)[:, None] * frequency[None, :]
    bias = lax.dynamic_slice_in_dim(qkv_bias, c * width, width, 1).astype(f32)
    projected = jnp.einsum("nd,cde->cne", low_one, w_qkv, preferred_element_type=f32)
    projected = projected + bias[:, None, :]
    heads = width // HEAD
    query = rotary(projected[0].reshape(length, heads, HEAD), angles).astype(bf16)
    keys = rotary(projected[1].reshape(length, heads, HEAD), angles).astype(bf16)
    values = projected[2].reshape(length, heads, HEAD).astype(bf16)
    scale = HEAD ** (-0.5)
    allowed = (positions[None, :] <= positions[:, None]) & (positions[None, :] >= starts[:, None])
    scores = jnp.einsum("qhe,khe->hqk", query, keys, preferred_element_type=f32) * scale
    masked = jnp.where(allowed[None], scores, -1e30)
    raised = jnp.where(
        allowed[None], jnp.exp(masked - jnp.max(masked, axis=-1, keepdims=True)), 0.0
    )
    shares = raised / jnp.sum(raised, axis=-1, keepdims=True)
    shares_low = shares.astype(bf16)
    mixed = jnp.einsum("hqk,khe->qhe", shares_low, values, preferred_element_type=f32)
    mixed_low = mixed.reshape(length, width).astype(bf16)

    up_part = lax.dynamic_slice_in_dim(up_bias, c * units, units, 0).astype(f32)
    hidden = jnp.dot(low_two, w_up, preferred_element_type=f32) + up_part
    activated = jax.nn.gelu(hidden, approximate=False).astype(bf16)
    branches = jnp.dot(mixed_low, w_out, preferred_element_type=f32) + jnp.dot(
        activated, w_down, preferred_element_type=f32
    )

    _, gelu_back = jax.vjp(partial(jax.nn.gelu, approximate=False), hidden)
    activated_grad = jnp.dot(upstream, w_down.T, preferred_element_type=f32)
    hidden_grad = gelu_back(activated_grad)[0].astype(bf16)
    down_grad = jnp.dot(activated.T, upstream, preferred_element_type=f32)
    up_grad = jnp.dot(low_two.T, hidden_grad, preferred_element_type=f32)
    out_grad = jnp.dot(mixed_low.T, upstream, preferred_element_type=f32)
    mixed_grad = (
        jnp.dot(upstream, w_out.T, preferred_element_type=f32)
        .astype(bf16)
        .reshape(length, heads, HEAD)
    )
    delta = jnp.sum(mixed_grad.astype(f32) * mixed, axis=-1).T
    share_grad = jnp.einsum("qhe,khe->hqk", mixed_grad, values, preferred_element_type=f32)
    score_grad = (shares * (share_grad - delta[..., None])).astype(bf16)
    query_grad = (
        jnp.einsum("hqk,khe->qhe", score_grad, keys, preferred_element_type=f32) * scale
    )
    key_grad = jnp.einsum("hqk,qhe->khe", score_grad, query, preferred_element_type=f32) * scale
    value_grad = jnp.einsum("hqk,qhe->khe", shares_low, mixed_grad, preferred_element_type=f32)
    projected_grad = jnp.stack(
        [
            rotary(query_grad, -angles).reshape(length, width),
            rotary(key_grad, -angles).reshape(length, width),
            value_grad.reshape(length, width),
        ]
    ).astype(bf16)
    qkv_grad = jnp.einsum("nd,cne->cde", low_one, projected_grad, preferred_element_type=f32)
    normed_one_grad = jnp.einsum("cne,cde->nd", projected_grad, w_qkv, preferred_element_type=f32)
    normed_two_grad = jnp.dot(hidden_grad, w_up.T, preferred_element_type=f32)

    joint = lax.psum(
        lax.psum_scatter(branches.astype(bf16), "ctx", scatter_dimension=0, tiled=True), "head"
    ).astype(f32)
    inward = gain_one * normed_one_grad + gain_two * normed_two_grad
    inward = lax.psum(
        lax.psum_scatter(inward.astype(bf16), "ctx", scatter_dimension=0, tiled=True), "head"
    ).astype(f32)

    own = tokens[0].astype(f32)
    own_upstream = cotangent[0].astype(f32)
    output = own + joint + out_bias.astype(f32) + down_bias.astype(f32)
    own_centred = own - jnp.mean(own, axis=-1, keepdims=True)
    own_scale = lax.rsqrt(jnp.mean(own_centred * own_centred, axis=-1, keepdims=True) + 1e-05)
    own_unit = own_centred * own_scale
    input_grad = own_upstream + own_scale * (
        inward
        - jnp.mean(inward, axis=-1, keepdims=True)
        - own_unit * jnp.mean(inward * own_unit, axis=-1, keepdims=True)
    )

    bias_grad = jnp.sum(own_upstream, axis=0) * (1.0 / head_count)
    qkv_small = lax.dynamic_update_slice(
        jnp.zeros((3, head_count * ctx_count * width), f32),
        jnp.sum(projected_grad.astype(f32), axis=1),
        (0, (h * ctx_count + c) * width),
    )
    up_small = lax.dynamic_update_slice(
        jnp.zeros((head_count * ctx_count * units,), f32),
        jnp.sum(hidden_grad.astype(f32), axis=0),
        ((h * ctx_count + c) * units,),
    )
    small = lax.psum(
        (
            jnp.sum(normed_one_grad * unit, axis=0),
            jnp.sum(normed_one_grad, axis=0),
            qkv_small,
            bias_grad,
            jnp.sum(normed_two_grad * unit, axis=0),
            jnp.sum(normed_two_grad, axis=0),
            up_small,
        ),
        ("stream", "ctx", "head"),
    )
    qkv_bias_grad = lax.dynamic_slice_in_dim(small[2], h * ctx_count * width, ctx_count * width, 1)
    up_bias_grad = lax.dynamic_slice_in_dim(small[6], h * ctx_count * units, ctx_count * units, 0)

    def settle(grad):
        part = lax.psum_scatter(
            grad.astype(bf16), "stream", scatter_dimension=1, tiled=True
        )[:, 0]
        part = lax.all_to_all(part, "ctx", split_axis=0, concat_axis=0, tiled=True)
        return lax.all_gather(part, "stream", axis=1, tiled=False)

    n, k = ctx_count, stream_count
    qkv_out = settle(
        qkv_grad.reshape(3, n, k, slab // k, width).transpose(1, 2, 0, 3, 4)
    )
    qkv_out = qkv_out.transpose(2, 1, 3, 0, 4).reshape(3, slab, n * width)
    up_out = settle(up_grad.reshape(n, k, slab // k, units))
    up_out = up_out.transpose(1, 2, 0, 3).reshape(slab, n * units)
    out_out = settle(out_grad.reshape(k, width // k, n, slab).transpose(2, 0, 1, 3))
    out_out = out_out.reshape(n * width, slab)
    down_out = settle(down_grad.reshape(k, units // k, n, slab).transpose(2, 0, 1, 3))
    down_out = down_out.reshape(n * units, slab)
    return (
        output.astype(bf16)[None],
        input_grad[None],
        small[0],
        small[1],
        qkv_out.astype(f32),
        qkv_bias_grad,
        out_out.astype(f32),
        small[3],
        small[4],
        small[5],
        up_out.astype(f32),
        up_bias_grad,
        down_out.astype(f32),
        small[3],
    )


def solution(mesh):
    in_specs = (
        P("stream", "ctx", None),
        P("stream", None),
        P(),
        P(),
        P(None, "ctx", "head"),
        P(None, "head"),
        P("head", "ctx"),
        P(),
        P(),
        P(),
        P("ctx", "head"),
        P("head"),
        P("head", "ctx"),
        P(),
        P("stream", "ctx", None),
    )
    out_specs = (
        P("stream", "ctx", None),
        P("stream", "ctx", None),
        P(),
        P(),
        P(None, "ctx", "head"),
        P(None, "head"),
        P("head", "ctx"),
        P(),
        P(),
        P(),
        P("ctx", "head"),
        P("head"),
        P("head", "ctx"),
        P(),
    )
    split = mesh.shape["ctx"] * mesh.shape["head"]

    def whole(*arrays):
        heads, units = arrays[4].shape[2] // HEAD, arrays[10].shape[1]
        fits = heads % split == 0 and units % (split * 128 * mesh.shape["stream"]) == 0
        return jax.shard_map(
            per_device if fits else general_device,
            mesh=mesh,
            in_specs=in_specs,
            out_specs=out_specs,
            check_vma=False,
        )(*arrays)

    return whole
```

```python
from functools import partial
import math

import jax
import jax.numpy as jnp
from jax import lax
from jax.experimental import pallas as pl
from jax.experimental.pallas import tpu as pltpu
from jax.sharding import PartitionSpec as P

HEAD = 256
ROT = 64


def layer_norm(values, gain, offset):
    centre = jnp.mean(values, axis=-1, keepdims=True)
    centred = values - centre
    spread = jnp.mean(centred * centred, axis=-1, keepdims=True)
    return centred * lax.rsqrt(spread + 1e-05) * gain + offset


def rotary(values, angles):
    half = angles.shape[-1]
    cosine = jnp.cos(angles)[:, None, :]
    sine = jnp.sin(angles)[:, None, :]
    first = values[..., :half]
    second = values[..., half : 2 * half]
    return jnp.concatenate(
        [first * cosine - second * sine, second * cosine + first * sine, values[..., 2 * half :]],
        axis=-1,
    )


def doc_starts(doc_sizes, positions):
    place = jnp.arange(doc_sizes.shape[0])
    before = place[None, :] < place[:, None]
    starts = jnp.sum(jnp.where(before, doc_sizes[None, :], 0), axis=1)
    return jnp.max(jnp.where(starts[None, :] <= positions[:, None], starts[None, :], 0), axis=1)


def general_device(
    tokens,
    doc_lengths,
    ln1_gain,
    ln1_bias,
    qkv_weight,
    qkv_bias,
    out_weight,
    out_bias,
    ln2_gain,
    ln2_bias,
    up_weight,
    up_bias,
    down_weight,
    down_bias,
    cotangent,
):
    inputs = tokens[0].astype(jnp.float32)
    count = inputs.shape[0]
    ctx_count = lax.axis_size("ctx")
    length = count * ctx_count
    positions = lax.axis_index("ctx") * count + jnp.arange(count, dtype=jnp.int32)
    starts = doc_starts(doc_lengths[0], positions)
    frequency = 10000.0 ** (-jnp.arange(0, ROT, 2, dtype=jnp.float32) / ROT)
    angles = (positions - starts).astype(jnp.float32)[:, None] * frequency[None, :]
    scale = HEAD ** (-0.5)
    full_qkv, full_out, full_up, full_down = (
        lax.all_gather(qkv_weight, "ctx", axis=1, tiled=True),
        lax.all_gather(out_weight, "ctx", axis=1, tiled=True),
        lax.all_gather(up_weight, "ctx", axis=0, tiled=True),
        lax.all_gather(down_weight, "ctx", axis=1, tiled=True),
    )
    gain_one = ln1_gain.astype(jnp.float32)
    offset_one = ln1_bias.astype(jnp.float32)
    gain_two = ln2_gain.astype(jnp.float32)
    offset_two = ln2_bias.astype(jnp.float32)
    low_one = layer_norm(inputs, gain_one, offset_one).astype(jnp.bfloat16)
    low_two = layer_norm(inputs, gain_two, offset_two).astype(jnp.bfloat16)
    projected = (
        jnp.einsum("nd,cde->cne", low_one, full_qkv, preferred_element_type=jnp.float32)
        + qkv_bias.astype(jnp.float32)[:, None, :]
    )
    width = projected.shape[2]
    local_heads = width // HEAD
    query = rotary(projected[0].reshape(count, local_heads, HEAD), angles).astype(jnp.bfloat16)
    keys_flat = (
        rotary(projected[1].reshape(count, local_heads, HEAD), angles)
        .reshape(count, width)
        .astype(jnp.bfloat16)
    )
    values_flat = projected[2].astype(jnp.bfloat16)
    all_keys, all_values = (
        lax.all_gather(keys_flat, "ctx", axis=0, tiled=True),
        lax.all_gather(values_flat, "ctx", axis=0, tiled=True),
    )
    block = math.gcd(length, 512)
    block_count = length // block
    key_blocks = all_keys.reshape(block_count, block, local_heads, HEAD)
    value_blocks = all_values.reshape(block_count, block, local_heads, HEAD)
    firsts = jnp.arange(block_count, dtype=jnp.int32) * block

    def block_scores(key_block, first):
        key_index = first + jnp.arange(block, dtype=jnp.int32)
        allowed = (key_index[None, :] <= positions[:, None]) & (
            key_index[None, :] >= starts[:, None]
        )
        scores = (
            jnp.einsum("qhe,khe->hqk", query, key_block, preferred_element_type=jnp.float32) * scale
        )
        return (jnp.where(allowed[None], scores, -1e30), allowed[None])

    def statistics(carry, item):
        running, norm_sum = carry
        key_block, first = item
        masked, allowed = block_scores(key_block, first)
        newest = jnp.maximum(running, jnp.max(masked, axis=-1))
        raised = jnp.where(allowed, jnp.exp(masked - newest[..., None]), 0.0)
        norm_sum = norm_sum * jnp.exp(running - newest) + jnp.sum(raised, axis=-1)
        return ((newest, norm_sum), None)

    initial = (
        jnp.full((local_heads, count), -1e30, jnp.float32),
        jnp.zeros((local_heads, count), jnp.float32),
    )
    (running, norm_sum), _ = lax.scan(statistics, initial, (key_blocks, firsts))
    log_norm = running + jnp.log(norm_sum)

    def share_block(key_block, first):
        masked, allowed = block_scores(key_block, first)
        return jnp.where(allowed, jnp.exp(masked - log_norm[..., None]), 0.0)

    def accumulate(mixed, item):
        key_block, value_block, first = item
        shares_low = share_block(key_block, first).astype(jnp.bfloat16)
        return (
            mixed
            + jnp.einsum(
                "hqk,khe->qhe", shares_low, value_block, preferred_element_type=jnp.float32
            ),
            None,
        )

    mixed, _ = lax.scan(
        accumulate,
        jnp.zeros((count, local_heads, HEAD), jnp.float32),
        (key_blocks, value_blocks, firsts),
    )
    mixed_low = mixed.reshape(count, width).astype(jnp.bfloat16)
    attention = jnp.dot(mixed_low, full_out, preferred_element_type=jnp.float32)
    hidden = jnp.dot(low_two, full_up, preferred_element_type=jnp.float32) + up_bias.astype(
        jnp.float32
    )
    activated = jax.nn.gelu(hidden, approximate=False).astype(jnp.bfloat16)
    branches = attention + jnp.dot(activated, full_down, preferred_element_type=jnp.float32)
    joint = lax.psum(branches.astype(jnp.bfloat16), "head").astype(jnp.float32)
    output = inputs + joint + out_bias.astype(jnp.float32) + down_bias.astype(jnp.float32)
    upstream = cotangent[0]
    down_grad = jnp.dot(activated.T, upstream, preferred_element_type=jnp.float32)
    activated_grad = jnp.dot(upstream, full_down.T, preferred_element_type=jnp.float32)
    _, gelu_back = jax.vjp(partial(jax.nn.gelu, approximate=False), hidden)
    hidden_grad = gelu_back(activated_grad)[0].astype(jnp.bfloat16)
    up_grad = jnp.dot(low_two.T, hidden_grad, preferred_element_type=jnp.float32)
    up_bias_grad = jnp.sum(hidden_grad.astype(jnp.float32), axis=0)
    normed_two_grad = jnp.dot(hidden_grad, full_up.T, preferred_element_type=jnp.float32)
    out_grad = jnp.dot(mixed_low.T, upstream, preferred_element_type=jnp.float32)
    mixed_grad = jnp.dot(upstream, full_out.T, preferred_element_type=jnp.float32).astype(
        jnp.bfloat16
    )
    mixed_grad_heads = mixed_grad.reshape(count, local_heads, HEAD)
    delta = jnp.sum(mixed_grad_heads.astype(jnp.float32) * mixed, axis=-1).T

    def backward_block(query_grad, item):
        key_block, value_block, first = item
        shares = share_block(key_block, first)
        share_grad = jnp.einsum(
            "qhe,khe->hqk", mixed_grad_heads, value_block, preferred_element_type=jnp.float32
        )
        score_grad = (shares * (share_grad - delta[..., None])).astype(jnp.bfloat16)
        query_grad = (
            query_grad
            + jnp.einsum("hqk,khe->qhe", score_grad, key_block, preferred_element_type=jnp.float32)
            * scale
        )
        key_grad = (
            jnp.einsum("hqk,qhe->khe", score_grad, query, preferred_element_type=jnp.float32)
            * scale
        )
        value_grad = jnp.einsum(
            "hqk,qhe->khe",
            shares.astype(jnp.bfloat16),
            mixed_grad_heads,
            preferred_element_type=jnp.float32,
        )
        return (
            query_grad,
            jnp.concatenate(
                [key_grad.reshape(block, width), value_grad.reshape(block, width)], axis=1
            ),
        )

    query_grad, key_terms = lax.scan(
        backward_block,
        jnp.zeros((count, local_heads, HEAD), jnp.float32),
        (key_blocks, value_blocks, firsts),
    )
    own_grads = lax.psum_scatter(
        key_terms.reshape(length, 2 * width).astype(jnp.bfloat16),
        "ctx",
        scatter_dimension=0,
        tiled=True,
    ).astype(jnp.float32)
    query_pre = rotary(query_grad, -angles).reshape(count, width)
    key_pre = rotary(own_grads[:, :width].reshape(count, local_heads, HEAD), -angles).reshape(
        count, width
    )
    projected_grad = jnp.stack([query_pre, key_pre, own_grads[:, width:]]).astype(jnp.bfloat16)
    qkv_grad = jnp.einsum(
        "nd,cne->cde", low_one, projected_grad, preferred_element_type=jnp.float32
    )
    qkv_bias_grad = jnp.sum(projected_grad.astype(jnp.float32), axis=1)
    normed_one_grad = jnp.einsum(
        "cne,cde->nd", projected_grad, full_qkv, preferred_element_type=jnp.float32
    )
    normed_one_grad, normed_two_grad = (
        lax.psum(normed_one_grad.astype(jnp.bfloat16), "head").astype(jnp.float32),
        lax.psum(normed_two_grad.astype(jnp.bfloat16), "head").astype(jnp.float32),
    )
    _, norm_back_one = jax.vjp(layer_norm, inputs, gain_one, offset_one)
    input_one, gain_grad_one, offset_grad_one = norm_back_one(normed_one_grad)
    _, norm_back_two = jax.vjp(layer_norm, inputs, gain_two, offset_two)
    input_two, gain_grad_two, offset_grad_two = norm_back_two(normed_two_grad)
    upstream_wide = upstream.astype(jnp.float32)
    input_grad = upstream_wide + input_one + input_two
    bias_grad = jnp.sum(upstream_wide, axis=0)
    small = lax.psum(
        (
            gain_grad_one,
            offset_grad_one,
            qkv_bias_grad,
            bias_grad,
            gain_grad_two,
            offset_grad_two,
            up_bias_grad,
        ),
        ("stream", "ctx"),
    )
    slices = (
        lax.psum_scatter(
            qkv_grad.astype(jnp.bfloat16), "ctx", scatter_dimension=1, tiled=True
        ).astype(jnp.float32),
        lax.psum_scatter(
            out_grad.astype(jnp.bfloat16), "ctx", scatter_dimension=1, tiled=True
        ).astype(jnp.float32),
        lax.psum_scatter(
            up_grad.astype(jnp.bfloat16), "ctx", scatter_dimension=0, tiled=True
        ).astype(jnp.float32),
        lax.psum_scatter(
            down_grad.astype(jnp.bfloat16), "ctx", scatter_dimension=1, tiled=True
        ).astype(jnp.float32),
    )
    shards = (
        lax.psum(slices[0].astype(jnp.bfloat16), "stream").astype(jnp.float32),
        lax.psum(slices[1].astype(jnp.bfloat16), "stream").astype(jnp.float32),
        lax.psum(slices[2].astype(jnp.bfloat16), "stream").astype(jnp.float32),
        lax.psum(slices[3].astype(jnp.bfloat16), "stream").astype(jnp.float32),
    )
    return (
        output.astype(jnp.bfloat16)[None],
        input_grad[None],
        small[0],
        small[1],
        shards[0],
        small[2],
        shards[1],
        small[3],
        small[4],
        small[5],
        shards[2],
        small[6],
        shards[3],
        small[3],
    )


def token_places(doc_sizes, length):
    positions = jnp.arange(length, dtype=jnp.int32)
    return positions, doc_starts(doc_sizes, positions)


MESH = pl.DeviceIdType.MESH


def span(index, size):
    return pl.ds(pl.multiple_of(index * size, size), size)


def places():
    return lax.axis_index("stream"), lax.axis_index("ctx"), lax.axis_index("head")


def greet(peers):
    barrier = pltpu.get_barrier_semaphore()
    for peer in peers:
        pl.semaphore_signal(barrier, inc=1, device_id=peer, device_id_type=MESH)
    pl.semaphore_wait(barrier, len(peers))


def gather_body(
    x_ref, g_ref, qkv_ref, up_ref, out_ref, down_ref,
    x_all, g_all, qkv_all, up_all, out_all, down_all,
    z_send, z_recv, x_send, x_recv, y_send, y_recv, fx_send, fx_recv, fy_send, fy_recv,
    line_send, line_recv, core_send, core_recv, own_sem,
    *held,
):
    s, c, h = places()
    x_peer = s + 1 - 2 * lax.rem(s, 2)
    y_peer = lax.rem(s + 2, 4)
    across = ((x_peer, c, h), (y_peer, c, h))
    core_peer = (s, c, 1 - h)
    ring = [(s, lax.rem(c + k, 4), h) for k in (1, 2, 3)]
    greet([*across, core_peer, *ring])

    count = x_ref.shape[0]
    slab, width, units = up_ref.shape[0], out_ref.shape[0] // 4, down_ref.shape[0] // 4
    quarter, half_count = slab // 4, count // 2

    def rows(base, size):
        return pl.ds(pl.multiple_of(base, size), size)

    def landed(m, r, part, half):
        def cut(total):
            size = total // 4
            if half is None:
                return part * size, size
            return part * size + half * (size // 2), size // 2

        if m == 0:
            at, size = cut(slab)
            return qkv_all.at[:, rows(r * slab + at, size), :]
        if m == 1:
            at, size = cut(slab)
            return up_all.at[rows(r * slab + at, size), :]
        if m == 2:
            at, size = cut(width)
            return out_all.at[rows(at, size), span(r, slab)]
        at, size = cut(units)
        return down_all.at[rows(at, size), span(r, slab)]

    def piece(m, to, part=None):
        if m == 0:
            inner = slice(None) if part is None else span(part, quarter)
            return qkv_ref.at[:, inner, span(to, width)]
        if m == 1:
            inner = slice(None) if part is None else span(part, quarter)
            return up_ref.at[inner, span(to, units)]
        size = width if m == 2 else units
        ref = out_ref if m == 2 else down_ref
        if part is None:
            return ref.at[span(to, size), :]
        return ref.at[rows(to * size + part * (size // 4), size // 4), :]

    def whole_piece(m, r):
        if m == 0:
            return qkv_all.at[:, span(r, slab), :]
        if m == 1:
            return up_all.at[span(r, slab), :]
        return (out_all if m == 2 else down_all).at[:, span(r, slab)]

    def remote(src, dst, send, recv, to):
        return pltpu.make_async_remote_copy(
            src_ref=src, dst_ref=dst, send_sem=send, recv_sem=recv, device_id=to, device_id_type=MESH
        )

    def z_copy(m, k):
        to = lax.rem(c + 4 - k, 4)
        return remote(
            piece(m, to, s), landed(m, c, s, None), z_send.at[m, k - 1], z_recv.at[m, k - 1], (s, to, h)
        )

    def direct(m, k, axis):
        r = lax.rem(c + k, 4)
        send, recv = (x_send, x_recv) if axis == 0 else (y_send, y_recv)
        here = landed(m, r, s, None)
        return remote(here, here, send.at[m, k - 1], recv.at[m, k - 1], across[axis])

    def onward(m, k, axis):
        r = lax.rem(c + k, 4)
        send, recv = (fx_send, fx_recv) if axis == 0 else (fy_send, fy_recv)
        here = landed(m, r, y_peer if axis == 0 else x_peer, 1 if axis == 0 else 0)
        return remote(here, here, send.at[m, k - 1], recv.at[m, k - 1], across[axis])

    lines = ((x_ref, x_all), (g_ref, g_all))

    def block(a, origin):
        return lines[a][1].at[rows(origin * count + h * half_count, half_count), :]

    def line_copy(a, t, side):
        origin = c - t if side == 0 else c + t
        src = lines[a][0].at[span(h, half_count), :] if t == 0 else block(a, origin)
        to = c + 1 if side == 0 else c - 1
        return remote(
            src, block(a, origin), line_send.at[a, side, t], line_recv.at[a, side, t], (s, to, h)
        )

    def core_copy(a, t, side):
        origin = c - t if side == 0 else c + t
        here = block(a, origin)
        return remote(here, here, core_send.at[a, side, t - 1], core_recv.at[a, side, t - 1], core_peer)

    def sends(t, side):
        if side == 0:
            return (c >= t) & (c < 3)
        return (c + t <= 3) & (c > 0)

    def gets(t, side):
        return c >= t if side == 0 else c + t <= 3

    def line_step(a, t):
        for side in (0, 1):
            @pl.when(gets(t, side))
            def _():
                line_copy(a, t - 1, side).wait_recv()
                core_copy(a, t, side).start()

            if t < 3:
                @pl.when(sends(t, side))
                def _():
                    line_copy(a, t, side).start()

    near = (1, 3, 2)
    order = [(m, k) for m in (0, 1, 3, 2) for k in near]

    def start_lines():
        for a in (0, 1):
            for side in (0, 1):
                @pl.when(sends(0, side))
                def _():
                    line_copy(a, 0, side).start()

    def start_z(m):
        for k in near:
            z_copy(m, k).start()

    def pass_on(m):
        for k in near:
            direct(m, k, 0).wait_recv()
            onward(m, k, 1).start()
            direct(m, k, 1).wait_recv()
            onward(m, k, 0).start()

    def spread(m):
        for k in near:
            z_copy(m, k).wait_recv()
            direct(m, k, 0).start()
            direct(m, k, 1).start()

    start_z(0)
    start_lines()
    start_z(1)
    sources = [lines[0][0], lines[1][0]] + [piece(m, c) for m in range(4)]
    ends = [lines[a][1].at[span(c, count), :] for a in (0, 1)] + [whole_piece(m, c) for m in range(4)]
    ins = [pltpu.make_async_copy(a, b, own_sem.at[i]) for i, (a, b) in enumerate(zip(sources, held))]
    own = [pltpu.make_async_copy(b, e, own_sem.at[i]) for i, (b, e) in enumerate(zip(held, ends))]
    for copy in ins:
        copy.start()
    for copy, out in zip(ins, own):
        copy.wait()
        out.start()

    spread(0)
    line_step(0, 1)
    line_step(1, 1)
    start_z(3)
    spread(1)
    pass_on(0)
    start_z(2)
    line_step(0, 2)
    line_step(1, 2)
    spread(3)
    pass_on(1)
    spread(2)
    pass_on(3)
    line_step(0, 3)
    line_step(1, 3)
    pass_on(2)
    for m, k in order:
        onward(m, k, 0).wait_recv()
        onward(m, k, 1).wait_recv()
    for a in (0, 1):
        for side in (0, 1):
            for t in (1, 2, 3):
                @pl.when(gets(t, side))
                def _():
                    core_copy(a, t, side).wait()
                @pl.when(sends(t - 1, side))
                def _():
                    line_copy(a, t - 1, side).wait_send()
    for m, k in order:
        z_copy(m, k).wait_send()
        for axis in (0, 1):
            direct(m, k, axis).wait_send()
            onward(m, k, axis).wait_send()
    for copy in own:
        copy.wait()


def gather_all(tokens, cotangent, w_qkv, w_up, w_out, w_down):
    count, model = tokens.shape
    slab = w_up.shape[0]
    width, units = w_out.shape[0] // 4, w_down.shape[0] // 4
    bf16 = jnp.bfloat16
    dma = pltpu.SemaphoreType.DMA
    return pl.pallas_call(
        gather_body,
        out_shape=[
            jax.ShapeDtypeStruct((4 * count, model), bf16),
            jax.ShapeDtypeStruct((4 * count, model), bf16),
            jax.ShapeDtypeStruct((3, model, width), bf16),
            jax.ShapeDtypeStruct((model, units), bf16),
            jax.ShapeDtypeStruct((width, model), bf16),
            jax.ShapeDtypeStruct((units, model), bf16),
        ],
        in_specs=[pl.BlockSpec(memory_space=pl.ANY)] * 6,
        out_specs=[pl.BlockSpec(memory_space=pl.ANY)] * 6,
        scratch_shapes=[dma((4, 3))] * 10 + [dma((2, 2, 3))] * 4 + [dma((6,))]
        + [
            pltpu.VMEM(shape, bf16)
            for shape in (
                (count, model), (count, model), (3, slab, width), (slab, units), (width, slab), (units, slab)
            )
        ],
        compiler_params=pltpu.CompilerParams(
            collective_id=0, has_side_effects=True, vmem_limit_bytes=32 << 20
        ),
        name="gather",
    )(tokens, cotangent, w_qkv, w_up, w_out, w_down)


LEADS = (12, 4, 1, 1)


def settle_body(
    bra_ref, inw_ref, g0, g1, g2, g3,
    joint, inward, o0, o1, o2, o3,
    s1x_send, s1x_recv, s1y_send, s1y_recv, s2x_send, s2x_recv, s2y_send, s2y_recv,
    z_send, z_recv, x_send, x_recv, y_send, y_recv, fx_send, fx_recv, fy_send, fy_recv,
    own_sem, core_send, core_recv, row_send, row_recv, back_send, back_recv, keep_sem, half_sem,
    *bufs,
):
    s, c, h = places()
    x_at, y_at = lax.rem(s, 2), lax.div(s, 2)
    x_off, y_off = 1 - x_at, 1 - y_at
    x_peer, y_peer = y_at * 2 + x_off, y_off * 2 + x_at
    across = ((x_peer, c, h), (y_peer, c, h))
    core_peer = (s, c, 1 - h)
    ring = [(s, lax.rem(c + k, 4), h) for k in (1, 2, 3)]
    greet([*across, core_peer, *ring])
    grads, outs = (g0, g1, g2, g3), (o0, o1, o2, o3)
    mine = [bufs[2 * m : 2 * m + 2] for m in range(4)]
    first = [bufs[8 + 2 * m : 10 + 2 * m] for m in range(4)]
    second = [bufs[16 + 2 * m : 18 + 2 * m] for m in range(4)]
    own_half, core_half, row_parts, done_half = bufs[24:26], bufs[26:28], bufs[28:30], bufs[30:32]
    slab = o2.shape[-1]

    def remote(src, dst, send, recv, to):
        return pltpu.make_async_remote_copy(
            src_ref=src, dst_ref=dst, send_sem=send, recv_sem=recv, device_id=to, device_id_type=MESH
        )

    def one(m, half):
        src = grads[m].at[:, :, x_off, 0] if half == 0 else grads[m].at[:, y_off, :, 1]
        send, recv = (s1x_send, s1x_recv) if half == 0 else (s1y_send, s1y_recv)
        return remote(src, first[m][half], send.at[m], recv.at[m], across[half])

    def load(m, half):
        src = grads[m].at[:, :, x_at, 0] if half == 0 else grads[m].at[:, y_at, :, 1]
        return pltpu.make_async_copy(src, mine[m][half], own_sem.at[m, half])

    def two(m, half):
        src = mine[m][half].at[:, y_off if half == 0 else x_off]
        send, recv = (s2y_send, s2y_recv) if half == 0 else (s2x_send, s2x_recv)
        return remote(src, second[m][half], send.at[m], recv.at[m], across[1 - half])

    def add_first(m, half):
        into, more = mine[m][half], first[m][half]
        lead, _, height, _ = into.shape
        tall = min(height, 32)

        @pl.loop(0, lead * 2 * (height // tall))
        def _(i):
            at = lax.rem(i, height // tall)
            pair = lax.div(i, height // tall)
            l, j, rows = lax.div(pair, 2), lax.rem(pair, 2), span(at, tall)
            total = into[l, j, rows, :].astype(jnp.float32) + more[l, j, rows, :].astype(jnp.float32)
            into[l, j, rows, :] = total.astype(into.dtype)

    def add_second(m, half):
        into, more = second[m][half], mine[m][half]
        keep = y_at if half == 0 else x_at
        lead, height, _ = into.shape
        tall = min(height, 32)

        @pl.loop(0, lead * (height // tall))
        def _(i):
            l, rows = lax.div(i, height // tall), span(lax.rem(i, height // tall), tall)
            total = into[l, rows, :].astype(jnp.float32) + more[l, keep, rows, :].astype(jnp.float32)
            into[l, rows, :] = total.astype(into.dtype)

    def share_of(m, half, to):
        ref = second[m][half]
        if m == 0:
            return ref.reshape(3, 4, *ref.shape[1:]).at[:, to]
        if m == 1:
            return ref.at[to]
        return ref.at[0, :, span(to, slab)]

    def home(m, half):
        if m == 0:
            return outs[0].at[:, s, half, :, span(c, second[0][0].shape[-1])]
        if m == 1:
            return outs[1].at[s, half, :, span(c, second[1][0].shape[-1])]
        return outs[m].at[c, s, half]

    def z_copy(m, half, k):
        to = lax.rem(c + 4 - k, 4)
        i = (m * 2 + half) * 3 + k - 1
        return remote(share_of(m, half, to), home(m, half), z_send.at[i], z_recv.at[i], (s, to, h))

    def keep(m, half):
        return pltpu.make_async_copy(share_of(m, half, c), home(m, half), keep_sem.at[m, half])

    def quarter(m, q, half=None):
        if half is None:
            return outs[m].at[q] if m == 1 else outs[m].at[:, q]
        return outs[m].at[q, half] if m == 1 else outs[m].at[:, q, half]

    def direct(m, axis):
        send, recv = (x_send, x_recv) if axis == 0 else (y_send, y_recv)
        here = quarter(m, s)
        return remote(here, here, send.at[m], recv.at[m], across[axis])

    def onward(m, axis):
        send, recv = (fx_send, fx_recv) if axis == 0 else (fy_send, fy_recv)
        here = quarter(m, y_peer if axis == 0 else x_peer, 1 - axis)
        return remote(here, here, send.at[m], recv.at[m], across[axis])

    wholes, sums = (bra_ref, inw_ref), (joint, inward)
    span_cols = own_half[0].shape[1]
    count = joint.shape[0]

    def core_copy(a):
        return remote(
            wholes[a].at[:, span(1 - h, span_cols)], core_half[a], core_send.at[a], core_recv.at[a], core_peer
        )

    def half_load(a):
        return pltpu.make_async_copy(wholes[a].at[:, span(h, span_cols)], own_half[a], half_sem.at[a])

    def row_copy(a, k):
        to = lax.rem(c + 4 - k, 4)
        return remote(
            own_half[a].at[span(to, count)], row_parts[a].at[k - 1],
            row_send.at[a, k - 1], row_recv.at[a, k - 1], (s, to, h),
        )

    def back_copy(a):
        here = sums[a].at[:, span(h, span_cols)]
        return remote(done_half[a], here, back_send.at[a], back_recv.at[a], core_peer)

    def back_keep(a):
        return pltpu.make_async_copy(done_half[a], sums[a].at[:, span(h, span_cols)], half_sem.at[a])

    order = (3, 1, 0, 2)
    for m in order:
        for half in (0, 1):
            one(m, half).start()
    for a in (0, 1):
        core_copy(a).start()
        half_load(a).start()
    for m in order:
        for half in (0, 1):
            load(m, half).start()
    for a in (0, 1):
        half_load(a).wait()
        core_copy(a).wait_recv()
        tall = 32

        @pl.loop(0, own_half[a].shape[0] // tall)
        def _(i):
            rows = span(i, tall)
            total = own_half[a][rows, :].astype(jnp.float32) + core_half[a][rows, :].astype(jnp.float32)
            own_half[a][rows, :] = total.astype(own_half[a].dtype)

        for k in (1, 3, 2):
            row_copy(a, k).start()

    def stage_two(m):
        for half in (0, 1):
            load(m, half).wait()
            one(m, half).wait_recv()
            add_first(m, half)
            two(m, half).start()

    def stage_z(m):
        for half in (0, 1):
            two(m, half).wait_recv()
            add_second(m, half)
            for k in (1, 3, 2):
                z_copy(m, half, k).start()
            keep(m, half).start()

    def stage_out(m):
        for half in (0, 1):
            for k in (1, 3, 2):
                z_copy(m, half, k).wait_recv()
            keep(m, half).wait()
        for axis in (0, 1):
            direct(m, axis).start()

    def stage_on(m):
        direct(m, 0).wait_recv()
        onward(m, 1).start()
        direct(m, 1).wait_recv()
        onward(m, 0).start()

    def line_sum(a):
        for k in (1, 3, 2):
            row_copy(a, k).wait_recv()
        tall = 32

        @pl.loop(0, count // tall)
        def _(i):
            rows = span(i, tall)
            total = own_half[a][pl.ds(pl.multiple_of(c * count + i * tall, tall), tall), :].astype(jnp.float32)
            for k in range(3):
                total = total + row_parts[a][k, rows, :].astype(jnp.float32)
            done_half[a][rows, :] = total.astype(done_half[a].dtype)

        back_copy(a).start()
        back_keep(a).start()

    stages = (stage_two, stage_z, stage_out, stage_on)
    lag = 1
    for step in range(len(order) + lag * (len(stages) - 1)):
        for i, stage in enumerate(stages):
            j = step - i * lag
            if 0 <= j < len(order):
                stage(order[j])
        if step in (2, 3):
            line_sum(step - 2)
    for m in order:
        for axis in (0, 1):
            onward(m, axis).wait_recv()
    for a in (0, 1):
        back_copy(a).wait()
        back_keep(a).wait()
        core_copy(a).wait_send()
        for k in (1, 2, 3):
            row_copy(a, k).wait_send()
    for m in order:
        for half in (0, 1):
            one(m, half).wait_send()
            two(m, half).wait_send()
            for k in (1, 2, 3):
                z_copy(m, half, k).wait_send()
        for axis in (0, 1):
            direct(m, axis).wait_send()
            onward(m, axis).wait_send()


def settle_all(branches, inward, g_qkv, g_up, g_out, g_down):
    length, model = branches.shape
    width, units = g_qkv.shape[2], g_up.shape[1]
    slab, count = model // 4, length // 4
    bf16 = jnp.bfloat16
    dma = pltpu.SemaphoreType.DMA
    rows = (slab // 8, slab // 8, width // 8, units // 8)
    cols = (width, units, model, model)
    views = [
        g.reshape(lead, 2, 2, 2, r, k)
        for g, lead, r, k in zip((g_qkv, g_up, g_out, g_down), LEADS, rows, cols)
    ]
    out_shapes = [
        (count, model), (count, model),
        (3, 4, 2, rows[0], 4 * width), (4, 2, rows[1], 4 * units),
        (4, 4, 2, rows[2], slab), (4, 4, 2, rows[3], slab),
    ]
    pairs = [(l, 2, r, k) for l, r, k in zip(LEADS, rows, cols)]
    scratch = [dma((4,))] * 8 + [dma((24,))] * 2 + [dma((4,))] * 8
    scratch += [dma((4, 2)), dma((2,)), dma((2,)), dma((2, 3)), dma((2, 3)), dma((2,)), dma((2,)), dma((4, 2)), dma((2,))]
    vmem = [p for p in pairs for _ in (0, 1)] * 2 + [(p[0], p[2], p[3]) for p in pairs for _ in (0, 1)]
    vmem += [(length, model // 2)] * 4 + [(3, count, model // 2)] * 2 + [(count, model // 2)] * 2
    scratch += [pltpu.VMEM(v, bf16) for v in vmem]
    joint, inward, q, u, o, d = pl.pallas_call(
        settle_body,
        out_shape=[jax.ShapeDtypeStruct(v, bf16) for v in out_shapes],
        in_specs=[pl.BlockSpec(memory_space=pl.ANY)] * 6,
        out_specs=[pl.BlockSpec(memory_space=pl.ANY)] * 6,
        scratch_shapes=scratch,
        compiler_params=pltpu.CompilerParams(
            collective_id=1, has_side_effects=True, vmem_limit_bytes=48 << 20
        ),
        name="settle",
    )(branches, inward, *views)
    return joint, inward, q.reshape(3, slab, 4 * width), u.reshape(slab, 4 * units), o.reshape(4 * width, slab), d.reshape(4 * units, slab)


def per_device(
    tokens,
    doc_lengths,
    ln1_gain,
    ln1_bias,
    qkv_weight,
    qkv_bias,
    out_weight,
    out_bias,
    ln2_gain,
    ln2_bias,
    up_weight,
    up_bias,
    down_weight,
    down_bias,
    cotangent,
):
    f32, bf16 = jnp.float32, jnp.bfloat16
    ctx_count = lax.axis_size("ctx")
    head_count = lax.axis_size("head")
    c = lax.axis_index("ctx")
    h = lax.axis_index("head")
    count, model = tokens.shape[1], tokens.shape[2]
    length = count * ctx_count
    slab = model // ctx_count
    width = qkv_weight.shape[2] // ctx_count
    units = up_weight.shape[1] // ctx_count

    all_tokens, upstream, w_qkv, w_up, w_out, w_down = gather_all(
        tokens[0], cotangent[0], qkv_weight, up_weight, out_weight, down_weight
    )

    gain_one, offset_one = ln1_gain.astype(f32), ln1_bias.astype(f32)
    gain_two, offset_two = ln2_gain.astype(f32), ln2_bias.astype(f32)
    wide = all_tokens.astype(f32)
    centred = wide - jnp.mean(wide, axis=-1, keepdims=True)
    scale_of = lax.rsqrt(jnp.mean(centred * centred, axis=-1, keepdims=True) + 1e-05)
    unit = centred * scale_of
    low_one = (unit * gain_one + offset_one).astype(bf16)
    low_two = (unit * gain_two + offset_two).astype(bf16)

    positions, starts = token_places(doc_lengths[0], length)
    frequency = 10000.0 ** (-jnp.arange(0, ROT, 2, dtype=f32) / ROT)
    angles = (positions - starts).astype(f32)[:, None] * frequency[None, :]
    bias = lax.dynamic_slice_in_dim(qkv_bias, c * width, width, 1).astype(f32)
    projected = jnp.einsum("nd,cde->cne", low_one, w_qkv, preferred_element_type=f32)
    projected = projected + bias[:, None, :]
    heads = width // HEAD
    query = rotary(projected[0].reshape(length, heads, HEAD), angles).astype(bf16)
    keys = rotary(projected[1].reshape(length, heads, HEAD), angles).astype(bf16)
    values = projected[2].reshape(length, heads, HEAD).astype(bf16)
    scale = HEAD ** (-0.5)
    allowed = (positions[None, :] <= positions[:, None]) & (positions[None, :] >= starts[:, None])
    scores = jnp.einsum("qhe,khe->hqk", query, keys, preferred_element_type=f32) * scale
    masked = jnp.where(allowed[None], scores, -1e30)
    raised = jnp.where(
        allowed[None], jnp.exp(masked - jnp.max(masked, axis=-1, keepdims=True)), 0.0
    )
    shares = raised / jnp.sum(raised, axis=-1, keepdims=True)
    shares_low = shares.astype(bf16)
    mixed = jnp.einsum("hqk,khe->qhe", shares_low, values, preferred_element_type=f32)
    mixed_low = mixed.reshape(length, width).astype(bf16)

    up_part = lax.dynamic_slice_in_dim(up_bias, c * units, units, 0).astype(f32)
    hidden = jnp.dot(low_two, w_up, preferred_element_type=f32) + up_part
    activated = jax.nn.gelu(hidden, approximate=False).astype(bf16)
    branches = jnp.dot(mixed_low, w_out, preferred_element_type=f32) + jnp.dot(
        activated, w_down, preferred_element_type=f32
    )

    _, gelu_back = jax.vjp(partial(jax.nn.gelu, approximate=False), hidden)
    activated_grad = jnp.dot(upstream, w_down.T, preferred_element_type=f32)
    hidden_grad = gelu_back(activated_grad)[0].astype(bf16)
    down_grad = jnp.dot(activated.T, upstream, preferred_element_type=f32)
    up_grad = jnp.dot(low_two.T, hidden_grad, preferred_element_type=f32)
    out_grad = jnp.dot(mixed_low.T, upstream, preferred_element_type=f32)
    mixed_grad = (
        jnp.dot(upstream, w_out.T, preferred_element_type=f32)
        .astype(bf16)
        .reshape(length, heads, HEAD)
    )
    delta = jnp.sum(mixed_grad.astype(f32) * mixed, axis=-1).T
    share_grad = jnp.einsum("qhe,khe->hqk", mixed_grad, values, preferred_element_type=f32)
    score_grad = (shares * (share_grad - delta[..., None])).astype(bf16)
    query_grad = (
        jnp.einsum("hqk,khe->qhe", score_grad, keys, preferred_element_type=f32) * scale
    )
    key_grad = jnp.einsum("hqk,qhe->khe", score_grad, query, preferred_element_type=f32) * scale
    value_grad = jnp.einsum("hqk,qhe->khe", shares_low, mixed_grad, preferred_element_type=f32)
    projected_grad = jnp.stack(
        [
            rotary(query_grad, -angles).reshape(length, width),
            rotary(key_grad, -angles).reshape(length, width),
            value_grad.reshape(length, width),
        ]
    ).astype(bf16)
    qkv_grad = jnp.einsum("nd,cne->cde", low_one, projected_grad, preferred_element_type=f32)
    normed_one_grad = jnp.einsum("cne,cde->nd", projected_grad, w_qkv, preferred_element_type=f32)
    normed_two_grad = jnp.dot(hidden_grad, w_up.T, preferred_element_type=f32)

    inward = gain_one * normed_one_grad + gain_two * normed_two_grad
    joint, inward, qkv_out, up_out, out_out, down_out = settle_all(
        branches.astype(bf16),
        inward.astype(bf16),
        qkv_grad.astype(bf16),
        up_grad.astype(bf16),
        out_grad.astype(bf16),
        down_grad.astype(bf16),
    )
    joint, inward = joint.astype(f32), inward.astype(f32)

    own = tokens[0].astype(f32)
    own_upstream = cotangent[0].astype(f32)
    output = own + joint + out_bias.astype(f32) + down_bias.astype(f32)
    own_centred = own - jnp.mean(own, axis=-1, keepdims=True)
    own_scale = lax.rsqrt(jnp.mean(own_centred * own_centred, axis=-1, keepdims=True) + 1e-05)
    own_unit = own_centred * own_scale
    input_grad = own_upstream + own_scale * (
        inward
        - jnp.mean(inward, axis=-1, keepdims=True)
        - own_unit * jnp.mean(inward * own_unit, axis=-1, keepdims=True)
    )

    bias_grad = jnp.sum(own_upstream, axis=0) * (1.0 / head_count)
    qkv_small = lax.dynamic_update_slice(
        jnp.zeros((3, head_count * ctx_count * width), f32),
        jnp.sum(projected_grad.astype(f32), axis=1),
        (0, (h * ctx_count + c) * width),
    )
    up_small = lax.dynamic_update_slice(
        jnp.zeros((head_count * ctx_count * units,), f32),
        jnp.sum(hidden_grad.astype(f32), axis=0),
        ((h * ctx_count + c) * units,),
    )
    small = lax.psum(
        (
            jnp.sum(normed_one_grad * unit, axis=0),
            jnp.sum(normed_one_grad, axis=0),
            qkv_small,
            bias_grad,
            jnp.sum(normed_two_grad * unit, axis=0),
            jnp.sum(normed_two_grad, axis=0),
            up_small,
        ),
        ("stream", "ctx", "head"),
    )
    qkv_bias_grad = lax.dynamic_slice_in_dim(small[2], h * ctx_count * width, ctx_count * width, 1)
    up_bias_grad = lax.dynamic_slice_in_dim(small[6], h * ctx_count * units, ctx_count * units, 0)

    return (
        output.astype(bf16)[None],
        input_grad[None],
        small[0],
        small[1],
        qkv_out.astype(f32),
        qkv_bias_grad,
        out_out.astype(f32),
        small[3],
        small[4],
        small[5],
        up_out.astype(f32),
        up_bias_grad,
        down_out.astype(f32),
        small[3],
    )


def solution(mesh):
    in_specs = (
        P("stream", "ctx", None),
        P("stream", None),
        P(),
        P(),
        P(None, "ctx", "head"),
        P(None, "head"),
        P("head", "ctx"),
        P(),
        P(),
        P(),
        P("ctx", "head"),
        P("head"),
        P("head", "ctx"),
        P(),
        P("stream", "ctx", None),
    )
    out_specs = (
        P("stream", "ctx", None),
        P("stream", "ctx", None),
        P(),
        P(),
        P(None, "ctx", "head"),
        P(None, "head"),
        P("head", "ctx"),
        P(),
        P(),
        P(),
        P("ctx", "head"),
        P("head"),
        P("head", "ctx"),
        P(),
    )
    split = mesh.shape["ctx"] * mesh.shape["head"]

    def whole(*arrays):
        heads, units = arrays[4].shape[2] // HEAD, arrays[10].shape[1]
        grouped = (mesh.shape["stream"], mesh.shape["ctx"], mesh.shape["head"]) == (4, 4, 2)
        fits = grouped and heads == split and units % (split * 128) == 0
        return jax.shard_map(
            per_device if fits else general_device,
            mesh=mesh,
            in_specs=in_specs,
            out_specs=out_specs,
            check_vma=False,
        )(*arrays)

    return whole
```

```python
from functools import partial
import math

import jax
import jax.numpy as jnp
from jax import lax
from jax.experimental import pallas as pl
from jax.experimental.pallas import tpu as pltpu
from jax.sharding import PartitionSpec as P

HEAD = 256
ROT = 64


def layer_norm(values, gain, offset):
    centre = jnp.mean(values, axis=-1, keepdims=True)
    centred = values - centre
    spread = jnp.mean(centred * centred, axis=-1, keepdims=True)
    return centred * lax.rsqrt(spread + 1e-05) * gain + offset


def rotary(values, angles):
    half = angles.shape[-1]
    cosine = jnp.cos(angles)[:, None, :]
    sine = jnp.sin(angles)[:, None, :]
    first = values[..., :half]
    second = values[..., half : 2 * half]
    return jnp.concatenate(
        [first * cosine - second * sine, second * cosine + first * sine, values[..., 2 * half :]],
        axis=-1,
    )


def doc_starts(doc_sizes, positions):
    place = jnp.arange(doc_sizes.shape[0])
    before = place[None, :] < place[:, None]
    starts = jnp.sum(jnp.where(before, doc_sizes[None, :], 0), axis=1)
    return jnp.max(jnp.where(starts[None, :] <= positions[:, None], starts[None, :], 0), axis=1)


def general_device(
    tokens,
    doc_lengths,
    ln1_gain,
    ln1_bias,
    qkv_weight,
    qkv_bias,
    out_weight,
    out_bias,
    ln2_gain,
    ln2_bias,
    up_weight,
    up_bias,
    down_weight,
    down_bias,
    cotangent,
):
    inputs = tokens[0].astype(jnp.float32)
    count = inputs.shape[0]
    ctx_count = lax.axis_size("ctx")
    length = count * ctx_count
    positions = lax.axis_index("ctx") * count + jnp.arange(count, dtype=jnp.int32)
    starts = doc_starts(doc_lengths[0], positions)
    frequency = 10000.0 ** (-jnp.arange(0, ROT, 2, dtype=jnp.float32) / ROT)
    angles = (positions - starts).astype(jnp.float32)[:, None] * frequency[None, :]
    scale = HEAD ** (-0.5)
    full_qkv, full_out, full_up, full_down = (
        lax.all_gather(qkv_weight, "ctx", axis=1, tiled=True),
        lax.all_gather(out_weight, "ctx", axis=1, tiled=True),
        lax.all_gather(up_weight, "ctx", axis=0, tiled=True),
        lax.all_gather(down_weight, "ctx", axis=1, tiled=True),
    )
    gain_one = ln1_gain.astype(jnp.float32)
    offset_one = ln1_bias.astype(jnp.float32)
    gain_two = ln2_gain.astype(jnp.float32)
    offset_two = ln2_bias.astype(jnp.float32)
    low_one = layer_norm(inputs, gain_one, offset_one).astype(jnp.bfloat16)
    low_two = layer_norm(inputs, gain_two, offset_two).astype(jnp.bfloat16)
    projected = (
        jnp.einsum("nd,cde->cne", low_one, full_qkv, preferred_element_type=jnp.float32)
        + qkv_bias.astype(jnp.float32)[:, None, :]
    )
    width = projected.shape[2]
    local_heads = width // HEAD
    query = rotary(projected[0].reshape(count, local_heads, HEAD), angles).astype(jnp.bfloat16)
    keys_flat = (
        rotary(projected[1].reshape(count, local_heads, HEAD), angles)
        .reshape(count, width)
        .astype(jnp.bfloat16)
    )
    values_flat = projected[2].astype(jnp.bfloat16)
    all_keys, all_values = (
        lax.all_gather(keys_flat, "ctx", axis=0, tiled=True),
        lax.all_gather(values_flat, "ctx", axis=0, tiled=True),
    )
    block = math.gcd(length, 512)
    block_count = length // block
    key_blocks = all_keys.reshape(block_count, block, local_heads, HEAD)
    value_blocks = all_values.reshape(block_count, block, local_heads, HEAD)
    firsts = jnp.arange(block_count, dtype=jnp.int32) * block

    def block_scores(key_block, first):
        key_index = first + jnp.arange(block, dtype=jnp.int32)
        allowed = (key_index[None, :] <= positions[:, None]) & (
            key_index[None, :] >= starts[:, None]
        )
        scores = (
            jnp.einsum("qhe,khe->hqk", query, key_block, preferred_element_type=jnp.float32) * scale
        )
        return (jnp.where(allowed[None], scores, -1e30), allowed[None])

    def statistics(carry, item):
        running, norm_sum = carry
        key_block, first = item
        masked, allowed = block_scores(key_block, first)
        newest = jnp.maximum(running, jnp.max(masked, axis=-1))
        raised = jnp.where(allowed, jnp.exp(masked - newest[..., None]), 0.0)
        norm_sum = norm_sum * jnp.exp(running - newest) + jnp.sum(raised, axis=-1)
        return ((newest, norm_sum), None)

    initial = (
        jnp.full((local_heads, count), -1e30, jnp.float32),
        jnp.zeros((local_heads, count), jnp.float32),
    )
    (running, norm_sum), _ = lax.scan(statistics, initial, (key_blocks, firsts))
    log_norm = running + jnp.log(norm_sum)

    def share_block(key_block, first):
        masked, allowed = block_scores(key_block, first)
        return jnp.where(allowed, jnp.exp(masked - log_norm[..., None]), 0.0)

    def accumulate(mixed, item):
        key_block, value_block, first = item
        shares_low = share_block(key_block, first).astype(jnp.bfloat16)
        return (
            mixed
            + jnp.einsum(
                "hqk,khe->qhe", shares_low, value_block, preferred_element_type=jnp.float32
            ),
            None,
        )

    mixed, _ = lax.scan(
        accumulate,
        jnp.zeros((count, local_heads, HEAD), jnp.float32),
        (key_blocks, value_blocks, firsts),
    )
    mixed_low = mixed.reshape(count, width).astype(jnp.bfloat16)
    attention = jnp.dot(mixed_low, full_out, preferred_element_type=jnp.float32)
    hidden = jnp.dot(low_two, full_up, preferred_element_type=jnp.float32) + up_bias.astype(
        jnp.float32
    )
    activated = jax.nn.gelu(hidden, approximate=False).astype(jnp.bfloat16)
    branches = attention + jnp.dot(activated, full_down, preferred_element_type=jnp.float32)
    joint = lax.psum(branches.astype(jnp.bfloat16), "head").astype(jnp.float32)
    output = inputs + joint + out_bias.astype(jnp.float32) + down_bias.astype(jnp.float32)
    upstream = cotangent[0]
    down_grad = jnp.dot(activated.T, upstream, preferred_element_type=jnp.float32)
    activated_grad = jnp.dot(upstream, full_down.T, preferred_element_type=jnp.float32)
    _, gelu_back = jax.vjp(partial(jax.nn.gelu, approximate=False), hidden)
    hidden_grad = gelu_back(activated_grad)[0].astype(jnp.bfloat16)
    up_grad = jnp.dot(low_two.T, hidden_grad, preferred_element_type=jnp.float32)
    up_bias_grad = jnp.sum(hidden_grad.astype(jnp.float32), axis=0)
    normed_two_grad = jnp.dot(hidden_grad, full_up.T, preferred_element_type=jnp.float32)
    out_grad = jnp.dot(mixed_low.T, upstream, preferred_element_type=jnp.float32)
    mixed_grad = jnp.dot(upstream, full_out.T, preferred_element_type=jnp.float32).astype(
        jnp.bfloat16
    )
    mixed_grad_heads = mixed_grad.reshape(count, local_heads, HEAD)
    delta = jnp.sum(mixed_grad_heads.astype(jnp.float32) * mixed, axis=-1).T

    def backward_block(query_grad, item):
        key_block, value_block, first = item
        shares = share_block(key_block, first)
        share_grad = jnp.einsum(
            "qhe,khe->hqk", mixed_grad_heads, value_block, preferred_element_type=jnp.float32
        )
        score_grad = (shares * (share_grad - delta[..., None])).astype(jnp.bfloat16)
        query_grad = (
            query_grad
            + jnp.einsum("hqk,khe->qhe", score_grad, key_block, preferred_element_type=jnp.float32)
            * scale
        )
        key_grad = (
            jnp.einsum("hqk,qhe->khe", score_grad, query, preferred_element_type=jnp.float32)
            * scale
        )
        value_grad = jnp.einsum(
            "hqk,qhe->khe",
            shares.astype(jnp.bfloat16),
            mixed_grad_heads,
            preferred_element_type=jnp.float32,
        )
        return (
            query_grad,
            jnp.concatenate(
                [key_grad.reshape(block, width), value_grad.reshape(block, width)], axis=1
            ),
        )

    query_grad, key_terms = lax.scan(
        backward_block,
        jnp.zeros((count, local_heads, HEAD), jnp.float32),
        (key_blocks, value_blocks, firsts),
    )
    own_grads = lax.psum_scatter(
        key_terms.reshape(length, 2 * width).astype(jnp.bfloat16),
        "ctx",
        scatter_dimension=0,
        tiled=True,
    ).astype(jnp.float32)
    query_pre = rotary(query_grad, -angles).reshape(count, width)
    key_pre = rotary(own_grads[:, :width].reshape(count, local_heads, HEAD), -angles).reshape(
        count, width
    )
    projected_grad = jnp.stack([query_pre, key_pre, own_grads[:, width:]]).astype(jnp.bfloat16)
    qkv_grad = jnp.einsum(
        "nd,cne->cde", low_one, projected_grad, preferred_element_type=jnp.float32
    )
    qkv_bias_grad = jnp.sum(projected_grad.astype(jnp.float32), axis=1)
    normed_one_grad = jnp.einsum(
        "cne,cde->nd", projected_grad, full_qkv, preferred_element_type=jnp.float32
    )
    normed_one_grad, normed_two_grad = (
        lax.psum(normed_one_grad.astype(jnp.bfloat16), "head").astype(jnp.float32),
        lax.psum(normed_two_grad.astype(jnp.bfloat16), "head").astype(jnp.float32),
    )
    _, norm_back_one = jax.vjp(layer_norm, inputs, gain_one, offset_one)
    input_one, gain_grad_one, offset_grad_one = norm_back_one(normed_one_grad)
    _, norm_back_two = jax.vjp(layer_norm, inputs, gain_two, offset_two)
    input_two, gain_grad_two, offset_grad_two = norm_back_two(normed_two_grad)
    upstream_wide = upstream.astype(jnp.float32)
    input_grad = upstream_wide + input_one + input_two
    bias_grad = jnp.sum(upstream_wide, axis=0)
    small = lax.psum(
        (
            gain_grad_one,
            offset_grad_one,
            qkv_bias_grad,
            bias_grad,
            gain_grad_two,
            offset_grad_two,
            up_bias_grad,
        ),
        ("stream", "ctx"),
    )
    slices = (
        lax.psum_scatter(
            qkv_grad.astype(jnp.bfloat16), "ctx", scatter_dimension=1, tiled=True
        ).astype(jnp.float32),
        lax.psum_scatter(
            out_grad.astype(jnp.bfloat16), "ctx", scatter_dimension=1, tiled=True
        ).astype(jnp.float32),
        lax.psum_scatter(
            up_grad.astype(jnp.bfloat16), "ctx", scatter_dimension=0, tiled=True
        ).astype(jnp.float32),
        lax.psum_scatter(
            down_grad.astype(jnp.bfloat16), "ctx", scatter_dimension=1, tiled=True
        ).astype(jnp.float32),
    )
    shards = (
        lax.psum(slices[0].astype(jnp.bfloat16), "stream").astype(jnp.float32),
        lax.psum(slices[1].astype(jnp.bfloat16), "stream").astype(jnp.float32),
        lax.psum(slices[2].astype(jnp.bfloat16), "stream").astype(jnp.float32),
        lax.psum(slices[3].astype(jnp.bfloat16), "stream").astype(jnp.float32),
    )
    return (
        output.astype(jnp.bfloat16)[None],
        input_grad[None],
        small[0],
        small[1],
        shards[0],
        small[2],
        shards[1],
        small[3],
        small[4],
        small[5],
        shards[2],
        small[6],
        shards[3],
        small[3],
    )


def token_places(doc_sizes, length):
    positions = jnp.arange(length, dtype=jnp.int32)
    return positions, doc_starts(doc_sizes, positions)


MESH = pl.DeviceIdType.MESH


def span(index, size):
    return pl.ds(pl.multiple_of(index * size, size), size)


def places():
    return lax.axis_index("stream"), lax.axis_index("ctx"), lax.axis_index("head")


def greet(peers):
    barrier = pltpu.get_barrier_semaphore()
    for peer in peers:
        pl.semaphore_signal(barrier, inc=1, device_id=peer, device_id_type=MESH)
    pl.semaphore_wait(barrier, len(peers))


def gather_body(
    x_ref, g_ref, qkv_ref, up_ref, out_ref, down_ref,
    x_all, g_all, qkv_all, up_all, out_all, down_all,
    z_send, z_recv, x_send, x_recv, y_send, y_recv, fx_send, fx_recv, fy_send, fy_recv,
    line_send, line_recv, core_send, core_recv, own_sem,
    *held,
):
    s, c, h = places()
    x_peer = s + 1 - 2 * lax.rem(s, 2)
    y_peer = lax.rem(s + 2, 4)
    across = ((x_peer, c, h), (y_peer, c, h))
    core_peer = (s, c, 1 - h)
    ring = [(s, lax.rem(c + k, 4), h) for k in (1, 2, 3)]
    greet([*across, core_peer, *ring])

    count = x_ref.shape[0]
    slab, width, units = up_ref.shape[0], out_ref.shape[0] // 4, down_ref.shape[0] // 4
    quarter, half_count = slab // 4, count // 2

    def rows(base, size):
        return pl.ds(pl.multiple_of(base, size), size)

    def landed(m, r, part, half):
        def cut(total):
            size = total // 4
            if half is None:
                return part * size, size
            return part * size + half * (size // 2), size // 2

        if m == 0:
            at, size = cut(slab)
            return qkv_all.at[:, rows(r * slab + at, size), :]
        if m == 1:
            at, size = cut(slab)
            return up_all.at[rows(r * slab + at, size), :]
        if m == 2:
            at, size = cut(width)
            return out_all.at[rows(at, size), span(r, slab)]
        at, size = cut(units)
        return down_all.at[rows(at, size), span(r, slab)]

    def piece(m, to, part=None):
        if m == 0:
            inner = slice(None) if part is None else span(part, quarter)
            return qkv_ref.at[:, inner, span(to, width)]
        if m == 1:
            inner = slice(None) if part is None else span(part, quarter)
            return up_ref.at[inner, span(to, units)]
        size = width if m == 2 else units
        ref = out_ref if m == 2 else down_ref
        if part is None:
            return ref.at[span(to, size), :]
        return ref.at[rows(to * size + part * (size // 4), size // 4), :]

    def whole_piece(m, r):
        if m == 0:
            return qkv_all.at[:, span(r, slab), :]
        if m == 1:
            return up_all.at[span(r, slab), :]
        return (out_all if m == 2 else down_all).at[:, span(r, slab)]

    def remote(src, dst, send, recv, to):
        return pltpu.make_async_remote_copy(
            src_ref=src, dst_ref=dst, send_sem=send, recv_sem=recv, device_id=to, device_id_type=MESH
        )

    def z_copy(m, k):
        to = lax.rem(c + 4 - k, 4)
        return remote(
            piece(m, to, s), landed(m, c, s, None), z_send.at[m, k - 1], z_recv.at[m, k - 1], (s, to, h)
        )

    def direct(m, k, axis):
        r = lax.rem(c + k, 4)
        send, recv = (x_send, x_recv) if axis == 0 else (y_send, y_recv)
        here = landed(m, r, s, None)
        return remote(here, here, send.at[m, k - 1], recv.at[m, k - 1], across[axis])

    def onward(m, k, axis):
        r = lax.rem(c + k, 4)
        send, recv = (fx_send, fx_recv) if axis == 0 else (fy_send, fy_recv)
        here = landed(m, r, y_peer if axis == 0 else x_peer, 1 if axis == 0 else 0)
        return remote(here, here, send.at[m, k - 1], recv.at[m, k - 1], across[axis])

    lines = ((x_ref, x_all), (g_ref, g_all))

    def block(a, origin):
        return lines[a][1].at[rows(origin * count + h * half_count, half_count), :]

    def line_copy(a, t, side):
        origin = c - t if side == 0 else c + t
        src = lines[a][0].at[span(h, half_count), :] if t == 0 else block(a, origin)
        to = c + 1 if side == 0 else c - 1
        return remote(
            src, block(a, origin), line_send.at[a, side, t], line_recv.at[a, side, t], (s, to, h)
        )

    def core_copy(a, t, side):
        origin = c - t if side == 0 else c + t
        here = block(a, origin)
        return remote(here, here, core_send.at[a, side, t - 1], core_recv.at[a, side, t - 1], core_peer)

    def sends(t, side):
        if side == 0:
            return (c >= t) & (c < 3)
        return (c + t <= 3) & (c > 0)

    def gets(t, side):
        return c >= t if side == 0 else c + t <= 3

    def line_step(a, t):
        for side in (0, 1):
            @pl.when(gets(t, side))
            def _():
                line_copy(a, t - 1, side).wait_recv()
                core_copy(a, t, side).start()

            if t < 3:
                @pl.when(sends(t, side))
                def _():
                    line_copy(a, t, side).start()

    near = (1, 3, 2)
    order = [(m, k) for m in (0, 1, 3, 2) for k in near]

    def start_lines():
        for a in (0, 1):
            for side in (0, 1):
                @pl.when(sends(0, side))
                def _():
                    line_copy(a, 0, side).start()

    def start_z(m):
        for k in near:
            z_copy(m, k).start()

    def pass_on(m):
        for k in near:
            direct(m, k, 0).wait_recv()
            onward(m, k, 1).start()
            direct(m, k, 1).wait_recv()
            onward(m, k, 0).start()

    def spread(m):
        for k in near:
            z_copy(m, k).wait_recv()
            direct(m, k, 0).start()
            direct(m, k, 1).start()

    start_z(0)
    start_lines()
    start_z(1)
    sources = [lines[0][0], lines[1][0]] + [piece(m, c) for m in range(4)]
    ends = [lines[a][1].at[span(c, count), :] for a in (0, 1)] + [whole_piece(m, c) for m in range(4)]
    ins = [pltpu.make_async_copy(a, b, own_sem.at[i]) for i, (a, b) in enumerate(zip(sources, held))]
    own = [pltpu.make_async_copy(b, e, own_sem.at[i]) for i, (b, e) in enumerate(zip(held, ends))]
    for copy in ins:
        copy.start()
    for copy, out in zip(ins, own):
        copy.wait()
        out.start()

    spread(0)
    line_step(0, 1)
    line_step(1, 1)
    start_z(3)
    spread(1)
    pass_on(0)
    start_z(2)
    line_step(0, 2)
    line_step(1, 2)
    spread(3)
    pass_on(1)
    spread(2)
    pass_on(3)
    line_step(0, 3)
    line_step(1, 3)
    pass_on(2)
    for m, k in order:
        onward(m, k, 0).wait_recv()
        onward(m, k, 1).wait_recv()
    for a in (0, 1):
        for side in (0, 1):
            for t in (1, 2, 3):
                @pl.when(gets(t, side))
                def _():
                    core_copy(a, t, side).wait()
                @pl.when(sends(t - 1, side))
                def _():
                    line_copy(a, t - 1, side).wait_send()
    for m, k in order:
        z_copy(m, k).wait_send()
        for axis in (0, 1):
            direct(m, k, axis).wait_send()
            onward(m, k, axis).wait_send()
    for copy in own:
        copy.wait()


def gather_all(tokens, cotangent, w_qkv, w_up, w_out, w_down):
    count, model = tokens.shape
    slab = w_up.shape[0]
    width, units = w_out.shape[0] // 4, w_down.shape[0] // 4
    bf16 = jnp.bfloat16
    dma = pltpu.SemaphoreType.DMA
    return pl.pallas_call(
        gather_body,
        out_shape=[
            jax.ShapeDtypeStruct((4 * count, model), bf16),
            jax.ShapeDtypeStruct((4 * count, model), bf16),
            jax.ShapeDtypeStruct((3, model, width), bf16),
            jax.ShapeDtypeStruct((model, units), bf16),
            jax.ShapeDtypeStruct((width, model), bf16),
            jax.ShapeDtypeStruct((units, model), bf16),
        ],
        in_specs=[pl.BlockSpec(memory_space=pl.ANY)] * 6,
        out_specs=[pl.BlockSpec(memory_space=pl.ANY)] * 6,
        scratch_shapes=[dma((4, 3))] * 10 + [dma((2, 2, 3))] * 4 + [dma((6,))]
        + [
            pltpu.VMEM(shape, bf16)
            for shape in (
                (count, model), (count, model), (3, slab, width), (slab, units), (width, slab), (units, slab)
            )
        ],
        compiler_params=pltpu.CompilerParams(
            collective_id=0, has_side_effects=True, vmem_limit_bytes=32 << 20
        ),
        name="gather",
    )(tokens, cotangent, w_qkv, w_up, w_out, w_down)


LEADS = (12, 4, 1, 1)
F32, BF16 = jnp.float32, jnp.bfloat16


def dot(a, b, over):
    return lax.dot_general(a, b, ((over[0:1], over[1:2]), ((), ())), preferred_element_type=F32)


def settle_body(
    act_in, up_in, unit_in, dh_in, dqkv_in, mixed_in, wq_in, wu_in, wo_in, wd_in, cols_ref, rows_ref,
    joint, inward, o0, o1, o2, o3, small_out,
    s1x_send, s1x_recv, s1y_send, s1y_recv, s2x_send, s2x_recv, s2y_send, s2y_recv,
    x_send, x_recv, y_send, y_recv, fx_send, fx_recv, fy_send, fy_recv,
    z_send, z_recv, keep_sem, load_sem, weight_sem,
    core_send, core_recv, row_send, row_recv, back_send, back_recv, back_sem,
    sum_send, sum_recv, sum_sem,
    act, up, unit, dh, dqkv, mixed, w_wide, w_out, w_qkv,
    gb0, gb1, gb2, gb3, fa0, fb0, fa1, fb1, fa2, fb2, fa3, fb3, ga0, hb0, ga1, hb1, ga2, hb2, ga3, hb3,
    own_half, core_half, send_half, row_parts, done_half,
    sums, sums_core, slots, total_own, total_x, total_y,
):
    s, c, h = places()
    x_at, y_at = lax.rem(s, 2), lax.div(s, 2)
    x_off, y_off = 1 - x_at, 1 - y_at
    x_peer, y_peer = y_at * 2 + x_off, y_off * 2 + x_at
    across = ((x_peer, c, h), (y_peer, c, h))
    core_peer = (s, c, 1 - h)
    near = (1, 3, 2)
    greet([*across, core_peer, *[(s, lax.rem(c + k, 4), h) for k in near]])
    grads, outs = (gb0, gb1, gb2, gb3), (o0, o1, o2, o3)
    first = ((fa0, fb0), (fa1, fb1), (fa2, fb2), (fa3, fb3))
    second = ((ga0, hb0), (ga1, hb1), (ga2, hb2), (ga3, hb3))
    slab = o2.shape[-1]
    length, model = up.shape
    units, width = act.shape[1], mixed.shape[1]
    half_cols = model // 2
    count = joint.shape[0]
    tile = 256

    def remote(src, dst, send, recv, to):
        return pltpu.make_async_remote_copy(
            src_ref=src, dst_ref=dst, send_sem=send, recv_sem=recv, device_id=to, device_id_type=MESH
        )

    loads = [
        pltpu.make_async_copy(a, b, load_sem.at[i])
        for i, (a, b) in enumerate(
            ((act_in, act), (up_in, up), (dh_in, dh), (unit_in, unit), (dqkv_in, dqkv), (mixed_in, mixed))
        )
    ]
    for load in loads:
        load.start()

    def side(which):
        return 1 - h if which == 0 else h

    def weight_load(i):
        at = span(side(i % 2), half_cols)
        if i < 2:
            return pltpu.make_async_copy(wd_in.at[:, at], w_wide.at[i], weight_sem.at[i])
        if i < 4:
            return pltpu.make_async_copy(wu_in.at[at, :], w_wide.at[i % 2], weight_sem.at[i])
        if i < 6:
            return pltpu.make_async_copy(wo_in.at[:, at], w_out.at[i % 2], weight_sem.at[i])
        return pltpu.make_async_copy(wq_in.at[:, at, :], w_qkv.at[i % 2], weight_sem.at[i])

    for i in (0, 4, 1, 5, 6, 7):
        weight_load(i).start()

    def one(m, half):
        src = grads[m].at[:, :, x_off, 0] if half == 0 else grads[m].at[:, y_off, :, 1]
        send, recv = (s1x_send, s1x_recv) if half == 0 else (s1y_send, s1y_recv)
        return remote(src, first[m][half], send.at[m], recv.at[m], across[half])

    def two(m, half):
        src = first[m][half].at[:, y_off if half == 0 else x_off]
        send, recv = (s2y_send, s2y_recv) if half == 0 else (s2x_send, s2x_recv)
        return remote(src, second[m][half], send.at[m], recv.at[m], across[1 - half])

    def add_first(m, half):
        into, more = first[m][half], grads[m]
        lead, _, height, _ = into.shape
        tall = min(height, 32)

        @pl.loop(0, lead * 2 * (height // tall))
        def _(i):
            at = lax.rem(i, height // tall)
            pair = lax.div(i, height // tall)
            l, j, rows = lax.div(pair, 2), lax.rem(pair, 2), span(at, tall)
            term = more[l, j, x_at, 0, rows, :] if half == 0 else more[l, y_at, j, 1, rows, :]
            into[l, j, rows, :] = (into[l, j, rows, :].astype(F32) + term.astype(F32)).astype(BF16)

    def add_second(m, half):
        into, more = second[m][half], first[m][half]
        mine = y_at if half == 0 else x_at
        lead, height, _ = into.shape
        tall = min(height, 32)

        @pl.loop(0, lead * (height // tall))
        def _(i):
            l, rows = lax.div(i, height // tall), span(lax.rem(i, height // tall), tall)
            term = more[l, mine, rows, :].astype(F32)
            into[l, rows, :] = (into[l, rows, :].astype(F32) + term).astype(BF16)

    def share_of(m, half, to):
        ref = second[m][half]
        if m == 0:
            return ref.reshape(3, 4, *ref.shape[1:]).at[:, to]
        if m == 1:
            return ref.at[to]
        return ref.at[0, :, span(to, slab)]

    def home(m, half):
        if m == 0:
            return outs[0].at[:, s, half, :, span(c, width)]
        if m == 1:
            return outs[1].at[s, half, :, span(c, units)]
        return outs[m].at[c, s, half]

    def z_copy(m, half, k):
        to = lax.rem(c + 4 - k, 4)
        i = (m * 2 + half) * 3 + k - 1
        return remote(share_of(m, half, to), home(m, half), z_send.at[i], z_recv.at[i], (s, to, h))

    def keep(m, half):
        return pltpu.make_async_copy(share_of(m, half, c), home(m, half), keep_sem.at[m, half])

    def quarter(m, q, half=None):
        if half is None:
            return outs[m].at[q] if m == 1 else outs[m].at[:, q]
        return outs[m].at[q, half] if m == 1 else outs[m].at[:, q, half]

    def direct(m, axis):
        send, recv = (x_send, x_recv) if axis == 0 else (y_send, y_recv)
        here = quarter(m, s)
        return remote(here, here, send.at[m], recv.at[m], across[axis])

    def onward(m, axis):
        send, recv = (fx_send, fx_recv) if axis == 0 else (fy_send, fy_recv)
        here = quarter(m, y_peer if axis == 0 else x_peer, 1 - axis)
        return remote(here, here, send.at[m], recv.at[m], across[axis])

    finals = (joint, inward)

    def core_copy(a):
        return remote(send_half, core_half.at[a], core_send.at[a], core_recv.at[a], core_peer)

    def row_copy(a, k):
        to = lax.rem(c + 4 - k, 4)
        return remote(
            own_half.at[a, span(to, count)], row_parts.at[a, k - 1],
            row_send.at[a, k - 1], row_recv.at[a, k - 1], (s, to, h),
        )

    def back_copy(a):
        return remote(
            done_half.at[a], finals[a].at[:, span(h, half_cols)], back_send.at[a], back_recv.at[a], core_peer
        )

    def back_keep(a):
        return pltpu.make_async_copy(done_half.at[a], finals[a].at[:, span(h, half_cols)], back_sem.at[a])

    def line_start(a):
        core_copy(a).wait_recv()
        tall = 32

        @pl.loop(0, length // tall)
        def _(i):
            rows = span(i, tall)
            own_half[a, rows, :] = (
                own_half[a, rows, :].astype(F32) + core_half[a, rows, :].astype(F32)
            ).astype(BF16)

        for k in near:
            row_copy(a, k).start()

    def line_sum(a):
        for k in near:
            row_copy(a, k).wait_recv()
        tall = 32

        @pl.loop(0, count // tall)
        def _(i):
            rows = span(i, tall)
            total = own_half[a, pl.ds(pl.multiple_of(c * count + i * tall, tall), tall), :].astype(F32)
            for k in range(3):
                total = total + row_parts[a, k, rows, :].astype(F32)
            done_half[a, rows, :] = total.astype(BF16)

        back_copy(a).start()
        back_keep(a).start()

    def down_grad():
        rows = units // 8

        @pl.loop(0, 4)
        def _(q):
            left = act[:, span(q, 2 * rows)]
            for j in range(model // 512):
                part = dot(left, up[:, j * 512 : (j + 1) * 512], (0, 0)).astype(BF16)
                for half in (0, 1):
                    gb3[0, lax.div(q, 2), lax.rem(q, 2), half, :, j * 512 : (j + 1) * 512] = part[
                        half * rows : (half + 1) * rows
                    ]

    def out_grad():
        rows = width // 8
        for j in range(model // 512):
            part = dot(mixed[...], up[:, j * 512 : (j + 1) * 512], (0, 0)).astype(BF16)
            for i in range(8):
                gb2[0, i // 4, (i // 2) % 2, i % 2, :, j * 512 : (j + 1) * 512] = part[i * rows : (i + 1) * rows]

    def scaled(part, t, at, column_sum):
        rows = span(t, tile)
        return (part * cols_ref[rows, at : at + 1] + cols_ref[rows, at + 1 : at + 2] * column_sum).astype(BF16)

    def column_sum(ref, cols):
        total = jnp.zeros((1, cols.stop - cols.start), F32)
        for i in range(length // tile):
            total = total + jnp.sum(ref[i * tile : (i + 1) * tile, cols].astype(F32), axis=0, keepdims=True)
        return total

    def up_grad():
        rows = tile // 4

        @pl.loop(0, model // tile)
        def _(t):
            left = unit[:, span(t, tile)]
            for j in range(units // 512):
                cols = slice(j * 512, (j + 1) * 512)
                near_sum = sums[5:6, 3 * width + j * 512 : 3 * width + (j + 1) * 512]
                part = scaled(dot(left, dh[:, cols], (0, 0)), t, 2, near_sum)
                for i in range(4):
                    gb1[lax.div(t, 2), lax.rem(t, 2), i // 2, i % 2, :, cols] = part[i * rows : (i + 1) * rows]

    def qkv_grad():
        rows = tile // 4

        @pl.loop(0, model // tile)
        def _(t):
            left = unit[:, span(t, tile)]
            for p in range(3):
                cols = slice(p * width, (p + 1) * width)
                part = scaled(dot(left, dqkv[:, cols], (0, 0)), t, 0, sums[5:6, cols])
                for i in range(4):
                    gb0[p * 4 + lax.div(t, 2), lax.rem(t, 2), i // 2, i % 2] = part[i * rows : (i + 1) * rows]

    def branches(which):
        into = send_half if which == 0 else own_half.at[0]

        @pl.loop(0, length // tile)
        def _(i):
            rows = span(i, tile)
            for j in range(half_cols // 512):
                cols = slice(j * 512, (j + 1) * 512)
                part = dot(mixed[rows, :], w_out[which, :, cols], (1, 0))
                part = part + dot(act[rows, :], w_wide[which, :, cols], (1, 0))
                into[rows, cols] = part.astype(BF16)

    def inwards(which):
        into = send_half if which == 0 else own_half.at[1]
        base = side(which) * half_cols
        for j in range(half_cols // 512):
            cols = slice(j * 512, (j + 1) * 512)
            far = span(side(which) * (half_cols // 512) + j, 512)
            zero = jnp.zeros((8, 512), F32)

            def step(i, carry):
                rows = span(i, tile)
                one_part = dot(dqkv[rows, 0:width], w_qkv[which, 0, cols, :], (1, 1))
                for p in (1, 2):
                    one_part = one_part + dot(
                        dqkv[rows, p * width : (p + 1) * width], w_qkv[which, p, cols, :], (1, 1)
                    )
                two_part = dot(dh[rows, :], w_wide[which, cols, :], (1, 1))
                into[rows, cols] = (one_part * rows_ref[0:1, far] + two_part * rows_ref[2:3, far]).astype(BF16)
                place = unit[rows, far].astype(F32)

                def fold(v):
                    return jnp.sum(v.reshape(tile // 8, 8, 512), axis=0)

                return (
                    carry[0] + fold(one_part * place),
                    carry[1] + fold(one_part),
                    carry[2] + fold(two_part * place),
                    carry[3] + fold(two_part),
                )

            found = lax.fori_loop(0, length // tile, step, (zero, zero, zero, zero))
            for n in range(4):
                sums[n : n + 1, far] = jnp.sum(found[n], axis=0, keepdims=True)

    def sum_core():
        return remote(sums, sums_core, sum_send.at[0], sum_recv.at[0], core_peer)

    def sum_line(k):
        return remote(
            sums, slots.at[c], sum_send.at[k], sum_recv.at[k], (s, lax.rem(c + 4 - k, 4), h)
        )

    def sum_x():
        return remote(total_own, total_x, sum_send.at[4], sum_recv.at[4], across[0])

    def sum_y():
        return remote(total_own, total_y, sum_send.at[5], sum_recv.at[5], across[1])

    order = (3, 1, 0, 2)
    loads[0].wait()
    loads[1].wait()
    down_grad()
    one(3, 0).start()
    one(3, 1).start()
    sums[4:5, :] = jnp.sum(up[span(c, count), :].astype(F32), axis=0, keepdims=True) * 0.5
    sums[5:8, :] = jnp.zeros((3, model), F32)
    loads[2].wait()
    loads[3].wait()
    for j in range(units // 512):
        sums[5:6, 3 * width + j * 512 : 3 * width + (j + 1) * 512] = column_sum(dh, slice(j * 512, (j + 1) * 512))
    up_grad()
    one(1, 0).start()
    one(1, 1).start()
    loads[4].wait()
    for p in range(3):
        sums[5:6, p * width : (p + 1) * width] = column_sum(dqkv, slice(p * width, (p + 1) * width))
    qkv_grad()
    one(0, 0).start()
    one(0, 1).start()
    loads[5].wait()
    out_grad()
    one(2, 0).start()
    one(2, 1).start()
    weight_load(0).wait()
    weight_load(4).wait()
    branches(0)
    core_copy(0).start()
    weight_load(2).start()
    weight_load(1).wait()
    weight_load(5).wait()
    branches(1)
    weight_load(3).start()

    def stage_two(m):
        for half in (0, 1):
            one(m, half).wait_recv()
            add_first(m, half)
            two(m, half).start()

    def stage_z(m):
        for half in (0, 1):
            two(m, half).wait_recv()
            add_second(m, half)
            for k in near:
                z_copy(m, half, k).start()
            keep(m, half).start()

    def stage_out(m):
        for half in (0, 1):
            for k in near:
                z_copy(m, half, k).wait_recv()
            keep(m, half).wait()
        for axis in (0, 1):
            direct(m, axis).start()

    def stage_on(m):
        direct(m, 0).wait_recv()
        onward(m, 1).start()
        direct(m, 1).wait_recv()
        onward(m, 0).start()

    stage_two(3)
    line_start(0)
    core_copy(0).wait_send()
    weight_load(2).wait()
    weight_load(6).wait()
    inwards(0)
    core_copy(1).start()
    weight_load(3).wait()
    weight_load(7).wait()
    inwards(1)
    sum_core().start()
    stage_two(1)
    stage_z(3)
    line_start(1)
    sum_core().wait()
    sums[0:5, :] = sums[0:5, :] + sums_core[0:5, :]
    for k in near:
        sum_line(k).start()
    slots[c] = sums[...]
    stage_two(0)
    stage_z(1)
    stage_out(3)
    line_sum(0)
    for k in near:
        sum_line(k).wait()
    total_own[0:8, :] = slots[0] + slots[1] + slots[2] + slots[3]
    for i in range(4):
        total_own[8 + i : 9 + i, :] = slots[i, 5:6, :]
    total_own[12:16, :] = jnp.zeros((4, model), F32)
    sum_x().start()
    stage_two(2)
    stage_z(0)
    stage_out(1)
    stage_on(3)
    line_sum(1)
    sum_x().wait()
    total_own[...] = total_own[...] + total_x[...]
    sum_y().start()
    stage_z(2)
    stage_out(0)
    stage_on(1)
    sum_y().wait()
    total_own[...] = total_own[...] + total_y[...]
    small_copy = pltpu.make_async_copy(total_own, small_out, sum_sem.at[0])
    small_copy.start()
    stage_out(2)
    stage_on(0)
    stage_on(2)
    for m in order:
        for axis in (0, 1):
            onward(m, axis).wait_recv()
    small_copy.wait()
    for a in (0, 1):
        back_copy(a).wait()
        back_keep(a).wait()
        for k in near:
            row_copy(a, k).wait_send()
    core_copy(1).wait_send()
    for m in order:
        for half in (0, 1):
            one(m, half).wait_send()
            two(m, half).wait_send()
            for k in near:
                z_copy(m, half, k).wait_send()
        for axis in (0, 1):
            direct(m, axis).wait_send()
            onward(m, axis).wait_send()


def settle_all(act, up, unit, dh, dqkv, mixed, w_qkv, w_up, w_out, w_down, cols, rows):
    length, model = up.shape
    units, width = act.shape[1], mixed.shape[1]
    slab, count, half = model // 4, length // 4, model // 2
    dma = pltpu.SemaphoreType.DMA
    heights = (slab // 8, slab // 8, width // 8, units // 8)
    widths = (width, units, model, model)
    out_shapes = [
        (count, model), (count, model),
        (3, 4, 2, heights[0], 4 * width), (4, 2, heights[1], 4 * units),
        (4, 4, 2, heights[2], slab), (4, 4, 2, heights[3], slab),
    ]
    scratch = [dma((4,))] * 16 + [dma((24,))] * 2 + [dma((4, 2)), dma((6,)), dma((8,))]
    scratch += [dma((2,)), dma((2,)), dma((2, 3)), dma((2, 3)), dma((2,)), dma((2,)), dma((2,))]
    scratch += [dma((6,)), dma((6,)), dma((1,))]
    vmem = [(length, units), (length, model), (length, model), (length, units), (length, 3 * width), (length, width)]
    vmem += [(2, units, half), (2, width, half), (2, 3, half, width)]
    shapes = list(zip(LEADS, heights, widths))
    vmem += [(l, 2, 2, 2, r, k) for l, r, k in shapes]
    vmem += [(l, 2, r, k) for l, r, k in shapes for _ in (0, 1)]
    vmem += [(l, r, k) for l, r, k in shapes for _ in (0, 1)]
    vmem += [(2, length, half), (2, length, half), (length, half), (2, 3, count, half), (2, count, half)]
    scratch += [pltpu.VMEM(v, BF16) for v in vmem]
    scratch += [pltpu.VMEM(v, F32) for v in ((8, model), (8, model), (4, 8, model), (16, model), (16, model), (16, model))]
    any_space = pl.BlockSpec(memory_space=pl.ANY)
    vmem_space = pl.BlockSpec(memory_space=pltpu.VMEM)
    joint, inward, q, u, o, d, small = pl.pallas_call(
        settle_body,
        out_shape=[jax.ShapeDtypeStruct(v, BF16) for v in out_shapes] + [jax.ShapeDtypeStruct((16, model), F32)],
        in_specs=[any_space] * 10 + [vmem_space] * 2,
        out_specs=[any_space] * 7,
        scratch_shapes=scratch,
        compiler_params=pltpu.CompilerParams(
            collective_id=1, has_side_effects=True, vmem_limit_bytes=63 << 20
        ),
        name="settle",
    )(act, up, unit, dh, dqkv, mixed, w_qkv, w_up, w_out, w_down, cols, rows)
    return (
        joint, inward, q.reshape(3, slab, 4 * width), u.reshape(slab, 4 * units),
        o.reshape(4 * width, slab), d.reshape(4 * units, slab), small,
    )


def per_device(
    tokens,
    doc_lengths,
    ln1_gain,
    ln1_bias,
    qkv_weight,
    qkv_bias,
    out_weight,
    out_bias,
    ln2_gain,
    ln2_bias,
    up_weight,
    up_bias,
    down_weight,
    down_bias,
    cotangent,
):
    f32, bf16 = jnp.float32, jnp.bfloat16
    ctx_count = lax.axis_size("ctx")
    c = lax.axis_index("ctx")
    count, model = tokens.shape[1], tokens.shape[2]
    length = count * ctx_count
    width = qkv_weight.shape[2] // ctx_count
    units = up_weight.shape[1] // ctx_count

    all_tokens, upstream, w_qkv, w_up, w_out, w_down = gather_all(
        tokens[0], cotangent[0], qkv_weight, up_weight, out_weight, down_weight
    )

    gain_one, offset_one = ln1_gain.astype(f32), ln1_bias.astype(f32)
    gain_two, offset_two = ln2_gain.astype(f32), ln2_bias.astype(f32)
    wide = all_tokens.astype(f32)
    centred = wide - jnp.mean(wide, axis=-1, keepdims=True)
    scale_of = lax.rsqrt(jnp.mean(centred * centred, axis=-1, keepdims=True) + 1e-05)
    unit = centred * scale_of
    low_one = (unit * gain_one + offset_one).astype(bf16)
    low_two = (unit * gain_two + offset_two).astype(bf16)

    positions, starts = token_places(doc_lengths[0], length)
    frequency = 10000.0 ** (-jnp.arange(0, ROT, 2, dtype=f32) / ROT)
    angles = (positions - starts).astype(f32)[:, None] * frequency[None, :]
    bias = lax.dynamic_slice_in_dim(qkv_bias, c * width, width, 1).astype(f32)
    projected = jnp.einsum("nd,cde->cne", low_one, w_qkv, preferred_element_type=f32)
    projected = projected + bias[:, None, :]
    heads = width // HEAD
    query = rotary(projected[0].reshape(length, heads, HEAD), angles).astype(bf16)
    keys = rotary(projected[1].reshape(length, heads, HEAD), angles).astype(bf16)
    values = projected[2].reshape(length, heads, HEAD).astype(bf16)
    scale = HEAD ** (-0.5)
    allowed = (positions[None, :] <= positions[:, None]) & (positions[None, :] >= starts[:, None])
    scores = jnp.einsum("qhe,khe->hqk", query, keys, preferred_element_type=f32) * scale
    masked = jnp.where(allowed[None], scores, -1e30)
    raised = jnp.where(
        allowed[None], jnp.exp(masked - jnp.max(masked, axis=-1, keepdims=True)), 0.0
    )
    shares = raised / jnp.sum(raised, axis=-1, keepdims=True)
    shares_low = shares.astype(bf16)
    mixed = jnp.einsum("hqk,khe->qhe", shares_low, values, preferred_element_type=f32)
    mixed_low = mixed.reshape(length, width).astype(bf16)

    up_part = lax.dynamic_slice_in_dim(up_bias, c * units, units, 0).astype(f32)
    hidden = jnp.dot(low_two, w_up, preferred_element_type=f32) + up_part
    activated = jax.nn.gelu(hidden, approximate=False).astype(bf16)
    _, gelu_back = jax.vjp(partial(jax.nn.gelu, approximate=False), hidden)
    activated_grad = jnp.dot(upstream, w_down.T, preferred_element_type=f32)
    hidden_grad = gelu_back(activated_grad)[0].astype(bf16)
    mixed_grad = (
        jnp.dot(upstream, w_out.T, preferred_element_type=f32)
        .astype(bf16)
        .reshape(length, heads, HEAD)
    )
    delta = jnp.sum(mixed_grad.astype(f32) * mixed, axis=-1).T
    share_grad = jnp.einsum("qhe,khe->hqk", mixed_grad, values, preferred_element_type=f32)
    score_grad = (shares * (share_grad - delta[..., None])).astype(bf16)
    query_grad = (
        jnp.einsum("hqk,khe->qhe", score_grad, keys, preferred_element_type=f32) * scale
    )
    key_grad = jnp.einsum("hqk,qhe->khe", score_grad, query, preferred_element_type=f32) * scale
    value_grad = jnp.einsum("hqk,qhe->khe", shares_low, mixed_grad, preferred_element_type=f32)
    projected_grad = jnp.concatenate(
        [
            rotary(query_grad, -angles).reshape(length, width),
            rotary(key_grad, -angles).reshape(length, width),
            value_grad.reshape(length, width),
        ],
        axis=1,
    ).astype(bf16)

    gains = jnp.stack([gain_one, offset_one, gain_two, offset_two])
    joint, inward, qkv_out, up_out, out_out, down_out, small = settle_all(
        activated,
        upstream,
        unit.astype(bf16),
        hidden_grad,
        projected_grad,
        mixed_low,
        w_qkv,
        w_up,
        w_out,
        w_down,
        jnp.pad(gains.T, ((0, 0), (0, 124))),
        jnp.pad(gains, ((0, 4), (0, 0))),
    )
    joint, inward = joint.astype(f32), inward.astype(f32)

    own = tokens[0].astype(f32)
    own_upstream = cotangent[0].astype(f32)
    output = own + joint + out_bias.astype(f32) + down_bias.astype(f32)
    own_centred = own - jnp.mean(own, axis=-1, keepdims=True)
    own_scale = lax.rsqrt(jnp.mean(own_centred * own_centred, axis=-1, keepdims=True) + 1e-05)
    own_unit = own_centred * own_scale
    input_grad = own_upstream + own_scale * (
        inward
        - jnp.mean(inward, axis=-1, keepdims=True)
        - own_unit * jnp.mean(inward * own_unit, axis=-1, keepdims=True)
    )

    qkv_bias_grad = (
        small[8:12, : 3 * width].reshape(ctx_count, 3, width).transpose(1, 0, 2).reshape(3, -1)
    )
    up_bias_grad = small[8:12, 3 * width : 3 * width + units].reshape(-1)
    return (
        output.astype(bf16)[None],
        input_grad[None],
        small[0],
        small[1],
        qkv_out.astype(f32),
        qkv_bias_grad,
        out_out.astype(f32),
        small[4],
        small[2],
        small[3],
        up_out.astype(f32),
        up_bias_grad,
        down_out.astype(f32),
        small[4],
    )


def solution(mesh):
    in_specs = (
        P("stream", "ctx", None),
        P("stream", None),
        P(),
        P(),
        P(None, "ctx", "head"),
        P(None, "head"),
        P("head", "ctx"),
        P(),
        P(),
        P(),
        P("ctx", "head"),
        P("head"),
        P("head", "ctx"),
        P(),
        P("stream", "ctx", None),
    )
    out_specs = (
        P("stream", "ctx", None),
        P("stream", "ctx", None),
        P(),
        P(),
        P(None, "ctx", "head"),
        P(None, "head"),
        P("head", "ctx"),
        P(),
        P(),
        P(),
        P("ctx", "head"),
        P("head"),
        P("head", "ctx"),
        P(),
    )
    split = mesh.shape["ctx"] * mesh.shape["head"]

    def whole(*arrays):
        heads, units = arrays[4].shape[2] // HEAD, arrays[10].shape[1]
        grouped = (mesh.shape["stream"], mesh.shape["ctx"], mesh.shape["head"]) == (4, 4, 2)
        fits = grouped and heads == split and units % (split * 512) == 0
        return jax.shard_map(
            per_device if fits else general_device,
            mesh=mesh,
            in_specs=in_specs,
            out_specs=out_specs,
            check_vma=False,
        )(*arrays)

    return whole
```

```python
from functools import partial
import math

import jax
import jax.numpy as jnp
from jax import lax
from jax.experimental import pallas as pl
from jax.experimental.pallas import tpu as pltpu
from jax.sharding import PartitionSpec as P

HEAD = 256
ROT = 64


def layer_norm(values, gain, offset):
    centre = jnp.mean(values, axis=-1, keepdims=True)
    centred = values - centre
    spread = jnp.mean(centred * centred, axis=-1, keepdims=True)
    return centred * lax.rsqrt(spread + 1e-05) * gain + offset


def rotary(values, angles):
    half = angles.shape[-1]
    cosine = jnp.cos(angles)[:, None, :]
    sine = jnp.sin(angles)[:, None, :]
    first = values[..., :half]
    second = values[..., half : 2 * half]
    return jnp.concatenate(
        [first * cosine - second * sine, second * cosine + first * sine, values[..., 2 * half :]],
        axis=-1,
    )


def doc_starts(doc_sizes, positions):
    place = jnp.arange(doc_sizes.shape[0])
    before = place[None, :] < place[:, None]
    starts = jnp.sum(jnp.where(before, doc_sizes[None, :], 0), axis=1)
    return jnp.max(jnp.where(starts[None, :] <= positions[:, None], starts[None, :], 0), axis=1)


def general_device(
    tokens,
    doc_lengths,
    ln1_gain,
    ln1_bias,
    qkv_weight,
    qkv_bias,
    out_weight,
    out_bias,
    ln2_gain,
    ln2_bias,
    up_weight,
    up_bias,
    down_weight,
    down_bias,
    cotangent,
):
    inputs = tokens[0].astype(jnp.float32)
    count = inputs.shape[0]
    ctx_count = lax.axis_size("ctx")
    length = count * ctx_count
    positions = lax.axis_index("ctx") * count + jnp.arange(count, dtype=jnp.int32)
    starts = doc_starts(doc_lengths[0], positions)
    frequency = 10000.0 ** (-jnp.arange(0, ROT, 2, dtype=jnp.float32) / ROT)
    angles = (positions - starts).astype(jnp.float32)[:, None] * frequency[None, :]
    scale = HEAD ** (-0.5)
    full_qkv, full_out, full_up, full_down = (
        lax.all_gather(qkv_weight, "ctx", axis=1, tiled=True),
        lax.all_gather(out_weight, "ctx", axis=1, tiled=True),
        lax.all_gather(up_weight, "ctx", axis=0, tiled=True),
        lax.all_gather(down_weight, "ctx", axis=1, tiled=True),
    )
    gain_one = ln1_gain.astype(jnp.float32)
    offset_one = ln1_bias.astype(jnp.float32)
    gain_two = ln2_gain.astype(jnp.float32)
    offset_two = ln2_bias.astype(jnp.float32)
    low_one = layer_norm(inputs, gain_one, offset_one).astype(jnp.bfloat16)
    low_two = layer_norm(inputs, gain_two, offset_two).astype(jnp.bfloat16)
    projected = (
        jnp.einsum("nd,cde->cne", low_one, full_qkv, preferred_element_type=jnp.float32)
        + qkv_bias.astype(jnp.float32)[:, None, :]
    )
    width = projected.shape[2]
    local_heads = width // HEAD
    query = rotary(projected[0].reshape(count, local_heads, HEAD), angles).astype(jnp.bfloat16)
    keys_flat = (
        rotary(projected[1].reshape(count, local_heads, HEAD), angles)
        .reshape(count, width)
        .astype(jnp.bfloat16)
    )
    values_flat = projected[2].astype(jnp.bfloat16)
    all_keys, all_values = (
        lax.all_gather(keys_flat, "ctx", axis=0, tiled=True),
        lax.all_gather(values_flat, "ctx", axis=0, tiled=True),
    )
    block = math.gcd(length, 512)
    block_count = length // block
    key_blocks = all_keys.reshape(block_count, block, local_heads, HEAD)
    value_blocks = all_values.reshape(block_count, block, local_heads, HEAD)
    firsts = jnp.arange(block_count, dtype=jnp.int32) * block

    def block_scores(key_block, first):
        key_index = first + jnp.arange(block, dtype=jnp.int32)
        allowed = (key_index[None, :] <= positions[:, None]) & (
            key_index[None, :] >= starts[:, None]
        )
        scores = (
            jnp.einsum("qhe,khe->hqk", query, key_block, preferred_element_type=jnp.float32) * scale
        )
        return (jnp.where(allowed[None], scores, -1e30), allowed[None])

    def statistics(carry, item):
        running, norm_sum = carry
        key_block, first = item
        masked, allowed = block_scores(key_block, first)
        newest = jnp.maximum(running, jnp.max(masked, axis=-1))
        raised = jnp.where(allowed, jnp.exp(masked - newest[..., None]), 0.0)
        norm_sum = norm_sum * jnp.exp(running - newest) + jnp.sum(raised, axis=-1)
        return ((newest, norm_sum), None)

    initial = (
        jnp.full((local_heads, count), -1e30, jnp.float32),
        jnp.zeros((local_heads, count), jnp.float32),
    )
    (running, norm_sum), _ = lax.scan(statistics, initial, (key_blocks, firsts))
    log_norm = running + jnp.log(norm_sum)

    def share_block(key_block, first):
        masked, allowed = block_scores(key_block, first)
        return jnp.where(allowed, jnp.exp(masked - log_norm[..., None]), 0.0)

    def accumulate(mixed, item):
        key_block, value_block, first = item
        shares_low = share_block(key_block, first).astype(jnp.bfloat16)
        return (
            mixed
            + jnp.einsum(
                "hqk,khe->qhe", shares_low, value_block, preferred_element_type=jnp.float32
            ),
            None,
        )

    mixed, _ = lax.scan(
        accumulate,
        jnp.zeros((count, local_heads, HEAD), jnp.float32),
        (key_blocks, value_blocks, firsts),
    )
    mixed_low = mixed.reshape(count, width).astype(jnp.bfloat16)
    attention = jnp.dot(mixed_low, full_out, preferred_element_type=jnp.float32)
    hidden = jnp.dot(low_two, full_up, preferred_element_type=jnp.float32) + up_bias.astype(
        jnp.float32
    )
    activated = jax.nn.gelu(hidden, approximate=False).astype(jnp.bfloat16)
    branches = attention + jnp.dot(activated, full_down, preferred_element_type=jnp.float32)
    joint = lax.psum(branches.astype(jnp.bfloat16), "head").astype(jnp.float32)
    output = inputs + joint + out_bias.astype(jnp.float32) + down_bias.astype(jnp.float32)
    upstream = cotangent[0]
    down_grad = jnp.dot(activated.T, upstream, preferred_element_type=jnp.float32)
    activated_grad = jnp.dot(upstream, full_down.T, preferred_element_type=jnp.float32)
    _, gelu_back = jax.vjp(partial(jax.nn.gelu, approximate=False), hidden)
    hidden_grad = gelu_back(activated_grad)[0].astype(jnp.bfloat16)
    up_grad = jnp.dot(low_two.T, hidden_grad, preferred_element_type=jnp.float32)
    up_bias_grad = jnp.sum(hidden_grad.astype(jnp.float32), axis=0)
    normed_two_grad = jnp.dot(hidden_grad, full_up.T, preferred_element_type=jnp.float32)
    out_grad = jnp.dot(mixed_low.T, upstream, preferred_element_type=jnp.float32)
    mixed_grad = jnp.dot(upstream, full_out.T, preferred_element_type=jnp.float32).astype(
        jnp.bfloat16
    )
    mixed_grad_heads = mixed_grad.reshape(count, local_heads, HEAD)
    delta = jnp.sum(mixed_grad_heads.astype(jnp.float32) * mixed, axis=-1).T

    def backward_block(query_grad, item):
        key_block, value_block, first = item
        shares = share_block(key_block, first)
        share_grad = jnp.einsum(
            "qhe,khe->hqk", mixed_grad_heads, value_block, preferred_element_type=jnp.float32
        )
        score_grad = (shares * (share_grad - delta[..., None])).astype(jnp.bfloat16)
        query_grad = (
            query_grad
            + jnp.einsum("hqk,khe->qhe", score_grad, key_block, preferred_element_type=jnp.float32)
            * scale
        )
        key_grad = (
            jnp.einsum("hqk,qhe->khe", score_grad, query, preferred_element_type=jnp.float32)
            * scale
        )
        value_grad = jnp.einsum(
            "hqk,qhe->khe",
            shares.astype(jnp.bfloat16),
            mixed_grad_heads,
            preferred_element_type=jnp.float32,
        )
        return (
            query_grad,
            jnp.concatenate(
                [key_grad.reshape(block, width), value_grad.reshape(block, width)], axis=1
            ),
        )

    query_grad, key_terms = lax.scan(
        backward_block,
        jnp.zeros((count, local_heads, HEAD), jnp.float32),
        (key_blocks, value_blocks, firsts),
    )
    own_grads = lax.psum_scatter(
        key_terms.reshape(length, 2 * width).astype(jnp.bfloat16),
        "ctx",
        scatter_dimension=0,
        tiled=True,
    ).astype(jnp.float32)
    query_pre = rotary(query_grad, -angles).reshape(count, width)
    key_pre = rotary(own_grads[:, :width].reshape(count, local_heads, HEAD), -angles).reshape(
        count, width
    )
    projected_grad = jnp.stack([query_pre, key_pre, own_grads[:, width:]]).astype(jnp.bfloat16)
    qkv_grad = jnp.einsum(
        "nd,cne->cde", low_one, projected_grad, preferred_element_type=jnp.float32
    )
    qkv_bias_grad = jnp.sum(projected_grad.astype(jnp.float32), axis=1)
    normed_one_grad = jnp.einsum(
        "cne,cde->nd", projected_grad, full_qkv, preferred_element_type=jnp.float32
    )
    normed_one_grad, normed_two_grad = (
        lax.psum(normed_one_grad.astype(jnp.bfloat16), "head").astype(jnp.float32),
        lax.psum(normed_two_grad.astype(jnp.bfloat16), "head").astype(jnp.float32),
    )
    _, norm_back_one = jax.vjp(layer_norm, inputs, gain_one, offset_one)
    input_one, gain_grad_one, offset_grad_one = norm_back_one(normed_one_grad)
    _, norm_back_two = jax.vjp(layer_norm, inputs, gain_two, offset_two)
    input_two, gain_grad_two, offset_grad_two = norm_back_two(normed_two_grad)
    upstream_wide = upstream.astype(jnp.float32)
    input_grad = upstream_wide + input_one + input_two
    bias_grad = jnp.sum(upstream_wide, axis=0)
    small = lax.psum(
        (
            gain_grad_one,
            offset_grad_one,
            qkv_bias_grad,
            bias_grad,
            gain_grad_two,
            offset_grad_two,
            up_bias_grad,
        ),
        ("stream", "ctx"),
    )
    slices = (
        lax.psum_scatter(
            qkv_grad.astype(jnp.bfloat16), "ctx", scatter_dimension=1, tiled=True
        ).astype(jnp.float32),
        lax.psum_scatter(
            out_grad.astype(jnp.bfloat16), "ctx", scatter_dimension=1, tiled=True
        ).astype(jnp.float32),
        lax.psum_scatter(
            up_grad.astype(jnp.bfloat16), "ctx", scatter_dimension=0, tiled=True
        ).astype(jnp.float32),
        lax.psum_scatter(
            down_grad.astype(jnp.bfloat16), "ctx", scatter_dimension=1, tiled=True
        ).astype(jnp.float32),
    )
    shards = (
        lax.psum(slices[0].astype(jnp.bfloat16), "stream").astype(jnp.float32),
        lax.psum(slices[1].astype(jnp.bfloat16), "stream").astype(jnp.float32),
        lax.psum(slices[2].astype(jnp.bfloat16), "stream").astype(jnp.float32),
        lax.psum(slices[3].astype(jnp.bfloat16), "stream").astype(jnp.float32),
    )
    return (
        output.astype(jnp.bfloat16)[None],
        input_grad[None],
        small[0],
        small[1],
        shards[0],
        small[2],
        shards[1],
        small[3],
        small[4],
        small[5],
        shards[2],
        small[6],
        shards[3],
        small[3],
    )


def token_places(doc_sizes, length):
    positions = jnp.arange(length, dtype=jnp.int32)
    return positions, doc_starts(doc_sizes, positions)


MESH = pl.DeviceIdType.MESH
F32, BF16 = jnp.float32, jnp.bfloat16


def dot(a, b, over):
    return lax.dot_general(a, b, ((over[0:1], over[1:2]), ((), ())), preferred_element_type=F32)


def span(index, size):
    return pl.ds(pl.multiple_of(index * size, size), size)


def places():
    return lax.axis_index("stream"), lax.axis_index("ctx"), lax.axis_index("head")


def greet(peers):
    barrier = pltpu.get_barrier_semaphore()
    for peer in peers:
        pl.semaphore_signal(barrier, inc=1, device_id=peer, device_id_type=MESH)
    pl.semaphore_wait(barrier, len(peers))


def gather_body(
    x_ref, g_ref, qkv_ref, up_ref, out_ref, down_ref, rows_ref, bias_ref, turn_ref, start_ref,
    g_out, unit_out, act_out, dh_out, dqkv_out, mixed_out, qkv_out, up_out, out_out, down_out,
    z_send, z_recv, x_send, x_recv, y_send, y_recv, fx_send, fx_recv, fy_send, fy_recv,
    line_send, line_recv, core_send, core_recv, own_sem, give_sem, block_sem,
    x_all, g_all, qkv_all, up_all, out_all, down_all,
    low_one, low_two, unit, query, keys, values, act, dh, dqkv, mixed_low,
    slope, mixed, norm, key_grad, value_grad,
):
    s, c, h = places()
    x_peer = s + 1 - 2 * lax.rem(s, 2)
    y_peer = lax.rem(s + 2, 4)
    across = ((x_peer, c, h), (y_peer, c, h))
    core_peer = (s, c, 1 - h)
    ring = [(s, lax.rem(c + k, 4), h) for k in (1, 2, 3)]
    greet([*across, core_peer, *ring])

    count = x_ref.shape[0]
    slab, width, units = up_ref.shape[0], out_ref.shape[0] // 4, down_ref.shape[0] // 4
    quarter, half_count = slab // 4, count // 2

    def rows(base, size):
        return pl.ds(pl.multiple_of(base, size), size)

    def landed(m, r, part, half):
        def cut(total):
            size = total // 4
            if half is None:
                return part * size, size
            return part * size + half * (size // 2), size // 2

        if m == 0:
            at, size = cut(slab)
            return qkv_all.at[:, rows(r * slab + at, size), :]
        if m == 1:
            at, size = cut(slab)
            return up_all.at[rows(r * slab + at, size), :]
        if m == 2:
            at, size = cut(width)
            return out_all.at[rows(at, size), span(r, slab)]
        at, size = cut(units)
        return down_all.at[rows(at, size), span(r, slab)]

    def piece(m, to, part=None):
        if m == 0:
            inner = slice(None) if part is None else span(part, quarter)
            return qkv_ref.at[:, inner, span(to, width)]
        if m == 1:
            inner = slice(None) if part is None else span(part, quarter)
            return up_ref.at[inner, span(to, units)]
        size = width if m == 2 else units
        ref = out_ref if m == 2 else down_ref
        if part is None:
            return ref.at[span(to, size), :]
        return ref.at[rows(to * size + part * (size // 4), size // 4), :]

    def whole_piece(m, r):
        if m == 0:
            return qkv_all.at[:, span(r, slab), :]
        if m == 1:
            return up_all.at[span(r, slab), :]
        return (out_all if m == 2 else down_all).at[:, span(r, slab)]

    def remote(src, dst, send, recv, to):
        return pltpu.make_async_remote_copy(
            src_ref=src, dst_ref=dst, send_sem=send, recv_sem=recv, device_id=to, device_id_type=MESH
        )

    def z_copy(m, k):
        to = lax.rem(c + 4 - k, 4)
        return remote(
            piece(m, to, s), landed(m, c, s, None), z_send.at[m, k - 1], z_recv.at[m, k - 1], (s, to, h)
        )

    def direct(m, k, axis):
        r = lax.rem(c + k, 4)
        send, recv = (x_send, x_recv) if axis == 0 else (y_send, y_recv)
        here = landed(m, r, s, None)
        return remote(here, here, send.at[m, k - 1], recv.at[m, k - 1], across[axis])

    def onward(m, k, axis):
        r = lax.rem(c + k, 4)
        send, recv = (fx_send, fx_recv) if axis == 0 else (fy_send, fy_recv)
        here = landed(m, r, y_peer if axis == 0 else x_peer, 1 if axis == 0 else 0)
        return remote(here, here, send.at[m, k - 1], recv.at[m, k - 1], across[axis])

    lines = ((x_ref, x_all), (g_ref, g_all))

    def block(a, origin):
        return lines[a][1].at[rows(origin * count + h * half_count, half_count), :]

    def line_copy(a, t, side):
        origin = c - t if side == 0 else c + t
        src = lines[a][0].at[span(h, half_count), :] if t == 0 else block(a, origin)
        to = c + 1 if side == 0 else c - 1
        return remote(
            src, block(a, origin), line_send.at[a, side, t], line_recv.at[a, side, t], (s, to, h)
        )

    def core_copy(a, t, side):
        origin = c - t if side == 0 else c + t
        here = block(a, origin)
        return remote(here, here, core_send.at[a, side, t - 1], core_recv.at[a, side, t - 1], core_peer)

    def sends(t, side):
        if side == 0:
            return (c >= t) & (c < 3)
        return (c + t <= 3) & (c > 0)

    def gets(t, side):
        return c >= t if side == 0 else c + t <= 3

    def line_step(a, t):
        for side in (0, 1):
            @pl.when(gets(t, side))
            def _():
                line_copy(a, t - 1, side).wait_recv()
                core_copy(a, t, side).start()

            if t < 3:
                @pl.when(sends(t, side))
                def _():
                    line_copy(a, t, side).start()

    near = (1, 3, 2)
    order = [(m, k) for m in (0, 1, 3, 2) for k in near]

    def start_z(m):
        for k in near:
            z_copy(m, k).start()

    def pass_on(m):
        for k in near:
            direct(m, k, 0).wait_recv()
            onward(m, k, 1).start()
            direct(m, k, 1).wait_recv()
            onward(m, k, 0).start()

    def spread(m):
        for k in near:
            z_copy(m, k).wait_recv()
            direct(m, k, 0).start()
            direct(m, k, 1).start()

    ins = [
        pltpu.make_async_copy(a, b, own_sem.at[i])
        for i, (a, b) in enumerate(
            [(lines[a][0], lines[a][1].at[span(c, count), :]) for a in (0, 1)]
            + [(piece(m, c), whole_piece(m, c)) for m in range(4)]
        )
    ]
    for copy in ins:
        copy.start()
    tile = count
    length, model = x_all.shape
    rot = turn_ref.shape[2]
    scale = width**-0.5

    def finish(m):
        for k in near:
            onward(m, k, 0).wait_recv()
            onward(m, k, 1).wait_recv()
        ins[2 + m].wait()

    def give(i):
        pairs = (
            (qkv_all, qkv_out), (up_all, up_out), (out_all, out_out), (down_all, down_out),
            (act, act_out), (dh, dh_out), (dqkv, dqkv_out), (mixed_low, mixed_out),
        )
        return pltpu.make_async_copy(*pairs[i], give_sem.at[i])

    def give_block(a, origin):
        src, dst = ((unit, unit_out), (g_all, g_out))[a]
        at = span(origin, tile)
        return pltpu.make_async_copy(src.at[at, :], dst.at[at, :], block_sem.at[a])

    def blocks_of(t, do):
        if t == 0:
            do(c)
            return

        @pl.loop(0, 2)
        def _(side):
            origin = c + t * (2 * side - 1)

            @pl.when((origin >= 0) & (origin <= 3))
            def _():
                do(origin)

    def core_wait(a, t):
        for side in (0, 1):
            @pl.when(gets(t, side))
            def _():
                core_copy(a, t, side).wait_recv()

    def norm_block(origin):
        tall = 32

        @pl.loop(0, tile // tall)
        def _(i):
            at = pl.ds(pl.multiple_of(origin * tile + i * tall, tall), tall)
            wide = x_all[at, :].astype(F32)
            centred = wide - jnp.mean(wide, axis=-1, keepdims=True)
            spread_of = jnp.mean(centred * centred, axis=-1, keepdims=True)
            found = centred * lax.rsqrt(spread_of + 1e-05)
            unit[at, :] = found.astype(BF16)
            low_one[at, :] = (found * rows_ref[0:1, :] + rows_ref[1:2, :]).astype(BF16)
            low_two[at, :] = (found * rows_ref[2:3, :] + rows_ref[3:4, :]).astype(BF16)

        give_block(0, origin).start()

    def turned(v, at, sign):
        near_part = v[:, :rot]
        moved = pltpu.roll(near_part, 32, 1) * turn_ref[1, at, :] + pltpu.roll(near_part, rot - 32, 1) * turn_ref[2, at, :]
        return jnp.concatenate([near_part * turn_ref[0, at, :] + sign * moved, v[:, rot:]], axis=1)

    def project():
        @pl.loop(0, length // tile)
        def _(i):
            at = span(i, tile)
            for p, into in enumerate((query, keys, values)):
                part = dot(low_one[at, :], qkv_all[p], (1, 0)) + bias_ref[0:1, p * width : (p + 1) * width]
                into[at, :] = (turned(part, at, 1.0) if p < 2 else part).astype(BF16)

    def allowed_of(i, wide):
        first = lax.broadcasted_iota(jnp.int32, (tile, wide), 1)
        place = i * tile + lax.broadcasted_iota(jnp.int32, (tile, wide), 0)
        return (first <= place) & (first >= start_ref[span(i, tile), :])

    def attend(i):
        wide = (i + 1) * tile
        at = slice(i * tile, wide)
        scores = dot(query[at, :], keys[0:wide, :], (1, 1)) * scale
        allowed = allowed_of(i, wide)
        masked = jnp.where(allowed, scores, -1e30)
        peak = jnp.max(masked, axis=-1, keepdims=True)
        raised = jnp.where(allowed, jnp.exp(masked - peak), 0.0)
        total = jnp.sum(raised, axis=-1, keepdims=True)
        norm[at, :] = peak + jnp.log(total)
        found = dot((raised / total).astype(BF16), values[0:wide, :], (1, 0))
        mixed[at, :] = found
        mixed_low[at, :] = found.astype(BF16)

    def feed(i):
        at = span(i, tile)
        for j in range(units // 256):
            cols = slice(j * 256, (j + 1) * 256)
            hidden = dot(low_two[at, :], up_all[:, cols], (1, 0)) + bias_ref[1:2, cols]
            share = 0.5 + 0.5 * lax.erf(hidden * (0.5**0.5))
            act[at, cols] = (hidden * share).astype(BF16)
            slope[at, cols] = share + hidden * jnp.exp(-0.5 * hidden * hidden) * ((0.5 / jnp.pi) ** 0.5)

    def back_attend(origin):
        at = span(origin, tile)
        grad = dot(g_all[at, :], out_all[...], (1, 1)).astype(BF16)
        scores = dot(query[at, :], keys[...], (1, 1)) * scale
        shares = jnp.where(allowed_of(origin, length), jnp.exp(scores - norm[at, :]), 0.0)
        delta = jnp.sum(grad.astype(F32) * mixed[at, :], axis=-1, keepdims=True)
        share_grad = dot(grad, values[...], (1, 1))
        score_grad = (shares * (share_grad - delta)).astype(BF16)
        value_grad[...] += dot(shares.astype(BF16), grad, (0, 0))
        key_grad[...] += dot(score_grad, query[at, :], (0, 0))
        part = dot(score_grad, keys[...], (1, 0)) * scale
        dqkv[at, 0:width] = turned(part, at, -1.0).astype(BF16)

    def back_feed(origin):
        at = span(origin, tile)
        for j in range(units // 256):
            cols = slice(j * 256, (j + 1) * 256)
            part = dot(g_all[at, :], down_all[cols, :], (1, 1))
            dh[at, cols] = (part * slope[at, cols]).astype(BF16)

    def start_line(a):
        for side in (0, 1):
            @pl.when(sends(0, side))
            def _():
                line_copy(a, 0, side).start()

    start_line(0)
    start_z(0)
    key_grad[...] = jnp.zeros_like(key_grad)
    value_grad[...] = jnp.zeros_like(value_grad)
    ins[0].wait()
    norm_block(c)
    line_step(0, 1)
    start_z(1)
    core_wait(0, 1)
    blocks_of(1, norm_block)
    spread(0)
    line_step(0, 2)
    start_z(3)
    pass_on(0)
    core_wait(0, 2)
    blocks_of(2, norm_block)
    line_step(0, 3)
    start_line(1)
    core_wait(0, 3)
    blocks_of(3, norm_block)
    finish(0)
    give(0).start()
    project()
    spread(1)
    start_z(2)
    for i in range(4):
        attend(i)
        if i == 1:
            pass_on(1)
    give(7).start()
    finish(1)
    give(1).start()
    line_step(1, 1)
    for i in range(4):
        feed(i)
        if i == 0:
            spread(3)
        if i == 2:
            spread(2)
            line_step(1, 2)
            pass_on(3)
    give(4).start()
    pass_on(2)
    line_step(1, 3)
    finish(2)
    give(2).start()
    ins[1].wait()
    give_block(1, c).start()
    back_attend(c)
    core_wait(1, 1)
    blocks_of(1, back_attend)
    finish(3)
    give(3).start()
    back_feed(c)
    blocks_of(1, back_feed)
    core_wait(1, 2)

    def both(origin):
        back_attend(origin)
        back_feed(origin)

    blocks_of(2, both)
    core_wait(1, 3)
    blocks_of(3, both)

    @pl.loop(0, length // tile)
    def _(i):
        at = span(i, tile)
        dqkv[at, width : 2 * width] = turned(key_grad[at, :] * scale, at, -1.0).astype(BF16)
        dqkv[at, 2 * width : 3 * width] = value_grad[at, :].astype(BF16)

    give(5).start()
    give(6).start()
    for t in (1, 2, 3):
        blocks_of(t, lambda origin: give_block(1, origin).start())
    for a in (0, 1):
        for side in (0, 1):
            for t in (1, 2, 3):
                @pl.when(gets(t, side))
                def _():
                    core_copy(a, t, side).wait_send()
                @pl.when(sends(t - 1, side))
                def _():
                    line_copy(a, t - 1, side).wait_send()
    for m, k in order:
        z_copy(m, k).wait_send()
        for axis in (0, 1):
            direct(m, k, axis).wait_send()
            onward(m, k, axis).wait_send()
    pltpu.make_async_copy(unit, unit_out, block_sem.at[0]).wait()
    pltpu.make_async_copy(g_all, g_out, block_sem.at[1]).wait()
    for i in range(8):
        give(i).wait()


def gather_all(tokens, cotangent, w_qkv, w_up, w_out, w_down, rows, bias, turn, starts):
    count, model = tokens.shape
    length = 4 * count
    width, units = w_out.shape[0] // 4, w_down.shape[0] // 4
    dma = pltpu.SemaphoreType.DMA
    weights = [(3, model, width), (model, units), (width, model), (units, model)]
    wide, narrow = (length, model), (length, width)
    results = [wide, wide, (length, units), (length, units), (length, 3 * width), narrow] + weights
    scratch = [dma((4, 3))] * 10 + [dma((2, 2, 3))] * 4 + [dma((6,)), dma((8,)), dma((2,))]
    scratch += [
        pltpu.VMEM(v, BF16)
        for v in [wide, wide] + weights + [wide] * 3 + [narrow] * 3
        + [(length, units)] * 2 + [(length, 3 * width), narrow]
    ]
    scratch += [pltpu.VMEM(v, F32) for v in ((length, units), narrow, (length, 1), narrow, narrow)]
    any_space = pl.BlockSpec(memory_space=pl.ANY)
    vmem_space = pl.BlockSpec(memory_space=pltpu.VMEM)
    return pl.pallas_call(
        gather_body,
        out_shape=[jax.ShapeDtypeStruct(v, BF16) for v in results],
        in_specs=[any_space] * 6 + [vmem_space] * 4,
        out_specs=[any_space] * 10,
        scratch_shapes=scratch,
        compiler_params=pltpu.CompilerParams(
            collective_id=0, has_side_effects=True, vmem_limit_bytes=63 << 20
        ),
        name="gather",
    )(tokens, cotangent, w_qkv, w_up, w_out, w_down, rows, bias, turn, starts)


LEADS = (12, 4, 1, 1)

def settle_body(
    act_in, up_in, unit_in, dh_in, dqkv_in, mixed_in, wq_in, wu_in, wo_in, wd_in, cols_ref, rows_ref,
    joint, inward, o0, o1, o2, o3, small_out,
    s1x_send, s1x_recv, s1y_send, s1y_recv, s2x_send, s2x_recv, s2y_send, s2y_recv,
    x_send, x_recv, y_send, y_recv, fx_send, fx_recv, fy_send, fy_recv,
    z_send, z_recv, keep_sem, load_sem, weight_sem,
    core_send, core_recv, row_send, row_recv, back_send, back_recv, back_sem,
    sum_send, sum_recv, sum_sem,
    act, up, unit, dh, dqkv, mixed, w_wide, w_out, w_qkv,
    gb0, gb1, gb2, gb3, fa0, fb0, fa1, fb1, fa2, fb2, fa3, fb3, ga0, hb0, ga1, hb1, ga2, hb2, ga3, hb3,
    own_half, core_half, send_half, row_parts, done_half,
    sums, sums_core, slots, total_own, total_x, total_y,
):
    s, c, h = places()
    x_at, y_at = lax.rem(s, 2), lax.div(s, 2)
    x_off, y_off = 1 - x_at, 1 - y_at
    x_peer, y_peer = y_at * 2 + x_off, y_off * 2 + x_at
    across = ((x_peer, c, h), (y_peer, c, h))
    core_peer = (s, c, 1 - h)
    near = (1, 3, 2)
    greet([*across, core_peer, *[(s, lax.rem(c + k, 4), h) for k in near]])
    grads, outs = (gb0, gb1, gb2, gb3), (o0, o1, o2, o3)
    first = ((fa0, fb0), (fa1, fb1), (fa2, fb2), (fa3, fb3))
    second = ((ga0, hb0), (ga1, hb1), (ga2, hb2), (ga3, hb3))
    slab = o2.shape[-1]
    length, model = up.shape
    units, width = act.shape[1], mixed.shape[1]
    half_cols = model // 2
    count = joint.shape[0]
    tile = 256

    def remote(src, dst, send, recv, to):
        return pltpu.make_async_remote_copy(
            src_ref=src, dst_ref=dst, send_sem=send, recv_sem=recv, device_id=to, device_id_type=MESH
        )

    loads = [
        pltpu.make_async_copy(a, b, load_sem.at[i])
        for i, (a, b) in enumerate(
            ((act_in, act), (up_in, up), (dh_in, dh), (unit_in, unit), (dqkv_in, dqkv), (mixed_in, mixed))
        )
    ]
    for load in loads:
        load.start()

    def side(which):
        return 1 - h if which == 0 else h

    def weight_load(i):
        at = span(side(i % 2), half_cols)
        if i < 2:
            return pltpu.make_async_copy(wd_in.at[:, at], w_wide.at[i], weight_sem.at[i])
        if i < 4:
            return pltpu.make_async_copy(wu_in.at[at, :], w_wide.at[i % 2], weight_sem.at[i])
        if i < 6:
            return pltpu.make_async_copy(wo_in.at[:, at], w_out.at[i % 2], weight_sem.at[i])
        return pltpu.make_async_copy(wq_in.at[:, at, :], w_qkv.at[i % 2], weight_sem.at[i])

    for i in (0, 4, 1, 5, 6, 7):
        weight_load(i).start()

    def one(m, half):
        src = grads[m].at[:, :, x_off, 0] if half == 0 else grads[m].at[:, y_off, :, 1]
        send, recv = (s1x_send, s1x_recv) if half == 0 else (s1y_send, s1y_recv)
        return remote(src, first[m][half], send.at[m], recv.at[m], across[half])

    def two(m, half):
        src = first[m][half].at[:, y_off if half == 0 else x_off]
        send, recv = (s2y_send, s2y_recv) if half == 0 else (s2x_send, s2x_recv)
        return remote(src, second[m][half], send.at[m], recv.at[m], across[1 - half])

    def add_first(m, half):
        into, more = first[m][half], grads[m]
        lead, _, height, _ = into.shape
        tall = min(height, 32)

        @pl.loop(0, lead * 2 * (height // tall))
        def _(i):
            at = lax.rem(i, height // tall)
            pair = lax.div(i, height // tall)
            l, j, rows = lax.div(pair, 2), lax.rem(pair, 2), span(at, tall)
            term = more[l, j, x_at, 0, rows, :] if half == 0 else more[l, y_at, j, 1, rows, :]
            into[l, j, rows, :] = (into[l, j, rows, :].astype(F32) + term.astype(F32)).astype(BF16)

    def add_second(m, half):
        into, more = second[m][half], first[m][half]
        mine = y_at if half == 0 else x_at
        lead, height, _ = into.shape
        tall = min(height, 32)

        @pl.loop(0, lead * (height // tall))
        def _(i):
            l, rows = lax.div(i, height // tall), span(lax.rem(i, height // tall), tall)
            term = more[l, mine, rows, :].astype(F32)
            into[l, rows, :] = (into[l, rows, :].astype(F32) + term).astype(BF16)

    def share_of(m, half, to):
        ref = second[m][half]
        if m == 0:
            return ref.reshape(3, 4, *ref.shape[1:]).at[:, to]
        if m == 1:
            return ref.at[to]
        return ref.at[0, :, span(to, slab)]

    def home(m, half):
        if m == 0:
            return outs[0].at[:, s, half, :, span(c, width)]
        if m == 1:
            return outs[1].at[s, half, :, span(c, units)]
        return outs[m].at[c, s, half]

    def z_copy(m, half, k):
        to = lax.rem(c + 4 - k, 4)
        i = (m * 2 + half) * 3 + k - 1
        return remote(share_of(m, half, to), home(m, half), z_send.at[i], z_recv.at[i], (s, to, h))

    def keep(m, half):
        return pltpu.make_async_copy(share_of(m, half, c), home(m, half), keep_sem.at[m, half])

    def quarter(m, q, half=None):
        if half is None:
            return outs[m].at[q] if m == 1 else outs[m].at[:, q]
        return outs[m].at[q, half] if m == 1 else outs[m].at[:, q, half]

    def direct(m, axis):
        send, recv = (x_send, x_recv) if axis == 0 else (y_send, y_recv)
        here = quarter(m, s)
        return remote(here, here, send.at[m], recv.at[m], across[axis])

    def onward(m, axis):
        send, recv = (fx_send, fx_recv) if axis == 0 else (fy_send, fy_recv)
        here = quarter(m, y_peer if axis == 0 else x_peer, 1 - axis)
        return remote(here, here, send.at[m], recv.at[m], across[axis])

    finals = (joint, inward)

    def core_copy(a):
        return remote(send_half, core_half.at[a], core_send.at[a], core_recv.at[a], core_peer)

    def row_copy(a, k):
        to = lax.rem(c + 4 - k, 4)
        return remote(
            own_half.at[a, span(to, count)], row_parts.at[a, k - 1],
            row_send.at[a, k - 1], row_recv.at[a, k - 1], (s, to, h),
        )

    def back_copy(a):
        return remote(
            done_half.at[a], finals[a].at[:, span(h, half_cols)], back_send.at[a], back_recv.at[a], core_peer
        )

    def back_keep(a):
        return pltpu.make_async_copy(done_half.at[a], finals[a].at[:, span(h, half_cols)], back_sem.at[a])

    def line_start(a):
        core_copy(a).wait_recv()
        tall = 32

        @pl.loop(0, length // tall)
        def _(i):
            rows = span(i, tall)
            own_half[a, rows, :] = (
                own_half[a, rows, :].astype(F32) + core_half[a, rows, :].astype(F32)
            ).astype(BF16)

        for k in near:
            row_copy(a, k).start()

    def line_sum(a):
        for k in near:
            row_copy(a, k).wait_recv()
        tall = 32

        @pl.loop(0, count // tall)
        def _(i):
            rows = span(i, tall)
            total = own_half[a, pl.ds(pl.multiple_of(c * count + i * tall, tall), tall), :].astype(F32)
            for k in range(3):
                total = total + row_parts[a, k, rows, :].astype(F32)
            done_half[a, rows, :] = total.astype(BF16)

        back_copy(a).start()
        back_keep(a).start()

    def down_grad():
        rows = units // 8

        @pl.loop(0, 4)
        def _(q):
            left = act[:, span(q, 2 * rows)]
            for j in range(model // 512):
                part = dot(left, up[:, j * 512 : (j + 1) * 512], (0, 0)).astype(BF16)
                for half in (0, 1):
                    gb3[0, lax.div(q, 2), lax.rem(q, 2), half, :, j * 512 : (j + 1) * 512] = part[
                        half * rows : (half + 1) * rows
                    ]

    def out_grad():
        rows = width // 8
        for j in range(model // 512):
            part = dot(mixed[...], up[:, j * 512 : (j + 1) * 512], (0, 0)).astype(BF16)
            for i in range(8):
                gb2[0, i // 4, (i // 2) % 2, i % 2, :, j * 512 : (j + 1) * 512] = part[i * rows : (i + 1) * rows]

    def scaled(part, t, at, column_sum):
        rows = span(t, tile)
        return (part * cols_ref[rows, at : at + 1] + cols_ref[rows, at + 1 : at + 2] * column_sum).astype(BF16)

    def column_sum(ref, cols):
        total = jnp.zeros((1, cols.stop - cols.start), F32)
        for i in range(length // tile):
            total = total + jnp.sum(ref[i * tile : (i + 1) * tile, cols].astype(F32), axis=0, keepdims=True)
        return total

    def up_grad():
        rows = tile // 4

        @pl.loop(0, model // tile)
        def _(t):
            left = unit[:, span(t, tile)]
            for j in range(units // 512):
                cols = slice(j * 512, (j + 1) * 512)
                near_sum = sums[5:6, 3 * width + j * 512 : 3 * width + (j + 1) * 512]
                part = scaled(dot(left, dh[:, cols], (0, 0)), t, 2, near_sum)
                for i in range(4):
                    gb1[lax.div(t, 2), lax.rem(t, 2), i // 2, i % 2, :, cols] = part[i * rows : (i + 1) * rows]

    def qkv_grad():
        rows = tile // 4

        @pl.loop(0, model // tile)
        def _(t):
            left = unit[:, span(t, tile)]
            for p in range(3):
                cols = slice(p * width, (p + 1) * width)
                part = scaled(dot(left, dqkv[:, cols], (0, 0)), t, 0, sums[5:6, cols])
                for i in range(4):
                    gb0[p * 4 + lax.div(t, 2), lax.rem(t, 2), i // 2, i % 2] = part[i * rows : (i + 1) * rows]

    def branches(which):
        into = send_half if which == 0 else own_half.at[0]

        @pl.loop(0, length // tile)
        def _(i):
            rows = span(i, tile)
            for j in range(half_cols // 512):
                cols = slice(j * 512, (j + 1) * 512)
                part = dot(mixed[rows, :], w_out[which, :, cols], (1, 0))
                part = part + dot(act[rows, :], w_wide[which, :, cols], (1, 0))
                into[rows, cols] = part.astype(BF16)

    def inwards(which):
        into = send_half if which == 0 else own_half.at[1]
        base = side(which) * half_cols
        for j in range(half_cols // 512):
            cols = slice(j * 512, (j + 1) * 512)
            far = span(side(which) * (half_cols // 512) + j, 512)
            zero = jnp.zeros((8, 512), F32)

            def step(i, carry):
                rows = span(i, tile)
                one_part = dot(dqkv[rows, 0:width], w_qkv[which, 0, cols, :], (1, 1))
                for p in (1, 2):
                    one_part = one_part + dot(
                        dqkv[rows, p * width : (p + 1) * width], w_qkv[which, p, cols, :], (1, 1)
                    )
                two_part = dot(dh[rows, :], w_wide[which, cols, :], (1, 1))
                into[rows, cols] = (one_part * rows_ref[0:1, far] + two_part * rows_ref[2:3, far]).astype(BF16)
                place = unit[rows, far].astype(F32)

                def fold(v):
                    return jnp.sum(v.reshape(tile // 8, 8, 512), axis=0)

                return (
                    carry[0] + fold(one_part * place),
                    carry[1] + fold(one_part),
                    carry[2] + fold(two_part * place),
                    carry[3] + fold(two_part),
                )

            found = lax.fori_loop(0, length // tile, step, (zero, zero, zero, zero))
            for n in range(4):
                sums[n : n + 1, far] = jnp.sum(found[n], axis=0, keepdims=True)

    def sum_core():
        return remote(sums, sums_core, sum_send.at[0], sum_recv.at[0], core_peer)

    def sum_line(k):
        return remote(
            sums, slots.at[c], sum_send.at[k], sum_recv.at[k], (s, lax.rem(c + 4 - k, 4), h)
        )

    def sum_x():
        return remote(total_own, total_x, sum_send.at[4], sum_recv.at[4], across[0])

    def sum_y():
        return remote(total_own, total_y, sum_send.at[5], sum_recv.at[5], across[1])

    order = (3, 1, 0, 2)
    loads[0].wait()
    loads[1].wait()
    down_grad()
    one(3, 0).start()
    one(3, 1).start()
    sums[4:5, :] = jnp.sum(up[span(c, count), :].astype(F32), axis=0, keepdims=True) * 0.5
    sums[5:8, :] = jnp.zeros((3, model), F32)
    loads[2].wait()
    loads[3].wait()
    for j in range(units // 512):
        sums[5:6, 3 * width + j * 512 : 3 * width + (j + 1) * 512] = column_sum(dh, slice(j * 512, (j + 1) * 512))
    up_grad()
    one(1, 0).start()
    one(1, 1).start()
    loads[4].wait()
    for p in range(3):
        sums[5:6, p * width : (p + 1) * width] = column_sum(dqkv, slice(p * width, (p + 1) * width))
    qkv_grad()
    one(0, 0).start()
    one(0, 1).start()
    loads[5].wait()
    out_grad()
    one(2, 0).start()
    one(2, 1).start()
    weight_load(0).wait()
    weight_load(4).wait()
    branches(0)
    core_copy(0).start()
    weight_load(2).start()
    weight_load(1).wait()
    weight_load(5).wait()
    branches(1)
    weight_load(3).start()

    def stage_two(m):
        for half in (0, 1):
            one(m, half).wait_recv()
            add_first(m, half)
            two(m, half).start()

    def stage_z(m):
        for half in (0, 1):
            two(m, half).wait_recv()
            add_second(m, half)
            for k in near:
                z_copy(m, half, k).start()
            keep(m, half).start()

    def stage_out(m):
        for half in (0, 1):
            for k in near:
                z_copy(m, half, k).wait_recv()
            keep(m, half).wait()
        for axis in (0, 1):
            direct(m, axis).start()

    def stage_on(m):
        direct(m, 0).wait_recv()
        onward(m, 1).start()
        direct(m, 1).wait_recv()
        onward(m, 0).start()

    stage_two(3)
    line_start(0)
    core_copy(0).wait_send()
    weight_load(2).wait()
    weight_load(6).wait()
    inwards(0)
    core_copy(1).start()
    weight_load(3).wait()
    weight_load(7).wait()
    inwards(1)
    sum_core().start()
    stage_two(1)
    stage_two(0)
    sum_core().wait()
    sums[0:5, :] = sums[0:5, :] + sums_core[0:5, :]
    for k in near:
        sum_line(k).start()
    slots[c] = sums[...]
    stage_z(3)
    stage_two(2)
    line_sum(0)
    for k in near:
        sum_line(k).wait()
    total_own[0:8, :] = slots[0] + slots[1] + slots[2] + slots[3]
    for i in range(4):
        total_own[8 + i : 9 + i, :] = slots[i, 5:6, :]
    total_own[12:16, :] = jnp.zeros((4, model), F32)
    sum_x().start()
    stage_z(1)
    stage_z(0)
    stage_z(2)
    line_start(1)
    stage_out(3)
    sum_x().wait()
    total_own[...] = total_own[...] + total_x[...]
    sum_y().start()
    stage_on(3)
    stage_out(1)
    sum_y().wait()
    total_own[...] = total_own[...] + total_y[...]
    small_copy = pltpu.make_async_copy(total_own, small_out, sum_sem.at[0])
    small_copy.start()
    stage_on(1)
    stage_out(0)
    stage_on(0)
    stage_out(2)
    stage_on(2)
    line_sum(1)
    for m in order:
        for axis in (0, 1):
            onward(m, axis).wait_recv()
    small_copy.wait()
    for a in (0, 1):
        back_copy(a).wait()
        back_keep(a).wait()
        for k in near:
            row_copy(a, k).wait_send()
    core_copy(1).wait_send()
    for m in order:
        for half in (0, 1):
            one(m, half).wait_send()
            two(m, half).wait_send()
            for k in near:
                z_copy(m, half, k).wait_send()
        for axis in (0, 1):
            direct(m, axis).wait_send()
            onward(m, axis).wait_send()


def settle_all(act, up, unit, dh, dqkv, mixed, w_qkv, w_up, w_out, w_down, cols, rows):
    length, model = up.shape
    units, width = act.shape[1], mixed.shape[1]
    slab, count, half = model // 4, length // 4, model // 2
    dma = pltpu.SemaphoreType.DMA
    heights = (slab // 8, slab // 8, width // 8, units // 8)
    widths = (width, units, model, model)
    out_shapes = [
        (count, model), (count, model),
        (3, 4, 2, heights[0], 4 * width), (4, 2, heights[1], 4 * units),
        (4, 4, 2, heights[2], slab), (4, 4, 2, heights[3], slab),
    ]
    scratch = [dma((4,))] * 16 + [dma((24,))] * 2 + [dma((4, 2)), dma((6,)), dma((8,))]
    scratch += [dma((2,)), dma((2,)), dma((2, 3)), dma((2, 3)), dma((2,)), dma((2,)), dma((2,))]
    scratch += [dma((6,)), dma((6,)), dma((1,))]
    vmem = [(length, units), (length, model), (length, model), (length, units), (length, 3 * width), (length, width)]
    vmem += [(2, units, half), (2, width, half), (2, 3, half, width)]
    shapes = list(zip(LEADS, heights, widths))
    vmem += [(l, 2, 2, 2, r, k) for l, r, k in shapes]
    vmem += [(l, 2, r, k) for l, r, k in shapes for _ in (0, 1)]
    vmem += [(l, r, k) for l, r, k in shapes for _ in (0, 1)]
    vmem += [(2, length, half), (2, length, half), (length, half), (2, 3, count, half), (2, count, half)]
    scratch += [pltpu.VMEM(v, BF16) for v in vmem]
    scratch += [pltpu.VMEM(v, F32) for v in ((8, model), (8, model), (4, 8, model), (16, model), (16, model), (16, model))]
    any_space = pl.BlockSpec(memory_space=pl.ANY)
    vmem_space = pl.BlockSpec(memory_space=pltpu.VMEM)
    joint, inward, q, u, o, d, small = pl.pallas_call(
        settle_body,
        out_shape=[jax.ShapeDtypeStruct(v, BF16) for v in out_shapes] + [jax.ShapeDtypeStruct((16, model), F32)],
        in_specs=[any_space] * 10 + [vmem_space] * 2,
        out_specs=[any_space] * 7,
        scratch_shapes=scratch,
        compiler_params=pltpu.CompilerParams(
            collective_id=1, has_side_effects=True, vmem_limit_bytes=63 << 20
        ),
        name="settle",
    )(act, up, unit, dh, dqkv, mixed, w_qkv, w_up, w_out, w_down, cols, rows)
    return (
        joint, inward, q.reshape(3, slab, 4 * width), u.reshape(slab, 4 * units),
        o.reshape(4 * width, slab), d.reshape(4 * units, slab), small,
    )


def per_device(
    tokens,
    doc_lengths,
    ln1_gain,
    ln1_bias,
    qkv_weight,
    qkv_bias,
    out_weight,
    out_bias,
    ln2_gain,
    ln2_bias,
    up_weight,
    up_bias,
    down_weight,
    down_bias,
    cotangent,
):
    f32, bf16 = jnp.float32, jnp.bfloat16
    ctx_count = lax.axis_size("ctx")
    c = lax.axis_index("ctx")
    count, model = tokens.shape[1], tokens.shape[2]
    length = count * ctx_count
    width = qkv_weight.shape[2] // ctx_count
    units = up_weight.shape[1] // ctx_count

    gains = jnp.stack([ln1_gain, ln1_bias, ln2_gain, ln2_bias]).astype(f32)
    gain_rows = jnp.pad(gains, ((0, 4), (0, 0)))
    biases = jnp.stack(
        [
            jnp.pad(
                lax.dynamic_slice_in_dim(qkv_bias, c * width, width, 1).reshape(-1),
                (0, units - 3 * width),
            ),
            lax.dynamic_slice_in_dim(up_bias, c * units, units, 0),
        ]
    ).astype(f32)
    biases = jnp.pad(biases, ((0, 6), (0, 0)))
    positions, starts = token_places(doc_lengths[0], length)
    half = ROT // 2
    lane = jnp.arange(2 * ROT)
    frequency = 10000.0 ** (-jnp.arange(0, ROT, 2, dtype=f32) / ROT)
    angles = (positions - starts).astype(f32)[:, None] * frequency[None, :]
    cosine, sine = jnp.tile(jnp.cos(angles), (1, 4)), jnp.tile(jnp.sin(angles), (1, 4))
    turn = jnp.stack(
        [
            jnp.where(lane < ROT, cosine, 1.0),
            jnp.where((lane >= half) & (lane < ROT), sine, 0.0),
            jnp.where(lane < half, -sine, 0.0),
        ]
    )

    upstream, unit, activated, hidden_grad, projected_grad, mixed_low, w_qkv, w_up, w_out, w_down = (
        gather_all(
            tokens[0],
            cotangent[0],
            qkv_weight,
            up_weight,
            out_weight,
            down_weight,
            gain_rows,
            biases,
            turn,
            starts[:, None],
        )
    )

    joint, inward, qkv_out, up_out, out_out, down_out, small = settle_all(
        activated,
        upstream,
        unit,
        hidden_grad,
        projected_grad,
        mixed_low,
        w_qkv,
        w_up,
        w_out,
        w_down,
        jnp.pad(gains.T, ((0, 0), (0, 124))),
        gain_rows,
    )
    joint, inward = joint.astype(f32), inward.astype(f32)

    own = tokens[0].astype(f32)
    own_upstream = cotangent[0].astype(f32)
    output = own + joint + out_bias.astype(f32) + down_bias.astype(f32)
    own_centred = own - jnp.mean(own, axis=-1, keepdims=True)
    own_scale = lax.rsqrt(jnp.mean(own_centred * own_centred, axis=-1, keepdims=True) + 1e-05)
    own_unit = own_centred * own_scale
    input_grad = own_upstream + own_scale * (
        inward
        - jnp.mean(inward, axis=-1, keepdims=True)
        - own_unit * jnp.mean(inward * own_unit, axis=-1, keepdims=True)
    )

    qkv_bias_grad = (
        small[8:12, : 3 * width].reshape(ctx_count, 3, width).transpose(1, 0, 2).reshape(3, -1)
    )
    up_bias_grad = small[8:12, 3 * width : 3 * width + units].reshape(-1)
    return (
        output.astype(bf16)[None],
        input_grad[None],
        small[0],
        small[1],
        qkv_out.astype(f32),
        qkv_bias_grad,
        out_out.astype(f32),
        small[4],
        small[2],
        small[3],
        up_out.astype(f32),
        up_bias_grad,
        down_out.astype(f32),
        small[4],
    )


def solution(mesh):
    in_specs = (
        P("stream", "ctx", None),
        P("stream", None),
        P(),
        P(),
        P(None, "ctx", "head"),
        P(None, "head"),
        P("head", "ctx"),
        P(),
        P(),
        P(),
        P("ctx", "head"),
        P("head"),
        P("head", "ctx"),
        P(),
        P("stream", "ctx", None),
    )
    out_specs = (
        P("stream", "ctx", None),
        P("stream", "ctx", None),
        P(),
        P(),
        P(None, "ctx", "head"),
        P(None, "head"),
        P("head", "ctx"),
        P(),
        P(),
        P(),
        P("ctx", "head"),
        P("head"),
        P("head", "ctx"),
        P(),
    )
    split = mesh.shape["ctx"] * mesh.shape["head"]

    def whole(*arrays):
        heads, units = arrays[4].shape[2] // HEAD, arrays[10].shape[1]
        grouped = (mesh.shape["stream"], mesh.shape["ctx"], mesh.shape["head"]) == (4, 4, 2)
        fits = grouped and heads == split and units % (split * 512) == 0
        return jax.shard_map(
            per_device if fits else general_device,
            mesh=mesh,
            in_specs=in_specs,
            out_specs=out_specs,
            check_vma=False,
        )(*arrays)

    return whole
```

```python
from functools import partial
import math

import jax
import jax.numpy as jnp
import numpy as np
from jax import lax
from jax.experimental import pallas as pl
from jax.experimental.pallas import tpu as pltpu
from jax.sharding import PartitionSpec as P

HEAD = 256
ROT = 64


def layer_norm(values, gain, offset):
    centre = jnp.mean(values, axis=-1, keepdims=True)
    centred = values - centre
    spread = jnp.mean(centred * centred, axis=-1, keepdims=True)
    return centred * lax.rsqrt(spread + 1e-05) * gain + offset


def rotary(values, angles):
    half = angles.shape[-1]
    cosine = jnp.cos(angles)[:, None, :]
    sine = jnp.sin(angles)[:, None, :]
    first = values[..., :half]
    second = values[..., half : 2 * half]
    return jnp.concatenate(
        [first * cosine - second * sine, second * cosine + first * sine, values[..., 2 * half :]],
        axis=-1,
    )


def doc_starts(doc_sizes, positions):
    place = jnp.arange(doc_sizes.shape[0])
    before = place[None, :] < place[:, None]
    starts = jnp.sum(jnp.where(before, doc_sizes[None, :], 0), axis=1)
    return jnp.max(jnp.where(starts[None, :] <= positions[:, None], starts[None, :], 0), axis=1)


def general_device(
    tokens,
    doc_lengths,
    ln1_gain,
    ln1_bias,
    qkv_weight,
    qkv_bias,
    out_weight,
    out_bias,
    ln2_gain,
    ln2_bias,
    up_weight,
    up_bias,
    down_weight,
    down_bias,
    cotangent,
):
    inputs = tokens[0].astype(jnp.float32)
    count = inputs.shape[0]
    ctx_count = lax.axis_size("ctx")
    length = count * ctx_count
    positions = lax.axis_index("ctx") * count + jnp.arange(count, dtype=jnp.int32)
    starts = doc_starts(doc_lengths[0], positions)
    frequency = 10000.0 ** (-jnp.arange(0, ROT, 2, dtype=jnp.float32) / ROT)
    angles = (positions - starts).astype(jnp.float32)[:, None] * frequency[None, :]
    scale = HEAD ** (-0.5)
    full_qkv, full_out, full_up, full_down = (
        lax.all_gather(qkv_weight, "ctx", axis=1, tiled=True),
        lax.all_gather(out_weight, "ctx", axis=1, tiled=True),
        lax.all_gather(up_weight, "ctx", axis=0, tiled=True),
        lax.all_gather(down_weight, "ctx", axis=1, tiled=True),
    )
    gain_one = ln1_gain.astype(jnp.float32)
    offset_one = ln1_bias.astype(jnp.float32)
    gain_two = ln2_gain.astype(jnp.float32)
    offset_two = ln2_bias.astype(jnp.float32)
    low_one = layer_norm(inputs, gain_one, offset_one).astype(jnp.bfloat16)
    low_two = layer_norm(inputs, gain_two, offset_two).astype(jnp.bfloat16)
    projected = (
        jnp.einsum("nd,cde->cne", low_one, full_qkv, preferred_element_type=jnp.float32)
        + qkv_bias.astype(jnp.float32)[:, None, :]
    )
    width = projected.shape[2]
    local_heads = width // HEAD
    query = rotary(projected[0].reshape(count, local_heads, HEAD), angles).astype(jnp.bfloat16)
    keys_flat = (
        rotary(projected[1].reshape(count, local_heads, HEAD), angles)
        .reshape(count, width)
        .astype(jnp.bfloat16)
    )
    values_flat = projected[2].astype(jnp.bfloat16)
    all_keys, all_values = (
        lax.all_gather(keys_flat, "ctx", axis=0, tiled=True),
        lax.all_gather(values_flat, "ctx", axis=0, tiled=True),
    )
    block = math.gcd(length, 512)
    block_count = length // block
    key_blocks = all_keys.reshape(block_count, block, local_heads, HEAD)
    value_blocks = all_values.reshape(block_count, block, local_heads, HEAD)
    firsts = jnp.arange(block_count, dtype=jnp.int32) * block

    def block_scores(key_block, first):
        key_index = first + jnp.arange(block, dtype=jnp.int32)
        allowed = (key_index[None, :] <= positions[:, None]) & (
            key_index[None, :] >= starts[:, None]
        )
        scores = (
            jnp.einsum("qhe,khe->hqk", query, key_block, preferred_element_type=jnp.float32) * scale
        )
        return (jnp.where(allowed[None], scores, -1e30), allowed[None])

    def statistics(carry, item):
        running, norm_sum = carry
        key_block, first = item
        masked, allowed = block_scores(key_block, first)
        newest = jnp.maximum(running, jnp.max(masked, axis=-1))
        raised = jnp.where(allowed, jnp.exp(masked - newest[..., None]), 0.0)
        norm_sum = norm_sum * jnp.exp(running - newest) + jnp.sum(raised, axis=-1)
        return ((newest, norm_sum), None)

    initial = (
        jnp.full((local_heads, count), -1e30, jnp.float32),
        jnp.zeros((local_heads, count), jnp.float32),
    )
    (running, norm_sum), _ = lax.scan(statistics, initial, (key_blocks, firsts))
    log_norm = running + jnp.log(norm_sum)

    def share_block(key_block, first):
        masked, allowed = block_scores(key_block, first)
        return jnp.where(allowed, jnp.exp(masked - log_norm[..., None]), 0.0)

    def accumulate(mixed, item):
        key_block, value_block, first = item
        shares_low = share_block(key_block, first).astype(jnp.bfloat16)
        return (
            mixed
            + jnp.einsum(
                "hqk,khe->qhe", shares_low, value_block, preferred_element_type=jnp.float32
            ),
            None,
        )

    mixed, _ = lax.scan(
        accumulate,
        jnp.zeros((count, local_heads, HEAD), jnp.float32),
        (key_blocks, value_blocks, firsts),
    )
    mixed_low = mixed.reshape(count, width).astype(jnp.bfloat16)
    attention = jnp.dot(mixed_low, full_out, preferred_element_type=jnp.float32)
    hidden = jnp.dot(low_two, full_up, preferred_element_type=jnp.float32) + up_bias.astype(
        jnp.float32
    )
    activated = jax.nn.gelu(hidden, approximate=False).astype(jnp.bfloat16)
    branches = attention + jnp.dot(activated, full_down, preferred_element_type=jnp.float32)
    joint = lax.psum(branches.astype(jnp.bfloat16), "head").astype(jnp.float32)
    output = inputs + joint + out_bias.astype(jnp.float32) + down_bias.astype(jnp.float32)
    upstream = cotangent[0]
    down_grad = jnp.dot(activated.T, upstream, preferred_element_type=jnp.float32)
    activated_grad = jnp.dot(upstream, full_down.T, preferred_element_type=jnp.float32)
    _, gelu_back = jax.vjp(partial(jax.nn.gelu, approximate=False), hidden)
    hidden_grad = gelu_back(activated_grad)[0].astype(jnp.bfloat16)
    up_grad = jnp.dot(low_two.T, hidden_grad, preferred_element_type=jnp.float32)
    up_bias_grad = jnp.sum(hidden_grad.astype(jnp.float32), axis=0)
    normed_two_grad = jnp.dot(hidden_grad, full_up.T, preferred_element_type=jnp.float32)
    out_grad = jnp.dot(mixed_low.T, upstream, preferred_element_type=jnp.float32)
    mixed_grad = jnp.dot(upstream, full_out.T, preferred_element_type=jnp.float32).astype(
        jnp.bfloat16
    )
    mixed_grad_heads = mixed_grad.reshape(count, local_heads, HEAD)
    delta = jnp.sum(mixed_grad_heads.astype(jnp.float32) * mixed, axis=-1).T

    def backward_block(query_grad, item):
        key_block, value_block, first = item
        shares = share_block(key_block, first)
        share_grad = jnp.einsum(
            "qhe,khe->hqk", mixed_grad_heads, value_block, preferred_element_type=jnp.float32
        )
        score_grad = (shares * (share_grad - delta[..., None])).astype(jnp.bfloat16)
        query_grad = (
            query_grad
            + jnp.einsum("hqk,khe->qhe", score_grad, key_block, preferred_element_type=jnp.float32)
            * scale
        )
        key_grad = (
            jnp.einsum("hqk,qhe->khe", score_grad, query, preferred_element_type=jnp.float32)
            * scale
        )
        value_grad = jnp.einsum(
            "hqk,qhe->khe",
            shares.astype(jnp.bfloat16),
            mixed_grad_heads,
            preferred_element_type=jnp.float32,
        )
        return (
            query_grad,
            jnp.concatenate(
                [key_grad.reshape(block, width), value_grad.reshape(block, width)], axis=1
            ),
        )

    query_grad, key_terms = lax.scan(
        backward_block,
        jnp.zeros((count, local_heads, HEAD), jnp.float32),
        (key_blocks, value_blocks, firsts),
    )
    own_grads = lax.psum_scatter(
        key_terms.reshape(length, 2 * width).astype(jnp.bfloat16),
        "ctx",
        scatter_dimension=0,
        tiled=True,
    ).astype(jnp.float32)
    query_pre = rotary(query_grad, -angles).reshape(count, width)
    key_pre = rotary(own_grads[:, :width].reshape(count, local_heads, HEAD), -angles).reshape(
        count, width
    )
    projected_grad = jnp.stack([query_pre, key_pre, own_grads[:, width:]]).astype(jnp.bfloat16)
    qkv_grad = jnp.einsum(
        "nd,cne->cde", low_one, projected_grad, preferred_element_type=jnp.float32
    )
    qkv_bias_grad = jnp.sum(projected_grad.astype(jnp.float32), axis=1)
    normed_one_grad = jnp.einsum(
        "cne,cde->nd", projected_grad, full_qkv, preferred_element_type=jnp.float32
    )
    normed_one_grad, normed_two_grad = (
        lax.psum(normed_one_grad.astype(jnp.bfloat16), "head").astype(jnp.float32),
        lax.psum(normed_two_grad.astype(jnp.bfloat16), "head").astype(jnp.float32),
    )
    _, norm_back_one = jax.vjp(layer_norm, inputs, gain_one, offset_one)
    input_one, gain_grad_one, offset_grad_one = norm_back_one(normed_one_grad)
    _, norm_back_two = jax.vjp(layer_norm, inputs, gain_two, offset_two)
    input_two, gain_grad_two, offset_grad_two = norm_back_two(normed_two_grad)
    upstream_wide = upstream.astype(jnp.float32)
    input_grad = upstream_wide + input_one + input_two
    bias_grad = jnp.sum(upstream_wide, axis=0)
    small = lax.psum(
        (
            gain_grad_one,
            offset_grad_one,
            qkv_bias_grad,
            bias_grad,
            gain_grad_two,
            offset_grad_two,
            up_bias_grad,
        ),
        ("stream", "ctx"),
    )
    slices = (
        lax.psum_scatter(
            qkv_grad.astype(jnp.bfloat16), "ctx", scatter_dimension=1, tiled=True
        ).astype(jnp.float32),
        lax.psum_scatter(
            out_grad.astype(jnp.bfloat16), "ctx", scatter_dimension=1, tiled=True
        ).astype(jnp.float32),
        lax.psum_scatter(
            up_grad.astype(jnp.bfloat16), "ctx", scatter_dimension=0, tiled=True
        ).astype(jnp.float32),
        lax.psum_scatter(
            down_grad.astype(jnp.bfloat16), "ctx", scatter_dimension=1, tiled=True
        ).astype(jnp.float32),
    )
    shards = (
        lax.psum(slices[0].astype(jnp.bfloat16), "stream").astype(jnp.float32),
        lax.psum(slices[1].astype(jnp.bfloat16), "stream").astype(jnp.float32),
        lax.psum(slices[2].astype(jnp.bfloat16), "stream").astype(jnp.float32),
        lax.psum(slices[3].astype(jnp.bfloat16), "stream").astype(jnp.float32),
    )
    return (
        output.astype(jnp.bfloat16)[None],
        input_grad[None],
        small[0],
        small[1],
        shards[0],
        small[2],
        shards[1],
        small[3],
        small[4],
        small[5],
        shards[2],
        small[6],
        shards[3],
        small[3],
    )


MESH = pl.DeviceIdType.MESH
FRONT_PLAN = (
    "z0", "z1", "l0", "P", "T", "N0", "s0", "z3", "s1", "p0", "L01", "z2", "p1", "N1", "L02", "l1", "s3", "N2", "L03", "p3", "s2", "N3", "f0", "Q", "L11", "p2", "A0", "A1", "A2",
    "A3", "L12", "f1", "F0", "F1", "F2", "F3", "L13", "f2", "B0", "B1", "f3", "D0", "D1", "B2", "D2", "B3", "D3", "E",
)
F32, BF16 = jnp.float32, jnp.bfloat16


def dot(a, b, over):
    return lax.dot_general(a, b, ((over[0:1], over[1:2]), ((), ())), preferred_element_type=F32)


def span(index, size):
    return pl.ds(pl.multiple_of(index * size, size), size)


def places():
    return lax.axis_index("stream"), lax.axis_index("ctx"), lax.axis_index("head")


def greet(peers):
    barrier = pltpu.get_barrier_semaphore()
    for peer in peers:
        pl.semaphore_signal(barrier, inc=1, device_id=peer, device_id_type=MESH)
    pl.semaphore_wait(barrier, len(peers))


def gather_body(
    x_ref, g_ref, qkv_ref, up_ref, out_ref, down_ref,
    gain_a_ref, off_a_ref, gain_b_ref, off_b_ref, qkv_bias_ref, up_bias_ref, rate_in, docs_ref,
    g_out, unit_out, act_out, dh_out, dqkv_out, mixed_out, qkv_out, up_out, out_out, down_out,
    z_send, z_recv, x_send, x_recv, y_send, y_recv, fx_send, fx_recv, fy_send, fy_recv,
    line_send, line_recv, core_send, core_recv, own_sem, give_sem, block_sem, small_sem,
    x_all, g_all, qkv_all, up_all, out_all, down_all,
    low_one, low_two, unit, query, keys, values, act, dh, dqkv, mixed_low,
    slope, mixed, norm, key_grad, value_grad, turn_ref, start_ref,
    gain_a, off_a, gain_b, off_b, qkv_bias, up_bias, rate_ref, rows_ref, bias_ref,
):
    s, c, h = places()
    x_peer = s + 1 - 2 * lax.rem(s, 2)
    y_peer = lax.rem(s + 2, 4)
    across = ((x_peer, c, h), (y_peer, c, h))
    core_peer = (s, c, 1 - h)
    ring = [(s, lax.rem(c + k, 4), h) for k in (1, 2, 3)]
    greet([*across, core_peer, *ring])

    count = x_ref.shape[0]
    slab, width, units = up_ref.shape[0], out_ref.shape[0] // 4, down_ref.shape[0] // 4
    quarter, half_count = slab // 4, count // 2

    def rows(base, size):
        return pl.ds(pl.multiple_of(base, size), size)

    def landed(m, r, part, half):
        def cut(total):
            size = total // 4
            if half is None:
                return part * size, size
            return part * size + half * (size // 2), size // 2

        if m == 0:
            at, size = cut(slab)
            return qkv_all.at[:, rows(r * slab + at, size), :]
        if m == 1:
            at, size = cut(slab)
            return up_all.at[rows(r * slab + at, size), :]
        if m == 2:
            at, size = cut(width)
            return out_all.at[rows(at, size), span(r, slab)]
        at, size = cut(units)
        return down_all.at[rows(at, size), span(r, slab)]

    def piece(m, to, part=None):
        if m == 0:
            inner = slice(None) if part is None else span(part, quarter)
            return qkv_ref.at[:, inner, span(to, width)]
        if m == 1:
            inner = slice(None) if part is None else span(part, quarter)
            return up_ref.at[inner, span(to, units)]
        size = width if m == 2 else units
        ref = out_ref if m == 2 else down_ref
        if part is None:
            return ref.at[span(to, size), :]
        return ref.at[rows(to * size + part * (size // 4), size // 4), :]

    def whole_piece(m, r):
        if m == 0:
            return qkv_all.at[:, span(r, slab), :]
        if m == 1:
            return up_all.at[span(r, slab), :]
        return (out_all if m == 2 else down_all).at[:, span(r, slab)]

    def remote(src, dst, send, recv, to):
        return pltpu.make_async_remote_copy(
            src_ref=src, dst_ref=dst, send_sem=send, recv_sem=recv, device_id=to, device_id_type=MESH
        )

    def z_copy(m, k):
        to = lax.rem(c + 4 - k, 4)
        return remote(
            piece(m, to, s), landed(m, c, s, None), z_send.at[m, k - 1], z_recv.at[m, k - 1], (s, to, h)
        )

    def direct(m, k, axis):
        r = lax.rem(c + k, 4)
        send, recv = (x_send, x_recv) if axis == 0 else (y_send, y_recv)
        here = landed(m, r, s, None)
        return remote(here, here, send.at[m, k - 1], recv.at[m, k - 1], across[axis])

    def onward(m, k, axis):
        r = lax.rem(c + k, 4)
        send, recv = (fx_send, fx_recv) if axis == 0 else (fy_send, fy_recv)
        here = landed(m, r, y_peer if axis == 0 else x_peer, 1 if axis == 0 else 0)
        return remote(here, here, send.at[m, k - 1], recv.at[m, k - 1], across[axis])

    lines = ((x_ref, x_all), (g_ref, g_all))

    def block(a, origin):
        return lines[a][1].at[rows(origin * count + h * half_count, half_count), :]

    def line_copy(a, t, side):
        origin = c - t if side == 0 else c + t
        src = lines[a][0].at[span(h, half_count), :] if t == 0 else block(a, origin)
        to = c + 1 if side == 0 else c - 1
        return remote(
            src, block(a, origin), line_send.at[a, side, t], line_recv.at[a, side, t], (s, to, h)
        )

    def core_copy(a, t, side):
        origin = c - t if side == 0 else c + t
        here = block(a, origin)
        return remote(here, here, core_send.at[a, side, t - 1], core_recv.at[a, side, t - 1], core_peer)

    def sends(t, side):
        if side == 0:
            return (c >= t) & (c < 3)
        return (c + t <= 3) & (c > 0)

    def gets(t, side):
        return c >= t if side == 0 else c + t <= 3

    def line_step(a, t):
        for side in (0, 1):
            @pl.when(gets(t, side))
            def _():
                line_copy(a, t - 1, side).wait_recv()
                core_copy(a, t, side).start()

            if t < 3:
                @pl.when(sends(t, side))
                def _():
                    line_copy(a, t, side).start()

    near = (1, 3, 2)
    order = [(m, k) for m in (0, 1, 3, 2) for k in near]

    def start_z(m):
        for k in near:
            z_copy(m, k).start()

    def pass_on(m):
        for k in near:
            direct(m, k, 0).wait_recv()
            onward(m, k, 1).start()
            direct(m, k, 1).wait_recv()
            onward(m, k, 0).start()

    def spread(m):
        for k in near:
            z_copy(m, k).wait_recv()
            direct(m, k, 0).start()
            direct(m, k, 1).start()

    ins = [
        pltpu.make_async_copy(a, b, own_sem.at[i])
        for i, (a, b) in enumerate(
            [(lines[a][0], lines[a][1].at[span(c, count), :]) for a in (0, 1)]
            + [(piece(m, c), whole_piece(m, c)) for m in range(4)]
        )
    ]
    for copy in ins:
        copy.start()
    tile = count
    length, model = x_all.shape
    rot = turn_ref.shape[2]
    span_rot = rot // 4
    scale = width**-0.5

    def finish(m):
        for k in near:
            onward(m, k, 0).wait_recv()
            onward(m, k, 1).wait_recv()
        ins[2 + m].wait()

    def give(i):
        pairs = (
            (qkv_all, qkv_out), (up_all, up_out), (out_all, out_out), (down_all, down_out),
            (act, act_out), (dh, dh_out), (dqkv, dqkv_out), (mixed_low, mixed_out),
        )
        return pltpu.make_async_copy(*pairs[i], give_sem.at[i])

    def give_block(a, origin):
        src, dst = ((unit, unit_out), (g_all, g_out))[a]
        at = span(origin, tile)
        return pltpu.make_async_copy(src.at[at, :], dst.at[at, :], block_sem.at[a])

    def blocks_of(t, do):
        if t == 0:
            do(c)
            return

        @pl.loop(0, 2)
        def _(side):
            origin = c + t * (2 * side - 1)

            @pl.when((origin >= 0) & (origin <= 3))
            def _():
                do(origin)

    def core_wait(a, t):
        for side in (0, 1):
            @pl.when(gets(t, side))
            def _():
                core_copy(a, t, side).wait_recv()

    def norm_block(origin):
        tall = 32

        @pl.loop(0, tile // tall)
        def _(i):
            at = pl.ds(pl.multiple_of(origin * tile + i * tall, tall), tall)
            wide = x_all[at, :].astype(F32)
            centred = wide - jnp.mean(wide, axis=-1, keepdims=True)
            spread_of = jnp.mean(centred * centred, axis=-1, keepdims=True)
            found = centred * lax.rsqrt(spread_of + 1e-05)
            unit[at, :] = found.astype(BF16)
            low_one[at, :] = (found * rows_ref[0:1, :] + rows_ref[1:2, :]).astype(BF16)
            low_two[at, :] = (found * rows_ref[2:3, :] + rows_ref[3:4, :]).astype(BF16)

        give_block(0, origin).start()

    smalls = [
        pltpu.make_async_copy(a, b, small_sem.at[i])
        for i, (a, b) in enumerate(
            (
                (gain_a_ref, gain_a), (off_a_ref, off_a), (gain_b_ref, gain_b), (off_b_ref, off_b),
                (qkv_bias_ref, qkv_bias), (up_bias_ref, up_bias), (rate_in, rate_ref),
            )
        )
    ]
    for copy in smalls:
        copy.start()

    def parameters():
        for copy in smalls:
            copy.wait()
        for i, ref in enumerate((gain_a, off_a, gain_b, off_b)):
            rows_ref[i : i + 1, :] = ref[...].astype(F32).reshape(1, model)
        part = qkv_bias[:, span(c, width)].astype(F32)
        for p in range(3):
            bias_ref[0:1, p * width : (p + 1) * width] = part[p : p + 1]
        bias_ref[1:2, :] = up_bias[span(c, units)].astype(F32).reshape(1, units)

    def tables():
        starts, total = [], docs_ref[0, 0] * 0
        for j in range(docs_ref.shape[1]):
            starts.append(total)
            total = total + docs_ref[0, j]

        @pl.loop(0, length // tile)
        def _(i):
            at = span(i, tile)
            place = i * tile + lax.broadcasted_iota(jnp.int32, (tile, rot), 0)
            lane = lax.broadcasted_iota(jnp.int32, (tile, rot), 1)
            first = jnp.zeros((tile, rot), jnp.int32)
            for start in starts:
                first = jnp.where(start <= place, jnp.maximum(first, start), first)
            start_ref[at, :] = first[:, 0:1]
            angle = (place - first).astype(F32) * rate_ref[0:1, :]
            sine = jnp.sin(angle)
            turn_ref[0, at, :] = jnp.where(lane < 2 * span_rot, jnp.cos(angle), 1.0)
            turn_ref[1, at, :] = jnp.where((lane >= span_rot) & (lane < 2 * span_rot), sine, 0.0)
            turn_ref[2, at, :] = jnp.where(lane < span_rot, -sine, 0.0)

    def turned(v, at, sign):
        near_part = v[:, :rot]
        moved = pltpu.roll(near_part, span_rot, 1) * turn_ref[1, at, :] + pltpu.roll(near_part, rot - span_rot, 1) * turn_ref[2, at, :]
        return jnp.concatenate([near_part * turn_ref[0, at, :] + sign * moved, v[:, rot:]], axis=1)

    def project():
        @pl.loop(0, length // tile)
        def _(i):
            at = span(i, tile)
            for p, into in enumerate((query, keys, values)):
                part = dot(low_one[at, :], qkv_all[p], (1, 0)) + bias_ref[0:1, p * width : (p + 1) * width]
                into[at, :] = (turned(part, at, 1.0) if p < 2 else part).astype(BF16)

    def allowed_of(i, wide):
        first = lax.broadcasted_iota(jnp.int32, (tile, wide), 1)
        place = i * tile + lax.broadcasted_iota(jnp.int32, (tile, wide), 0)
        return (first <= place) & (first >= start_ref[span(i, tile), :])

    def attend(i):
        wide = (i + 1) * tile
        at = slice(i * tile, wide)
        scores = dot(query[at, :], keys[0:wide, :], (1, 1)) * scale
        allowed = allowed_of(i, wide)
        masked = jnp.where(allowed, scores, -1e30)
        peak = jnp.max(masked, axis=-1, keepdims=True)
        raised = jnp.where(allowed, jnp.exp(masked - peak), 0.0)
        total = jnp.sum(raised, axis=-1, keepdims=True)
        norm[at, :] = peak + jnp.log(total)
        found = dot((raised / total).astype(BF16), values[0:wide, :], (1, 0))
        mixed[at, :] = found
        mixed_low[at, :] = found.astype(BF16)

    def feed(i):
        at = span(i, tile)
        for j in range(units // 256):
            cols = slice(j * 256, (j + 1) * 256)
            hidden = dot(low_two[at, :], up_all[:, cols], (1, 0)) + bias_ref[1:2, cols]
            share = 0.5 + 0.5 * lax.erf(hidden * (0.5**0.5))
            act[at, cols] = (hidden * share).astype(BF16)
            slope[at, cols] = share + hidden * jnp.exp(-0.5 * hidden * hidden) * ((0.5 / jnp.pi) ** 0.5)

    def back_attend(origin):
        at = span(origin, tile)
        grad = dot(g_all[at, :], out_all[...], (1, 1)).astype(BF16)
        scores = dot(query[at, :], keys[...], (1, 1)) * scale
        shares = jnp.where(allowed_of(origin, length), jnp.exp(scores - norm[at, :]), 0.0)
        delta = jnp.sum(grad.astype(F32) * mixed[at, :], axis=-1, keepdims=True)
        share_grad = dot(grad, values[...], (1, 1))
        score_grad = (shares * (share_grad - delta)).astype(BF16)
        value_grad[...] += dot(shares.astype(BF16), grad, (0, 0))
        key_grad[...] += dot(score_grad, query[at, :], (0, 0))
        part = dot(score_grad, keys[...], (1, 0)) * scale
        dqkv[at, 0:width] = turned(part, at, -1.0).astype(BF16)

    def back_feed(origin):
        at = span(origin, tile)
        for j in range(units // 256):
            cols = slice(j * 256, (j + 1) * 256)
            part = dot(g_all[at, :], down_all[cols, :], (1, 1))
            dh[at, cols] = (part * slope[at, cols]).astype(BF16)

    def start_line(a):
        for side in (0, 1):
            @pl.when(sends(0, side))
            def _():
                line_copy(a, 0, side).start()

    def close():
        @pl.loop(0, length // tile)
        def _(i):
            at = span(i, tile)
            dqkv[at, width : 2 * width] = turned(key_grad[at, :] * scale, at, -1.0).astype(BF16)
            dqkv[at, 2 * width : 3 * width] = value_grad[at, :].astype(BF16)

        give(5).start()
        give(6).start()

    def run(step):
        op, rest = step[0], [int(d) for d in step[1:]]
        if op == "z":
            start_z(*rest)
        elif op == "s":
            spread(*rest)
        elif op == "p":
            pass_on(*rest)
        elif op == "f":
            finish(*rest)
            give(*rest).start()
        elif op == "l":
            start_line(*rest)
        elif op == "L":
            line_step(*rest)
        elif op == "N":
            if rest[0]:
                core_wait(0, *rest)
            else:
                ins[0].wait()
            blocks_of(*rest, norm_block)
        elif op == "P":
            parameters()
        elif op == "T":
            tables()
        elif op == "Q":
            project()
        elif op == "A":
            attend(*rest)
            if rest[0] == 3:
                give(7).start()
        elif op == "F":
            feed(*rest)
            if rest[0] == 3:
                give(4).start()
        elif op == "B":
            if rest[0]:
                core_wait(1, *rest)
            else:
                ins[1].wait()
            blocks_of(*rest, back_attend)
        elif op == "D":
            blocks_of(*rest, back_feed)
        elif op == "E":
            close()

    key_grad[...] = jnp.zeros_like(key_grad)
    value_grad[...] = jnp.zeros_like(value_grad)
    for step in FRONT_PLAN:
        run(step)
    for t in (0, 1, 2, 3):
        blocks_of(t, lambda origin: give_block(1, origin).start())
    for a in (0, 1):
        for side in (0, 1):
            for t in (1, 2, 3):
                @pl.when(gets(t, side))
                def _():
                    core_copy(a, t, side).wait_send()
                @pl.when(sends(t - 1, side))
                def _():
                    line_copy(a, t - 1, side).wait_send()
    for m, k in order:
        z_copy(m, k).wait_send()
        for axis in (0, 1):
            direct(m, k, axis).wait_send()
            onward(m, k, axis).wait_send()
    pltpu.make_async_copy(unit, unit_out, block_sem.at[0]).wait()
    pltpu.make_async_copy(g_all, g_out, block_sem.at[1]).wait()
    for i in range(8):
        give(i).wait()


def gather_all(tokens, cotangent, w_qkv, w_up, w_out, w_down, gain_a, off_a, gain_b, off_b, b_qkv, b_up, docs):
    count, model = tokens.shape
    length = 4 * count
    width, units = w_out.shape[0] // 4, w_down.shape[0] // 4
    frequency = 10000.0 ** (-np.arange(0, ROT, 2, dtype=np.float32) / np.float32(ROT))
    rate = jnp.asarray(np.tile(frequency.astype(np.float32), (8, 4)))
    dma = pltpu.SemaphoreType.DMA
    weights = [(3, model, width), (model, units), (width, model), (units, model)]
    wide, narrow = (length, model), (length, width)
    results = [wide, wide, (length, units), (length, units), (length, 3 * width), narrow] + weights
    scratch = [dma((4, 3))] * 10 + [dma((2, 2, 3))] * 4 + [dma((6,)), dma((8,)), dma((2,)), dma((7,))]
    scratch += [
        pltpu.VMEM(v, BF16)
        for v in [wide, wide] + weights + [wide] * 3 + [narrow] * 3
        + [(length, units)] * 2 + [(length, 3 * width), narrow]
    ]
    scratch += [pltpu.VMEM(v, F32) for v in ((length, units), narrow, (length, 1), narrow, narrow)]
    scratch += [pltpu.VMEM((3, length, rate.shape[1]), F32), pltpu.VMEM((length, 1), jnp.int32)]
    scratch += [pltpu.VMEM((model,), BF16)] * 4 + [pltpu.VMEM(b_qkv.shape, BF16), pltpu.VMEM(b_up.shape, BF16)]
    scratch += [pltpu.VMEM(v, F32) for v in (rate.shape, (8, model), (8, units))]
    any_space = pl.BlockSpec(memory_space=pl.ANY)
    return pl.pallas_call(
        gather_body,
        out_shape=[jax.ShapeDtypeStruct(v, BF16) for v in results],
        in_specs=[any_space] * 13 + [pl.BlockSpec(memory_space=pltpu.SMEM)],
        out_specs=[any_space] * 10,
        scratch_shapes=scratch,
        compiler_params=pltpu.CompilerParams(
            collective_id=0, has_side_effects=True, vmem_limit_bytes=63 << 20
        ),
        name="gather",
    )(
        tokens, cotangent, w_qkv, w_up, w_out, w_down, gain_a, off_a, gain_b, off_b, b_qkv, b_up, rate, docs
    )


LEADS = (4, 4, 4, 4, 1, 1)
BACK_PLAN = (
    "D", "15", "P", "U", "13", "Q", "10", "11", "12", "O", "14", "B0", "B1", "25", "R0", "I0", "I1", "a", "23", "20", "21", "22", "b", "Z5", "24", "S0", "c", "Z3", "Z0", "Z1", "Z2", "Z4",
    "R1", "X5", "d", "N5", "X3", "e", "N3", "X0", "X1", "X2", "N0", "N1", "N2", "X4", "N4", "S1",
)
def settle_body(
    act_in, up_in, unit_in, dh_in, dqkv_in, mixed_in, wq_in, wu_in, wo_in, wd_in,
    gain_a_ref, off_a_ref, gain_b_ref, off_b_ref,
    joint, inward, o0, o1, o2, o3, small_out,
    s1x_send, s1x_recv, s1y_send, s1y_recv, s2x_send, s2x_recv, s2y_send, s2y_recv,
    x_send, x_recv, y_send, y_recv, fx_send, fx_recv, fy_send, fy_recv,
    z_send, z_recv, keep_sem, load_sem, weight_sem,
    core_send, core_recv, row_send, row_recv, back_send, back_recv, back_sem,
    sum_send, sum_recv, sum_sem, small_sem,
    act, up, unit, dh, dqkv, mixed, w_wide, w_out, w_qkv, *rest,
):
    grads, first, second = rest[0:6], (rest[6:18:2], rest[7:18:2]), (rest[18:30:2], rest[19:30:2])
    (
        own_half, core_half, send_half, row_parts, done_half,
        sums, sums_core, slots, total_own, total_x, total_y,
        gain_a, off_a, gain_b, off_b, rows_ref, low_ref,
    ) = rest[30:]
    s, c, h = places()
    x_at, y_at = lax.rem(s, 2), lax.div(s, 2)
    x_off, y_off = 1 - x_at, 1 - y_at
    x_peer, y_peer = y_at * 2 + x_off, y_off * 2 + x_at
    across = ((x_peer, c, h), (y_peer, c, h))
    core_peer = (s, c, 1 - h)
    near = (1, 3, 2)
    greet([*across, core_peer, *[(s, lax.rem(c + k, 4), h) for k in near]])
    outs = (o0, o1, o2, o3)
    first, second = list(zip(*first)), list(zip(*second))
    slab = o2.shape[-1]
    length, model = up.shape
    units, width = act.shape[1], mixed.shape[1]
    half_cols = model // 2
    count = joint.shape[0]
    tile = 256

    def remote(src, dst, send, recv, to):
        return pltpu.make_async_remote_copy(
            src_ref=src, dst_ref=dst, send_sem=send, recv_sem=recv, device_id=to, device_id_type=MESH
        )

    loads = [
        pltpu.make_async_copy(a, b, load_sem.at[i])
        for i, (a, b) in enumerate(
            ((act_in, act), (up_in, up), (dh_in, dh), (unit_in, unit), (dqkv_in, dqkv), (mixed_in, mixed))
        )
    ]
    for load in loads:
        load.start()

    smalls = [
        pltpu.make_async_copy(a, b, small_sem.at[i])
        for i, (a, b) in enumerate(
            ((gain_a_ref, gain_a), (off_a_ref, off_a), (gain_b_ref, gain_b), (off_b_ref, off_b))
        )
    ]
    for copy in smalls:
        copy.start()

    def side(which):
        return 1 - h if which == 0 else h

    def weight_load(i):
        at = span(side(i % 2), half_cols)
        if i < 2:
            return pltpu.make_async_copy(wd_in.at[:, at], w_wide.at[i], weight_sem.at[i])
        if i < 4:
            return pltpu.make_async_copy(wu_in.at[at, :], w_wide.at[i % 2], weight_sem.at[i])
        if i < 6:
            return pltpu.make_async_copy(wo_in.at[:, at], w_out.at[i % 2], weight_sem.at[i])
        return pltpu.make_async_copy(wq_in.at[:, at, :], w_qkv.at[i % 2], weight_sem.at[i])

    for i in (0, 4, 1, 5, 6, 7):
        weight_load(i).start()

    def one(m, half):
        src = grads[m].at[:, :, x_off, 0] if half == 0 else grads[m].at[:, y_off, :, 1]
        send, recv = (s1x_send, s1x_recv) if half == 0 else (s1y_send, s1y_recv)
        return remote(src, first[m][half], send.at[m], recv.at[m], across[half])

    def two(m, half):
        src = first[m][half].at[:, y_off if half == 0 else x_off]
        send, recv = (s2y_send, s2y_recv) if half == 0 else (s2x_send, s2x_recv)
        return remote(src, second[m][half], send.at[m], recv.at[m], across[1 - half])

    def add_first(m, half):
        into, more = first[m][half], grads[m]
        lead, _, height, _ = into.shape
        tall = min(height, 32)

        @pl.loop(0, lead * 2 * (height // tall))
        def _(i):
            at = lax.rem(i, height // tall)
            pair = lax.div(i, height // tall)
            l, j, rows = lax.div(pair, 2), lax.rem(pair, 2), span(at, tall)
            term = more[l, j, x_at, 0, rows, :] if half == 0 else more[l, y_at, j, 1, rows, :]
            into[l, j, rows, :] = (into[l, j, rows, :].astype(F32) + term.astype(F32)).astype(BF16)

    def add_second(m, half):
        into, more = second[m][half], first[m][half]
        mine = y_at if half == 0 else x_at
        lead, height, _ = into.shape
        tall = min(height, 32)

        @pl.loop(0, lead * (height // tall))
        def _(i):
            l, rows = lax.div(i, height // tall), span(lax.rem(i, height // tall), tall)
            term = more[l, mine, rows, :].astype(F32)
            into[l, rows, :] = (into[l, rows, :].astype(F32) + term).astype(BF16)

    def share_of(m, half, to):
        ref = second[m][half]
        return ref.at[to] if m < 4 else ref.at[0, :, span(to, slab)]

    def home(m, half):
        if m < 3:
            return outs[0].at[m, s, half, :, span(c, width)]
        if m == 3:
            return outs[1].at[s, half, :, span(c, units)]
        return outs[m - 2].at[c, s, half]

    def z_copy(m, half, k):
        to = lax.rem(c + 4 - k, 4)
        i = (m * 2 + half) * 3 + k - 1
        return remote(share_of(m, half, to), home(m, half), z_send.at[i], z_recv.at[i], (s, to, h))

    def keep(m, half):
        return pltpu.make_async_copy(share_of(m, half, c), home(m, half), keep_sem.at[m, half])

    def quarter(m, q, half=None):
        at = (q,) if half is None else (q, half)
        if m < 3:
            return outs[0].at[(m, *at)]
        if m == 3:
            return outs[1].at[at]
        return outs[m - 2].at[(slice(None), *at)]

    def direct(m, axis):
        send, recv = (x_send, x_recv) if axis == 0 else (y_send, y_recv)
        here = quarter(m, s)
        return remote(here, here, send.at[m], recv.at[m], across[axis])

    def onward(m, axis):
        send, recv = (fx_send, fx_recv) if axis == 0 else (fy_send, fy_recv)
        here = quarter(m, y_peer if axis == 0 else x_peer, 1 - axis)
        return remote(here, here, send.at[m], recv.at[m], across[axis])

    finals = (joint, inward)

    def core_copy(a):
        return remote(send_half, core_half.at[a], core_send.at[a], core_recv.at[a], core_peer)

    def row_copy(a, k):
        to = lax.rem(c + 4 - k, 4)
        return remote(
            own_half.at[a, span(to, count)], row_parts.at[a, k - 1],
            row_send.at[a, k - 1], row_recv.at[a, k - 1], (s, to, h),
        )

    def back_copy(a):
        return remote(
            done_half.at[a], finals[a].at[:, span(h, half_cols)], back_send.at[a], back_recv.at[a], core_peer
        )

    def back_keep(a):
        return pltpu.make_async_copy(done_half.at[a], finals[a].at[:, span(h, half_cols)], back_sem.at[a])

    def line_start(a):
        core_copy(a).wait_recv()
        tall = 32

        @pl.loop(0, length // tall)
        def _(i):
            rows = span(i, tall)
            own_half[a, rows, :] = (
                own_half[a, rows, :].astype(F32) + core_half[a, rows, :].astype(F32)
            ).astype(BF16)

        for k in near:
            row_copy(a, k).start()

    def line_sum(a):
        for k in near:
            row_copy(a, k).wait_recv()
        tall = 32

        @pl.loop(0, count // tall)
        def _(i):
            rows = span(i, tall)
            total = own_half[a, pl.ds(pl.multiple_of(c * count + i * tall, tall), tall), :].astype(F32)
            for k in range(3):
                total = total + row_parts[a, k, rows, :].astype(F32)
            done_half[a, rows, :] = total.astype(BF16)

        back_copy(a).start()
        back_keep(a).start()

    def down_grad():
        rows = units // 8

        @pl.loop(0, 4)
        def _(q):
            left = act[:, span(q, 2 * rows)]
            for j in range(model // 512):
                part = dot(left, up[:, j * 512 : (j + 1) * 512], (0, 0)).astype(BF16)
                for half in (0, 1):
                    grads[5][0, lax.div(q, 2), lax.rem(q, 2), half, :, j * 512 : (j + 1) * 512] = part[
                        half * rows : (half + 1) * rows
                    ]

    def out_grad():
        rows = width // 8
        for j in range(model // 512):
            part = dot(mixed[...], up[:, j * 512 : (j + 1) * 512], (0, 0)).astype(BF16)
            for i in range(8):
                grads[4][0, i // 4, (i // 2) % 2, i % 2, :, j * 512 : (j + 1) * 512] = part[i * rows : (i + 1) * rows]

    same = lax.broadcasted_iota(jnp.int32, (tile, tile), 0) == lax.broadcasted_iota(jnp.int32, (tile, tile), 1)
    eye = jnp.where(same, 1.0, 0.0).astype(BF16)

    def columns(t):
        return dot(eye, low_ref[:, span(t, tile)], (1, 1))

    def scaled(part, column, at, column_sum):
        return (part * column[:, at : at + 1] + column[:, at + 1 : at + 2] * column_sum).astype(BF16)

    def column_sum(ref, cols):
        total = jnp.zeros((1, cols.stop - cols.start), F32)
        for i in range(length // tile):
            total = total + jnp.sum(ref[i * tile : (i + 1) * tile, cols].astype(F32), axis=0, keepdims=True)
        return total

    def up_grad():
        rows = tile // 4

        @pl.loop(0, model // tile)
        def _(t):
            left, column = unit[:, span(t, tile)], columns(t)
            for j in range(units // 512):
                cols = slice(j * 512, (j + 1) * 512)
                near_sum = sums[5:6, 3 * width + j * 512 : 3 * width + (j + 1) * 512]
                part = scaled(dot(left, dh[:, cols], (0, 0)), column, 2, near_sum)
                for i in range(4):
                    grads[3][lax.div(t, 2), lax.rem(t, 2), i // 2, i % 2, :, cols] = part[i * rows : (i + 1) * rows]

    def qkv_grad():
        rows = tile // 4

        @pl.loop(0, model // tile)
        def _(t):
            left, column = unit[:, span(t, tile)], columns(t)
            for p in range(3):
                cols = slice(p * width, (p + 1) * width)
                part = scaled(dot(left, dqkv[:, cols], (0, 0)), column, 0, sums[5:6, cols])
                for i in range(4):
                    grads[p][lax.div(t, 2), lax.rem(t, 2), i // 2, i % 2] = part[i * rows : (i + 1) * rows]

    def branches(which):
        into = send_half if which == 0 else own_half.at[0]

        @pl.loop(0, length // tile)
        def _(i):
            rows = span(i, tile)
            for j in range(half_cols // 512):
                cols = slice(j * 512, (j + 1) * 512)
                part = dot(mixed[rows, :], w_out[which, :, cols], (1, 0))
                part = part + dot(act[rows, :], w_wide[which, :, cols], (1, 0))
                into[rows, cols] = part.astype(BF16)

    def inwards(which):
        into = send_half if which == 0 else own_half.at[1]
        base = side(which) * half_cols
        for j in range(half_cols // 512):
            cols = slice(j * 512, (j + 1) * 512)
            far = span(side(which) * (half_cols // 512) + j, 512)
            zero = jnp.zeros((8, 512), F32)

            def step(i, carry):
                rows = span(i, tile)
                one_part = dot(dqkv[rows, 0:width], w_qkv[which, 0, cols, :], (1, 1))
                for p in (1, 2):
                    one_part = one_part + dot(
                        dqkv[rows, p * width : (p + 1) * width], w_qkv[which, p, cols, :], (1, 1)
                    )
                two_part = dot(dh[rows, :], w_wide[which, cols, :], (1, 1))
                into[rows, cols] = (one_part * rows_ref[0:1, far] + two_part * rows_ref[2:3, far]).astype(BF16)
                place = unit[rows, far].astype(F32)

                def fold(v):
                    return jnp.sum(v.reshape(tile // 8, 8, 512), axis=0)

                return (
                    carry[0] + fold(one_part * place),
                    carry[1] + fold(one_part),
                    carry[2] + fold(two_part * place),
                    carry[3] + fold(two_part),
                )

            found = lax.fori_loop(0, length // tile, step, (zero, zero, zero, zero))
            for n in range(4):
                sums[n : n + 1, far] = jnp.sum(found[n], axis=0, keepdims=True)

    def sum_core():
        return remote(sums, sums_core, sum_send.at[0], sum_recv.at[0], core_peer)

    def sum_line(k):
        return remote(
            sums, slots.at[c], sum_send.at[k], sum_recv.at[k], (s, lax.rem(c + 4 - k, 4), h)
        )

    def sum_x():
        return remote(total_own, total_x, sum_send.at[4], sum_recv.at[4], across[0])

    def sum_y():
        return remote(total_own, total_y, sum_send.at[5], sum_recv.at[5], across[1])

    kinds = range(6)
    loaded = set()

    def need(*which):
        for i in which:
            if i not in loaded:
                loads[i].wait()
                loaded.add(i)

    def parameters():
        for copy in smalls:
            copy.wait()
        rows_ref[...] = jnp.zeros_like(rows_ref)
        for i, ref in enumerate((gain_a, off_a, gain_b, off_b)):
            rows_ref[i : i + 1, :] = ref[...].astype(F32).reshape(1, model)
        low_ref[...] = rows_ref[...].astype(BF16)

    def compute_sums():
        sums[4:5, :] = jnp.sum(up[span(c, count), :].astype(F32), axis=0, keepdims=True) * 0.5
        sums[5:8, :] = jnp.zeros((3, model), F32)

    def small_copy():
        return pltpu.make_async_copy(total_own, small_out, sum_sem.at[0])

    def stage_two(m):
        for half in (0, 1):
            one(m, half).wait_recv()
            add_first(m, half)
            two(m, half).start()

    def stage_z(m):
        for half in (0, 1):
            two(m, half).wait_recv()
            add_second(m, half)
            for k in near:
                z_copy(m, half, k).start()
            keep(m, half).start()

    def stage_out(m):
        for half in (0, 1):
            for k in near:
                z_copy(m, half, k).wait_recv()
            keep(m, half).wait()
        for axis in (0, 1):
            direct(m, axis).start()

    def stage_on(m):
        direct(m, 0).wait_recv()
        onward(m, 1).start()
        direct(m, 1).wait_recv()
        onward(m, 0).start()

    def run(step):
        op, m = step[0], int(step[1]) if len(step) > 1 else None
        if op == "D":
            need(0, 1)
            down_grad()
        elif op == "P":
            parameters()
        elif op == "U":
            need(1, 2, 3)
            compute_sums()
            for j in range(units // 512):
                cols = slice(j * 512, (j + 1) * 512)
                sums[5:6, 3 * width + cols.start : 3 * width + cols.stop] = column_sum(dh, cols)
            up_grad()
        elif op == "Q":
            need(3, 4)
            for p in range(3):
                cols = slice(p * width, (p + 1) * width)
                sums[5:6, cols] = column_sum(dqkv, cols)
            qkv_grad()
        elif op == "O":
            need(1, 5)
            out_grad()
        elif op == "1":
            one(m, 0).start()
            one(m, 1).start()
        elif op == "B":
            need(0, 5)
            weight_load(m).wait()
            weight_load(4 + m).wait()
            branches(m)
            weight_load(2 + m).start()
            if m == 0:
                core_copy(0).start()
        elif op == "I":
            need(2, 3, 4)
            if m == 0:
                core_copy(0).wait_send()
            weight_load(2 + m).wait()
            weight_load(6 + m).wait()
            inwards(m)
            if m == 0:
                core_copy(1).start()
        elif op == "2":
            stage_two(m)
        elif op == "Z":
            stage_z(m)
        elif op == "X":
            stage_out(m)
        elif op == "N":
            stage_on(m)
        elif op == "R":
            line_start(m)
        elif op == "S":
            line_sum(m)
        elif op == "a":
            sum_core().start()
        elif op == "b":
            sum_core().wait()
            sums[0:5, :] = sums[0:5, :] + sums_core[0:5, :]
            for k in near:
                sum_line(k).start()
            slots[c] = sums[...]
        elif op == "c":
            for k in near:
                sum_line(k).wait()
            total_own[0:8, :] = slots[0] + slots[1] + slots[2] + slots[3]
            for i in range(4):
                total_own[8 + i : 9 + i, :] = slots[i, 5:6, :]
            total_own[12:16, :] = jnp.zeros((4, model), F32)
            sum_x().start()
        elif op == "d":
            sum_x().wait()
            total_own[...] = total_own[...] + total_x[...]
            sum_y().start()
        elif op == "e":
            sum_y().wait()
            total_own[...] = total_own[...] + total_y[...]
            small_copy().start()

    for step in BACK_PLAN:
        run(step)
    for m in kinds:
        for axis in (0, 1):
            onward(m, axis).wait_recv()
    small_copy().wait()
    for a in (0, 1):
        back_copy(a).wait()
        back_keep(a).wait()
        for k in near:
            row_copy(a, k).wait_send()
    core_copy(1).wait_send()
    for m in kinds:
        for half in (0, 1):
            one(m, half).wait_send()
            two(m, half).wait_send()
            for k in near:
                z_copy(m, half, k).wait_send()
        for axis in (0, 1):
            direct(m, axis).wait_send()
            onward(m, axis).wait_send()


def settle_all(act, up, unit, dh, dqkv, mixed, w_qkv, w_up, w_out, w_down, gain_a, off_a, gain_b, off_b):
    length, model = up.shape
    units, width = act.shape[1], mixed.shape[1]
    slab, count, half = model // 4, length // 4, model // 2
    dma = pltpu.SemaphoreType.DMA
    heights = (*[slab // 8] * 4, width // 8, units // 8)
    widths = (width, width, width, units, model, model)
    out_shapes = [
        (count, model), (count, model),
        (3, 4, 2, heights[0], 4 * width), (4, 2, heights[3], 4 * units),
        (4, 4, 2, heights[4], slab), (4, 4, 2, heights[5], slab),
    ]
    scratch = [dma((6,))] * 16 + [dma((36,))] * 2 + [dma((6, 2)), dma((6,)), dma((8,))]
    scratch += [dma((2,)), dma((2,)), dma((2, 3)), dma((2, 3)), dma((2,)), dma((2,)), dma((2,))]
    scratch += [dma((6,)), dma((6,)), dma((1,)), dma((4,))]
    vmem = [(length, units), (length, model), (length, model), (length, units), (length, 3 * width), (length, width)]
    vmem += [(2, units, half), (2, width, half), (2, 3, half, width)]
    shapes = list(zip(LEADS, heights, widths))
    vmem += [(l, 2, 2, 2, r, k) for l, r, k in shapes]
    vmem += [(l, 2, r, k) for l, r, k in shapes for _ in (0, 1)]
    vmem += [(l, r, k) for l, r, k in shapes for _ in (0, 1)]
    vmem += [(2, length, half), (2, length, half), (length, half), (2, 3, count, half), (2, count, half)]
    scratch += [pltpu.VMEM(v, BF16) for v in vmem]
    scratch += [pltpu.VMEM(v, F32) for v in ((8, model), (8, model), (4, 8, model), (16, model), (16, model), (16, model))]
    scratch += [pltpu.VMEM((model,), BF16)] * 4 + [pltpu.VMEM((8, model), F32), pltpu.VMEM((8, model), BF16)]
    any_space = pl.BlockSpec(memory_space=pl.ANY)
    joint, inward, q, u, o, d, small = pl.pallas_call(
        settle_body,
        out_shape=[jax.ShapeDtypeStruct(v, BF16) for v in out_shapes] + [jax.ShapeDtypeStruct((16, model), F32)],
        in_specs=[any_space] * 14,
        out_specs=[any_space] * 7,
        scratch_shapes=scratch,
        compiler_params=pltpu.CompilerParams(
            collective_id=1, has_side_effects=True, vmem_limit_bytes=63 << 20
        ),
        name="settle",
    )(act, up, unit, dh, dqkv, mixed, w_qkv, w_up, w_out, w_down, gain_a, off_a, gain_b, off_b)
    return (
        joint, inward, q.reshape(3, slab, 4 * width), u.reshape(slab, 4 * units),
        o.reshape(4 * width, slab), d.reshape(4 * units, slab), small,
    )


def finish_body(
    q_ref, u_ref, o_ref, d_ref, joint_ref, inward_ref, own_ref, up_ref,
    small_ref, bias_a, bias_b,
    q_out, u_out, o_out, d_out, y_out, g_out, v0, v1, v2, v3, v4, v5, qb_out, ub_out,
):
    q_out[...] = q_ref[...].astype(F32)
    u_out[...] = u_ref[...].astype(F32)
    o_out[...] = o_ref[...].astype(F32)
    d_out[...] = d_ref[...].astype(F32)
    wide = own_ref[...].astype(F32)
    bias = (bias_a[...].astype(F32) + bias_b[...].astype(F32)).reshape(1, wide.shape[1])
    y_out[...] = (wide + joint_ref[...].astype(F32) + bias).astype(BF16)
    centred = wide - jnp.mean(wide, axis=-1, keepdims=True)
    scale = lax.rsqrt(jnp.mean(centred * centred, axis=-1, keepdims=True) + 1e-05)
    unit = centred * scale
    inward = inward_ref[...].astype(F32)
    inward = inward - jnp.mean(inward, axis=-1, keepdims=True) - unit * jnp.mean(inward * unit, axis=-1, keepdims=True)
    g_out[...] = up_ref[...].astype(F32) + scale * inward

    @pl.when(pl.program_id(0) == 0)
    def _():
        for i, out in zip((0, 1, 4, 2, 3, 4), (v0, v1, v2, v3, v4, v5)):
            out[...] = small_ref[i : i + 1, :].reshape(out.shape)
        width, units = qb_out.shape[1] // 4, ub_out.shape[0] // 4
        for i in range(4):
            row = small_ref[8 + i : 9 + i, :]
            for p in range(3):
                qb_out[p : p + 1, i * width : (i + 1) * width] = row[:, p * width : (p + 1) * width]
            ub_out[i * units : (i + 1) * units] = row[:, 3 * width : 3 * width + units].reshape(units)


def finish_all(q, u, o, d, joint, inward, own, upstream, small, bias_a, bias_b):
    steps = 16
    arrays = [q, u, o, d, joint, inward, own, upstream]

    def spec(a):
        return pl.BlockSpec((a.shape[0] // steps, a.shape[1]), lambda i: (i, 0))

    results = [(a.shape, F32) for a in (q, u, o, d)] + [(own.shape, BF16), (own.shape, F32)]
    smalls = [(own.shape[1:], F32)] * 6 + [((3, q.shape[1]), F32), (u.shape[1:], F32)]
    results += smalls

    def whole(shape):
        return pl.BlockSpec(shape, lambda i: (0,) * len(shape))

    return pl.pallas_call(
        finish_body,
        grid=(steps,),
        out_shape=[jax.ShapeDtypeStruct(v, t) for v, t in results],
        in_specs=[spec(a) for a in arrays] + [whole(v.shape) for v in (small, bias_a, bias_b)],
        out_specs=[spec(a) for a in (q, u, o, d, own, own)] + [whole(v) for v, _ in smalls],
        compiler_params=pltpu.CompilerParams(vmem_limit_bytes=63 << 20),
        name="finish",
    )(*arrays, small, bias_a, bias_b)


def per_device(
    tokens,
    doc_lengths,
    ln1_gain,
    ln1_bias,
    qkv_weight,
    qkv_bias,
    out_weight,
    out_bias,
    ln2_gain,
    ln2_bias,
    up_weight,
    up_bias,
    down_weight,
    down_bias,
    cotangent,
):
    upstream, unit, activated, hidden_grad, projected_grad, mixed_low, w_qkv, w_up, w_out, w_down = (
        gather_all(
            tokens[0],
            cotangent[0],
            qkv_weight,
            up_weight,
            out_weight,
            down_weight,
            ln1_gain,
            ln1_bias,
            ln2_gain,
            ln2_bias,
            qkv_bias,
            up_bias,
            doc_lengths,
        )
    )

    joint, inward, qkv_out, up_out, out_out, down_out, small = settle_all(
        activated,
        upstream,
        unit,
        hidden_grad,
        projected_grad,
        mixed_low,
        w_qkv,
        w_up,
        w_out,
        w_down,
        ln1_gain,
        ln1_bias,
        ln2_gain,
        ln2_bias,
    )
    q_grad, u_grad, o_grad, d_grad, output, input_grad, *rest = finish_all(
        qkv_out.reshape(-1, qkv_out.shape[-1]),
        up_out,
        out_out,
        down_out,
        joint,
        inward,
        tokens[0],
        cotangent[0],
        small,
        out_bias,
        down_bias,
    )
    return (
        output[None],
        input_grad[None],
        rest[0],
        rest[1],
        q_grad.reshape(qkv_out.shape),
        rest[6],
        o_grad,
        rest[2],
        rest[3],
        rest[4],
        u_grad,
        rest[7],
        d_grad,
        rest[5],
    )


def solution(mesh):
    in_specs = (
        P("stream", "ctx", None),
        P("stream", None),
        P(),
        P(),
        P(None, "ctx", "head"),
        P(None, "head"),
        P("head", "ctx"),
        P(),
        P(),
        P(),
        P("ctx", "head"),
        P("head"),
        P("head", "ctx"),
        P(),
        P("stream", "ctx", None),
    )
    out_specs = (
        P("stream", "ctx", None),
        P("stream", "ctx", None),
        P(),
        P(),
        P(None, "ctx", "head"),
        P(None, "head"),
        P("head", "ctx"),
        P(),
        P(),
        P(),
        P("ctx", "head"),
        P("head"),
        P("head", "ctx"),
        P(),
    )
    split = mesh.shape["ctx"] * mesh.shape["head"]

    def whole(*arrays):
        heads, units = arrays[4].shape[2] // HEAD, arrays[10].shape[1]
        grouped = (mesh.shape["stream"], mesh.shape["ctx"], mesh.shape["head"]) == (4, 4, 2)
        fits = grouped and heads == split and units % (split * 512) == 0
        return jax.shard_map(
            per_device if fits else general_device,
            mesh=mesh,
            in_specs=in_specs,
            out_specs=out_specs,
            check_vma=False,
        )(*arrays)

    return whole
```

```python
from functools import partial
import math

import jax
import jax.numpy as jnp
import numpy as np
from jax import lax
from jax.experimental import pallas as pl
from jax.experimental.pallas import tpu as pltpu
from jax.sharding import PartitionSpec as P

HEAD = 256
ROT = 64


def layer_norm(values, gain, offset):
    centre = jnp.mean(values, axis=-1, keepdims=True)
    centred = values - centre
    spread = jnp.mean(centred * centred, axis=-1, keepdims=True)
    return centred * lax.rsqrt(spread + 1e-05) * gain + offset


def rotary(values, angles):
    half = angles.shape[-1]
    cosine = jnp.cos(angles)[:, None, :]
    sine = jnp.sin(angles)[:, None, :]
    first = values[..., :half]
    second = values[..., half : 2 * half]
    return jnp.concatenate(
        [first * cosine - second * sine, second * cosine + first * sine, values[..., 2 * half :]],
        axis=-1,
    )


def doc_starts(doc_sizes, positions):
    place = jnp.arange(doc_sizes.shape[0])
    before = place[None, :] < place[:, None]
    starts = jnp.sum(jnp.where(before, doc_sizes[None, :], 0), axis=1)
    return jnp.max(jnp.where(starts[None, :] <= positions[:, None], starts[None, :], 0), axis=1)


def general_device(
    tokens,
    doc_lengths,
    ln1_gain,
    ln1_bias,
    qkv_weight,
    qkv_bias,
    out_weight,
    out_bias,
    ln2_gain,
    ln2_bias,
    up_weight,
    up_bias,
    down_weight,
    down_bias,
    cotangent,
):
    inputs = tokens[0].astype(jnp.float32)
    count = inputs.shape[0]
    ctx_count = lax.axis_size("ctx")
    length = count * ctx_count
    positions = lax.axis_index("ctx") * count + jnp.arange(count, dtype=jnp.int32)
    starts = doc_starts(doc_lengths[0], positions)
    frequency = 10000.0 ** (-jnp.arange(0, ROT, 2, dtype=jnp.float32) / ROT)
    angles = (positions - starts).astype(jnp.float32)[:, None] * frequency[None, :]
    scale = HEAD ** (-0.5)
    full_qkv, full_out, full_up, full_down = (
        lax.all_gather(qkv_weight, "ctx", axis=1, tiled=True),
        lax.all_gather(out_weight, "ctx", axis=1, tiled=True),
        lax.all_gather(up_weight, "ctx", axis=0, tiled=True),
        lax.all_gather(down_weight, "ctx", axis=1, tiled=True),
    )
    gain_one = ln1_gain.astype(jnp.float32)
    offset_one = ln1_bias.astype(jnp.float32)
    gain_two = ln2_gain.astype(jnp.float32)
    offset_two = ln2_bias.astype(jnp.float32)
    low_one = layer_norm(inputs, gain_one, offset_one).astype(jnp.bfloat16)
    low_two = layer_norm(inputs, gain_two, offset_two).astype(jnp.bfloat16)
    projected = (
        jnp.einsum("nd,cde->cne", low_one, full_qkv, preferred_element_type=jnp.float32)
        + qkv_bias.astype(jnp.float32)[:, None, :]
    )
    width = projected.shape[2]
    local_heads = width // HEAD
    query = rotary(projected[0].reshape(count, local_heads, HEAD), angles).astype(jnp.bfloat16)
    keys_flat = (
        rotary(projected[1].reshape(count, local_heads, HEAD), angles)
        .reshape(count, width)
        .astype(jnp.bfloat16)
    )
    values_flat = projected[2].astype(jnp.bfloat16)
    all_keys, all_values = (
        lax.all_gather(keys_flat, "ctx", axis=0, tiled=True),
        lax.all_gather(values_flat, "ctx", axis=0, tiled=True),
    )
    block = math.gcd(length, 512)
    block_count = length // block
    key_blocks = all_keys.reshape(block_count, block, local_heads, HEAD)
    value_blocks = all_values.reshape(block_count, block, local_heads, HEAD)
    firsts = jnp.arange(block_count, dtype=jnp.int32) * block

    def block_scores(key_block, first):
        key_index = first + jnp.arange(block, dtype=jnp.int32)
        allowed = (key_index[None, :] <= positions[:, None]) & (
            key_index[None, :] >= starts[:, None]
        )
        scores = (
            jnp.einsum("qhe,khe->hqk", query, key_block, preferred_element_type=jnp.float32) * scale
        )
        return (jnp.where(allowed[None], scores, -1e30), allowed[None])

    def statistics(carry, item):
        running, norm_sum = carry
        key_block, first = item
        masked, allowed = block_scores(key_block, first)
        newest = jnp.maximum(running, jnp.max(masked, axis=-1))
        raised = jnp.where(allowed, jnp.exp(masked - newest[..., None]), 0.0)
        norm_sum = norm_sum * jnp.exp(running - newest) + jnp.sum(raised, axis=-1)
        return ((newest, norm_sum), None)

    initial = (
        jnp.full((local_heads, count), -1e30, jnp.float32),
        jnp.zeros((local_heads, count), jnp.float32),
    )
    (running, norm_sum), _ = lax.scan(statistics, initial, (key_blocks, firsts))
    log_norm = running + jnp.log(norm_sum)

    def share_block(key_block, first):
        masked, allowed = block_scores(key_block, first)
        return jnp.where(allowed, jnp.exp(masked - log_norm[..., None]), 0.0)

    def accumulate(mixed, item):
        key_block, value_block, first = item
        shares_low = share_block(key_block, first).astype(jnp.bfloat16)
        return (
            mixed
            + jnp.einsum(
                "hqk,khe->qhe", shares_low, value_block, preferred_element_type=jnp.float32
            ),
            None,
        )

    mixed, _ = lax.scan(
        accumulate,
        jnp.zeros((count, local_heads, HEAD), jnp.float32),
        (key_blocks, value_blocks, firsts),
    )
    mixed_low = mixed.reshape(count, width).astype(jnp.bfloat16)
    attention = jnp.dot(mixed_low, full_out, preferred_element_type=jnp.float32)
    hidden = jnp.dot(low_two, full_up, preferred_element_type=jnp.float32) + up_bias.astype(
        jnp.float32
    )
    activated = jax.nn.gelu(hidden, approximate=False).astype(jnp.bfloat16)
    branches = attention + jnp.dot(activated, full_down, preferred_element_type=jnp.float32)
    joint = lax.psum(branches.astype(jnp.bfloat16), "head").astype(jnp.float32)
    output = inputs + joint + out_bias.astype(jnp.float32) + down_bias.astype(jnp.float32)
    upstream = cotangent[0]
    down_grad = jnp.dot(activated.T, upstream, preferred_element_type=jnp.float32)
    activated_grad = jnp.dot(upstream, full_down.T, preferred_element_type=jnp.float32)
    _, gelu_back = jax.vjp(partial(jax.nn.gelu, approximate=False), hidden)
    hidden_grad = gelu_back(activated_grad)[0].astype(jnp.bfloat16)
    up_grad = jnp.dot(low_two.T, hidden_grad, preferred_element_type=jnp.float32)
    up_bias_grad = jnp.sum(hidden_grad.astype(jnp.float32), axis=0)
    normed_two_grad = jnp.dot(hidden_grad, full_up.T, preferred_element_type=jnp.float32)
    out_grad = jnp.dot(mixed_low.T, upstream, preferred_element_type=jnp.float32)
    mixed_grad = jnp.dot(upstream, full_out.T, preferred_element_type=jnp.float32).astype(
        jnp.bfloat16
    )
    mixed_grad_heads = mixed_grad.reshape(count, local_heads, HEAD)
    delta = jnp.sum(mixed_grad_heads.astype(jnp.float32) * mixed, axis=-1).T

    def backward_block(query_grad, item):
        key_block, value_block, first = item
        shares = share_block(key_block, first)
        share_grad = jnp.einsum(
            "qhe,khe->hqk", mixed_grad_heads, value_block, preferred_element_type=jnp.float32
        )
        score_grad = (shares * (share_grad - delta[..., None])).astype(jnp.bfloat16)
        query_grad = (
            query_grad
            + jnp.einsum("hqk,khe->qhe", score_grad, key_block, preferred_element_type=jnp.float32)
            * scale
        )
        key_grad = (
            jnp.einsum("hqk,qhe->khe", score_grad, query, preferred_element_type=jnp.float32)
            * scale
        )
        value_grad = jnp.einsum(
            "hqk,qhe->khe",
            shares.astype(jnp.bfloat16),
            mixed_grad_heads,
            preferred_element_type=jnp.float32,
        )
        return (
            query_grad,
            jnp.concatenate(
                [key_grad.reshape(block, width), value_grad.reshape(block, width)], axis=1
            ),
        )

    query_grad, key_terms = lax.scan(
        backward_block,
        jnp.zeros((count, local_heads, HEAD), jnp.float32),
        (key_blocks, value_blocks, firsts),
    )
    own_grads = lax.psum_scatter(
        key_terms.reshape(length, 2 * width).astype(jnp.bfloat16),
        "ctx",
        scatter_dimension=0,
        tiled=True,
    ).astype(jnp.float32)
    query_pre = rotary(query_grad, -angles).reshape(count, width)
    key_pre = rotary(own_grads[:, :width].reshape(count, local_heads, HEAD), -angles).reshape(
        count, width
    )
    projected_grad = jnp.stack([query_pre, key_pre, own_grads[:, width:]]).astype(jnp.bfloat16)
    qkv_grad = jnp.einsum(
        "nd,cne->cde", low_one, projected_grad, preferred_element_type=jnp.float32
    )
    qkv_bias_grad = jnp.sum(projected_grad.astype(jnp.float32), axis=1)
    normed_one_grad = jnp.einsum(
        "cne,cde->nd", projected_grad, full_qkv, preferred_element_type=jnp.float32
    )
    normed_one_grad, normed_two_grad = (
        lax.psum(normed_one_grad.astype(jnp.bfloat16), "head").astype(jnp.float32),
        lax.psum(normed_two_grad.astype(jnp.bfloat16), "head").astype(jnp.float32),
    )
    _, norm_back_one = jax.vjp(layer_norm, inputs, gain_one, offset_one)
    input_one, gain_grad_one, offset_grad_one = norm_back_one(normed_one_grad)
    _, norm_back_two = jax.vjp(layer_norm, inputs, gain_two, offset_two)
    input_two, gain_grad_two, offset_grad_two = norm_back_two(normed_two_grad)
    upstream_wide = upstream.astype(jnp.float32)
    input_grad = upstream_wide + input_one + input_two
    bias_grad = jnp.sum(upstream_wide, axis=0)
    small = lax.psum(
        (
            gain_grad_one,
            offset_grad_one,
            qkv_bias_grad,
            bias_grad,
            gain_grad_two,
            offset_grad_two,
            up_bias_grad,
        ),
        ("stream", "ctx"),
    )
    slices = (
        lax.psum_scatter(
            qkv_grad.astype(jnp.bfloat16), "ctx", scatter_dimension=1, tiled=True
        ).astype(jnp.float32),
        lax.psum_scatter(
            out_grad.astype(jnp.bfloat16), "ctx", scatter_dimension=1, tiled=True
        ).astype(jnp.float32),
        lax.psum_scatter(
            up_grad.astype(jnp.bfloat16), "ctx", scatter_dimension=0, tiled=True
        ).astype(jnp.float32),
        lax.psum_scatter(
            down_grad.astype(jnp.bfloat16), "ctx", scatter_dimension=1, tiled=True
        ).astype(jnp.float32),
    )
    shards = (
        lax.psum(slices[0].astype(jnp.bfloat16), "stream").astype(jnp.float32),
        lax.psum(slices[1].astype(jnp.bfloat16), "stream").astype(jnp.float32),
        lax.psum(slices[2].astype(jnp.bfloat16), "stream").astype(jnp.float32),
        lax.psum(slices[3].astype(jnp.bfloat16), "stream").astype(jnp.float32),
    )
    return (
        output.astype(jnp.bfloat16)[None],
        input_grad[None],
        small[0],
        small[1],
        shards[0],
        small[2],
        shards[1],
        small[3],
        small[4],
        small[5],
        shards[2],
        small[6],
        shards[3],
        small[3],
    )


MESH = pl.DeviceIdType.MESH
FRONT_PLAN = (
    "z0", "l0", "z1", "P", "T", "N0", "s0", "L01", "z2", "l1", "z3", "p0", "N1", "f0", "Q0", "Q1", "s1", "L02", "s2", "p1", "L11", "p2", "N2", "Q2", "f1", "F0", "F1", "F2", "s3",
    "L03", "L12", "N3", "Q3", "p3", "F3", "A0", "A1", "A2", "A3", "f2", "B0", "B1", "L13", "f3", "D0", "D1", "B2", "D2", "B3", "D3", "E",
)
F32, BF16 = jnp.float32, jnp.bfloat16


def dot(a, b, over):
    return lax.dot_general(a, b, ((over[0:1], over[1:2]), ((), ())), preferred_element_type=F32)


def span(index, size):
    return pl.ds(pl.multiple_of(index * size, size), size)


def places():
    return lax.axis_index("stream"), lax.axis_index("ctx"), lax.axis_index("head")


def greet(peers):
    barrier = pltpu.get_barrier_semaphore()
    for peer in peers:
        pl.semaphore_signal(barrier, inc=1, device_id=peer, device_id_type=MESH)
    pl.semaphore_wait(barrier, len(peers))


def gather_body(
    x_ref, g_ref, qkv_ref, up_ref, out_ref, down_ref,
    gain_a_ref, off_a_ref, gain_b_ref, off_b_ref, qkv_bias_ref, up_bias_ref, rate_in, docs_ref,
    g_out, unit_out, act_out, dh_out, dqkv_out, mixed_out, qkv_out, up_out, out_out, down_out,
    z_send, z_recv, x_send, x_recv, y_send, y_recv, fx_send, fx_recv, fy_send, fy_recv,
    line_send, line_recv, core_send, core_recv, own_sem, give_sem, block_sem, small_sem,
    x_all, g_all, qkv_all, up_all, out_all, down_all,
    low_one, low_two, unit, query, keys, values, act, dh, dqkv, mixed_low,
    slope, mixed, norm, key_grad, value_grad, turn_ref, start_ref,
    gain_a, off_a, gain_b, off_b, qkv_bias, up_bias, rate_ref, rows_ref, bias_ref,
):
    s, c, h = places()
    x_peer = s + 1 - 2 * lax.rem(s, 2)
    y_peer = lax.rem(s + 2, 4)
    across = ((x_peer, c, h), (y_peer, c, h))
    core_peer = (s, c, 1 - h)
    ring = [(s, lax.rem(c + k, 4), h) for k in (1, 2, 3)]

    count = x_ref.shape[0]
    slab, width, units = up_ref.shape[0], out_ref.shape[0] // 4, down_ref.shape[0] // 4
    quarter, half_count = slab // 4, count // 2

    def rows(base, size):
        return pl.ds(pl.multiple_of(base, size), size)

    def landed(m, r, part, half):
        def cut(total):
            size = total // 4
            if half is None:
                return part * size, size
            return part * size + half * (size // 2), size // 2

        if m == 0:
            at, size = cut(slab)
            return qkv_all.at[:, rows(r * slab + at, size), :]
        if m == 1:
            at, size = cut(slab)
            return up_all.at[rows(r * slab + at, size), :]
        if m == 2:
            at, size = cut(width)
            return out_all.at[rows(at, size), span(r, slab)]
        at, size = cut(units)
        return down_all.at[rows(at, size), span(r, slab)]

    def piece(m, to, part=None):
        if m == 0:
            inner = slice(None) if part is None else span(part, quarter)
            return qkv_ref.at[:, inner, span(to, width)]
        if m == 1:
            inner = slice(None) if part is None else span(part, quarter)
            return up_ref.at[inner, span(to, units)]
        size = width if m == 2 else units
        ref = out_ref if m == 2 else down_ref
        if part is None:
            return ref.at[span(to, size), :]
        return ref.at[rows(to * size + part * (size // 4), size // 4), :]

    def whole_piece(m, r):
        if m == 0:
            return qkv_all.at[:, span(r, slab), :]
        if m == 1:
            return up_all.at[span(r, slab), :]
        return (out_all if m == 2 else down_all).at[:, span(r, slab)]

    def remote(src, dst, send, recv, to):
        return pltpu.make_async_remote_copy(
            src_ref=src, dst_ref=dst, send_sem=send, recv_sem=recv, device_id=to, device_id_type=MESH
        )

    def z_copy(m, k):
        to = lax.rem(c + 4 - k, 4)
        return remote(
            piece(m, to, s), landed(m, c, s, None), z_send.at[m, k - 1], z_recv.at[m, k - 1], (s, to, h)
        )

    def direct(m, k, axis):
        r = lax.rem(c + k, 4)
        send, recv = (x_send, x_recv) if axis == 0 else (y_send, y_recv)
        here = landed(m, r, s, None)
        return remote(here, here, send.at[m, k - 1], recv.at[m, k - 1], across[axis])

    def onward(m, k, axis):
        r = lax.rem(c + k, 4)
        send, recv = (fx_send, fx_recv) if axis == 0 else (fy_send, fy_recv)
        here = landed(m, r, y_peer if axis == 0 else x_peer, 1 if axis == 0 else 0)
        return remote(here, here, send.at[m, k - 1], recv.at[m, k - 1], across[axis])

    lines = ((x_ref, x_all), (g_ref, g_all))

    def block(a, origin):
        return lines[a][1].at[rows(origin * count + h * half_count, half_count), :]

    def line_copy(a, t, side):
        origin = c - t if side == 0 else c + t
        src = lines[a][0].at[span(h, half_count), :] if t == 0 else block(a, origin)
        to = c + 1 if side == 0 else c - 1
        return remote(
            src, block(a, origin), line_send.at[a, side, t], line_recv.at[a, side, t], (s, to, h)
        )

    def core_copy(a, t, side):
        origin = c - t if side == 0 else c + t
        here = block(a, origin)
        return remote(here, here, core_send.at[a, side, t - 1], core_recv.at[a, side, t - 1], core_peer)

    def sends(t, side):
        if side == 0:
            return (c >= t) & (c < 3)
        return (c + t <= 3) & (c > 0)

    def gets(t, side):
        return c >= t if side == 0 else c + t <= 3

    def line_step(a, t):
        for side in (0, 1):
            @pl.when(gets(t, side))
            def _():
                line_copy(a, t - 1, side).wait_recv()
                core_copy(a, t, side).start()

            if t < 3:
                @pl.when(sends(t, side))
                def _():
                    line_copy(a, t, side).start()

    near = (1, 3, 2)
    order = [(m, k) for m in (0, 1, 3, 2) for k in near]

    def start_z(m):
        for k in near:
            z_copy(m, k).start()

    def pass_on(m):
        for k in near:
            direct(m, k, 0).wait_recv()
            onward(m, k, 1).start()
            direct(m, k, 1).wait_recv()
            onward(m, k, 0).start()

    def spread(m):
        for k in near:
            z_copy(m, k).wait_recv()
            direct(m, k, 0).start()
            direct(m, k, 1).start()

    ins = [
        pltpu.make_async_copy(a, b, own_sem.at[i])
        for i, (a, b) in enumerate(
            [(lines[a][0], lines[a][1].at[span(c, count), :]) for a in (0, 1)]
            + [(piece(m, c), whole_piece(m, c)) for m in range(4)]
        )
    ]
    for copy in ins:
        copy.start()
    tile = count
    length, model = x_all.shape
    rot = turn_ref.shape[2]
    span_rot = rot // 4
    scale = width**-0.5

    def finish(m):
        for k in near:
            onward(m, k, 0).wait_recv()
            onward(m, k, 1).wait_recv()
        ins[2 + m].wait()

    def give(i):
        pairs = (
            (qkv_all, qkv_out), (up_all, up_out), (out_all, out_out), (down_all, down_out),
            (act, act_out), (dh, dh_out), (dqkv, dqkv_out), (mixed_low, mixed_out),
        )
        return pltpu.make_async_copy(*pairs[i], give_sem.at[i])

    def give_block(a, origin):
        src, dst = ((unit, unit_out), (g_all, g_out))[a]
        at = span(origin, tile)
        return pltpu.make_async_copy(src.at[at, :], dst.at[at, :], block_sem.at[a])

    def blocks_of(t, do):
        if t == 0:
            do(c)
            return

        @pl.loop(0, 2)
        def _(side):
            origin = c + t * (2 * side - 1)

            @pl.when((origin >= 0) & (origin <= 3))
            def _():
                do(origin)

    def core_wait(a, t):
        for side in (0, 1):
            @pl.when(gets(t, side))
            def _():
                core_copy(a, t, side).wait_recv()

    def norm_block(origin):
        tall = 32

        @pl.loop(0, tile // tall)
        def _(i):
            at = pl.ds(pl.multiple_of(origin * tile + i * tall, tall), tall)
            wide = x_all[at, :].astype(F32)
            centred = wide - jnp.mean(wide, axis=-1, keepdims=True)
            spread_of = jnp.mean(centred * centred, axis=-1, keepdims=True)
            found = centred * lax.rsqrt(spread_of + 1e-05)
            unit[at, :] = found.astype(BF16)
            low_one[at, :] = (found * rows_ref[0:1, :] + rows_ref[1:2, :]).astype(BF16)
            low_two[at, :] = (found * rows_ref[2:3, :] + rows_ref[3:4, :]).astype(BF16)

        give_block(0, origin).start()

    smalls = [
        pltpu.make_async_copy(a, b, small_sem.at[i])
        for i, (a, b) in enumerate(
            (
                (gain_a_ref, gain_a), (off_a_ref, off_a), (gain_b_ref, gain_b), (off_b_ref, off_b),
                (qkv_bias_ref, qkv_bias), (up_bias_ref, up_bias), (rate_in, rate_ref),
            )
        )
    ]
    for copy in smalls:
        copy.start()

    def parameters():
        for copy in smalls:
            copy.wait()
        for i, ref in enumerate((gain_a, off_a, gain_b, off_b)):
            rows_ref[i : i + 1, :] = ref[...].astype(F32).reshape(1, model)
        part = qkv_bias[:, span(c, width)].astype(F32)
        for p in range(3):
            bias_ref[0:1, p * width : (p + 1) * width] = part[p : p + 1]
        bias_ref[1:2, :] = up_bias[span(c, units)].astype(F32).reshape(1, units)

    def tables():
        starts, total = [], docs_ref[0, 0] * 0
        for j in range(docs_ref.shape[1]):
            starts.append(total)
            total = total + docs_ref[0, j]

        @pl.loop(0, length // tile)
        def _(i):
            at = span(i, tile)
            place = i * tile + lax.broadcasted_iota(jnp.int32, (tile, rot), 0)
            lane = lax.broadcasted_iota(jnp.int32, (tile, rot), 1)
            first = jnp.zeros((tile, rot), jnp.int32)
            for start in starts:
                first = jnp.where(start <= place, jnp.maximum(first, start), first)
            start_ref[at, :] = first[:, 0:1]
            angle = (place - first).astype(F32) * rate_ref[0:1, :]
            sine = jnp.sin(angle)
            turn_ref[0, at, :] = jnp.where(lane < 2 * span_rot, jnp.cos(angle), 1.0)
            turn_ref[1, at, :] = jnp.where((lane >= span_rot) & (lane < 2 * span_rot), sine, 0.0)
            turn_ref[2, at, :] = jnp.where(lane < span_rot, -sine, 0.0)

    def turned(v, at, sign):
        near_part = v[:, :rot]
        moved = pltpu.roll(near_part, span_rot, 1) * turn_ref[1, at, :] + pltpu.roll(near_part, rot - span_rot, 1) * turn_ref[2, at, :]
        return jnp.concatenate([near_part * turn_ref[0, at, :] + sign * moved, v[:, rot:]], axis=1)

    def project(i):
        at = span(i, tile)
        for p, into in enumerate((query, keys, values)):
            part = dot(low_one[at, :], qkv_all[p], (1, 0)) + bias_ref[0:1, p * width : (p + 1) * width]
            into[at, :] = (turned(part, at, 1.0) if p < 2 else part).astype(BF16)

    def allowed_of(i, wide):
        first = lax.broadcasted_iota(jnp.int32, (tile, wide), 1)
        place = i * tile + lax.broadcasted_iota(jnp.int32, (tile, wide), 0)
        return (first <= place) & (first >= start_ref[span(i, tile), :])

    def attend(i):
        wide = (i + 1) * tile
        at = slice(i * tile, wide)
        scores = dot(query[at, :], keys[0:wide, :], (1, 1)) * scale
        allowed = allowed_of(i, wide)
        masked = jnp.where(allowed, scores, -1e30)
        peak = jnp.max(masked, axis=-1, keepdims=True)
        raised = jnp.where(allowed, jnp.exp(masked - peak), 0.0)
        total = jnp.sum(raised, axis=-1, keepdims=True)
        norm[at, :] = peak + jnp.log(total)
        found = dot((raised / total).astype(BF16), values[0:wide, :], (1, 0))
        mixed[at, :] = found
        mixed_low[at, :] = found.astype(BF16)

    def feed(i):
        at = span(i, tile)
        for j in range(units // 256):
            cols = slice(j * 256, (j + 1) * 256)
            hidden = dot(low_two[at, :], up_all[:, cols], (1, 0)) + bias_ref[1:2, cols]
            share = 0.5 + 0.5 * lax.erf(hidden * (0.5**0.5))
            act[at, cols] = (hidden * share).astype(BF16)
            slope[at, cols] = share + hidden * jnp.exp(-0.5 * hidden * hidden) * ((0.5 / jnp.pi) ** 0.5)

    def back_attend(origin):
        at = span(origin, tile)
        grad = dot(g_all[at, :], out_all[...], (1, 1)).astype(BF16)
        scores = dot(query[at, :], keys[...], (1, 1)) * scale
        shares = jnp.where(allowed_of(origin, length), jnp.exp(scores - norm[at, :]), 0.0)
        delta = jnp.sum(grad.astype(F32) * mixed[at, :], axis=-1, keepdims=True)
        share_grad = dot(grad, values[...], (1, 1))
        score_grad = (shares * (share_grad - delta)).astype(BF16)
        value_grad[...] += dot(shares.astype(BF16), grad, (0, 0))
        key_grad[...] += dot(score_grad, query[at, :], (0, 0))
        part = dot(score_grad, keys[...], (1, 0)) * scale
        dqkv[at, 0:width] = turned(part, at, -1.0).astype(BF16)

    def back_feed(origin):
        at = span(origin, tile)
        for j in range(units // 256):
            cols = slice(j * 256, (j + 1) * 256)
            part = dot(g_all[at, :], down_all[cols, :], (1, 1))
            dh[at, cols] = (part * slope[at, cols]).astype(BF16)

    def start_line(a):
        for side in (0, 1):
            @pl.when(sends(0, side))
            def _():
                line_copy(a, 0, side).start()

    def close():
        @pl.loop(0, length // tile)
        def _(i):
            at = span(i, tile)
            dqkv[at, width : 2 * width] = turned(key_grad[at, :] * scale, at, -1.0).astype(BF16)
            dqkv[at, 2 * width : 3 * width] = value_grad[at, :].astype(BF16)

        give(5).start()
        give(6).start()

    def run(step):
        op, rest = step[0], [int(d) for d in step[1:]]
        if op == "z":
            start_z(*rest)
        elif op == "s":
            spread(*rest)
        elif op == "p":
            pass_on(*rest)
        elif op == "f":
            finish(*rest)
            give(*rest).start()
        elif op == "l":
            start_line(*rest)
        elif op == "L":
            line_step(*rest)
        elif op == "N":
            if rest[0]:
                core_wait(0, *rest)
            else:
                ins[0].wait()
            blocks_of(*rest, norm_block)
        elif op == "P":
            parameters()
        elif op == "T":
            tables()
        elif op == "Q":
            blocks_of(*rest, project)
        elif op == "A":
            attend(*rest)
            if rest[0] == 3:
                give(7).start()
        elif op == "F":
            blocks_of(*rest, feed)
            if rest[0] == 3:
                give(4).start()
        elif op == "B":
            if rest[0]:
                core_wait(1, *rest)
            else:
                ins[1].wait()
            blocks_of(*rest, back_attend)
        elif op == "D":
            blocks_of(*rest, back_feed)
        elif op == "E":
            close()

    greet([*across, core_peer, *ring])
    key_grad[...] = jnp.zeros_like(key_grad)
    value_grad[...] = jnp.zeros_like(value_grad)
    for step in FRONT_PLAN:
        run(step)
    for t in (0, 1, 2, 3):
        blocks_of(t, lambda origin: give_block(1, origin).start())
    for a in (0, 1):
        for side in (0, 1):
            for t in (1, 2, 3):
                @pl.when(gets(t, side))
                def _():
                    core_copy(a, t, side).wait_send()
                @pl.when(sends(t - 1, side))
                def _():
                    line_copy(a, t - 1, side).wait_send()
    for m, k in order:
        z_copy(m, k).wait_send()
        for axis in (0, 1):
            direct(m, k, axis).wait_send()
            onward(m, k, axis).wait_send()
    pltpu.make_async_copy(unit, unit_out, block_sem.at[0]).wait()
    pltpu.make_async_copy(g_all, g_out, block_sem.at[1]).wait()
    for i in range(8):
        give(i).wait()


def gather_all(tokens, cotangent, w_qkv, w_up, w_out, w_down, gain_a, off_a, gain_b, off_b, b_qkv, b_up, docs):
    count, model = tokens.shape
    length = 4 * count
    width, units = w_out.shape[0] // 4, w_down.shape[0] // 4
    frequency = 10000.0 ** (-np.arange(0, ROT, 2, dtype=np.float32) / np.float32(ROT))
    rate = jnp.asarray(np.tile(frequency.astype(np.float32), (8, 4)))
    dma = pltpu.SemaphoreType.DMA
    weights = [(3, model, width), (model, units), (width, model), (units, model)]
    wide, narrow = (length, model), (length, width)
    results = [wide, wide, (length, units), (length, units), (length, 3 * width), narrow] + weights
    scratch = [dma((4, 3))] * 10 + [dma((2, 2, 3))] * 4 + [dma((6,)), dma((8,)), dma((2,)), dma((7,))]
    scratch += [
        pltpu.VMEM(v, BF16)
        for v in [wide, wide] + weights + [wide] * 3 + [narrow] * 3
        + [(length, units)] * 2 + [(length, 3 * width), narrow]
    ]
    scratch += [pltpu.VMEM(v, F32) for v in ((length, units), narrow, (length, 1), narrow, narrow)]
    scratch += [pltpu.VMEM((3, length, rate.shape[1]), F32), pltpu.VMEM((length, 1), jnp.int32)]
    scratch += [pltpu.VMEM((model,), BF16)] * 4 + [pltpu.VMEM(b_qkv.shape, BF16), pltpu.VMEM(b_up.shape, BF16)]
    scratch += [pltpu.VMEM(v, F32) for v in (rate.shape, (8, model), (8, units))]
    any_space = pl.BlockSpec(memory_space=pl.ANY)
    return pl.pallas_call(
        gather_body,
        out_shape=[jax.ShapeDtypeStruct(v, BF16) for v in results],
        in_specs=[any_space] * 13 + [pl.BlockSpec(memory_space=pltpu.SMEM)],
        out_specs=[any_space] * 10,
        scratch_shapes=scratch,
        compiler_params=pltpu.CompilerParams(
            collective_id=0, has_side_effects=True, vmem_limit_bytes=63 << 20
        ),
        name="gather",
    )(
        tokens, cotangent, w_qkv, w_up, w_out, w_down, gain_a, off_a, gain_b, off_b, b_qkv, b_up, rate, docs
    )


LEADS = (4, 4, 4, 4, 1, 1)
BACK_PLAN = (
    "O", "14", "D", "B0", "24", "B1", "R0", "P", "Q", "12", "25", "Z4", "I0", "22", "11", "U", "13", "10", "I1", "Z5", "X4", "20", "23", "21", "a", "Z0", "Z2", "b", "X5", "X0", "S0", "N4",
    "Z3", "Z1", "N5", "X3", "X2", "c", "R1", "X1", "N3", "N1", "d", "N0", "N2", "e", "S1",
)
def settle_body(
    act_in, up_in, unit_in, dh_in, dqkv_in, mixed_in, wq_in, wu_in, wo_in, wd_in,
    gain_a_ref, off_a_ref, gain_b_ref, off_b_ref,
    joint, inward, o0, o1, o2, o3, small_out,
    s1x_send, s1x_recv, s1y_send, s1y_recv, s2x_send, s2x_recv, s2y_send, s2y_recv,
    x_send, x_recv, y_send, y_recv, fx_send, fx_recv, fy_send, fy_recv,
    z_send, z_recv, keep_sem, load_sem, weight_sem,
    core_send, core_recv, row_send, row_recv, back_send, back_recv, back_sem,
    sum_send, sum_recv, sum_sem, small_sem,
    act, up, unit, dh, dqkv, mixed, w_wide, w_out, w_qkv, *rest,
):
    grads, first, second = rest[0:6], (rest[6:18:2], rest[7:18:2]), (rest[18:30:2], rest[19:30:2])
    (
        own_half, core_half, send_half, row_parts, done_half,
        sums, sums_core, slots, total_own, total_x, total_y,
        gain_a, off_a, gain_b, off_b, rows_ref, low_ref,
    ) = rest[30:]
    s, c, h = places()
    x_at, y_at = lax.rem(s, 2), lax.div(s, 2)
    x_off, y_off = 1 - x_at, 1 - y_at
    x_peer, y_peer = y_at * 2 + x_off, y_off * 2 + x_at
    across = ((x_peer, c, h), (y_peer, c, h))
    core_peer = (s, c, 1 - h)
    near = (1, 3, 2)
    outs = (o0, o1, o2, o3)
    first, second = list(zip(*first)), list(zip(*second))
    slab = o2.shape[-1]
    length, model = up.shape
    units, width = act.shape[1], mixed.shape[1]
    half_cols = model // 2
    count = joint.shape[0]
    tile = 256

    def remote(src, dst, send, recv, to):
        return pltpu.make_async_remote_copy(
            src_ref=src, dst_ref=dst, send_sem=send, recv_sem=recv, device_id=to, device_id_type=MESH
        )

    loads = [
        pltpu.make_async_copy(a, b, load_sem.at[i])
        for i, (a, b) in enumerate(
            ((act_in, act), (up_in, up), (dh_in, dh), (unit_in, unit), (dqkv_in, dqkv), (mixed_in, mixed))
        )
    ]
    for load in loads[:2]:
        load.start()
    greet([*across, core_peer, *[(s, lax.rem(c + k, 4), h) for k in near]])

    smalls = [
        pltpu.make_async_copy(a, b, small_sem.at[i])
        for i, (a, b) in enumerate(
            ((gain_a_ref, gain_a), (off_a_ref, off_a), (gain_b_ref, gain_b), (off_b_ref, off_b))
        )
    ]
    for copy in smalls:
        copy.start()

    def side(which):
        return 1 - h if which == 0 else h

    def weight_load(i):
        at = span(side(i % 2), half_cols)
        if i < 2:
            return pltpu.make_async_copy(wd_in.at[:, at], w_wide.at[i], weight_sem.at[i])
        if i < 4:
            return pltpu.make_async_copy(wu_in.at[at, :], w_wide.at[i % 2], weight_sem.at[i])
        if i < 6:
            return pltpu.make_async_copy(wo_in.at[:, at], w_out.at[i % 2], weight_sem.at[i])
        return pltpu.make_async_copy(wq_in.at[:, at, :], w_qkv.at[i % 2], weight_sem.at[i])

    for load in loads[2:]:
        load.start()
    for i in (0, 4, 1, 5, 6, 7):
        weight_load(i).start()

    def one(m, half):
        src = grads[m].at[:, :, x_off, 0] if half == 0 else grads[m].at[:, y_off, :, 1]
        send, recv = (s1x_send, s1x_recv) if half == 0 else (s1y_send, s1y_recv)
        return remote(src, first[m][half], send.at[m], recv.at[m], across[half])

    def two(m, half):
        src = first[m][half].at[:, y_off if half == 0 else x_off]
        send, recv = (s2y_send, s2y_recv) if half == 0 else (s2x_send, s2x_recv)
        return remote(src, second[m][half], send.at[m], recv.at[m], across[1 - half])

    def add_first(m, half):
        into, more = first[m][half], grads[m]
        lead, _, height, _ = into.shape
        tall = min(height, 32)

        @pl.loop(0, lead * 2 * (height // tall))
        def _(i):
            at = lax.rem(i, height // tall)
            pair = lax.div(i, height // tall)
            l, j, rows = lax.div(pair, 2), lax.rem(pair, 2), span(at, tall)
            term = more[l, j, x_at, 0, rows, :] if half == 0 else more[l, y_at, j, 1, rows, :]
            into[l, j, rows, :] = (into[l, j, rows, :].astype(F32) + term.astype(F32)).astype(BF16)

    def add_second(m, half):
        into, more = second[m][half], first[m][half]
        mine = y_at if half == 0 else x_at
        lead, height, _ = into.shape
        tall = min(height, 32)

        @pl.loop(0, lead * (height // tall))
        def _(i):
            l, rows = lax.div(i, height // tall), span(lax.rem(i, height // tall), tall)
            term = more[l, mine, rows, :].astype(F32)
            into[l, rows, :] = (into[l, rows, :].astype(F32) + term).astype(BF16)

    def share_of(m, half, to):
        ref = second[m][half]
        return ref.at[to] if m < 4 else ref.at[0, :, span(to, slab)]

    def home(m, half):
        if m < 3:
            return outs[0].at[m, s, half, :, span(c, width)]
        if m == 3:
            return outs[1].at[s, half, :, span(c, units)]
        return outs[m - 2].at[c, s, half]

    def z_copy(m, half, k):
        to = lax.rem(c + 4 - k, 4)
        i = (m * 2 + half) * 3 + k - 1
        return remote(share_of(m, half, to), home(m, half), z_send.at[i], z_recv.at[i], (s, to, h))

    def keep(m, half):
        return pltpu.make_async_copy(share_of(m, half, c), home(m, half), keep_sem.at[m, half])

    def quarter(m, q, half=None):
        at = (q,) if half is None else (q, half)
        if m < 3:
            return outs[0].at[(m, *at)]
        if m == 3:
            return outs[1].at[at]
        return outs[m - 2].at[(slice(None), *at)]

    def direct(m, axis):
        send, recv = (x_send, x_recv) if axis == 0 else (y_send, y_recv)
        here = quarter(m, s)
        return remote(here, here, send.at[m], recv.at[m], across[axis])

    def onward(m, axis):
        send, recv = (fx_send, fx_recv) if axis == 0 else (fy_send, fy_recv)
        here = quarter(m, y_peer if axis == 0 else x_peer, 1 - axis)
        return remote(here, here, send.at[m], recv.at[m], across[axis])

    finals = (joint, inward)

    def core_copy(a):
        return remote(send_half, core_half.at[a], core_send.at[a], core_recv.at[a], core_peer)

    def row_copy(a, k):
        to = lax.rem(c + 4 - k, 4)
        return remote(
            own_half.at[a, span(to, count)], row_parts.at[a, k - 1],
            row_send.at[a, k - 1], row_recv.at[a, k - 1], (s, to, h),
        )

    def back_copy(a):
        return remote(
            done_half.at[a], finals[a].at[:, span(h, half_cols)], back_send.at[a], back_recv.at[a], core_peer
        )

    def back_keep(a):
        return pltpu.make_async_copy(done_half.at[a], finals[a].at[:, span(h, half_cols)], back_sem.at[a])

    def line_start(a):
        core_copy(a).wait_recv()
        tall = 32

        @pl.loop(0, length // tall)
        def _(i):
            rows = span(i, tall)
            own_half[a, rows, :] = (
                own_half[a, rows, :].astype(F32) + core_half[a, rows, :].astype(F32)
            ).astype(BF16)

        for k in near:
            row_copy(a, k).start()

    def line_sum(a):
        for k in near:
            row_copy(a, k).wait_recv()
        tall = 32

        @pl.loop(0, count // tall)
        def _(i):
            rows = span(i, tall)
            total = own_half[a, pl.ds(pl.multiple_of(c * count + i * tall, tall), tall), :].astype(F32)
            for k in range(3):
                total = total + row_parts[a, k, rows, :].astype(F32)
            done_half[a, rows, :] = total.astype(BF16)

        back_copy(a).start()
        back_keep(a).start()

    def down_grad():
        rows = units // 8

        def part_of(y, x):
            left = act[:, span(2 * y + x, 2 * rows)]
            for j in range(model // 512):
                cols = slice(j * 512, (j + 1) * 512)
                part = dot(left, up[:, cols], (0, 0)).astype(BF16)
                for half in (0, 1):
                    grads[5][0, y, x, half, :, cols] = part[half * rows : (half + 1) * rows]

        part_of(y_off, x_off)
        part_of(y_at, x_off)
        one(5, 0).start()
        part_of(y_off, x_at)
        one(5, 1).start()
        part_of(y_at, x_at)

    def out_grad():
        rows = width // 8
        for j in range(model // 512):
            part = dot(mixed[...], up[:, j * 512 : (j + 1) * 512], (0, 0)).astype(BF16)
            for i in range(8):
                grads[4][0, i // 4, (i // 2) % 2, i % 2, :, j * 512 : (j + 1) * 512] = part[i * rows : (i + 1) * rows]

    same = lax.broadcasted_iota(jnp.int32, (tile, tile), 0) == lax.broadcasted_iota(jnp.int32, (tile, tile), 1)
    eye = jnp.where(same, 1.0, 0.0).astype(BF16)

    def columns(t):
        return dot(eye, low_ref[:, span(t, tile)], (1, 1))

    def scaled(part, column, at, column_sum):
        return (part * column[:, at : at + 1] + column[:, at + 1 : at + 2] * column_sum).astype(BF16)

    def column_sum(ref, cols):
        total = jnp.zeros((1, cols.stop - cols.start), F32)
        for i in range(length // tile):
            total = total + jnp.sum(ref[i * tile : (i + 1) * tile, cols].astype(F32), axis=0, keepdims=True)
        return total

    def up_grad():
        rows = tile // 4

        @pl.loop(0, model // tile)
        def _(t):
            left, column = unit[:, span(t, tile)], columns(t)
            for j in range(units // 512):
                cols = slice(j * 512, (j + 1) * 512)
                near_sum = sums[5:6, 3 * width + j * 512 : 3 * width + (j + 1) * 512]
                part = scaled(dot(left, dh[:, cols], (0, 0)), column, 2, near_sum)
                for i in range(4):
                    grads[3][lax.div(t, 2), lax.rem(t, 2), i // 2, i % 2, :, cols] = part[i * rows : (i + 1) * rows]

    def qkv_grad():
        rows = tile // 4

        @pl.loop(0, model // tile)
        def _(t):
            left, column = unit[:, span(t, tile)], columns(t)
            for p in range(3):
                cols = slice(p * width, (p + 1) * width)
                part = scaled(dot(left, dqkv[:, cols], (0, 0)), column, 0, sums[5:6, cols])
                for i in range(4):
                    grads[p][lax.div(t, 2), lax.rem(t, 2), i // 2, i % 2] = part[i * rows : (i + 1) * rows]

    def branches(which):
        into = send_half if which == 0 else own_half.at[0]

        @pl.loop(0, length // tile)
        def _(i):
            rows = span(i, tile)
            for j in range(half_cols // 512):
                cols = slice(j * 512, (j + 1) * 512)
                part = dot(mixed[rows, :], w_out[which, :, cols], (1, 0))
                part = part + dot(act[rows, :], w_wide[which, :, cols], (1, 0))
                into[rows, cols] = part.astype(BF16)

    def inwards(which):
        into = send_half if which == 0 else own_half.at[1]
        base = side(which) * half_cols
        for j in range(half_cols // 512):
            cols = slice(j * 512, (j + 1) * 512)
            far = span(side(which) * (half_cols // 512) + j, 512)
            zero = jnp.zeros((8, 512), F32)

            def step(i, carry):
                rows = span(i, tile)
                one_part = dot(dqkv[rows, 0:width], w_qkv[which, 0, cols, :], (1, 1))
                for p in (1, 2):
                    one_part = one_part + dot(
                        dqkv[rows, p * width : (p + 1) * width], w_qkv[which, p, cols, :], (1, 1)
                    )
                two_part = dot(dh[rows, :], w_wide[which, cols, :], (1, 1))
                into[rows, cols] = (one_part * rows_ref[0:1, far] + two_part * rows_ref[2:3, far]).astype(BF16)
                place = unit[rows, far].astype(F32)

                def fold(v):
                    return jnp.sum(v.reshape(tile // 8, 8, 512), axis=0)

                return (
                    carry[0] + fold(one_part * place),
                    carry[1] + fold(one_part),
                    carry[2] + fold(two_part * place),
                    carry[3] + fold(two_part),
                )

            found = lax.fori_loop(0, length // tile, step, (zero, zero, zero, zero))
            for n in range(4):
                sums[n : n + 1, far] = jnp.sum(found[n], axis=0, keepdims=True)

    def sum_core():
        return remote(sums, sums_core, sum_send.at[0], sum_recv.at[0], core_peer)

    def sum_line(k):
        return remote(
            sums, slots.at[c], sum_send.at[k], sum_recv.at[k], (s, lax.rem(c + 4 - k, 4), h)
        )

    def sum_x():
        return remote(total_own, total_x, sum_send.at[4], sum_recv.at[4], across[0])

    def sum_y():
        return remote(total_own, total_y, sum_send.at[5], sum_recv.at[5], across[1])

    kinds = range(6)
    loaded = set()

    def need(*which):
        for i in which:
            if i not in loaded:
                loads[i].wait()
                loaded.add(i)

    def parameters():
        for copy in smalls:
            copy.wait()
        rows_ref[...] = jnp.zeros_like(rows_ref)
        for i, ref in enumerate((gain_a, off_a, gain_b, off_b)):
            rows_ref[i : i + 1, :] = ref[...].astype(F32).reshape(1, model)
        low_ref[...] = rows_ref[...].astype(BF16)

    def compute_sums():
        sums[4:5, :] = jnp.sum(up[span(c, count), :].astype(F32), axis=0, keepdims=True) * 0.5
        sums[5:8, :] = jnp.zeros((3, model), F32)

    def small_copy():
        return pltpu.make_async_copy(total_own, small_out, sum_sem.at[0])

    def stage_two(m):
        for half in (0, 1):
            one(m, half).wait_recv()
            add_first(m, half)
            two(m, half).start()

    def stage_z(m):
        for half in (0, 1):
            two(m, half).wait_recv()
            add_second(m, half)
            for k in near:
                z_copy(m, half, k).start()
            keep(m, half).start()

    def stage_out(m):
        for half in (0, 1):
            for k in near:
                z_copy(m, half, k).wait_recv()
            keep(m, half).wait()
        for axis in (0, 1):
            direct(m, axis).start()

    def stage_on(m):
        direct(m, 0).wait_recv()
        onward(m, 1).start()
        direct(m, 1).wait_recv()
        onward(m, 0).start()

    def run(step):
        op, m = step[0], int(step[1]) if len(step) > 1 else None
        if op == "D":
            need(0, 1)
            down_grad()
        elif op == "P":
            need(1)
            parameters()
            compute_sums()
        elif op == "U":
            need(1, 2, 3)
            for j in range(units // 512):
                cols = slice(j * 512, (j + 1) * 512)
                sums[5:6, 3 * width + cols.start : 3 * width + cols.stop] = column_sum(dh, cols)
            up_grad()
        elif op == "Q":
            need(3, 4)
            for p in range(3):
                cols = slice(p * width, (p + 1) * width)
                sums[5:6, cols] = column_sum(dqkv, cols)
            qkv_grad()
        elif op == "O":
            need(1, 5)
            out_grad()
        elif op == "1":
            one(m, 0).start()
            one(m, 1).start()
        elif op == "B":
            need(0, 5)
            weight_load(m).wait()
            weight_load(4 + m).wait()
            branches(m)
            weight_load(2 + m).start()
            if m == 0:
                core_copy(0).start()
        elif op == "I":
            need(2, 3, 4)
            if m == 0:
                core_copy(0).wait_send()
            weight_load(2 + m).wait()
            weight_load(6 + m).wait()
            inwards(m)
            if m == 0:
                core_copy(1).start()
        elif op == "2":
            stage_two(m)
        elif op == "Z":
            stage_z(m)
        elif op == "X":
            stage_out(m)
        elif op == "N":
            stage_on(m)
        elif op == "R":
            line_start(m)
        elif op == "S":
            line_sum(m)
        elif op == "a":
            sum_core().start()
        elif op == "b":
            sum_core().wait()
            sums[0:5, :] = sums[0:5, :] + sums_core[0:5, :]
            for k in near:
                sum_line(k).start()
            slots[c] = sums[...]
        elif op == "c":
            for k in near:
                sum_line(k).wait()
            total_own[0:8, :] = slots[0] + slots[1] + slots[2] + slots[3]
            for i in range(4):
                total_own[8 + i : 9 + i, :] = slots[i, 5:6, :]
            total_own[12:16, :] = jnp.zeros((4, model), F32)
            sum_x().start()
        elif op == "d":
            sum_x().wait()
            total_own[...] = total_own[...] + total_x[...]
            sum_y().start()
        elif op == "e":
            sum_y().wait()
            total_own[...] = total_own[...] + total_y[...]
            small_copy().start()

    for step in BACK_PLAN:
        run(step)
    for m in kinds:
        for axis in (0, 1):
            onward(m, axis).wait_recv()
    small_copy().wait()
    for a in (0, 1):
        back_copy(a).wait()
        back_keep(a).wait()
        for k in near:
            row_copy(a, k).wait_send()
    core_copy(1).wait_send()
    for m in kinds:
        for half in (0, 1):
            one(m, half).wait_send()
            two(m, half).wait_send()
            for k in near:
                z_copy(m, half, k).wait_send()
        for axis in (0, 1):
            direct(m, axis).wait_send()
            onward(m, axis).wait_send()


def settle_all(act, up, unit, dh, dqkv, mixed, w_qkv, w_up, w_out, w_down, gain_a, off_a, gain_b, off_b):
    length, model = up.shape
    units, width = act.shape[1], mixed.shape[1]
    slab, count, half = model // 4, length // 4, model // 2
    dma = pltpu.SemaphoreType.DMA
    heights = (*[slab // 8] * 4, width // 8, units // 8)
    widths = (width, width, width, units, model, model)
    out_shapes = [
        (count, model), (count, model),
        (3, 4, 2, heights[0], 4 * width), (4, 2, heights[3], 4 * units),
        (4, 4, 2, heights[4], slab), (4, 4, 2, heights[5], slab),
    ]
    scratch = [dma((6,))] * 16 + [dma((36,))] * 2 + [dma((6, 2)), dma((6,)), dma((8,))]
    scratch += [dma((2,)), dma((2,)), dma((2, 3)), dma((2, 3)), dma((2,)), dma((2,)), dma((2,))]
    scratch += [dma((6,)), dma((6,)), dma((1,)), dma((4,))]
    vmem = [(length, units), (length, model), (length, model), (length, units), (length, 3 * width), (length, width)]
    vmem += [(2, units, half), (2, width, half), (2, 3, half, width)]
    shapes = list(zip(LEADS, heights, widths))
    vmem += [(l, 2, 2, 2, r, k) for l, r, k in shapes]
    vmem += [(l, 2, r, k) for l, r, k in shapes for _ in (0, 1)]
    vmem += [(l, r, k) for l, r, k in shapes for _ in (0, 1)]
    vmem += [(2, length, half), (2, length, half), (length, half), (2, 3, count, half), (2, count, half)]
    scratch += [pltpu.VMEM(v, BF16) for v in vmem]
    scratch += [pltpu.VMEM(v, F32) for v in ((8, model), (8, model), (4, 8, model), (16, model), (16, model), (16, model))]
    scratch += [pltpu.VMEM((model,), BF16)] * 4 + [pltpu.VMEM((8, model), F32), pltpu.VMEM((8, model), BF16)]
    any_space = pl.BlockSpec(memory_space=pl.ANY)
    joint, inward, q, u, o, d, small = pl.pallas_call(
        settle_body,
        out_shape=[jax.ShapeDtypeStruct(v, BF16) for v in out_shapes] + [jax.ShapeDtypeStruct((16, model), F32)],
        in_specs=[any_space] * 14,
        out_specs=[any_space] * 7,
        scratch_shapes=scratch,
        compiler_params=pltpu.CompilerParams(
            collective_id=1, has_side_effects=True, vmem_limit_bytes=63 << 20
        ),
        name="settle",
    )(act, up, unit, dh, dqkv, mixed, w_qkv, w_up, w_out, w_down, gain_a, off_a, gain_b, off_b)
    return (
        joint, inward, q.reshape(3, slab, 4 * width), u.reshape(slab, 4 * units),
        o.reshape(4 * width, slab), d.reshape(4 * units, slab), small,
    )


def finish_body(
    q_ref, u_ref, o_ref, d_ref, joint_ref, inward_ref, own_ref, up_ref,
    small_ref, bias_a, bias_b,
    q_out, u_out, o_out, d_out, y_out, g_out, v0, v1, v2, v3, v4, v5, qb_out, ub_out,
):
    q_out[...] = q_ref[...].astype(F32)
    u_out[...] = u_ref[...].astype(F32)
    o_out[...] = o_ref[...].astype(F32)
    d_out[...] = d_ref[...].astype(F32)
    wide = own_ref[...].astype(F32)
    bias = (bias_a[...].astype(F32) + bias_b[...].astype(F32)).reshape(1, wide.shape[1])
    y_out[...] = (wide + joint_ref[...].astype(F32) + bias).astype(BF16)
    centred = wide - jnp.mean(wide, axis=-1, keepdims=True)
    scale = lax.rsqrt(jnp.mean(centred * centred, axis=-1, keepdims=True) + 1e-05)
    unit = centred * scale
    inward = inward_ref[...].astype(F32)
    inward = inward - jnp.mean(inward, axis=-1, keepdims=True) - unit * jnp.mean(inward * unit, axis=-1, keepdims=True)
    g_out[...] = up_ref[...].astype(F32) + scale * inward

    @pl.when(pl.program_id(0) == 0)
    def _():
        for i, out in zip((0, 1, 4, 2, 3, 4), (v0, v1, v2, v3, v4, v5)):
            out[...] = small_ref[i : i + 1, :].reshape(out.shape)
        width, units = qb_out.shape[1] // 4, ub_out.shape[0] // 4
        for i in range(4):
            row = small_ref[8 + i : 9 + i, :]
            for p in range(3):
                qb_out[p : p + 1, i * width : (i + 1) * width] = row[:, p * width : (p + 1) * width]
            ub_out[i * units : (i + 1) * units] = row[:, 3 * width : 3 * width + units].reshape(units)


def finish_all(q, u, o, d, joint, inward, own, upstream, small, bias_a, bias_b):
    steps = 8
    arrays = [q, u, o, d, joint, inward, own, upstream]

    def spec(a):
        return pl.BlockSpec((a.shape[0] // steps, a.shape[1]), lambda i: (i, 0))

    results = [(a.shape, F32) for a in (q, u, o, d)] + [(own.shape, BF16), (own.shape, F32)]
    smalls = [(own.shape[1:], F32)] * 6 + [((3, q.shape[1]), F32), (u.shape[1:], F32)]
    results += smalls

    def whole(shape):
        return pl.BlockSpec(shape, lambda i: (0,) * len(shape))

    return pl.pallas_call(
        finish_body,
        grid=(steps,),
        out_shape=[jax.ShapeDtypeStruct(v, t) for v, t in results],
        in_specs=[spec(a) for a in arrays] + [whole(v.shape) for v in (small, bias_a, bias_b)],
        out_specs=[spec(a) for a in (q, u, o, d, own, own)] + [whole(v) for v, _ in smalls],
        compiler_params=pltpu.CompilerParams(vmem_limit_bytes=63 << 20),
        name="finish",
    )(*arrays, small, bias_a, bias_b)


def per_device(
    tokens,
    doc_lengths,
    ln1_gain,
    ln1_bias,
    qkv_weight,
    qkv_bias,
    out_weight,
    out_bias,
    ln2_gain,
    ln2_bias,
    up_weight,
    up_bias,
    down_weight,
    down_bias,
    cotangent,
):
    upstream, unit, activated, hidden_grad, projected_grad, mixed_low, w_qkv, w_up, w_out, w_down = (
        gather_all(
            tokens[0],
            cotangent[0],
            qkv_weight,
            up_weight,
            out_weight,
            down_weight,
            ln1_gain,
            ln1_bias,
            ln2_gain,
            ln2_bias,
            qkv_bias,
            up_bias,
            doc_lengths,
        )
    )

    joint, inward, qkv_out, up_out, out_out, down_out, small = settle_all(
        activated,
        upstream,
        unit,
        hidden_grad,
        projected_grad,
        mixed_low,
        w_qkv,
        w_up,
        w_out,
        w_down,
        ln1_gain,
        ln1_bias,
        ln2_gain,
        ln2_bias,
    )
    q_grad, u_grad, o_grad, d_grad, output, input_grad, *rest = finish_all(
        qkv_out.reshape(-1, qkv_out.shape[-1]),
        up_out,
        out_out,
        down_out,
        joint,
        inward,
        tokens[0],
        cotangent[0],
        small,
        out_bias,
        down_bias,
    )
    return (
        output[None],
        input_grad[None],
        rest[0],
        rest[1],
        q_grad.reshape(qkv_out.shape),
        rest[6],
        o_grad,
        rest[2],
        rest[3],
        rest[4],
        u_grad,
        rest[7],
        d_grad,
        rest[5],
    )


def solution(mesh):
    in_specs = (
        P("stream", "ctx", None),
        P("stream", None),
        P(),
        P(),
        P(None, "ctx", "head"),
        P(None, "head"),
        P("head", "ctx"),
        P(),
        P(),
        P(),
        P("ctx", "head"),
        P("head"),
        P("head", "ctx"),
        P(),
        P("stream", "ctx", None),
    )
    out_specs = (
        P("stream", "ctx", None),
        P("stream", "ctx", None),
        P(),
        P(),
        P(None, "ctx", "head"),
        P(None, "head"),
        P("head", "ctx"),
        P(),
        P(),
        P(),
        P("ctx", "head"),
        P("head"),
        P("head", "ctx"),
        P(),
    )
    split = mesh.shape["ctx"] * mesh.shape["head"]

    def whole(*arrays):
        heads, units = arrays[4].shape[2] // HEAD, arrays[10].shape[1]
        grouped = (mesh.shape["stream"], mesh.shape["ctx"], mesh.shape["head"]) == (4, 4, 2)
        fits = grouped and heads == split and units % (split * 512) == 0
        return jax.shard_map(
            per_device if fits else general_device,
            mesh=mesh,
            in_specs=in_specs,
            out_specs=out_specs,
            check_vma=False,
        )(*arrays)

    return whole
```

```python
from functools import partial
import math

import jax
import jax.numpy as jnp
import numpy as np
from jax import lax
from jax.experimental import pallas as pl
from jax.experimental.pallas import tpu as pltpu
from jax.sharding import PartitionSpec as P

HEAD = 256
ROT = 64


def layer_norm(values, gain, offset):
    centre = jnp.mean(values, axis=-1, keepdims=True)
    centred = values - centre
    spread = jnp.mean(centred * centred, axis=-1, keepdims=True)
    return centred * lax.rsqrt(spread + 1e-05) * gain + offset


def rotary(values, angles):
    half = angles.shape[-1]
    cosine = jnp.cos(angles)[:, None, :]
    sine = jnp.sin(angles)[:, None, :]
    first = values[..., :half]
    second = values[..., half : 2 * half]
    return jnp.concatenate(
        [first * cosine - second * sine, second * cosine + first * sine, values[..., 2 * half :]],
        axis=-1,
    )


def doc_starts(doc_sizes, positions):
    place = jnp.arange(doc_sizes.shape[0])
    before = place[None, :] < place[:, None]
    starts = jnp.sum(jnp.where(before, doc_sizes[None, :], 0), axis=1)
    return jnp.max(jnp.where(starts[None, :] <= positions[:, None], starts[None, :], 0), axis=1)


def general_device(
    tokens,
    doc_lengths,
    ln1_gain,
    ln1_bias,
    qkv_weight,
    qkv_bias,
    out_weight,
    out_bias,
    ln2_gain,
    ln2_bias,
    up_weight,
    up_bias,
    down_weight,
    down_bias,
    cotangent,
):
    inputs = tokens[0].astype(jnp.float32)
    count = inputs.shape[0]
    ctx_count = lax.axis_size("ctx")
    length = count * ctx_count
    positions = lax.axis_index("ctx") * count + jnp.arange(count, dtype=jnp.int32)
    starts = doc_starts(doc_lengths[0], positions)
    frequency = 10000.0 ** (-jnp.arange(0, ROT, 2, dtype=jnp.float32) / ROT)
    angles = (positions - starts).astype(jnp.float32)[:, None] * frequency[None, :]
    scale = HEAD ** (-0.5)
    full_qkv, full_out, full_up, full_down = (
        lax.all_gather(qkv_weight, "ctx", axis=1, tiled=True),
        lax.all_gather(out_weight, "ctx", axis=1, tiled=True),
        lax.all_gather(up_weight, "ctx", axis=0, tiled=True),
        lax.all_gather(down_weight, "ctx", axis=1, tiled=True),
    )
    gain_one = ln1_gain.astype(jnp.float32)
    offset_one = ln1_bias.astype(jnp.float32)
    gain_two = ln2_gain.astype(jnp.float32)
    offset_two = ln2_bias.astype(jnp.float32)
    low_one = layer_norm(inputs, gain_one, offset_one).astype(jnp.bfloat16)
    low_two = layer_norm(inputs, gain_two, offset_two).astype(jnp.bfloat16)
    projected = (
        jnp.einsum("nd,cde->cne", low_one, full_qkv, preferred_element_type=jnp.float32)
        + qkv_bias.astype(jnp.float32)[:, None, :]
    )
    width = projected.shape[2]
    local_heads = width // HEAD
    query = rotary(projected[0].reshape(count, local_heads, HEAD), angles).astype(jnp.bfloat16)
    keys_flat = (
        rotary(projected[1].reshape(count, local_heads, HEAD), angles)
        .reshape(count, width)
        .astype(jnp.bfloat16)
    )
    values_flat = projected[2].astype(jnp.bfloat16)
    all_keys, all_values = (
        lax.all_gather(keys_flat, "ctx", axis=0, tiled=True),
        lax.all_gather(values_flat, "ctx", axis=0, tiled=True),
    )
    block = math.gcd(length, 512)
    block_count = length // block
    key_blocks = all_keys.reshape(block_count, block, local_heads, HEAD)
    value_blocks = all_values.reshape(block_count, block, local_heads, HEAD)
    firsts = jnp.arange(block_count, dtype=jnp.int32) * block

    def block_scores(key_block, first):
        key_index = first + jnp.arange(block, dtype=jnp.int32)
        allowed = (key_index[None, :] <= positions[:, None]) & (
            key_index[None, :] >= starts[:, None]
        )
        scores = (
            jnp.einsum("qhe,khe->hqk", query, key_block, preferred_element_type=jnp.float32) * scale
        )
        return (jnp.where(allowed[None], scores, -1e30), allowed[None])

    def statistics(carry, item):
        running, norm_sum = carry
        key_block, first = item
        masked, allowed = block_scores(key_block, first)
        newest = jnp.maximum(running, jnp.max(masked, axis=-1))
        raised = jnp.where(allowed, jnp.exp(masked - newest[..., None]), 0.0)
        norm_sum = norm_sum * jnp.exp(running - newest) + jnp.sum(raised, axis=-1)
        return ((newest, norm_sum), None)

    initial = (
        jnp.full((local_heads, count), -1e30, jnp.float32),
        jnp.zeros((local_heads, count), jnp.float32),
    )
    (running, norm_sum), _ = lax.scan(statistics, initial, (key_blocks, firsts))
    log_norm = running + jnp.log(norm_sum)

    def share_block(key_block, first):
        masked, allowed = block_scores(key_block, first)
        return jnp.where(allowed, jnp.exp(masked - log_norm[..., None]), 0.0)

    def accumulate(mixed, item):
        key_block, value_block, first = item
        shares_low = share_block(key_block, first).astype(jnp.bfloat16)
        return (
            mixed
            + jnp.einsum(
                "hqk,khe->qhe", shares_low, value_block, preferred_element_type=jnp.float32
            ),
            None,
        )

    mixed, _ = lax.scan(
        accumulate,
        jnp.zeros((count, local_heads, HEAD), jnp.float32),
        (key_blocks, value_blocks, firsts),
    )
    mixed_low = mixed.reshape(count, width).astype(jnp.bfloat16)
    attention = jnp.dot(mixed_low, full_out, preferred_element_type=jnp.float32)
    hidden = jnp.dot(low_two, full_up, preferred_element_type=jnp.float32) + up_bias.astype(
        jnp.float32
    )
    activated = jax.nn.gelu(hidden, approximate=False).astype(jnp.bfloat16)
    branches = attention + jnp.dot(activated, full_down, preferred_element_type=jnp.float32)
    joint = lax.psum(branches.astype(jnp.bfloat16), "head").astype(jnp.float32)
    output = inputs + joint + out_bias.astype(jnp.float32) + down_bias.astype(jnp.float32)
    upstream = cotangent[0]
    down_grad = jnp.dot(activated.T, upstream, preferred_element_type=jnp.float32)
    activated_grad = jnp.dot(upstream, full_down.T, preferred_element_type=jnp.float32)
    _, gelu_back = jax.vjp(partial(jax.nn.gelu, approximate=False), hidden)
    hidden_grad = gelu_back(activated_grad)[0].astype(jnp.bfloat16)
    up_grad = jnp.dot(low_two.T, hidden_grad, preferred_element_type=jnp.float32)
    up_bias_grad = jnp.sum(hidden_grad.astype(jnp.float32), axis=0)
    normed_two_grad = jnp.dot(hidden_grad, full_up.T, preferred_element_type=jnp.float32)
    out_grad = jnp.dot(mixed_low.T, upstream, preferred_element_type=jnp.float32)
    mixed_grad = jnp.dot(upstream, full_out.T, preferred_element_type=jnp.float32).astype(
        jnp.bfloat16
    )
    mixed_grad_heads = mixed_grad.reshape(count, local_heads, HEAD)
    delta = jnp.sum(mixed_grad_heads.astype(jnp.float32) * mixed, axis=-1).T

    def backward_block(query_grad, item):
        key_block, value_block, first = item
        shares = share_block(key_block, first)
        share_grad = jnp.einsum(
            "qhe,khe->hqk", mixed_grad_heads, value_block, preferred_element_type=jnp.float32
        )
        score_grad = (shares * (share_grad - delta[..., None])).astype(jnp.bfloat16)
        query_grad = (
            query_grad
            + jnp.einsum("hqk,khe->qhe", score_grad, key_block, preferred_element_type=jnp.float32)
            * scale
        )
        key_grad = (
            jnp.einsum("hqk,qhe->khe", score_grad, query, preferred_element_type=jnp.float32)
            * scale
        )
        value_grad = jnp.einsum(
            "hqk,qhe->khe",
            shares.astype(jnp.bfloat16),
            mixed_grad_heads,
            preferred_element_type=jnp.float32,
        )
        return (
            query_grad,
            jnp.concatenate(
                [key_grad.reshape(block, width), value_grad.reshape(block, width)], axis=1
            ),
        )

    query_grad, key_terms = lax.scan(
        backward_block,
        jnp.zeros((count, local_heads, HEAD), jnp.float32),
        (key_blocks, value_blocks, firsts),
    )
    own_grads = lax.psum_scatter(
        key_terms.reshape(length, 2 * width).astype(jnp.bfloat16),
        "ctx",
        scatter_dimension=0,
        tiled=True,
    ).astype(jnp.float32)
    query_pre = rotary(query_grad, -angles).reshape(count, width)
    key_pre = rotary(own_grads[:, :width].reshape(count, local_heads, HEAD), -angles).reshape(
        count, width
    )
    projected_grad = jnp.stack([query_pre, key_pre, own_grads[:, width:]]).astype(jnp.bfloat16)
    qkv_grad = jnp.einsum(
        "nd,cne->cde", low_one, projected_grad, preferred_element_type=jnp.float32
    )
    qkv_bias_grad = jnp.sum(projected_grad.astype(jnp.float32), axis=1)
    normed_one_grad = jnp.einsum(
        "cne,cde->nd", projected_grad, full_qkv, preferred_element_type=jnp.float32
    )
    normed_one_grad, normed_two_grad = (
        lax.psum(normed_one_grad.astype(jnp.bfloat16), "head").astype(jnp.float32),
        lax.psum(normed_two_grad.astype(jnp.bfloat16), "head").astype(jnp.float32),
    )
    _, norm_back_one = jax.vjp(layer_norm, inputs, gain_one, offset_one)
    input_one, gain_grad_one, offset_grad_one = norm_back_one(normed_one_grad)
    _, norm_back_two = jax.vjp(layer_norm, inputs, gain_two, offset_two)
    input_two, gain_grad_two, offset_grad_two = norm_back_two(normed_two_grad)
    upstream_wide = upstream.astype(jnp.float32)
    input_grad = upstream_wide + input_one + input_two
    bias_grad = jnp.sum(upstream_wide, axis=0)
    small = lax.psum(
        (
            gain_grad_one,
            offset_grad_one,
            qkv_bias_grad,
            bias_grad,
            gain_grad_two,
            offset_grad_two,
            up_bias_grad,
        ),
        ("stream", "ctx"),
    )
    slices = (
        lax.psum_scatter(
            qkv_grad.astype(jnp.bfloat16), "ctx", scatter_dimension=1, tiled=True
        ).astype(jnp.float32),
        lax.psum_scatter(
            out_grad.astype(jnp.bfloat16), "ctx", scatter_dimension=1, tiled=True
        ).astype(jnp.float32),
        lax.psum_scatter(
            up_grad.astype(jnp.bfloat16), "ctx", scatter_dimension=0, tiled=True
        ).astype(jnp.float32),
        lax.psum_scatter(
            down_grad.astype(jnp.bfloat16), "ctx", scatter_dimension=1, tiled=True
        ).astype(jnp.float32),
    )
    shards = (
        lax.psum(slices[0].astype(jnp.bfloat16), "stream").astype(jnp.float32),
        lax.psum(slices[1].astype(jnp.bfloat16), "stream").astype(jnp.float32),
        lax.psum(slices[2].astype(jnp.bfloat16), "stream").astype(jnp.float32),
        lax.psum(slices[3].astype(jnp.bfloat16), "stream").astype(jnp.float32),
    )
    return (
        output.astype(jnp.bfloat16)[None],
        input_grad[None],
        small[0],
        small[1],
        shards[0],
        small[2],
        shards[1],
        small[3],
        small[4],
        small[5],
        shards[2],
        small[6],
        shards[3],
        small[3],
    )


MESH = pl.DeviceIdType.MESH
FRONT_PLAN = (
    "z0", "l0", "z1", "P", "T", "N0", "s0", "L01", "z2", "l1", "z3", "p0", "N1", "f0", "Q0", "Q1", "s1", "L02", "s2", "p1", "L11", "p2", "N2", "Q2", "f1", "F0", "F1", "F2", "s3",
    "L03", "L12", "N3", "Q3", "p3", "F3", "A0", "A1", "A2", "A3", "f2", "B0", "B1", "L13", "f3", "D0", "D1", "B2", "D2", "B3", "D3", "E",
)
F32, BF16 = jnp.float32, jnp.bfloat16


def dot(a, b, over):
    return lax.dot_general(a, b, ((over[0:1], over[1:2]), ((), ())), preferred_element_type=F32)


def span(index, size):
    return pl.ds(pl.multiple_of(index * size, size), size)


def places():
    return lax.axis_index("stream"), lax.axis_index("ctx"), lax.axis_index("head")


def greet(peers):
    barrier = pltpu.get_barrier_semaphore()
    for peer in peers:
        pl.semaphore_signal(barrier, inc=1, device_id=peer, device_id_type=MESH)
    pl.semaphore_wait(barrier, len(peers))


def gather_body(
    x_ref, g_ref, qkv_ref, up_ref, out_ref, down_ref,
    gain_a_ref, off_a_ref, gain_b_ref, off_b_ref, qkv_bias_ref, up_bias_ref, rate_in, docs_ref,
    g_out, unit_out, act_out, dh_out, dqkv_out, mixed_out, qkv_out, up_out, out_out, down_out,
    z_send, z_recv, x_send, x_recv, y_send, y_recv, fx_send, fx_recv, fy_send, fy_recv,
    line_send, line_recv, core_send, core_recv, own_sem, give_sem, block_sem, small_sem,
    x_all, g_all, qkv_all, up_all, out_all, down_all,
    low_one, low_two, unit, query, keys, values, act, dh, dqkv, mixed_low,
    slope, mixed, norm, key_grad, value_grad, turn_ref, start_ref,
    gain_a, off_a, gain_b, off_b, qkv_bias, up_bias, rate_ref, rows_ref, bias_ref,
):
    s, c, h = places()
    x_peer = s + 1 - 2 * lax.rem(s, 2)
    y_peer = lax.rem(s + 2, 4)
    across = ((x_peer, c, h), (y_peer, c, h))
    core_peer = (s, c, 1 - h)
    ring = [(s, lax.rem(c + k, 4), h) for k in (1, 2, 3)]

    count = x_ref.shape[0]
    slab, width, units = up_ref.shape[0], out_ref.shape[0] // 4, down_ref.shape[0] // 4
    quarter, half_count = slab // 4, count // 2

    def rows(base, size):
        return pl.ds(pl.multiple_of(base, size), size)

    def landed(m, r, part, half):
        def cut(total):
            size = total // 4
            if half is None:
                return part * size, size
            return part * size + half * (size // 2), size // 2

        if m == 0:
            at, size = cut(slab)
            return qkv_all.at[:, rows(r * slab + at, size), :]
        if m == 1:
            at, size = cut(slab)
            return up_all.at[rows(r * slab + at, size), :]
        if m == 2:
            at, size = cut(width)
            return out_all.at[rows(at, size), span(r, slab)]
        at, size = cut(units)
        return down_all.at[rows(at, size), span(r, slab)]

    def piece(m, to, part=None):
        if m == 0:
            inner = slice(None) if part is None else span(part, quarter)
            return qkv_ref.at[:, inner, span(to, width)]
        if m == 1:
            inner = slice(None) if part is None else span(part, quarter)
            return up_ref.at[inner, span(to, units)]
        size = width if m == 2 else units
        ref = out_ref if m == 2 else down_ref
        if part is None:
            return ref.at[span(to, size), :]
        return ref.at[rows(to * size + part * (size // 4), size // 4), :]

    def whole_piece(m, r):
        if m == 0:
            return qkv_all.at[:, span(r, slab), :]
        if m == 1:
            return up_all.at[span(r, slab), :]
        return (out_all if m == 2 else down_all).at[:, span(r, slab)]

    def remote(src, dst, send, recv, to):
        return pltpu.make_async_remote_copy(
            src_ref=src, dst_ref=dst, send_sem=send, recv_sem=recv, device_id=to, device_id_type=MESH
        )

    def z_copy(m, k):
        to = lax.rem(c + 4 - k, 4)
        return remote(
            piece(m, to, s), landed(m, c, s, None), z_send.at[m, k - 1], z_recv.at[m, k - 1], (s, to, h)
        )

    def direct(m, k, axis):
        r = lax.rem(c + k, 4)
        send, recv = (x_send, x_recv) if axis == 0 else (y_send, y_recv)
        here = landed(m, r, s, None)
        return remote(here, here, send.at[m, k - 1], recv.at[m, k - 1], across[axis])

    def onward(m, k, axis):
        r = lax.rem(c + k, 4)
        send, recv = (fx_send, fx_recv) if axis == 0 else (fy_send, fy_recv)
        here = landed(m, r, y_peer if axis == 0 else x_peer, 1 if axis == 0 else 0)
        return remote(here, here, send.at[m, k - 1], recv.at[m, k - 1], across[axis])

    lines = ((x_ref, x_all), (g_ref, g_all))

    def block(a, origin):
        return lines[a][1].at[rows(origin * count + h * half_count, half_count), :]

    def line_copy(a, t, side):
        origin = c - t if side == 0 else c + t
        src = lines[a][0].at[span(h, half_count), :] if t == 0 else block(a, origin)
        to = c + 1 if side == 0 else c - 1
        return remote(
            src, block(a, origin), line_send.at[a, side, t], line_recv.at[a, side, t], (s, to, h)
        )

    def core_copy(a, t, side):
        origin = c - t if side == 0 else c + t
        here = block(a, origin)
        return remote(here, here, core_send.at[a, side, t - 1], core_recv.at[a, side, t - 1], core_peer)

    def sends(t, side):
        if side == 0:
            return (c >= t) & (c < 3)
        return (c + t <= 3) & (c > 0)

    def gets(t, side):
        return c >= t if side == 0 else c + t <= 3

    def line_step(a, t):
        for side in (0, 1):
            @pl.when(gets(t, side))
            def _():
                line_copy(a, t - 1, side).wait_recv()
                core_copy(a, t, side).start()

            if t < 3:
                @pl.when(sends(t, side))
                def _():
                    line_copy(a, t, side).start()

    near = (1, 3, 2)
    order = [(m, k) for m in (0, 1, 3, 2) for k in near]

    def start_z(m):
        for k in near:
            z_copy(m, k).start()

    def pass_on(m):
        for k in near:
            direct(m, k, 0).wait_recv()
            onward(m, k, 1).start()
            direct(m, k, 1).wait_recv()
            onward(m, k, 0).start()

    def spread(m):
        for k in near:
            z_copy(m, k).wait_recv()
            direct(m, k, 0).start()
            direct(m, k, 1).start()

    ins = [
        pltpu.make_async_copy(a, b, own_sem.at[i])
        for i, (a, b) in enumerate(
            [(lines[a][0], lines[a][1].at[span(c, count), :]) for a in (0, 1)]
            + [(piece(m, c), whole_piece(m, c)) for m in range(4)]
        )
    ]
    for copy in ins:
        copy.start()
    tile = count
    length, model = x_all.shape
    rot = turn_ref.shape[2]
    span_rot = rot // 4
    scale = width**-0.5

    def finish(m):
        for k in near:
            onward(m, k, 0).wait_recv()
            onward(m, k, 1).wait_recv()
        ins[2 + m].wait()

    def give(i):
        pairs = (
            (qkv_all, qkv_out), (up_all, up_out), (out_all, out_out), (down_all, down_out),
            (act, act_out), (dh, dh_out), (dqkv, dqkv_out), (mixed_low, mixed_out),
        )
        return pltpu.make_async_copy(*pairs[i], give_sem.at[i])

    def give_block(a, origin):
        src, dst = ((unit, unit_out), (g_all, g_out))[a]
        at = span(origin, tile)
        return pltpu.make_async_copy(src.at[at, :], dst.at[at, :], block_sem.at[a])

    def blocks_of(t, do):
        if t == 0:
            do(c)
            return

        @pl.loop(0, 2)
        def _(side):
            origin = c + t * (2 * side - 1)

            @pl.when((origin >= 0) & (origin <= 3))
            def _():
                do(origin)

    def core_wait(a, t):
        for side in (0, 1):
            @pl.when(gets(t, side))
            def _():
                core_copy(a, t, side).wait_recv()

    def norm_block(origin):
        tall = 32

        @pl.loop(0, tile // tall)
        def _(i):
            at = pl.ds(pl.multiple_of(origin * tile + i * tall, tall), tall)
            wide = x_all[at, :].astype(F32)
            centred = wide - jnp.mean(wide, axis=-1, keepdims=True)
            spread_of = jnp.mean(centred * centred, axis=-1, keepdims=True)
            found = centred * lax.rsqrt(spread_of + 1e-05)
            unit[at, :] = found.astype(BF16)
            low_one[at, :] = (found * rows_ref[0:1, :] + rows_ref[1:2, :]).astype(BF16)
            low_two[at, :] = (found * rows_ref[2:3, :] + rows_ref[3:4, :]).astype(BF16)

        give_block(0, origin).start()

    smalls = [
        pltpu.make_async_copy(a, b, small_sem.at[i])
        for i, (a, b) in enumerate(
            (
                (gain_a_ref, gain_a), (off_a_ref, off_a), (gain_b_ref, gain_b), (off_b_ref, off_b),
                (qkv_bias_ref, qkv_bias), (up_bias_ref, up_bias), (rate_in, rate_ref),
            )
        )
    ]
    for copy in smalls:
        copy.start()

    def parameters():
        for copy in smalls:
            copy.wait()
        for i, ref in enumerate((gain_a, off_a, gain_b, off_b)):
            rows_ref[i : i + 1, :] = ref[...].astype(F32).reshape(1, model)
        part = qkv_bias[:, span(c, width)].astype(F32)
        for p in range(3):
            bias_ref[0:1, p * width : (p + 1) * width] = part[p : p + 1]
        bias_ref[1:2, :] = up_bias[span(c, units)].astype(F32).reshape(1, units)

    def tables():
        starts, total = [], docs_ref[0, 0] * 0
        for j in range(docs_ref.shape[1]):
            starts.append(total)
            total = total + docs_ref[0, j]

        @pl.loop(0, length // tile)
        def _(i):
            at = span(i, tile)
            place = i * tile + lax.broadcasted_iota(jnp.int32, (tile, rot), 0)
            lane = lax.broadcasted_iota(jnp.int32, (tile, rot), 1)
            first = jnp.zeros((tile, rot), jnp.int32)
            for start in starts:
                first = jnp.where(start <= place, jnp.maximum(first, start), first)
            start_ref[at, :] = first[:, 0:1]
            angle = (place - first).astype(F32) * rate_ref[0:1, :]
            sine = jnp.sin(angle)
            turn_ref[0, at, :] = jnp.where(lane < 2 * span_rot, jnp.cos(angle), 1.0)
            turn_ref[1, at, :] = jnp.where((lane >= span_rot) & (lane < 2 * span_rot), sine, 0.0)
            turn_ref[2, at, :] = jnp.where(lane < span_rot, -sine, 0.0)

    def turned(v, at, sign):
        near_part = v[:, :rot]
        moved = pltpu.roll(near_part, span_rot, 1) * turn_ref[1, at, :] + pltpu.roll(near_part, rot - span_rot, 1) * turn_ref[2, at, :]
        return jnp.concatenate([near_part * turn_ref[0, at, :] + sign * moved, v[:, rot:]], axis=1)

    def project(i):
        at = span(i, tile)
        for p, into in enumerate((query, keys, values)):
            part = dot(low_one[at, :], qkv_all[p], (1, 0)) + bias_ref[0:1, p * width : (p + 1) * width]
            into[at, :] = (turned(part, at, 1.0) if p < 2 else part).astype(BF16)

    def allowed_of(i, wide):
        first = lax.broadcasted_iota(jnp.int32, (tile, wide), 1)
        place = i * tile + lax.broadcasted_iota(jnp.int32, (tile, wide), 0)
        return (first <= place) & (first >= start_ref[span(i, tile), :])

    def attend(i):
        wide = (i + 1) * tile
        at = slice(i * tile, wide)
        scores = dot(query[at, :], keys[0:wide, :], (1, 1)) * scale
        allowed = allowed_of(i, wide)
        masked = jnp.where(allowed, scores, -1e30)
        peak = jnp.max(masked, axis=-1, keepdims=True)
        raised = jnp.where(allowed, jnp.exp(masked - peak), 0.0)
        total = jnp.sum(raised, axis=-1, keepdims=True)
        norm[at, :] = peak + jnp.log(total)
        found = dot((raised / total).astype(BF16), values[0:wide, :], (1, 0))
        mixed[at, :] = found
        mixed_low[at, :] = found.astype(BF16)

    def feed(i):
        at = span(i, tile)
        for j in range(units // 256):
            cols = slice(j * 256, (j + 1) * 256)
            hidden = dot(low_two[at, :], up_all[:, cols], (1, 0)) + bias_ref[1:2, cols]
            share = 0.5 + 0.5 * lax.erf(hidden * (0.5**0.5))
            act[at, cols] = (hidden * share).astype(BF16)
            slope[at, cols] = share + hidden * jnp.exp(-0.5 * hidden * hidden) * ((0.5 / jnp.pi) ** 0.5)

    def back_attend(origin):
        at = span(origin, tile)
        grad = dot(g_all[at, :], out_all[...], (1, 1)).astype(BF16)
        scores = dot(query[at, :], keys[...], (1, 1)) * scale
        shares = jnp.where(allowed_of(origin, length), jnp.exp(scores - norm[at, :]), 0.0)
        delta = jnp.sum(grad.astype(F32) * mixed[at, :], axis=-1, keepdims=True)
        share_grad = dot(grad, values[...], (1, 1))
        score_grad = (shares * (share_grad - delta)).astype(BF16)
        value_grad[...] += dot(shares.astype(BF16), grad, (0, 0))
        key_grad[...] += dot(score_grad, query[at, :], (0, 0))
        part = dot(score_grad, keys[...], (1, 0)) * scale
        dqkv[at, 0:width] = turned(part, at, -1.0).astype(BF16)

    def back_feed(origin):
        at = span(origin, tile)
        for j in range(units // 256):
            cols = slice(j * 256, (j + 1) * 256)
            part = dot(g_all[at, :], down_all[cols, :], (1, 1))
            dh[at, cols] = (part * slope[at, cols]).astype(BF16)

    def start_line(a):
        for side in (0, 1):
            @pl.when(sends(0, side))
            def _():
                line_copy(a, 0, side).start()

    def close():
        give(5).start()

        @pl.loop(0, length // tile)
        def _(i):
            at = span(i, tile)
            dqkv[at, width : 2 * width] = turned(key_grad[at, :] * scale, at, -1.0).astype(BF16)
            dqkv[at, 2 * width : 3 * width] = value_grad[at, :].astype(BF16)

        give(6).start()

    def run(step):
        op, rest = step[0], [int(d) for d in step[1:]]
        if op == "z":
            start_z(*rest)
        elif op == "s":
            spread(*rest)
        elif op == "p":
            pass_on(*rest)
        elif op == "f":
            finish(*rest)
            give(*rest).start()
        elif op == "l":
            start_line(*rest)
        elif op == "L":
            line_step(*rest)
        elif op == "N":
            if rest[0]:
                core_wait(0, *rest)
            else:
                ins[0].wait()
            blocks_of(*rest, norm_block)
        elif op == "P":
            parameters()
        elif op == "T":
            tables()
        elif op == "Q":
            blocks_of(*rest, project)
        elif op == "A":
            attend(*rest)
            if rest[0] == 3:
                give(7).start()
        elif op == "F":
            blocks_of(*rest, feed)
            if rest[0] == 3:
                give(4).start()
        elif op == "B":
            if rest[0]:
                core_wait(1, *rest)
            else:
                ins[1].wait()
            blocks_of(*rest, back_attend)
        elif op == "D":
            blocks_of(*rest, back_feed)
        elif op == "E":
            close()

    greet([*across, core_peer, *ring])
    key_grad[...] = jnp.zeros_like(key_grad)
    value_grad[...] = jnp.zeros_like(value_grad)
    for step in FRONT_PLAN:
        run(step)
    for t in (0, 1, 2, 3):
        blocks_of(t, lambda origin: give_block(1, origin).start())
    for a in (0, 1):
        for side in (0, 1):
            for t in (1, 2, 3):
                @pl.when(gets(t, side))
                def _():
                    core_copy(a, t, side).wait_send()
                @pl.when(sends(t - 1, side))
                def _():
                    line_copy(a, t - 1, side).wait_send()
    for m, k in order:
        z_copy(m, k).wait_send()
        for axis in (0, 1):
            direct(m, k, axis).wait_send()
            onward(m, k, axis).wait_send()
    pltpu.make_async_copy(unit, unit_out, block_sem.at[0]).wait()
    pltpu.make_async_copy(g_all, g_out, block_sem.at[1]).wait()
    for i in range(8):
        give(i).wait()


def gather_all(tokens, cotangent, w_qkv, w_up, w_out, w_down, gain_a, off_a, gain_b, off_b, b_qkv, b_up, docs):
    count, model = tokens.shape
    length = 4 * count
    width, units = w_out.shape[0] // 4, w_down.shape[0] // 4
    frequency = 10000.0 ** (-np.arange(0, ROT, 2, dtype=np.float32) / np.float32(ROT))
    rate = jnp.asarray(np.tile(frequency.astype(np.float32), (8, 4)))
    dma = pltpu.SemaphoreType.DMA
    weights = [(3, model, width), (model, units), (width, model), (units, model)]
    wide, narrow = (length, model), (length, width)
    results = [wide, wide, (length, units), (length, units), (length, 3 * width), narrow] + weights
    scratch = [dma((4, 3))] * 10 + [dma((2, 2, 3))] * 4 + [dma((6,)), dma((8,)), dma((2,)), dma((7,))]
    scratch += [
        pltpu.VMEM(v, BF16)
        for v in [wide, wide] + weights + [wide] * 3 + [narrow] * 3
        + [(length, units)] * 2 + [(length, 3 * width), narrow]
    ]
    scratch += [pltpu.VMEM(v, F32) for v in ((length, units), narrow, (length, 1), narrow, narrow)]
    scratch += [pltpu.VMEM((3, length, rate.shape[1]), F32), pltpu.VMEM((length, 1), jnp.int32)]
    scratch += [pltpu.VMEM((model,), BF16)] * 4 + [pltpu.VMEM(b_qkv.shape, BF16), pltpu.VMEM(b_up.shape, BF16)]
    scratch += [pltpu.VMEM(v, F32) for v in (rate.shape, (8, model), (8, units))]
    any_space = pl.BlockSpec(memory_space=pl.ANY)
    return pl.pallas_call(
        gather_body,
        out_shape=[jax.ShapeDtypeStruct(v, BF16) for v in results],
        in_specs=[any_space] * 13 + [pl.BlockSpec(memory_space=pltpu.SMEM)],
        out_specs=[any_space] * 10,
        scratch_shapes=scratch,
        compiler_params=pltpu.CompilerParams(
            collective_id=0, has_side_effects=True, vmem_limit_bytes=63 << 20
        ),
        name="gather",
    )(
        tokens, cotangent, w_qkv, w_up, w_out, w_down, gain_a, off_a, gain_b, off_b, b_qkv, b_up, rate, docs
    )


LEADS = (4, 4, 4, 4, 1, 1)
BACK_PLAN = (
    "O", "14", "D", "B0", "24", "B1", "R0", "P", "Q", "11", "12", "25", "Z4", "22", "U", "13", "10", "I0", "I1", "Z5", "X4", "20", "23", "21", "a", "Z0", "Z2", "b", "X5", "X0", "S0", "N4",
    "Z3", "Z1", "N5", "X3", "c", "X2", "R1", "X1", "N3", "N1", "d", "N0", "N2", "e", "S1",
)
def settle_body(
    act_in, up_in, unit_in, dh_in, dqkv_in, mixed_in, wq_in, wu_in, wo_in, wd_in,
    gain_a_ref, off_a_ref, gain_b_ref, off_b_ref,
    joint, inward, o0, o1, o2, o3, small_out,
    s1x_send, s1x_recv, s1y_send, s1y_recv, s2x_send, s2x_recv, s2y_send, s2y_recv,
    x_send, x_recv, y_send, y_recv, fx_send, fx_recv, fy_send, fy_recv,
    z_send, z_recv, keep_sem, load_sem, weight_sem,
    core_send, core_recv, row_send, row_recv, back_send, back_recv, back_sem,
    sum_send, sum_recv, sum_sem, small_sem,
    act, up, unit, dh, dqkv, mixed, w_wide, w_out, w_qkv, *rest,
):
    grads, first, second = rest[0:6], (rest[6:18:2], rest[7:18:2]), (rest[18:30:2], rest[19:30:2])
    (
        own_half, core_half, send_half, row_parts, done_half,
        sums, sums_core, slots, total_own, total_x, total_y,
        gain_a, off_a, gain_b, off_b, rows_ref, low_ref,
    ) = rest[30:]
    s, c, h = places()
    x_at, y_at = lax.rem(s, 2), lax.div(s, 2)
    x_off, y_off = 1 - x_at, 1 - y_at
    x_peer, y_peer = y_at * 2 + x_off, y_off * 2 + x_at
    across = ((x_peer, c, h), (y_peer, c, h))
    core_peer = (s, c, 1 - h)
    near = (1, 3, 2)
    outs = (o0, o1, o2, o3)
    first, second = list(zip(*first)), list(zip(*second))
    slab = o2.shape[-1]
    length, model = up.shape
    units, width = act.shape[1], mixed.shape[1]
    half_cols = model // 2
    count = joint.shape[0]
    tile = 256

    def remote(src, dst, send, recv, to):
        return pltpu.make_async_remote_copy(
            src_ref=src, dst_ref=dst, send_sem=send, recv_sem=recv, device_id=to, device_id_type=MESH
        )

    loads = [
        pltpu.make_async_copy(a, b, load_sem.at[i])
        for i, (a, b) in enumerate(
            ((act_in, act), (up_in, up), (dh_in, dh), (unit_in, unit), (dqkv_in, dqkv), (mixed_in, mixed))
        )
    ]
    for load in loads[:2]:
        load.start()
    greet([*across, core_peer, *[(s, lax.rem(c + k, 4), h) for k in near]])

    smalls = [
        pltpu.make_async_copy(a, b, small_sem.at[i])
        for i, (a, b) in enumerate(
            ((gain_a_ref, gain_a), (off_a_ref, off_a), (gain_b_ref, gain_b), (off_b_ref, off_b))
        )
    ]
    for copy in smalls:
        copy.start()

    def side(which):
        return 1 - h if which == 0 else h

    def weight_load(i):
        at = span(side(i % 2), half_cols)
        if i < 2:
            return pltpu.make_async_copy(wd_in.at[:, at], w_wide.at[i], weight_sem.at[i])
        if i < 4:
            return pltpu.make_async_copy(wu_in.at[at, :], w_wide.at[i % 2], weight_sem.at[i])
        if i < 6:
            return pltpu.make_async_copy(wo_in.at[:, at], w_out.at[i % 2], weight_sem.at[i])
        return pltpu.make_async_copy(wq_in.at[:, at, :], w_qkv.at[i % 2], weight_sem.at[i])

    for load in loads[2:]:
        load.start()
    for i in (0, 4, 1, 5, 6, 7):
        weight_load(i).start()

    def one(m, half):
        src = grads[m].at[:, :, x_off, 0] if half == 0 else grads[m].at[:, y_off, :, 1]
        send, recv = (s1x_send, s1x_recv) if half == 0 else (s1y_send, s1y_recv)
        return remote(src, first[m][half], send.at[m], recv.at[m], across[half])

    def two(m, half):
        src = first[m][half].at[:, y_off if half == 0 else x_off]
        send, recv = (s2y_send, s2y_recv) if half == 0 else (s2x_send, s2x_recv)
        return remote(src, second[m][half], send.at[m], recv.at[m], across[1 - half])

    def add_first(m, half):
        into, more = first[m][half], grads[m]
        lead, _, height, _ = into.shape
        tall = min(height, 32)

        @pl.loop(0, lead * 2 * (height // tall))
        def _(i):
            at = lax.rem(i, height // tall)
            pair = lax.div(i, height // tall)
            l, j, rows = lax.div(pair, 2), lax.rem(pair, 2), span(at, tall)
            term = more[l, j, x_at, 0, rows, :] if half == 0 else more[l, y_at, j, 1, rows, :]
            into[l, j, rows, :] = (into[l, j, rows, :].astype(F32) + term.astype(F32)).astype(BF16)

    def add_second(m, half):
        into, more = second[m][half], first[m][half]
        mine = y_at if half == 0 else x_at
        lead, height, _ = into.shape
        tall = min(height, 32)

        @pl.loop(0, lead * (height // tall))
        def _(i):
            l, rows = lax.div(i, height // tall), span(lax.rem(i, height // tall), tall)
            term = more[l, mine, rows, :].astype(F32)
            into[l, rows, :] = (into[l, rows, :].astype(F32) + term).astype(BF16)

    def share_of(m, half, to):
        ref = second[m][half]
        return ref.at[to] if m < 4 else ref.at[0, :, span(to, slab)]

    def home(m, half):
        if m < 3:
            return outs[0].at[m, s, half, :, span(c, width)]
        if m == 3:
            return outs[1].at[s, half, :, span(c, units)]
        return outs[m - 2].at[c, s, half]

    def z_copy(m, half, k):
        to = lax.rem(c + 4 - k, 4)
        i = (m * 2 + half) * 3 + k - 1
        return remote(share_of(m, half, to), home(m, half), z_send.at[i], z_recv.at[i], (s, to, h))

    def keep(m, half):
        return pltpu.make_async_copy(share_of(m, half, c), home(m, half), keep_sem.at[m, half])

    def quarter(m, q, half=None):
        at = (q,) if half is None else (q, half)
        if m < 3:
            return outs[0].at[(m, *at)]
        if m == 3:
            return outs[1].at[at]
        return outs[m - 2].at[(slice(None), *at)]

    def direct(m, axis):
        send, recv = (x_send, x_recv) if axis == 0 else (y_send, y_recv)
        here = quarter(m, s)
        return remote(here, here, send.at[m], recv.at[m], across[axis])

    def onward(m, axis):
        send, recv = (fx_send, fx_recv) if axis == 0 else (fy_send, fy_recv)
        here = quarter(m, y_peer if axis == 0 else x_peer, 1 - axis)
        return remote(here, here, send.at[m], recv.at[m], across[axis])

    finals = (joint, inward)

    def core_copy(a):
        return remote(send_half, core_half.at[a], core_send.at[a], core_recv.at[a], core_peer)

    def row_copy(a, k):
        to = lax.rem(c + 4 - k, 4)
        return remote(
            own_half.at[a, span(to, count)], row_parts.at[a, k - 1],
            row_send.at[a, k - 1], row_recv.at[a, k - 1], (s, to, h),
        )

    def back_copy(a):
        return remote(
            done_half.at[a], finals[a].at[:, span(h, half_cols)], back_send.at[a], back_recv.at[a], core_peer
        )

    def back_keep(a):
        return pltpu.make_async_copy(done_half.at[a], finals[a].at[:, span(h, half_cols)], back_sem.at[a])

    def line_start(a):
        core_copy(a).wait_recv()
        tall = 32

        @pl.loop(0, length // tall)
        def _(i):
            rows = span(i, tall)
            own_half[a, rows, :] = (
                own_half[a, rows, :].astype(F32) + core_half[a, rows, :].astype(F32)
            ).astype(BF16)

        for k in near:
            row_copy(a, k).start()

    def line_sum(a):
        for k in near:
            row_copy(a, k).wait_recv()
        tall = 32

        @pl.loop(0, count // tall)
        def _(i):
            rows = span(i, tall)
            total = own_half[a, pl.ds(pl.multiple_of(c * count + i * tall, tall), tall), :].astype(F32)
            for k in range(3):
                total = total + row_parts[a, k, rows, :].astype(F32)
            done_half[a, rows, :] = total.astype(BF16)

        back_copy(a).start()
        back_keep(a).start()

    def down_grad():
        rows = units // 8

        def part_of(y, x):
            left = act[:, span(2 * y + x, 2 * rows)]
            for j in range(model // 512):
                cols = slice(j * 512, (j + 1) * 512)
                part = dot(left, up[:, cols], (0, 0)).astype(BF16)
                for half in (0, 1):
                    grads[5][0, y, x, half, :, cols] = part[half * rows : (half + 1) * rows]

        part_of(y_off, x_off)
        part_of(y_at, x_off)
        one(5, 0).start()
        part_of(y_off, x_at)
        one(5, 1).start()
        part_of(y_at, x_at)

    def out_grad():
        rows = width // 8
        for j in range(model // 512):
            part = dot(mixed[...], up[:, j * 512 : (j + 1) * 512], (0, 0)).astype(BF16)
            for i in range(8):
                grads[4][0, i // 4, (i // 2) % 2, i % 2, :, j * 512 : (j + 1) * 512] = part[i * rows : (i + 1) * rows]

    same = lax.broadcasted_iota(jnp.int32, (tile, tile), 0) == lax.broadcasted_iota(jnp.int32, (tile, tile), 1)
    eye = jnp.where(same, 1.0, 0.0).astype(BF16)

    def columns(t):
        return dot(eye, low_ref[:, span(t, tile)], (1, 1))

    def scaled(part, column, at, column_sum):
        return (part * column[:, at : at + 1] + column[:, at + 1 : at + 2] * column_sum).astype(BF16)

    def column_sum(ref, cols):
        total = jnp.zeros((1, cols.stop - cols.start), F32)
        for i in range(length // tile):
            total = total + jnp.sum(ref[i * tile : (i + 1) * tile, cols].astype(F32), axis=0, keepdims=True)
        return total

    def up_grad():
        rows = tile // 4

        @pl.loop(0, model // tile)
        def _(t):
            left, column = unit[:, span(t, tile)], columns(t)
            for j in range(units // 512):
                cols = slice(j * 512, (j + 1) * 512)
                near_sum = sums[5:6, 3 * width + j * 512 : 3 * width + (j + 1) * 512]
                part = scaled(dot(left, dh[:, cols], (0, 0)), column, 2, near_sum)
                for i in range(4):
                    grads[3][lax.div(t, 2), lax.rem(t, 2), i // 2, i % 2, :, cols] = part[i * rows : (i + 1) * rows]

    def qkv_grad():
        rows = tile // 4

        @pl.loop(0, model // tile)
        def _(t):
            left, column = unit[:, span(t, tile)], columns(t)
            for p in range(3):
                cols = slice(p * width, (p + 1) * width)
                part = scaled(dot(left, dqkv[:, cols], (0, 0)), column, 0, sums[5:6, cols])
                for i in range(4):
                    grads[p][lax.div(t, 2), lax.rem(t, 2), i // 2, i % 2] = part[i * rows : (i + 1) * rows]

    def branches(which):
        into = send_half if which == 0 else own_half.at[0]

        @pl.loop(0, length // tile)
        def _(i):
            rows = span(i, tile)
            for j in range(half_cols // 512):
                cols = slice(j * 512, (j + 1) * 512)
                part = dot(mixed[rows, :], w_out[which, :, cols], (1, 0))
                part = part + dot(act[rows, :], w_wide[which, :, cols], (1, 0))
                into[rows, cols] = part.astype(BF16)

    def inwards(which):
        into = send_half if which == 0 else own_half.at[1]
        base = side(which) * half_cols
        for j in range(half_cols // 512):
            cols = slice(j * 512, (j + 1) * 512)
            far = span(side(which) * (half_cols // 512) + j, 512)
            zero = jnp.zeros((8, 512), F32)

            def step(i, carry):
                rows = span(i, tile)
                one_part = dot(dqkv[rows, 0:width], w_qkv[which, 0, cols, :], (1, 1))
                for p in (1, 2):
                    one_part = one_part + dot(
                        dqkv[rows, p * width : (p + 1) * width], w_qkv[which, p, cols, :], (1, 1)
                    )
                two_part = dot(dh[rows, :], w_wide[which, cols, :], (1, 1))
                into[rows, cols] = (one_part * rows_ref[0:1, far] + two_part * rows_ref[2:3, far]).astype(BF16)
                place = unit[rows, far].astype(F32)

                def fold(v):
                    return jnp.sum(v.reshape(tile // 8, 8, 512), axis=0)

                return (
                    carry[0] + fold(one_part * place),
                    carry[1] + fold(one_part),
                    carry[2] + fold(two_part * place),
                    carry[3] + fold(two_part),
                )

            found = lax.fori_loop(0, length // tile, step, (zero, zero, zero, zero))
            for n in range(4):
                sums[n : n + 1, far] = jnp.sum(found[n], axis=0, keepdims=True)

    def sum_core():
        return remote(sums, sums_core, sum_send.at[0], sum_recv.at[0], core_peer)

    def sum_line(k):
        return remote(
            sums, slots.at[c], sum_send.at[k], sum_recv.at[k], (s, lax.rem(c + 4 - k, 4), h)
        )

    def sum_x():
        return remote(total_own, total_x, sum_send.at[4], sum_recv.at[4], across[0])

    def sum_y():
        return remote(total_own, total_y, sum_send.at[5], sum_recv.at[5], across[1])

    kinds = range(6)
    loaded = set()

    def need(*which):
        for i in which:
            if i not in loaded:
                loads[i].wait()
                loaded.add(i)

    def parameters():
        for copy in smalls:
            copy.wait()
        rows_ref[...] = jnp.zeros_like(rows_ref)
        for i, ref in enumerate((gain_a, off_a, gain_b, off_b)):
            rows_ref[i : i + 1, :] = ref[...].astype(F32).reshape(1, model)
        low_ref[...] = rows_ref[...].astype(BF16)

    def compute_sums():
        sums[4:5, :] = jnp.sum(up[span(c, count), :].astype(F32), axis=0, keepdims=True) * 0.5
        sums[5:8, :] = jnp.zeros((3, model), F32)

    def small_copy():
        return pltpu.make_async_copy(total_own, small_out, sum_sem.at[0])

    def stage_two(m):
        for half in (0, 1):
            one(m, half).wait_recv()
            add_first(m, half)
            two(m, half).start()

    def stage_z(m):
        for half in (0, 1):
            two(m, half).wait_recv()
            add_second(m, half)
            for k in near:
                z_copy(m, half, k).start()
            keep(m, half).start()

    def stage_out(m):
        for half in (0, 1):
            for k in near:
                z_copy(m, half, k).wait_recv()
            keep(m, half).wait()
        for axis in (0, 1):
            direct(m, axis).start()

    def stage_on(m):
        direct(m, 0).wait_recv()
        onward(m, 1).start()
        direct(m, 1).wait_recv()
        onward(m, 0).start()

    def run(step):
        op, m = step[0], int(step[1]) if len(step) > 1 else None
        if op == "D":
            need(0, 1)
            down_grad()
        elif op == "P":
            need(1)
            parameters()
            compute_sums()
        elif op == "U":
            need(1, 2, 3)
            for j in range(units // 512):
                cols = slice(j * 512, (j + 1) * 512)
                sums[5:6, 3 * width + cols.start : 3 * width + cols.stop] = column_sum(dh, cols)
            up_grad()
        elif op == "Q":
            need(3, 4)
            for p in range(3):
                cols = slice(p * width, (p + 1) * width)
                sums[5:6, cols] = column_sum(dqkv, cols)
            qkv_grad()
        elif op == "O":
            need(1, 5)
            out_grad()
        elif op == "1":
            one(m, 0).start()
            one(m, 1).start()
        elif op == "B":
            need(0, 5)
            weight_load(m).wait()
            weight_load(4 + m).wait()
            branches(m)
            weight_load(2 + m).start()
            if m == 0:
                core_copy(0).start()
        elif op == "I":
            need(2, 3, 4)
            if m == 0:
                core_copy(0).wait_send()
            weight_load(2 + m).wait()
            weight_load(6 + m).wait()
            inwards(m)
            if m == 0:
                core_copy(1).start()
        elif op == "2":
            stage_two(m)
        elif op == "Z":
            stage_z(m)
        elif op == "X":
            stage_out(m)
        elif op == "N":
            stage_on(m)
        elif op == "R":
            line_start(m)
        elif op == "S":
            line_sum(m)
        elif op == "a":
            sum_core().start()
        elif op == "b":
            sum_core().wait()
            sums[0:5, :] = sums[0:5, :] + sums_core[0:5, :]
            for k in near:
                sum_line(k).start()
            slots[c] = sums[...]
        elif op == "c":
            for k in near:
                sum_line(k).wait()
            total_own[0:8, :] = slots[0] + slots[1] + slots[2] + slots[3]
            for i in range(4):
                total_own[8 + i : 9 + i, :] = slots[i, 5:6, :]
            total_own[12:16, :] = jnp.zeros((4, model), F32)
            sum_x().start()
        elif op == "d":
            sum_x().wait()
            total_own[...] = total_own[...] + total_x[...]
            sum_y().start()
        elif op == "e":
            sum_y().wait()
            total_own[...] = total_own[...] + total_y[...]
            small_copy().start()

    for step in BACK_PLAN:
        run(step)
    for m in kinds:
        for axis in (0, 1):
            onward(m, axis).wait_recv()
    small_copy().wait()
    for a in (0, 1):
        back_copy(a).wait()
        back_keep(a).wait()
        for k in near:
            row_copy(a, k).wait_send()
    core_copy(1).wait_send()
    for m in kinds:
        for half in (0, 1):
            one(m, half).wait_send()
            two(m, half).wait_send()
            for k in near:
                z_copy(m, half, k).wait_send()
        for axis in (0, 1):
            direct(m, axis).wait_send()
            onward(m, axis).wait_send()


def settle_all(act, up, unit, dh, dqkv, mixed, w_qkv, w_up, w_out, w_down, gain_a, off_a, gain_b, off_b):
    length, model = up.shape
    units, width = act.shape[1], mixed.shape[1]
    slab, count, half = model // 4, length // 4, model // 2
    dma = pltpu.SemaphoreType.DMA
    heights = (*[slab // 8] * 4, width // 8, units // 8)
    widths = (width, width, width, units, model, model)
    out_shapes = [
        (count, model), (count, model),
        (3, 4, 2, heights[0], 4 * width), (4, 2, heights[3], 4 * units),
        (4, 4, 2, heights[4], slab), (4, 4, 2, heights[5], slab),
    ]
    scratch = [dma((6,))] * 16 + [dma((36,))] * 2 + [dma((6, 2)), dma((6,)), dma((8,))]
    scratch += [dma((2,)), dma((2,)), dma((2, 3)), dma((2, 3)), dma((2,)), dma((2,)), dma((2,))]
    scratch += [dma((6,)), dma((6,)), dma((1,)), dma((4,))]
    vmem = [(length, units), (length, model), (length, model), (length, units), (length, 3 * width), (length, width)]
    vmem += [(2, units, half), (2, width, half), (2, 3, half, width)]
    shapes = list(zip(LEADS, heights, widths))
    vmem += [(l, 2, 2, 2, r, k) for l, r, k in shapes]
    vmem += [(l, 2, r, k) for l, r, k in shapes for _ in (0, 1)]
    vmem += [(l, r, k) for l, r, k in shapes for _ in (0, 1)]
    vmem += [(2, length, half), (2, length, half), (length, half), (2, 3, count, half), (2, count, half)]
    scratch += [pltpu.VMEM(v, BF16) for v in vmem]
    scratch += [pltpu.VMEM(v, F32) for v in ((8, model), (8, model), (4, 8, model), (16, model), (16, model), (16, model))]
    scratch += [pltpu.VMEM((model,), BF16)] * 4 + [pltpu.VMEM((8, model), F32), pltpu.VMEM((8, model), BF16)]
    any_space = pl.BlockSpec(memory_space=pl.ANY)
    joint, inward, q, u, o, d, small = pl.pallas_call(
        settle_body,
        out_shape=[jax.ShapeDtypeStruct(v, BF16) for v in out_shapes] + [jax.ShapeDtypeStruct((16, model), F32)],
        in_specs=[any_space] * 14,
        out_specs=[any_space] * 7,
        scratch_shapes=scratch,
        compiler_params=pltpu.CompilerParams(
            collective_id=1, has_side_effects=True, vmem_limit_bytes=63 << 20
        ),
        name="settle",
    )(act, up, unit, dh, dqkv, mixed, w_qkv, w_up, w_out, w_down, gain_a, off_a, gain_b, off_b)
    return (
        joint, inward, q.reshape(3, slab, 4 * width), u.reshape(slab, 4 * units),
        o.reshape(4 * width, slab), d.reshape(4 * units, slab), small,
    )


def finish_body(
    q_ref, u_ref, o_ref, d_ref, joint_ref, inward_ref, own_ref, up_ref, small_ref, bias_a_ref, bias_b_ref,
    q_out, u_out, o_out, d_out, y_out, g_out, v0, v1, v2, v3, v4, v5, qb_out, ub_out,
    q_low, u_low, o_low, d_low, q_wide, u_wide, o_wide, d_wide,
    joint, inward, own, up, small, bias_a, bias_b, y, g, w0, w1, w2, w3, w4, qb, ub,
    read_sem, write_sem, in_sem, out_sem,
):
    sources, results = (q_ref, u_ref, o_ref, d_ref), (q_out, u_out, o_out, d_out)
    lows, wides = (q_low, u_low, o_low, d_low), (q_wide, u_wide, o_wide, d_wide)
    counts = [src.shape[0] // low.shape[1] for src, low in zip(sources, lows)]
    order = [(a, n) for n in range(max(counts)) for a in (3, 1, 0, 2) if n < counts[a]]

    def rows(a, n):
        size = lows[a].shape[1]
        return slice(n * size, (n + 1) * size)

    def read(a, n):
        return pltpu.make_async_copy(sources[a].at[rows(a, n), :], lows[a].at[n % 2], read_sem.at[a, n % 2])

    def write(a, n):
        return pltpu.make_async_copy(wides[a].at[n % 2], results[a].at[rows(a, n), :], write_sem.at[a, n % 2])

    loads = [
        pltpu.make_async_copy(a, b, in_sem.at[i])
        for i, (a, b) in enumerate(
            (
                (joint_ref, joint), (inward_ref, inward), (own_ref, own), (up_ref, up),
                (small_ref, small), (bias_a_ref, bias_a), (bias_b_ref, bias_b),
            )
        )
    ]
    stores = [
        pltpu.make_async_copy(a, b, out_sem.at[i])
        for i, (a, b) in enumerate(
            (
                (y, y_out), (g, g_out), (w0, v0), (w1, v1), (w4, v2), (w2, v3), (w3, v4), (w4, v5),
                (qb, qb_out), (ub, ub_out),
            )
        )
    ]
    for a, n in order:
        if n < 2:
            read(a, n).start()
    for load in loads:
        load.start()

    def rest():
        for load in loads:
            load.wait()
        for i, out in enumerate((w0, w1, w2, w3, w4)):
            out[...] = small[i : i + 1, :].reshape(out.shape)
        width, units = qb.shape[1] // 4, ub.shape[0] // 4
        for i in range(4):
            row = small[8 + i : 9 + i, :]
            for p in range(3):
                qb[p : p + 1, i * width : (i + 1) * width] = row[:, p * width : (p + 1) * width]
            ub[i * units : (i + 1) * units] = row[:, 3 * width : 3 * width + units].reshape(units)
        bias = (bias_a[...].astype(F32) + bias_b[...].astype(F32)).reshape(1, own.shape[1])
        tall = 32

        @pl.loop(0, own.shape[0] // tall)
        def _(i):
            at = span(i, tall)
            wide = own[at, :].astype(F32)
            y[at, :] = (wide + joint[at, :].astype(F32) + bias).astype(BF16)
            centred = wide - jnp.mean(wide, axis=-1, keepdims=True)
            scale = lax.rsqrt(jnp.mean(centred * centred, axis=-1, keepdims=True) + 1e-05)
            unit = centred * scale
            back = inward[at, :].astype(F32)
            back = back - jnp.mean(back, axis=-1, keepdims=True) - unit * jnp.mean(back * unit, axis=-1, keepdims=True)
            g[at, :] = up[at, :].astype(F32) + scale * back

        for store in stores:
            store.start()

    for i, (a, n) in enumerate(order):
        read(a, n).wait()
        if n >= 2:
            write(a, n - 2).wait()
        wides[a][n % 2] = lows[a][n % 2].astype(F32)
        write(a, n).start()
        if n + 2 < counts[a]:
            read(a, n + 2).start()
        if i == len(order) // 2:
            rest()
    for a in range(4):
        for n in range(max(0, counts[a] - 2), counts[a]):
            write(a, n).wait()
    for store in stores:
        store.wait()


def finish_all(q, u, o, d, joint, inward, own, upstream, small, bias_a, bias_b):
    arrays = [q, u, o, d, joint, inward, own, upstream, small, bias_a, bias_b]
    grads = (q, u, o, d)
    tall = (q.shape[0] // 6, u.shape[0] // 8, o.shape[0] // 2, d.shape[0] // 8)
    vector, qb, ub = own.shape[1:], (3, q.shape[1]), u.shape[1:]
    results = [(a.shape, F32) for a in grads] + [(own.shape, BF16), (own.shape, F32)]
    results += [(vector, F32)] * 6 + [(qb, F32), (ub, F32)]
    scratch = [pltpu.VMEM((2, t, a.shape[1]), k) for k in (BF16, F32) for t, a in zip(tall, grads)]
    scratch += [pltpu.VMEM(own.shape, BF16)] * 4
    scratch += [pltpu.VMEM(small.shape, F32), pltpu.VMEM(vector, BF16), pltpu.VMEM(vector, BF16)]
    scratch += [pltpu.VMEM(own.shape, BF16), pltpu.VMEM(own.shape, F32)]
    scratch += [pltpu.VMEM(v, F32) for v in [vector] * 5 + [qb, ub]]
    dma = pltpu.SemaphoreType.DMA
    scratch += [dma((4, 2)), dma((4, 2)), dma((7,)), dma((10,))]
    any_space = pl.BlockSpec(memory_space=pl.ANY)
    return pl.pallas_call(
        finish_body,
        out_shape=[jax.ShapeDtypeStruct(v, t) for v, t in results],
        in_specs=[any_space] * len(arrays),
        out_specs=[any_space] * len(results),
        scratch_shapes=scratch,
        compiler_params=pltpu.CompilerParams(vmem_limit_bytes=63 << 20),
        name="finish",
    )(*arrays)


def per_device(
    tokens,
    doc_lengths,
    ln1_gain,
    ln1_bias,
    qkv_weight,
    qkv_bias,
    out_weight,
    out_bias,
    ln2_gain,
    ln2_bias,
    up_weight,
    up_bias,
    down_weight,
    down_bias,
    cotangent,
):
    upstream, unit, activated, hidden_grad, projected_grad, mixed_low, w_qkv, w_up, w_out, w_down = (
        gather_all(
            tokens[0],
            cotangent[0],
            qkv_weight,
            up_weight,
            out_weight,
            down_weight,
            ln1_gain,
            ln1_bias,
            ln2_gain,
            ln2_bias,
            qkv_bias,
            up_bias,
            doc_lengths,
        )
    )

    joint, inward, qkv_out, up_out, out_out, down_out, small = settle_all(
        activated,
        upstream,
        unit,
        hidden_grad,
        projected_grad,
        mixed_low,
        w_qkv,
        w_up,
        w_out,
        w_down,
        ln1_gain,
        ln1_bias,
        ln2_gain,
        ln2_bias,
    )
    q_grad, u_grad, o_grad, d_grad, output, input_grad, *rest = finish_all(
        qkv_out.reshape(-1, qkv_out.shape[-1]),
        up_out,
        out_out,
        down_out,
        joint,
        inward,
        tokens[0],
        cotangent[0],
        small,
        out_bias,
        down_bias,
    )
    return (
        output[None],
        input_grad[None],
        rest[0],
        rest[1],
        q_grad.reshape(qkv_out.shape),
        rest[6],
        o_grad,
        rest[2],
        rest[3],
        rest[4],
        u_grad,
        rest[7],
        d_grad,
        rest[5],
    )


def solution(mesh):
    in_specs = (
        P("stream", "ctx", None),
        P("stream", None),
        P(),
        P(),
        P(None, "ctx", "head"),
        P(None, "head"),
        P("head", "ctx"),
        P(),
        P(),
        P(),
        P("ctx", "head"),
        P("head"),
        P("head", "ctx"),
        P(),
        P("stream", "ctx", None),
    )
    out_specs = (
        P("stream", "ctx", None),
        P("stream", "ctx", None),
        P(),
        P(),
        P(None, "ctx", "head"),
        P(None, "head"),
        P("head", "ctx"),
        P(),
        P(),
        P(),
        P("ctx", "head"),
        P("head"),
        P("head", "ctx"),
        P(),
    )
    split = mesh.shape["ctx"] * mesh.shape["head"]

    def whole(*arrays):
        heads, units = arrays[4].shape[2] // HEAD, arrays[10].shape[1]
        grouped = (mesh.shape["stream"], mesh.shape["ctx"], mesh.shape["head"]) == (4, 4, 2)
        fits = grouped and heads == split and units % (split * 512) == 0
        return jax.shard_map(
            per_device if fits else general_device,
            mesh=mesh,
            in_specs=in_specs,
            out_specs=out_specs,
            check_vma=False,
        )(*arrays)

    return whole
```

```python
from functools import partial
import math

import jax
import jax.numpy as jnp
import numpy as np
from jax import lax
from jax.experimental import pallas as pl
from jax.experimental.pallas import tpu as pltpu
from jax.sharding import PartitionSpec as P

HEAD = 256
ROT = 64


def layer_norm(values, gain, offset):
    centre = jnp.mean(values, axis=-1, keepdims=True)
    centred = values - centre
    spread = jnp.mean(centred * centred, axis=-1, keepdims=True)
    return centred * lax.rsqrt(spread + 1e-05) * gain + offset


def rotary(values, angles):
    half = angles.shape[-1]
    cosine = jnp.cos(angles)[:, None, :]
    sine = jnp.sin(angles)[:, None, :]
    first = values[..., :half]
    second = values[..., half : 2 * half]
    return jnp.concatenate(
        [first * cosine - second * sine, second * cosine + first * sine, values[..., 2 * half :]],
        axis=-1,
    )


def doc_starts(doc_sizes, positions):
    place = jnp.arange(doc_sizes.shape[0])
    before = place[None, :] < place[:, None]
    starts = jnp.sum(jnp.where(before, doc_sizes[None, :], 0), axis=1)
    return jnp.max(jnp.where(starts[None, :] <= positions[:, None], starts[None, :], 0), axis=1)


def general_device(
    tokens,
    doc_lengths,
    ln1_gain,
    ln1_bias,
    qkv_weight,
    qkv_bias,
    out_weight,
    out_bias,
    ln2_gain,
    ln2_bias,
    up_weight,
    up_bias,
    down_weight,
    down_bias,
    cotangent,
):
    inputs = tokens[0].astype(jnp.float32)
    count = inputs.shape[0]
    ctx_count = lax.axis_size("ctx")
    length = count * ctx_count
    positions = lax.axis_index("ctx") * count + jnp.arange(count, dtype=jnp.int32)
    starts = doc_starts(doc_lengths[0], positions)
    frequency = 10000.0 ** (-jnp.arange(0, ROT, 2, dtype=jnp.float32) / ROT)
    angles = (positions - starts).astype(jnp.float32)[:, None] * frequency[None, :]
    scale = HEAD ** (-0.5)
    full_qkv, full_out, full_up, full_down = (
        lax.all_gather(qkv_weight, "ctx", axis=1, tiled=True),
        lax.all_gather(out_weight, "ctx", axis=1, tiled=True),
        lax.all_gather(up_weight, "ctx", axis=0, tiled=True),
        lax.all_gather(down_weight, "ctx", axis=1, tiled=True),
    )
    gain_one = ln1_gain.astype(jnp.float32)
    offset_one = ln1_bias.astype(jnp.float32)
    gain_two = ln2_gain.astype(jnp.float32)
    offset_two = ln2_bias.astype(jnp.float32)
    low_one = layer_norm(inputs, gain_one, offset_one).astype(jnp.bfloat16)
    low_two = layer_norm(inputs, gain_two, offset_two).astype(jnp.bfloat16)
    projected = (
        jnp.einsum("nd,cde->cne", low_one, full_qkv, preferred_element_type=jnp.float32)
        + qkv_bias.astype(jnp.float32)[:, None, :]
    )
    width = projected.shape[2]
    local_heads = width // HEAD
    query = rotary(projected[0].reshape(count, local_heads, HEAD), angles).astype(jnp.bfloat16)
    keys_flat = (
        rotary(projected[1].reshape(count, local_heads, HEAD), angles)
        .reshape(count, width)
        .astype(jnp.bfloat16)
    )
    values_flat = projected[2].astype(jnp.bfloat16)
    all_keys, all_values = (
        lax.all_gather(keys_flat, "ctx", axis=0, tiled=True),
        lax.all_gather(values_flat, "ctx", axis=0, tiled=True),
    )
    block = math.gcd(length, 512)
    block_count = length // block
    key_blocks = all_keys.reshape(block_count, block, local_heads, HEAD)
    value_blocks = all_values.reshape(block_count, block, local_heads, HEAD)
    firsts = jnp.arange(block_count, dtype=jnp.int32) * block

    def block_scores(key_block, first):
        key_index = first + jnp.arange(block, dtype=jnp.int32)
        allowed = (key_index[None, :] <= positions[:, None]) & (
            key_index[None, :] >= starts[:, None]
        )
        scores = (
            jnp.einsum("qhe,khe->hqk", query, key_block, preferred_element_type=jnp.float32) * scale
        )
        return (jnp.where(allowed[None], scores, -1e30), allowed[None])

    def statistics(carry, item):
        running, norm_sum = carry
        key_block, first = item
        masked, allowed = block_scores(key_block, first)
        newest = jnp.maximum(running, jnp.max(masked, axis=-1))
        raised = jnp.where(allowed, jnp.exp(masked - newest[..., None]), 0.0)
        norm_sum = norm_sum * jnp.exp(running - newest) + jnp.sum(raised, axis=-1)
        return ((newest, norm_sum), None)

    initial = (
        jnp.full((local_heads, count), -1e30, jnp.float32),
        jnp.zeros((local_heads, count), jnp.float32),
    )
    (running, norm_sum), _ = lax.scan(statistics, initial, (key_blocks, firsts))
    log_norm = running + jnp.log(norm_sum)

    def share_block(key_block, first):
        masked, allowed = block_scores(key_block, first)
        return jnp.where(allowed, jnp.exp(masked - log_norm[..., None]), 0.0)

    def accumulate(mixed, item):
        key_block, value_block, first = item
        shares_low = share_block(key_block, first).astype(jnp.bfloat16)
        return (
            mixed
            + jnp.einsum(
                "hqk,khe->qhe", shares_low, value_block, preferred_element_type=jnp.float32
            ),
            None,
        )

    mixed, _ = lax.scan(
        accumulate,
        jnp.zeros((count, local_heads, HEAD), jnp.float32),
        (key_blocks, value_blocks, firsts),
    )
    mixed_low = mixed.reshape(count, width).astype(jnp.bfloat16)
    attention = jnp.dot(mixed_low, full_out, preferred_element_type=jnp.float32)
    hidden = jnp.dot(low_two, full_up, preferred_element_type=jnp.float32) + up_bias.astype(
        jnp.float32
    )
    activated = jax.nn.gelu(hidden, approximate=False).astype(jnp.bfloat16)
    branches = attention + jnp.dot(activated, full_down, preferred_element_type=jnp.float32)
    joint = lax.psum(branches.astype(jnp.bfloat16), "head").astype(jnp.float32)
    output = inputs + joint + out_bias.astype(jnp.float32) + down_bias.astype(jnp.float32)
    upstream = cotangent[0]
    down_grad = jnp.dot(activated.T, upstream, preferred_element_type=jnp.float32)
    activated_grad = jnp.dot(upstream, full_down.T, preferred_element_type=jnp.float32)
    _, gelu_back = jax.vjp(partial(jax.nn.gelu, approximate=False), hidden)
    hidden_grad = gelu_back(activated_grad)[0].astype(jnp.bfloat16)
    up_grad = jnp.dot(low_two.T, hidden_grad, preferred_element_type=jnp.float32)
    up_bias_grad = jnp.sum(hidden_grad.astype(jnp.float32), axis=0)
    normed_two_grad = jnp.dot(hidden_grad, full_up.T, preferred_element_type=jnp.float32)
    out_grad = jnp.dot(mixed_low.T, upstream, preferred_element_type=jnp.float32)
    mixed_grad = jnp.dot(upstream, full_out.T, preferred_element_type=jnp.float32).astype(
        jnp.bfloat16
    )
    mixed_grad_heads = mixed_grad.reshape(count, local_heads, HEAD)
    delta = jnp.sum(mixed_grad_heads.astype(jnp.float32) * mixed, axis=-1).T

    def backward_block(query_grad, item):
        key_block, value_block, first = item
        shares = share_block(key_block, first)
        share_grad = jnp.einsum(
            "qhe,khe->hqk", mixed_grad_heads, value_block, preferred_element_type=jnp.float32
        )
        score_grad = (shares * (share_grad - delta[..., None])).astype(jnp.bfloat16)
        query_grad = (
            query_grad
            + jnp.einsum("hqk,khe->qhe", score_grad, key_block, preferred_element_type=jnp.float32)
            * scale
        )
        key_grad = (
            jnp.einsum("hqk,qhe->khe", score_grad, query, preferred_element_type=jnp.float32)
            * scale
        )
        value_grad = jnp.einsum(
            "hqk,qhe->khe",
            shares.astype(jnp.bfloat16),
            mixed_grad_heads,
            preferred_element_type=jnp.float32,
        )
        return (
            query_grad,
            jnp.concatenate(
                [key_grad.reshape(block, width), value_grad.reshape(block, width)], axis=1
            ),
        )

    query_grad, key_terms = lax.scan(
        backward_block,
        jnp.zeros((count, local_heads, HEAD), jnp.float32),
        (key_blocks, value_blocks, firsts),
    )
    own_grads = lax.psum_scatter(
        key_terms.reshape(length, 2 * width).astype(jnp.bfloat16),
        "ctx",
        scatter_dimension=0,
        tiled=True,
    ).astype(jnp.float32)
    query_pre = rotary(query_grad, -angles).reshape(count, width)
    key_pre = rotary(own_grads[:, :width].reshape(count, local_heads, HEAD), -angles).reshape(
        count, width
    )
    projected_grad = jnp.stack([query_pre, key_pre, own_grads[:, width:]]).astype(jnp.bfloat16)
    qkv_grad = jnp.einsum(
        "nd,cne->cde", low_one, projected_grad, preferred_element_type=jnp.float32
    )
    qkv_bias_grad = jnp.sum(projected_grad.astype(jnp.float32), axis=1)
    normed_one_grad = jnp.einsum(
        "cne,cde->nd", projected_grad, full_qkv, preferred_element_type=jnp.float32
    )
    normed_one_grad, normed_two_grad = (
        lax.psum(normed_one_grad.astype(jnp.bfloat16), "head").astype(jnp.float32),
        lax.psum(normed_two_grad.astype(jnp.bfloat16), "head").astype(jnp.float32),
    )
    _, norm_back_one = jax.vjp(layer_norm, inputs, gain_one, offset_one)
    input_one, gain_grad_one, offset_grad_one = norm_back_one(normed_one_grad)
    _, norm_back_two = jax.vjp(layer_norm, inputs, gain_two, offset_two)
    input_two, gain_grad_two, offset_grad_two = norm_back_two(normed_two_grad)
    upstream_wide = upstream.astype(jnp.float32)
    input_grad = upstream_wide + input_one + input_two
    bias_grad = jnp.sum(upstream_wide, axis=0)
    small = lax.psum(
        (
            gain_grad_one,
            offset_grad_one,
            qkv_bias_grad,
            bias_grad,
            gain_grad_two,
            offset_grad_two,
            up_bias_grad,
        ),
        ("stream", "ctx"),
    )
    slices = (
        lax.psum_scatter(
            qkv_grad.astype(jnp.bfloat16), "ctx", scatter_dimension=1, tiled=True
        ).astype(jnp.float32),
        lax.psum_scatter(
            out_grad.astype(jnp.bfloat16), "ctx", scatter_dimension=1, tiled=True
        ).astype(jnp.float32),
        lax.psum_scatter(
            up_grad.astype(jnp.bfloat16), "ctx", scatter_dimension=0, tiled=True
        ).astype(jnp.float32),
        lax.psum_scatter(
            down_grad.astype(jnp.bfloat16), "ctx", scatter_dimension=1, tiled=True
        ).astype(jnp.float32),
    )
    shards = (
        lax.psum(slices[0].astype(jnp.bfloat16), "stream").astype(jnp.float32),
        lax.psum(slices[1].astype(jnp.bfloat16), "stream").astype(jnp.float32),
        lax.psum(slices[2].astype(jnp.bfloat16), "stream").astype(jnp.float32),
        lax.psum(slices[3].astype(jnp.bfloat16), "stream").astype(jnp.float32),
    )
    return (
        output.astype(jnp.bfloat16)[None],
        input_grad[None],
        small[0],
        small[1],
        shards[0],
        small[2],
        shards[1],
        small[3],
        small[4],
        small[5],
        shards[2],
        small[6],
        shards[3],
        small[3],
    )


MESH = pl.DeviceIdType.MESH
FRONT_PLAN = (
    "z0", "l0", "z1", "P", "T", "N0", "s0", "L01", "z2", "l1", "z3", "p0", "N1", "f0", "Q0", "Q1", "s1", "L02", "s2", "p1", "L11", "p2", "N2", "Q2", "f1", "F0", "F1", "F2", "s3",
    "L03", "L12", "N3", "Q3", "p3", "F3", "A0", "A1", "A2", "A3", "f2", "B0", "B1", "L13", "f3", "D0", "D1", "B2", "D2", "B3", "D3", "E",
)
F32, BF16 = jnp.float32, jnp.bfloat16


def dot(a, b, over):
    return lax.dot_general(a, b, ((over[0:1], over[1:2]), ((), ())), preferred_element_type=F32)


def span(index, size):
    return pl.ds(pl.multiple_of(index * size, size), size)


def places():
    return lax.axis_index("stream"), lax.axis_index("ctx"), lax.axis_index("head")


def greet(peers):
    barrier = pltpu.get_barrier_semaphore()
    for peer in peers:
        pl.semaphore_signal(barrier, inc=1, device_id=peer, device_id_type=MESH)
    pl.semaphore_wait(barrier, len(peers))


def gather_body(
    x_ref, g_ref, qkv_ref, up_ref, out_ref, down_ref,
    gain_a_ref, off_a_ref, gain_b_ref, off_b_ref, qkv_bias_ref, up_bias_ref, rate_in, docs_ref,
    g_out, unit_out, act_out, dh_out, dqkv_out, mixed_out, qkv_out, up_out, out_out, down_out,
    z_send, z_recv, x_send, x_recv, y_send, y_recv, fx_send, fx_recv, fy_send, fy_recv,
    line_send, line_recv, core_send, core_recv, own_sem, give_sem, block_sem, small_sem,
    x_all, g_all, qkv_all, up_all, out_all, down_all,
    low_one, low_two, unit, query, keys, values, act, dh, dqkv, mixed_low,
    slope, mixed, norm, key_grad, value_grad, turn_ref, start_ref,
    gain_a, off_a, gain_b, off_b, qkv_bias, up_bias, rate_ref, rows_ref, bias_ref,
):
    s, c, h = places()
    x_peer = s + 1 - 2 * lax.rem(s, 2)
    y_peer = lax.rem(s + 2, 4)
    across = ((x_peer, c, h), (y_peer, c, h))
    core_peer = (s, c, 1 - h)
    ring = [(s, lax.rem(c + k, 4), h) for k in (1, 2, 3)]

    count = x_ref.shape[0]
    slab, width, units = up_ref.shape[0], out_ref.shape[0] // 4, down_ref.shape[0] // 4
    quarter, half_count = slab // 4, count // 2

    def rows(base, size):
        return pl.ds(pl.multiple_of(base, size), size)

    def landed(m, r, part, half):
        def cut(total):
            size = total // 4
            if half is None:
                return part * size, size
            return part * size + half * (size // 2), size // 2

        if m == 0:
            at, size = cut(slab)
            return qkv_all.at[:, rows(r * slab + at, size), :]
        if m == 1:
            at, size = cut(slab)
            return up_all.at[rows(r * slab + at, size), :]
        if m == 2:
            at, size = cut(width)
            return out_all.at[rows(at, size), span(r, slab)]
        at, size = cut(units)
        return down_all.at[rows(at, size), span(r, slab)]

    def piece(m, to, part=None):
        if m == 0:
            inner = slice(None) if part is None else span(part, quarter)
            return qkv_ref.at[:, inner, span(to, width)]
        if m == 1:
            inner = slice(None) if part is None else span(part, quarter)
            return up_ref.at[inner, span(to, units)]
        size = width if m == 2 else units
        ref = out_ref if m == 2 else down_ref
        if part is None:
            return ref.at[span(to, size), :]
        return ref.at[rows(to * size + part * (size // 4), size // 4), :]

    def whole_piece(m, r):
        if m == 0:
            return qkv_all.at[:, span(r, slab), :]
        if m == 1:
            return up_all.at[span(r, slab), :]
        return (out_all if m == 2 else down_all).at[:, span(r, slab)]

    def remote(src, dst, send, recv, to):
        return pltpu.make_async_remote_copy(
            src_ref=src, dst_ref=dst, send_sem=send, recv_sem=recv, device_id=to, device_id_type=MESH
        )

    def z_copy(m, k):
        to = lax.rem(c + 4 - k, 4)
        return remote(
            piece(m, to, s), landed(m, c, s, None), z_send.at[m, k - 1], z_recv.at[m, k - 1], (s, to, h)
        )

    def direct(m, k, axis):
        r = lax.rem(c + k, 4)
        send, recv = (x_send, x_recv) if axis == 0 else (y_send, y_recv)
        here = landed(m, r, s, None)
        return remote(here, here, send.at[m, k - 1], recv.at[m, k - 1], across[axis])

    def onward(m, k, axis):
        r = lax.rem(c + k, 4)
        send, recv = (fx_send, fx_recv) if axis == 0 else (fy_send, fy_recv)
        here = landed(m, r, y_peer if axis == 0 else x_peer, 1 if axis == 0 else 0)
        return remote(here, here, send.at[m, k - 1], recv.at[m, k - 1], across[axis])

    lines = ((x_ref, x_all), (g_ref, g_all))

    def block(a, origin):
        return lines[a][1].at[rows(origin * count + h * half_count, half_count), :]

    def line_copy(a, t, side):
        origin = c - t if side == 0 else c + t
        src = lines[a][0].at[span(h, half_count), :] if t == 0 else block(a, origin)
        to = c + 1 if side == 0 else c - 1
        return remote(
            src, block(a, origin), line_send.at[a, side, t], line_recv.at[a, side, t], (s, to, h)
        )

    def core_copy(a, t, side):
        origin = c - t if side == 0 else c + t
        here = block(a, origin)
        return remote(here, here, core_send.at[a, side, t - 1], core_recv.at[a, side, t - 1], core_peer)

    def sends(t, side):
        if side == 0:
            return (c >= t) & (c < 3)
        return (c + t <= 3) & (c > 0)

    def gets(t, side):
        return c >= t if side == 0 else c + t <= 3

    def line_step(a, t):
        for side in (0, 1):
            @pl.when(gets(t, side))
            def _():
                line_copy(a, t - 1, side).wait_recv()
                core_copy(a, t, side).start()

            if t < 3:
                @pl.when(sends(t, side))
                def _():
                    line_copy(a, t, side).start()

    near = (1, 3, 2)
    order = [(m, k) for m in (0, 1, 3, 2) for k in near]

    def start_z(m):
        for k in near:
            z_copy(m, k).start()

    def pass_on(m):
        for k in near:
            direct(m, k, 0).wait_recv()
            onward(m, k, 1).start()
            direct(m, k, 1).wait_recv()
            onward(m, k, 0).start()

    def spread(m):
        for k in near:
            z_copy(m, k).wait_recv()
            direct(m, k, 0).start()
            direct(m, k, 1).start()

    ins = [
        pltpu.make_async_copy(a, b, own_sem.at[i])
        for i, (a, b) in enumerate(
            [(lines[a][0], lines[a][1].at[span(c, count), :]) for a in (0, 1)]
            + [(piece(m, c), whole_piece(m, c)) for m in range(4)]
        )
    ]
    for copy in ins:
        copy.start()
    tile = count
    length, model = x_all.shape
    rot = turn_ref.shape[2]
    span_rot = rot // 4
    scale = width**-0.5

    def finish(m):
        for k in near:
            onward(m, k, 0).wait_recv()
            onward(m, k, 1).wait_recv()
        ins[2 + m].wait()

    def give(i):
        pairs = (
            (qkv_all, qkv_out), (up_all, up_out), (out_all, out_out), (down_all, down_out),
            (act, act_out), (dh, dh_out), (dqkv, dqkv_out), (mixed_low, mixed_out),
        )
        return pltpu.make_async_copy(*pairs[i], give_sem.at[i])

    def give_block(a, origin):
        src, dst = ((unit, unit_out), (g_all, g_out))[a]
        at = span(origin, tile)
        return pltpu.make_async_copy(src.at[at, :], dst.at[at, :], block_sem.at[a])

    def blocks_of(t, do):
        if t == 0:
            do(c)
            return

        @pl.loop(0, 2)
        def _(side):
            origin = c + t * (2 * side - 1)

            @pl.when((origin >= 0) & (origin <= 3))
            def _():
                do(origin)

    def core_wait(a, t):
        for side in (0, 1):
            @pl.when(gets(t, side))
            def _():
                core_copy(a, t, side).wait_recv()

    def norm_block(origin):
        tall = 32

        @pl.loop(0, tile // tall)
        def _(i):
            at = pl.ds(pl.multiple_of(origin * tile + i * tall, tall), tall)
            wide = x_all[at, :].astype(F32)
            centred = wide - jnp.mean(wide, axis=-1, keepdims=True)
            spread_of = jnp.mean(centred * centred, axis=-1, keepdims=True)
            found = centred * lax.rsqrt(spread_of + 1e-05)
            unit[at, :] = found.astype(BF16)
            low_one[at, :] = (found * rows_ref[0:1, :] + rows_ref[1:2, :]).astype(BF16)
            low_two[at, :] = (found * rows_ref[2:3, :] + rows_ref[3:4, :]).astype(BF16)

        give_block(0, origin).start()

    smalls = [
        pltpu.make_async_copy(a, b, small_sem.at[i])
        for i, (a, b) in enumerate(
            (
                (gain_a_ref, gain_a), (off_a_ref, off_a), (gain_b_ref, gain_b), (off_b_ref, off_b),
                (qkv_bias_ref, qkv_bias), (up_bias_ref, up_bias), (rate_in, rate_ref),
            )
        )
    ]
    for copy in smalls:
        copy.start()

    def parameters():
        for copy in smalls:
            copy.wait()
        for i, ref in enumerate((gain_a, off_a, gain_b, off_b)):
            rows_ref[i : i + 1, :] = ref[...].astype(F32).reshape(1, model)
        part = qkv_bias[:, span(c, width)].astype(F32)
        for p in range(3):
            bias_ref[0:1, p * width : (p + 1) * width] = part[p : p + 1]
        bias_ref[1:2, :] = up_bias[span(c, units)].astype(F32).reshape(1, units)

    def tables():
        starts, total = [], docs_ref[0, 0] * 0
        for j in range(docs_ref.shape[1]):
            starts.append(total)
            total = total + docs_ref[0, j]

        @pl.loop(0, length // tile)
        def _(i):
            at = span(i, tile)
            place = i * tile + lax.broadcasted_iota(jnp.int32, (tile, rot), 0)
            lane = lax.broadcasted_iota(jnp.int32, (tile, rot), 1)
            first = jnp.zeros((tile, rot), jnp.int32)
            for start in starts:
                first = jnp.where(start <= place, jnp.maximum(first, start), first)
            start_ref[at, :] = first[:, 0:1]
            angle = (place - first).astype(F32) * rate_ref[0:1, :]
            sine = jnp.sin(angle)
            turn_ref[0, at, :] = jnp.where(lane < 2 * span_rot, jnp.cos(angle), 1.0)
            turn_ref[1, at, :] = jnp.where((lane >= span_rot) & (lane < 2 * span_rot), sine, 0.0)
            turn_ref[2, at, :] = jnp.where(lane < span_rot, -sine, 0.0)

    def turned(v, at, sign):
        near_part = v[:, :rot]
        moved = pltpu.roll(near_part, span_rot, 1) * turn_ref[1, at, :] + pltpu.roll(near_part, rot - span_rot, 1) * turn_ref[2, at, :]
        return jnp.concatenate([near_part * turn_ref[0, at, :] + sign * moved, v[:, rot:]], axis=1)

    def project(i):
        at = span(i, tile)
        for p, into in enumerate((query, keys, values)):
            part = dot(low_one[at, :], qkv_all[p], (1, 0)) + bias_ref[0:1, p * width : (p + 1) * width]
            into[at, :] = (turned(part, at, 1.0) if p < 2 else part).astype(BF16)

    def allowed_of(i, wide):
        first = lax.broadcasted_iota(jnp.int32, (tile, wide), 1)
        place = i * tile + lax.broadcasted_iota(jnp.int32, (tile, wide), 0)
        return (first <= place) & (first >= start_ref[span(i, tile), :])

    def attend(i):
        wide = (i + 1) * tile
        at = slice(i * tile, wide)
        scores = dot(query[at, :], keys[0:wide, :], (1, 1)) * scale
        allowed = allowed_of(i, wide)
        masked = jnp.where(allowed, scores, -1e30)
        peak = jnp.max(masked, axis=-1, keepdims=True)
        raised = jnp.where(allowed, jnp.exp(masked - peak), 0.0)
        total = jnp.sum(raised, axis=-1, keepdims=True)
        norm[at, :] = peak + jnp.log(total)
        found = dot((raised / total).astype(BF16), values[0:wide, :], (1, 0))
        mixed[at, :] = found
        mixed_low[at, :] = found.astype(BF16)

    def feed(i):
        at = span(i, tile)
        for j in range(units // 256):
            cols = slice(j * 256, (j + 1) * 256)
            hidden = dot(low_two[at, :], up_all[:, cols], (1, 0)) + bias_ref[1:2, cols]
            share = 0.5 + 0.5 * lax.erf(hidden * (0.5**0.5))
            act[at, cols] = (hidden * share).astype(BF16)
            slope[at, cols] = share + hidden * jnp.exp(-0.5 * hidden * hidden) * ((0.5 / jnp.pi) ** 0.5)

    def back_attend(origin):
        at = span(origin, tile)
        grad = dot(g_all[at, :], out_all[...], (1, 1)).astype(BF16)
        scores = dot(query[at, :], keys[...], (1, 1)) * scale
        shares = jnp.where(allowed_of(origin, length), jnp.exp(scores - norm[at, :]), 0.0)
        delta = jnp.sum(grad.astype(F32) * mixed[at, :], axis=-1, keepdims=True)
        share_grad = dot(grad, values[...], (1, 1))
        score_grad = (shares * (share_grad - delta)).astype(BF16)
        value_grad[...] += dot(shares.astype(BF16), grad, (0, 0))
        key_grad[...] += dot(score_grad, query[at, :], (0, 0))
        part = dot(score_grad, keys[...], (1, 0)) * scale
        dqkv[at, 0:width] = turned(part, at, -1.0).astype(BF16)

    def back_feed(origin):
        at = span(origin, tile)
        for j in range(units // 256):
            cols = slice(j * 256, (j + 1) * 256)
            part = dot(g_all[at, :], down_all[cols, :], (1, 1))
            dh[at, cols] = (part * slope[at, cols]).astype(BF16)

    def start_line(a):
        for side in (0, 1):
            @pl.when(sends(0, side))
            def _():
                line_copy(a, 0, side).start()

    def close():
        give(5).start()

        @pl.loop(0, length // tile)
        def _(i):
            at = span(i, tile)
            dqkv[at, width : 2 * width] = turned(key_grad[at, :] * scale, at, -1.0).astype(BF16)
            dqkv[at, 2 * width : 3 * width] = value_grad[at, :].astype(BF16)

        give(6).start()

    def run(step):
        op, rest = step[0], [int(d) for d in step[1:]]
        if op == "z":
            start_z(*rest)
        elif op == "s":
            spread(*rest)
        elif op == "p":
            pass_on(*rest)
        elif op == "f":
            finish(*rest)
            give(*rest).start()
        elif op == "l":
            start_line(*rest)
        elif op == "L":
            line_step(*rest)
        elif op == "N":
            if rest[0]:
                core_wait(0, *rest)
            else:
                ins[0].wait()
            blocks_of(*rest, norm_block)
        elif op == "P":
            parameters()
        elif op == "T":
            tables()
        elif op == "Q":
            blocks_of(*rest, project)
        elif op == "A":
            attend(*rest)
            if rest[0] == 3:
                give(7).start()
        elif op == "F":
            blocks_of(*rest, feed)
            if rest[0] == 3:
                give(4).start()
        elif op == "B":
            if rest[0]:
                core_wait(1, *rest)
            else:
                ins[1].wait()
            blocks_of(*rest, back_attend)
        elif op == "D":
            blocks_of(*rest, back_feed)
        elif op == "E":
            close()

    greet([*across, core_peer, *ring])
    key_grad[...] = jnp.zeros_like(key_grad)
    value_grad[...] = jnp.zeros_like(value_grad)
    for step in FRONT_PLAN:
        run(step)
    for t in (0, 1, 2, 3):
        blocks_of(t, lambda origin: give_block(1, origin).start())
    for a in (0, 1):
        for side in (0, 1):
            for t in (1, 2, 3):
                @pl.when(gets(t, side))
                def _():
                    core_copy(a, t, side).wait_send()
                @pl.when(sends(t - 1, side))
                def _():
                    line_copy(a, t - 1, side).wait_send()
    for m, k in order:
        z_copy(m, k).wait_send()
        for axis in (0, 1):
            direct(m, k, axis).wait_send()
            onward(m, k, axis).wait_send()
    pltpu.make_async_copy(unit, unit_out, block_sem.at[0]).wait()
    pltpu.make_async_copy(g_all, g_out, block_sem.at[1]).wait()
    for i in range(8):
        give(i).wait()


def gather_all(tokens, cotangent, w_qkv, w_up, w_out, w_down, gain_a, off_a, gain_b, off_b, b_qkv, b_up, docs):
    count, model = tokens.shape
    length = 4 * count
    width, units = w_out.shape[0] // 4, w_down.shape[0] // 4
    frequency = 10000.0 ** (-np.arange(0, ROT, 2, dtype=np.float32) / np.float32(ROT))
    rate = jnp.asarray(np.tile(frequency.astype(np.float32), (8, 4)))
    dma = pltpu.SemaphoreType.DMA
    weights = [(3, model, width), (model, units), (width, model), (units, model)]
    wide, narrow = (length, model), (length, width)
    results = [wide, wide, (length, units), (length, units), (length, 3 * width), narrow] + weights
    scratch = [dma((4, 3))] * 10 + [dma((2, 2, 3))] * 4 + [dma((6,)), dma((8,)), dma((2,)), dma((7,))]
    scratch += [
        pltpu.VMEM(v, BF16)
        for v in [wide, wide] + weights + [wide] * 3 + [narrow] * 3
        + [(length, units)] * 2 + [(length, 3 * width), narrow]
    ]
    scratch += [pltpu.VMEM(v, F32) for v in ((length, units), narrow, (length, 1), narrow, narrow)]
    scratch += [pltpu.VMEM((3, length, rate.shape[1]), F32), pltpu.VMEM((length, 1), jnp.int32)]
    scratch += [pltpu.VMEM((model,), BF16)] * 4 + [pltpu.VMEM(b_qkv.shape, BF16), pltpu.VMEM(b_up.shape, BF16)]
    scratch += [pltpu.VMEM(v, F32) for v in (rate.shape, (8, model), (8, units))]
    any_space = pl.BlockSpec(memory_space=pl.ANY)
    return pl.pallas_call(
        gather_body,
        out_shape=[jax.ShapeDtypeStruct(v, BF16) for v in results],
        in_specs=[any_space] * 13 + [pl.BlockSpec(memory_space=pltpu.SMEM)],
        out_specs=[any_space] * 10,
        scratch_shapes=scratch,
        compiler_params=pltpu.CompilerParams(
            collective_id=0, has_side_effects=True, vmem_limit_bytes=63 << 20
        ),
        name="gather",
    )(
        tokens, cotangent, w_qkv, w_up, w_out, w_down, gain_a, off_a, gain_b, off_b, b_qkv, b_up, rate, docs
    )


LEADS = (4, 4, 4, 4, 1, 1)
BACK_PLAN = (
    "O", "14", "D", "B0", "24", "B1", "R0", "P", "Q", "11", "12", "25", "Z4", "22", "U", "13", "10", "I0", "I1", "Z5", "X4", "20", "23", "21", "a", "Z0", "Z2", "b", "X5", "X0", "S0", "N4",
    "Z3", "Z1", "N5", "X3", "c", "X2", "R1", "X1", "N3", "N1", "d", "N0", "N2", "e", "S1",
)
def settle_body(
    act_in, up_in, unit_in, dh_in, dqkv_in, mixed_in, wq_in, wu_in, wo_in, wd_in,
    gain_a_ref, off_a_ref, gain_b_ref, off_b_ref,
    joint, inward, o0, o1, o2, o3, small_out,
    s1x_send, s1x_recv, s1y_send, s1y_recv, s2x_send, s2x_recv, s2y_send, s2y_recv,
    x_send, x_recv, y_send, y_recv, fx_send, fx_recv, fy_send, fy_recv,
    z_send, z_recv, keep_sem, load_sem, weight_sem,
    core_send, core_recv, row_send, row_recv, back_send, back_recv, back_sem,
    sum_send, sum_recv, sum_sem, small_sem,
    act, up, unit, dh, dqkv, mixed, w_wide, w_out, w_qkv, *rest,
):
    grads, first, second = rest[0:6], (rest[6:18:2], rest[7:18:2]), (rest[18:30:2], rest[19:30:2])
    (
        own_half, core_half, send_half, row_parts, done_half,
        sums, sums_core, slots, total_own, total_x, total_y,
        gain_a, off_a, gain_b, off_b, rows_ref, low_ref,
    ) = rest[30:]
    s, c, h = places()
    x_at, y_at = lax.rem(s, 2), lax.div(s, 2)
    x_off, y_off = 1 - x_at, 1 - y_at
    x_peer, y_peer = y_at * 2 + x_off, y_off * 2 + x_at
    across = ((x_peer, c, h), (y_peer, c, h))
    core_peer = (s, c, 1 - h)
    near = (1, 3, 2)
    outs = (o0, o1, o2, o3)
    first, second = list(zip(*first)), list(zip(*second))
    slab = o2.shape[-1]
    length, model = up.shape
    units, width = act.shape[1], mixed.shape[1]
    half_cols = model // 2
    count = joint.shape[0]
    tile = 256

    def remote(src, dst, send, recv, to):
        return pltpu.make_async_remote_copy(
            src_ref=src, dst_ref=dst, send_sem=send, recv_sem=recv, device_id=to, device_id_type=MESH
        )

    loads = [
        pltpu.make_async_copy(a, b, load_sem.at[i])
        for i, (a, b) in enumerate(
            ((act_in, act), (up_in, up), (dh_in, dh), (unit_in, unit), (dqkv_in, dqkv), (mixed_in, mixed))
        )
    ]
    for load in loads[:2]:
        load.start()
    greet([*across, core_peer, *[(s, lax.rem(c + k, 4), h) for k in near]])

    smalls = [
        pltpu.make_async_copy(a, b, small_sem.at[i])
        for i, (a, b) in enumerate(
            ((gain_a_ref, gain_a), (off_a_ref, off_a), (gain_b_ref, gain_b), (off_b_ref, off_b))
        )
    ]
    for copy in smalls:
        copy.start()

    def side(which):
        return 1 - h if which == 0 else h

    def weight_load(i):
        at = span(side(i % 2), half_cols)
        if i < 2:
            return pltpu.make_async_copy(wd_in.at[:, at], w_wide.at[i], weight_sem.at[i])
        if i < 4:
            return pltpu.make_async_copy(wu_in.at[at, :], w_wide.at[i % 2], weight_sem.at[i])
        if i < 6:
            return pltpu.make_async_copy(wo_in.at[:, at], w_out.at[i % 2], weight_sem.at[i])
        return pltpu.make_async_copy(wq_in.at[:, at, :], w_qkv.at[i % 2], weight_sem.at[i])

    for load in loads[2:]:
        load.start()
    for i in (0, 4, 1, 5, 6, 7):
        weight_load(i).start()

    def one(m, half):
        src = grads[m].at[:, :, x_off, 0] if half == 0 else grads[m].at[:, y_off, :, 1]
        send, recv = (s1x_send, s1x_recv) if half == 0 else (s1y_send, s1y_recv)
        return remote(src, first[m][half], send.at[m], recv.at[m], across[half])

    def two(m, half):
        src = first[m][half].at[:, y_off if half == 0 else x_off]
        send, recv = (s2y_send, s2y_recv) if half == 0 else (s2x_send, s2x_recv)
        return remote(src, second[m][half], send.at[m], recv.at[m], across[1 - half])

    def add_first(m, half):
        into, more = first[m][half], grads[m]
        lead, _, height, _ = into.shape
        tall = min(height, 32)

        @pl.loop(0, lead * 2 * (height // tall))
        def _(i):
            at = lax.rem(i, height // tall)
            pair = lax.div(i, height // tall)
            l, j, rows = lax.div(pair, 2), lax.rem(pair, 2), span(at, tall)
            term = more[l, j, x_at, 0, rows, :] if half == 0 else more[l, y_at, j, 1, rows, :]
            into[l, j, rows, :] = (into[l, j, rows, :].astype(F32) + term.astype(F32)).astype(BF16)

    def add_second(m, half):
        into, more = second[m][half], first[m][half]
        mine = y_at if half == 0 else x_at
        lead, height, _ = into.shape
        tall = min(height, 32)

        @pl.loop(0, lead * (height // tall))
        def _(i):
            l, rows = lax.div(i, height // tall), span(lax.rem(i, height // tall), tall)
            term = more[l, mine, rows, :].astype(F32)
            into[l, rows, :] = (into[l, rows, :].astype(F32) + term).astype(BF16)

    def share_of(m, half, to):
        ref = second[m][half]
        return ref.at[to] if m < 4 else ref.at[0, :, span(to, slab)]

    def home(m, half):
        if m < 3:
            return outs[0].at[m, s, half, :, span(c, width)]
        if m == 3:
            return outs[1].at[s, half, :, span(c, units)]
        return outs[m - 2].at[c, s, half]

    def z_copy(m, half, k):
        to = lax.rem(c + 4 - k, 4)
        i = (m * 2 + half) * 3 + k - 1
        return remote(share_of(m, half, to), home(m, half), z_send.at[i], z_recv.at[i], (s, to, h))

    def keep(m, half):
        return pltpu.make_async_copy(share_of(m, half, c), home(m, half), keep_sem.at[m, half])

    def quarter(m, q, half=None):
        at = (q,) if half is None else (q, half)
        if m < 3:
            return outs[0].at[(m, *at)]
        if m == 3:
            return outs[1].at[at]
        return outs[m - 2].at[(slice(None), *at)]

    def direct(m, axis):
        send, recv = (x_send, x_recv) if axis == 0 else (y_send, y_recv)
        here = quarter(m, s)
        return remote(here, here, send.at[m], recv.at[m], across[axis])

    def onward(m, axis):
        send, recv = (fx_send, fx_recv) if axis == 0 else (fy_send, fy_recv)
        here = quarter(m, y_peer if axis == 0 else x_peer, 1 - axis)
        return remote(here, here, send.at[m], recv.at[m], across[axis])

    finals = (joint, inward)

    def core_copy(a):
        return remote(send_half, core_half.at[a], core_send.at[a], core_recv.at[a], core_peer)

    def row_copy(a, k):
        to = lax.rem(c + 4 - k, 4)
        return remote(
            own_half.at[a, span(to, count)], row_parts.at[a, k - 1],
            row_send.at[a, k - 1], row_recv.at[a, k - 1], (s, to, h),
        )

    def back_copy(a):
        return remote(
            done_half.at[a], finals[a].at[:, span(h, half_cols)], back_send.at[a], back_recv.at[a], core_peer
        )

    def back_keep(a):
        return pltpu.make_async_copy(done_half.at[a], finals[a].at[:, span(h, half_cols)], back_sem.at[a])

    def line_start(a):
        core_copy(a).wait_recv()
        tall = 32

        @pl.loop(0, length // tall)
        def _(i):
            rows = span(i, tall)
            own_half[a, rows, :] = (
                own_half[a, rows, :].astype(F32) + core_half[a, rows, :].astype(F32)
            ).astype(BF16)

        for k in near:
            row_copy(a, k).start()

    def line_sum(a):
        for k in near:
            row_copy(a, k).wait_recv()
        tall = 32

        @pl.loop(0, count // tall)
        def _(i):
            rows = span(i, tall)
            total = own_half[a, pl.ds(pl.multiple_of(c * count + i * tall, tall), tall), :].astype(F32)
            for k in range(3):
                total = total + row_parts[a, k, rows, :].astype(F32)
            done_half[a, rows, :] = total.astype(BF16)

        back_copy(a).start()
        back_keep(a).start()

    def down_grad():
        rows = units // 8

        def part_of(y, x):
            left = act[:, span(2 * y + x, 2 * rows)]
            for j in range(model // 512):
                cols = slice(j * 512, (j + 1) * 512)
                part = dot(left, up[:, cols], (0, 0)).astype(BF16)
                for half in (0, 1):
                    grads[5][0, y, x, half, :, cols] = part[half * rows : (half + 1) * rows]

        part_of(y_off, x_off)
        part_of(y_at, x_off)
        one(5, 0).start()
        part_of(y_off, x_at)
        one(5, 1).start()
        part_of(y_at, x_at)

    def out_grad():
        rows = width // 8
        for j in range(model // 512):
            part = dot(mixed[...], up[:, j * 512 : (j + 1) * 512], (0, 0)).astype(BF16)
            for i in range(8):
                grads[4][0, i // 4, (i // 2) % 2, i % 2, :, j * 512 : (j + 1) * 512] = part[i * rows : (i + 1) * rows]

    same = lax.broadcasted_iota(jnp.int32, (tile, tile), 0) == lax.broadcasted_iota(jnp.int32, (tile, tile), 1)
    eye = jnp.where(same, 1.0, 0.0).astype(BF16)

    def columns(t):
        return dot(eye, low_ref[:, span(t, tile)], (1, 1))

    def scaled(part, column, at, column_sum):
        return (part * column[:, at : at + 1] + column[:, at + 1 : at + 2] * column_sum).astype(BF16)

    def column_sum(ref, cols):
        total = jnp.zeros((1, cols.stop - cols.start), F32)
        for i in range(length // tile):
            total = total + jnp.sum(ref[i * tile : (i + 1) * tile, cols].astype(F32), axis=0, keepdims=True)
        return total

    def up_grad():
        rows = tile // 4

        @pl.loop(0, model // tile)
        def _(t):
            left, column = unit[:, span(t, tile)], columns(t)
            for j in range(units // 512):
                cols = slice(j * 512, (j + 1) * 512)
                near_sum = sums[5:6, 3 * width + j * 512 : 3 * width + (j + 1) * 512]
                part = scaled(dot(left, dh[:, cols], (0, 0)), column, 2, near_sum)
                for i in range(4):
                    grads[3][lax.div(t, 2), lax.rem(t, 2), i // 2, i % 2, :, cols] = part[i * rows : (i + 1) * rows]

    def qkv_grad():
        rows = tile // 4

        @pl.loop(0, model // tile)
        def _(t):
            left, column = unit[:, span(t, tile)], columns(t)
            for p in range(3):
                cols = slice(p * width, (p + 1) * width)
                part = scaled(dot(left, dqkv[:, cols], (0, 0)), column, 0, sums[5:6, cols])
                for i in range(4):
                    grads[p][lax.div(t, 2), lax.rem(t, 2), i // 2, i % 2] = part[i * rows : (i + 1) * rows]

    def branches(which):
        into = send_half if which == 0 else own_half.at[0]

        @pl.loop(0, length // tile)
        def _(i):
            rows = span(i, tile)
            for j in range(half_cols // 512):
                cols = slice(j * 512, (j + 1) * 512)
                part = dot(mixed[rows, :], w_out[which, :, cols], (1, 0))
                part = part + dot(act[rows, :], w_wide[which, :, cols], (1, 0))
                into[rows, cols] = part.astype(BF16)

    def inwards(which):
        into = send_half if which == 0 else own_half.at[1]
        base = side(which) * half_cols
        for j in range(half_cols // 512):
            cols = slice(j * 512, (j + 1) * 512)
            far = span(side(which) * (half_cols // 512) + j, 512)
            zero = jnp.zeros((8, 512), F32)

            def step(i, carry):
                rows = span(i, tile)
                one_part = dot(dqkv[rows, 0:width], w_qkv[which, 0, cols, :], (1, 1))
                for p in (1, 2):
                    one_part = one_part + dot(
                        dqkv[rows, p * width : (p + 1) * width], w_qkv[which, p, cols, :], (1, 1)
                    )
                two_part = dot(dh[rows, :], w_wide[which, cols, :], (1, 1))
                into[rows, cols] = (one_part * rows_ref[0:1, far] + two_part * rows_ref[2:3, far]).astype(BF16)
                place = unit[rows, far].astype(F32)

                def fold(v):
                    return jnp.sum(v.reshape(tile // 8, 8, 512), axis=0)

                return (
                    carry[0] + fold(one_part * place),
                    carry[1] + fold(one_part),
                    carry[2] + fold(two_part * place),
                    carry[3] + fold(two_part),
                )

            found = lax.fori_loop(0, length // tile, step, (zero, zero, zero, zero))
            for n in range(4):
                sums[n : n + 1, far] = jnp.sum(found[n], axis=0, keepdims=True)

    def sum_core():
        return remote(sums, sums_core, sum_send.at[0], sum_recv.at[0], core_peer)

    def sum_line(k):
        return remote(
            sums, slots.at[c], sum_send.at[k], sum_recv.at[k], (s, lax.rem(c + 4 - k, 4), h)
        )

    def sum_x():
        return remote(total_own, total_x, sum_send.at[4], sum_recv.at[4], across[0])

    def sum_y():
        return remote(total_own, total_y, sum_send.at[5], sum_recv.at[5], across[1])

    kinds = range(6)
    loaded = set()

    def need(*which):
        for i in which:
            if i not in loaded:
                loads[i].wait()
                loaded.add(i)

    def parameters():
        for copy in smalls:
            copy.wait()
        rows_ref[...] = jnp.zeros_like(rows_ref)
        for i, ref in enumerate((gain_a, off_a, gain_b, off_b)):
            rows_ref[i : i + 1, :] = ref[...].astype(F32).reshape(1, model)
        low_ref[...] = rows_ref[...].astype(BF16)

    def compute_sums():
        sums[4:5, :] = jnp.sum(up[span(c, count), :].astype(F32), axis=0, keepdims=True) * 0.5
        sums[5:8, :] = jnp.zeros((3, model), F32)

    def small_copy():
        return pltpu.make_async_copy(total_own, small_out, sum_sem.at[0])

    def stage_two(m):
        for half in (0, 1):
            one(m, half).wait_recv()
            add_first(m, half)
            two(m, half).start()

    def stage_z(m):
        for half in (0, 1):
            two(m, half).wait_recv()
            add_second(m, half)
            for k in near:
                z_copy(m, half, k).start()
            keep(m, half).start()

    def stage_out(m):
        for half in (0, 1):
            for k in near:
                z_copy(m, half, k).wait_recv()
            keep(m, half).wait()
        for axis in (0, 1):
            direct(m, axis).start()

    def stage_on(m):
        direct(m, 0).wait_recv()
        onward(m, 1).start()
        direct(m, 1).wait_recv()
        onward(m, 0).start()

    def run(step):
        op, m = step[0], int(step[1]) if len(step) > 1 else None
        if op == "D":
            need(0, 1)
            down_grad()
        elif op == "P":
            need(1)
            parameters()
            compute_sums()
        elif op == "U":
            need(1, 2, 3)
            for j in range(units // 512):
                cols = slice(j * 512, (j + 1) * 512)
                sums[5:6, 3 * width + cols.start : 3 * width + cols.stop] = column_sum(dh, cols)
            up_grad()
        elif op == "Q":
            need(3, 4)
            for p in range(3):
                cols = slice(p * width, (p + 1) * width)
                sums[5:6, cols] = column_sum(dqkv, cols)
            qkv_grad()
        elif op == "O":
            need(1, 5)
            out_grad()
        elif op == "1":
            one(m, 0).start()
            one(m, 1).start()
        elif op == "B":
            need(0, 5)
            weight_load(m).wait()
            weight_load(4 + m).wait()
            branches(m)
            weight_load(2 + m).start()
            if m == 0:
                core_copy(0).start()
        elif op == "I":
            need(2, 3, 4)
            if m == 0:
                core_copy(0).wait_send()
            weight_load(2 + m).wait()
            weight_load(6 + m).wait()
            inwards(m)
            if m == 0:
                core_copy(1).start()
        elif op == "2":
            stage_two(m)
        elif op == "Z":
            stage_z(m)
        elif op == "X":
            stage_out(m)
        elif op == "N":
            stage_on(m)
        elif op == "R":
            line_start(m)
        elif op == "S":
            line_sum(m)
        elif op == "a":
            sum_core().start()
        elif op == "b":
            sum_core().wait()
            sums[0:5, :] = sums[0:5, :] + sums_core[0:5, :]
            for k in near:
                sum_line(k).start()
            slots[c] = sums[...]
        elif op == "c":
            for k in near:
                sum_line(k).wait()
            total_own[0:8, :] = slots[0] + slots[1] + slots[2] + slots[3]
            for i in range(4):
                total_own[8 + i : 9 + i, :] = slots[i, 5:6, :]
            total_own[12:16, :] = jnp.zeros((4, model), F32)
            sum_x().start()
        elif op == "d":
            sum_x().wait()
            total_own[...] = total_own[...] + total_x[...]
            sum_y().start()
        elif op == "e":
            sum_y().wait()
            total_own[...] = total_own[...] + total_y[...]
            small_copy().start()

    for step in BACK_PLAN:
        run(step)
    for m in kinds:
        for axis in (0, 1):
            onward(m, axis).wait_recv()
    small_copy().wait()
    for a in (0, 1):
        back_copy(a).wait()
        back_keep(a).wait()
        for k in near:
            row_copy(a, k).wait_send()
    core_copy(1).wait_send()
    for m in kinds:
        for half in (0, 1):
            one(m, half).wait_send()
            two(m, half).wait_send()
            for k in near:
                z_copy(m, half, k).wait_send()
        for axis in (0, 1):
            direct(m, axis).wait_send()
            onward(m, axis).wait_send()


def settle_all(act, up, unit, dh, dqkv, mixed, w_qkv, w_up, w_out, w_down, gain_a, off_a, gain_b, off_b):
    length, model = up.shape
    units, width = act.shape[1], mixed.shape[1]
    slab, count, half = model // 4, length // 4, model // 2
    dma = pltpu.SemaphoreType.DMA
    heights = (*[slab // 8] * 4, width // 8, units // 8)
    widths = (width, width, width, units, model, model)
    out_shapes = [
        (count, model), (count, model),
        (3, 4, 2, heights[0], 4 * width), (4, 2, heights[3], 4 * units),
        (4, 4, 2, heights[4], slab), (4, 4, 2, heights[5], slab),
    ]
    scratch = [dma((6,))] * 16 + [dma((36,))] * 2 + [dma((6, 2)), dma((6,)), dma((8,))]
    scratch += [dma((2,)), dma((2,)), dma((2, 3)), dma((2, 3)), dma((2,)), dma((2,)), dma((2,))]
    scratch += [dma((6,)), dma((6,)), dma((1,)), dma((4,))]
    vmem = [(length, units), (length, model), (length, model), (length, units), (length, 3 * width), (length, width)]
    vmem += [(2, units, half), (2, width, half), (2, 3, half, width)]
    shapes = list(zip(LEADS, heights, widths))
    vmem += [(l, 2, 2, 2, r, k) for l, r, k in shapes]
    vmem += [(l, 2, r, k) for l, r, k in shapes for _ in (0, 1)]
    vmem += [(l, r, k) for l, r, k in shapes for _ in (0, 1)]
    vmem += [(2, length, half), (2, length, half), (length, half), (2, 3, count, half), (2, count, half)]
    scratch += [pltpu.VMEM(v, BF16) for v in vmem]
    scratch += [pltpu.VMEM(v, F32) for v in ((8, model), (8, model), (4, 8, model), (16, model), (16, model), (16, model))]
    scratch += [pltpu.VMEM((model,), BF16)] * 4 + [pltpu.VMEM((8, model), F32), pltpu.VMEM((8, model), BF16)]
    any_space = pl.BlockSpec(memory_space=pl.ANY)
    joint, inward, q, u, o, d, small = pl.pallas_call(
        settle_body,
        out_shape=[jax.ShapeDtypeStruct(v, BF16) for v in out_shapes] + [jax.ShapeDtypeStruct((16, model), F32)],
        in_specs=[any_space] * 14,
        out_specs=[any_space] * 7,
        scratch_shapes=scratch,
        compiler_params=pltpu.CompilerParams(
            collective_id=1, has_side_effects=True, vmem_limit_bytes=63 << 20
        ),
        name="settle",
    )(act, up, unit, dh, dqkv, mixed, w_qkv, w_up, w_out, w_down, gain_a, off_a, gain_b, off_b)
    return (
        joint, inward, q.reshape(3, slab, 4 * width), u.reshape(slab, 4 * units),
        o.reshape(4 * width, slab), d.reshape(4 * units, slab), small,
    )


def finish_body(
    q_ref, u_ref, o_ref, d_ref, joint_ref, inward_ref, own_ref, up_ref,
    small_ref, bias_a, bias_b,
    q_out, u_out, o_out, d_out, y_out, g_out, v0, v1, v2, v3, v4, v5, qb_out, ub_out,
):
    q_out[...] = q_ref[...].astype(F32)
    u_out[...] = u_ref[...].astype(F32)
    o_out[...] = o_ref[...].astype(F32)
    d_out[...] = d_ref[...].astype(F32)
    wide = own_ref[...].astype(F32)
    bias = (bias_a[...].astype(F32) + bias_b[...].astype(F32)).reshape(1, wide.shape[1])
    y_out[...] = (wide + joint_ref[...].astype(F32) + bias).astype(BF16)
    centred = wide - jnp.mean(wide, axis=-1, keepdims=True)
    scale = lax.rsqrt(jnp.mean(centred * centred, axis=-1, keepdims=True) + 1e-05)
    unit = centred * scale
    inward = inward_ref[...].astype(F32)
    inward = inward - jnp.mean(inward, axis=-1, keepdims=True) - unit * jnp.mean(inward * unit, axis=-1, keepdims=True)
    g_out[...] = up_ref[...].astype(F32) + scale * inward

    @pl.when(pl.program_id(0) == 0)
    def _():
        for i, out in zip((0, 1, 4, 2, 3, 4), (v0, v1, v2, v3, v4, v5)):
            out[...] = small_ref[i : i + 1, :].reshape(out.shape)
        width, units = qb_out.shape[1] // 4, ub_out.shape[0] // 4
        for i in range(4):
            row = small_ref[8 + i : 9 + i, :]
            for p in range(3):
                qb_out[p : p + 1, i * width : (i + 1) * width] = row[:, p * width : (p + 1) * width]
            ub_out[i * units : (i + 1) * units] = row[:, 3 * width : 3 * width + units].reshape(units)


def finish_all(q, u, o, d, joint, inward, own, upstream, small, bias_a, bias_b):
    steps = 8
    arrays = [q, u, o, d, joint, inward, own, upstream]

    def spec(a):
        return pl.BlockSpec((a.shape[0] // steps, a.shape[1]), lambda i: (i, 0))

    results = [(a.shape, F32) for a in (q, u, o, d)] + [(own.shape, BF16), (own.shape, F32)]
    smalls = [(own.shape[1:], F32)] * 6 + [((3, q.shape[1]), F32), (u.shape[1:], F32)]
    results += smalls

    def whole(shape):
        return pl.BlockSpec(shape, lambda i: (0,) * len(shape))

    return pl.pallas_call(
        finish_body,
        grid=(steps,),
        out_shape=[jax.ShapeDtypeStruct(v, t) for v, t in results],
        in_specs=[spec(a) for a in arrays] + [whole(v.shape) for v in (small, bias_a, bias_b)],
        out_specs=[spec(a) for a in (q, u, o, d, own, own)] + [whole(v) for v, _ in smalls],
        compiler_params=pltpu.CompilerParams(vmem_limit_bytes=63 << 20),
        name="finish",
    )(*arrays, small, bias_a, bias_b)


def per_device(
    tokens,
    doc_lengths,
    ln1_gain,
    ln1_bias,
    qkv_weight,
    qkv_bias,
    out_weight,
    out_bias,
    ln2_gain,
    ln2_bias,
    up_weight,
    up_bias,
    down_weight,
    down_bias,
    cotangent,
):
    upstream, unit, activated, hidden_grad, projected_grad, mixed_low, w_qkv, w_up, w_out, w_down = (
        gather_all(
            tokens[0],
            cotangent[0],
            qkv_weight,
            up_weight,
            out_weight,
            down_weight,
            ln1_gain,
            ln1_bias,
            ln2_gain,
            ln2_bias,
            qkv_bias,
            up_bias,
            doc_lengths,
        )
    )

    joint, inward, qkv_out, up_out, out_out, down_out, small = settle_all(
        activated,
        upstream,
        unit,
        hidden_grad,
        projected_grad,
        mixed_low,
        w_qkv,
        w_up,
        w_out,
        w_down,
        ln1_gain,
        ln1_bias,
        ln2_gain,
        ln2_bias,
    )
    q_grad, u_grad, o_grad, d_grad, output, input_grad, *rest = finish_all(
        qkv_out.reshape(-1, qkv_out.shape[-1]),
        up_out,
        out_out,
        down_out,
        joint,
        inward,
        tokens[0],
        cotangent[0],
        small,
        out_bias,
        down_bias,
    )
    return (
        output[None],
        input_grad[None],
        rest[0],
        rest[1],
        q_grad.reshape(qkv_out.shape),
        rest[6],
        o_grad,
        rest[2],
        rest[3],
        rest[4],
        u_grad,
        rest[7],
        d_grad,
        rest[5],
    )


def solution(mesh):
    in_specs = (
        P("stream", "ctx", None),
        P("stream", None),
        P(),
        P(),
        P(None, "ctx", "head"),
        P(None, "head"),
        P("head", "ctx"),
        P(),
        P(),
        P(),
        P("ctx", "head"),
        P("head"),
        P("head", "ctx"),
        P(),
        P("stream", "ctx", None),
    )
    out_specs = (
        P("stream", "ctx", None),
        P("stream", "ctx", None),
        P(),
        P(),
        P(None, "ctx", "head"),
        P(None, "head"),
        P("head", "ctx"),
        P(),
        P(),
        P(),
        P("ctx", "head"),
        P("head"),
        P("head", "ctx"),
        P(),
    )
    split = mesh.shape["ctx"] * mesh.shape["head"]

    def whole(*arrays):
        heads, units = arrays[4].shape[2] // HEAD, arrays[10].shape[1]
        grouped = (mesh.shape["stream"], mesh.shape["ctx"], mesh.shape["head"]) == (4, 4, 2)
        fits = grouped and heads == split and units % (split * 512) == 0
        return jax.shard_map(
            per_device if fits else general_device,
            mesh=mesh,
            in_specs=in_specs,
            out_specs=out_specs,
            check_vma=False,
        )(*arrays)

    return whole
```
